32 devices in a mesh: batch: 8 (over y, x, core), rows: 4 (over z).
Axes of the slice: x: 2, y: 2, z: 4, core: 2. Of those that a mesh axis runs over, the one named last changes fastest.
Arguments:
- atoms: bfloat16 [32, 256, 512], P('batch', 'rows'), may hold values from -6 to 6
- pair_bias: bfloat16 [32, 64, 256, 256], P('batch', None, 'rows'), may hold values from -6 to 6
- lengths: int32 [32], P('batch'), may hold values from 64 to 256, as said below
- first_gain: bfloat16 [512], replicated, may hold values from 0.099609375 to 1.8984375
- first_shift: bfloat16 [512], replicated, may hold values from -3 to 3
- query_weight: bfloat16 [512, 512], replicated, may hold values from -0.25 to 0.25
- query_bias: bfloat16 [512], replicated, may hold values from -3 to 3
- key_weight: bfloat16 [512, 512], replicated, may hold values from -0.25 to 0.25
- value_weight: bfloat16 [512, 512], replicated, may hold values from -0.25 to 0.25
- value_bias: bfloat16 [512], replicated, may hold values from -3 to 3
- out_weight: bfloat16 [512, 512], replicated, may hold values from -1 to 1
- out_bias: bfloat16 [512], replicated, may hold values from -3 to 3
- second_gain: bfloat16 [512], replicated, may hold values from 0.099609375 to 1.8984375
- second_shift: bfloat16 [512], replicated, may hold values from -3 to 3
- inner_weight: bfloat16 [512, 2048], replicated, may hold values from -0.25 to 0.25
- inner_bias: bfloat16 [2048], replicated, may hold values from -3 to 3
- outer_weight: bfloat16 [2048, 512], replicated, may hold values from -0.125 to 0.125
- outer_bias: bfloat16 [512], replicated, may hold values from -3 to 3
- atoms_cotangent: bfloat16 [32, 256, 512], P('batch', 'rows'), may hold values from -6 to 6
- pair_cotangent: bfloat16 [32, 64, 256, 256], P('batch', None, 'rows'), may hold values from -6 to 6
Outputs:
- atoms_out: bfloat16 [32, 256, 512], P('batch', 'rows')
- pair_out: bfloat16 [32, 64, 256, 256], P('batch', None, 'rows')
- atoms_grad: bfloat16 [32, 256, 512], P('batch', 'rows')
- pair_grad: bfloat16 [32, 64, 256, 256], P('batch', None, 'rows')
- first_gain_grad: float32 [512], P('batch')
- first_shift_grad: float32 [512], P('batch')
- query_weight_grad: float32 [512, 512], P('batch')
- query_bias_grad: float32 [512], P('batch')
- key_weight_grad: float32 [512, 512], P('batch')
- value_weight_grad: float32 [512, 512], P('batch')
- value_bias_grad: float32 [512], P('batch')
- out_weight_grad: float32 [512, 512], P('batch')
- out_bias_grad: float32 [512], P('batch')
- second_gain_grad: float32 [512], P('batch')
- second_shift_grad: float32 [512], P('batch')
- inner_weight_grad: float32 [512, 2048], P('batch')
- inner_bias_grad: float32 [2048], P('batch')
- outer_weight_grad: float32 [2048, 512], P('batch')
- outer_bias_grad: float32 [512], P('batch')
The draws below stay inside these ranges and needn't reach their ends.
Inputs may be any that keep to these rules, and one draw needn't show every extreme that they name: Atoms at positions lengths[m] and beyond are padding and are masked as keys; of the 4 molecules at each index of batch, one (drawn from the seed) has exactly 256 atoms.
All inputs are finite; a program needn't handle non-finite values.
Results may differ from the reference program's by a relative error of at most 0.012.
Values may be sent and summed in bfloat16 or wider, within the bound.
No kernel may reach another device: no remote copies, remote signals or barrier semaphores. Data moves between devices by JAX's collectives and lax.ppermute only.
A program may use at most 128 MiB of HBM per device.

```python
from functools import partial
import jax
import jax.numpy as jnp
from jax import lax

D = 512
FF = 2048
HEADS = 64
HEAD_DIM = 8
ATOMS = 256
MOLS = 4
MOLECULES = 32


def draw_lengths(key, part):
    first_key, second_key = jax.random.split(jax.random.fold_in(key, 11))
    groups = MOLECULES // MOLS
    drawn = jax.random.randint(first_key, (groups, MOLS), ATOMS // 4, ATOMS + 1)
    chosen = jax.random.randint(second_key, (groups, 1), 0, MOLS)
    filled = jnp.arange(MOLS)[None, :] == chosen
    return jnp.where(filled, ATOMS, drawn).reshape(-1).astype(jnp.int32)


def shard_levels(own_key, shape, shards, smallest, high):
    def one(position, blocks):
        draws = jax.random.uniform(jax.random.fold_in(jax.random.fold_in(own_key, 6), position), (blocks,), jnp.float32, smallest / len(shards), high / len(shards))
        return jnp.repeat(jnp.exp(draws), shape[position] // blocks).reshape((-1,) + (1,) * (len(shape) - position - 1))

    level = one(*shards[0])
    for cut in shards[1:]:
        level = level * one(*cut)
    return level


def bell_draw(stream_key, dims, width, reach, shards=(), dtype=jnp.bfloat16):
    array = jax.random.normal(stream_key, dims, jnp.float32) * width
    if len(shards) > 0:
        array = shard_levels(stream_key, dims, shards, -0.22, 0.18) * array
    return jnp.clip(array, min=-reach, max=reach).astype(dtype)


def setup_inputs(seed: int = 0) -> dict:
    keys = jax.random.split(jax.random.key(seed), 21)
    return {
        "atoms": bell_draw(keys[0], (MOLECULES, ATOMS, D), 1.0, 6.0, ((0, 8), (1, 4))),
        "pair_bias": bell_draw(keys[1], (MOLECULES, HEADS, ATOMS, ATOMS), 1.0, 6.0, ((0, 8), (2, 4))),
        "lengths": draw_lengths(jax.random.fold_in(keys[20], 71), 0),
        "first_gain": jnp.clip(1.0 + 0.18 * jax.random.normal(keys[3], (D,), jnp.float32), 0.099609375, 1.8984375).astype(jnp.bfloat16),
        "first_shift": bell_draw(keys[4], (D,), 0.5, 3.0),
        "query_weight": bell_draw(keys[5], (D, D), D ** -0.5, 0.25),
        "query_bias": bell_draw(keys[6], (D,), 0.5, 3.0),
        "key_weight": bell_draw(keys[7], (D, D), D ** -0.5, 0.25),
        "value_weight": bell_draw(keys[8], (D, D), D ** -0.5, 0.25),
        "value_bias": bell_draw(keys[9], (D,), 0.5, 3.0),
        "out_weight": bell_draw(keys[10], (D, D), (D // 16) ** -0.5, 1.0),
        "out_bias": bell_draw(keys[11], (D,), 0.5, 3.0),
        "second_gain": jnp.clip(1.0 + 0.18 * jax.random.normal(keys[12], (D,), jnp.float32), 0.099609375, 1.8984375).astype(jnp.bfloat16),
        "second_shift": bell_draw(keys[13], (D,), 0.5, 3.0),
        "inner_weight": bell_draw(keys[14], (D, FF), D ** -0.5, 0.25),
        "inner_bias": bell_draw(keys[15], (FF,), 0.5, 3.0),
        "outer_weight": bell_draw(keys[16], (FF, D), FF ** -0.5, 0.125),
        "outer_bias": bell_draw(keys[17], (D,), 0.5, 3.0),
        "atoms_cotangent": bell_draw(keys[18], (MOLECULES, ATOMS, D), 1.0, 6.0, ((0, 8), (1, 4))),
        "pair_cotangent": bell_draw(keys[19], (MOLECULES, HEADS, ATOMS, ATOMS), 1.0, 6.0, ((0, 8), (2, 4))),
    }


EPSILON = 1e-05
MASKED = -1000000000.0
HIGHEST = lax.Precision.HIGHEST

@jax.custom_vjp
def low(v):
    return lax.optimization_barrier(v.astype(jnp.bfloat16)).astype(jnp.float32)

@jax.custom_vjp
def low_back(v):
    return v

def low_keep(v):
    return (low(v), None)

def low_pass(kept, grad):
    return (grad,)

def back_keep(v):
    return (v, None)

def back_low(kept, grad):
    return (low(grad),)
low.defvjp(low_keep, low_pass)
low_back.defvjp(back_keep, back_low)

def layer_norm(values_in, gain, shift):
    centre = values_in - lax.optimization_barrier(jnp.mean(values_in, -1, keepdims=True))
    normed = centre * lax.rsqrt(lax.optimization_barrier(jnp.mean(centre * centre, -1, keepdims=True)) + EPSILON)
    return normed * gain + shift

def product(left, right):
    return jnp.dot(left, right, precision=HIGHEST, preferred_element_type=jnp.float32)

def molecule(params, pieces):
    first_gain, first_shift, query_weight, query_bias, key_weight, value_weight, value_bias, out_weight, out_bias, second_gain, second_shift, inner_weight, inner_bias, outer_weight, outer_bias = params
    atom_rows, pair_rows, length = pieces
    hidden = low(layer_norm(atom_rows, first_gain, first_shift))
    query_rows = low_back(low(product(hidden, query_weight) + query_bias)).reshape(ATOMS, HEADS, HEAD_DIM)
    key_rows = low_back(low(product(hidden, key_weight))).reshape(ATOMS, HEADS, HEAD_DIM)
    value_rows = low_back(low(product(hidden, value_weight) + value_bias)).reshape(ATOMS, HEADS, HEAD_DIM)
    scores = low_back(HEAD_DIM ** (-0.5) * jnp.einsum('ihe,jhe->hij', query_rows, key_rows, precision=HIGHEST) + pair_rows)
    valid = jnp.arange(ATOMS) < length
    probs = low(jax.nn.softmax(jnp.where(valid[None, None, :], scores, MASKED), axis=-1))
    mixed = low_back(low(jnp.einsum('hij,jhe->ihe', probs, value_rows, precision=HIGHEST).reshape(ATOMS, D)))
    branch = low_back(product(mixed, out_weight) + out_bias)
    middle = atom_rows + branch
    second = low(layer_norm(middle, second_gain, second_shift))
    inner_pre = low_back(product(second, inner_weight) + inner_bias)
    activated = low(jax.nn.gelu(inner_pre))
    outer_part = low_back(product(activated, outer_weight) + outer_bias)
    return (middle + outer_part, scores)

def reference(atoms, pair_bias, lengths, first_gain, first_shift, query_weight, query_bias, key_weight, value_weight, value_bias, out_weight, out_bias, second_gain, second_shift, inner_weight, inner_bias, outer_weight, outer_bias, atoms_cotangent, pair_cotangent):
    params = tuple((weight.astype(jnp.float32) for weight in (first_gain, first_shift, query_weight, query_bias, key_weight, value_weight, value_bias, out_weight, out_bias, second_gain, second_shift, inner_weight, inner_bias, outer_weight, outer_bias)))

    def forward(weights, atom_values, pair_values):
        step_fn = jax.checkpoint(partial(molecule, weights))
        return lax.map(step_fn, (atom_values, pair_values, lengths))
    (atoms_new, pair_new), pullback = jax.vjp(forward, params, atoms.astype(jnp.float32), pair_bias.astype(jnp.float32))
    grads, atoms_back, pair_back = pullback((atoms_cotangent.astype(jnp.float32), pair_cotangent.astype(jnp.float32)))
    return (atoms_new.astype(jnp.bfloat16), pair_new.astype(jnp.bfloat16), atoms_back.astype(jnp.bfloat16), pair_back.astype(jnp.bfloat16), grads[0], grads[1], grads[2], grads[3], grads[4], grads[5], grads[6], grads[7], grads[8], grads[9], grads[10], grads[11], grads[12], grads[13], grads[14])
```

```python
import functools

import jax
import jax.numpy as jnp
from jax import lax
from jax.experimental import pallas as pl
from jax.experimental.pallas import tpu as pltpu
from jax.sharding import PartitionSpec as P

EPSILON = 1e-05
MASKED = -1000000000.0
F32 = jnp.float32
BF16 = jnp.bfloat16
LANES = 128


def norm_forward(values_in, gain, shift):
    centre = values_in - jnp.mean(values_in, -1, keepdims=True)
    inverse = lax.rsqrt(jnp.mean(centre * centre, -1, keepdims=True) + EPSILON)
    normed = centre * inverse
    return (normed * gain + shift, normed, inverse)


def norm_backward(upstream, normed, inverse, gain):
    scaled = upstream * gain
    return inverse * (
        scaled
        - jnp.mean(scaled, -1, keepdims=True)
        - normed * jnp.mean(scaled * normed, -1, keepdims=True)
    )


def dot(left, right):
    return jnp.dot(left, right, preferred_element_type=F32)


def across(left, right):
    return lax.dot_general(left, right, (((0,), (0,)), ((), ())), preferred_element_type=F32)


def against(left, right):
    return lax.dot_general(left, right, (((1,), (1,)), ((), ())), preferred_element_type=F32)


def column_sum(values_in):
    return jnp.sum(values_in.astype(F32), 0)


def forward_kernel(
    head_size,
    chunk,
    length_ref,
    all_ref,
    own_ref,
    pair_ref,
    gain_ref,
    shift_ref,
    query_weight_ref,
    query_bias_ref,
    key_weight_ref,
    value_weight_ref,
    value_bias_ref,
    pair_out_ref,
    weights_ref,
    mixed_ref,
    inverse_ref,
    hidden_ref,
    query_ref,
    key_ref,
    value_ref,
    query_scratch,
    key_scratch,
    value_scratch,
):
    molecule = pl.program_id(0)
    group = pl.program_id(1)
    groups, keys, width = key_scratch.shape
    heads = width // head_size
    rows, model_width = own_ref.shape[1:]
    factor = head_size**-0.5

    @pl.when(group == 0)
    def _():
        gain = gain_ref[...].astype(F32)
        shift = shift_ref[...].astype(F32)
        hidden = norm_forward(all_ref[...].reshape(keys, model_width).astype(F32), gain, shift)[0]
        hidden = hidden.astype(BF16)
        hidden_ref[...] = hidden.reshape(hidden_ref.shape)
        key_rows = dot(hidden, key_weight_ref[...]).astype(BF16)
        value_rows = dot(hidden, value_weight_ref[...]) + value_bias_ref[...].astype(F32)
        value_rows = value_rows.astype(BF16)
        own = norm_forward(own_ref[0].astype(F32), gain, shift)[0].astype(BF16)
        query_rows = dot(own, query_weight_ref[...]) + query_bias_ref[...].astype(F32)
        query_rows = (query_rows * factor).astype(BF16)
        ones = jnp.ones((keys, width), BF16)
        for t in range(groups):
            lanes = slice(t * width, (t + 1) * width)
            key_scratch[t] = key_rows[:, lanes]
            query_scratch[t] = query_rows[:, lanes]
            value_scratch[t, :, :width] = value_rows[:, lanes]
            value_scratch[t, :, width:] = ones

    query = query_scratch[group]
    key = key_scratch[group]
    value = value_scratch[group]
    query_ref[...] = query[None]
    key_ref[...] = key[None]
    value_ref[...] = value[None]
    valid = lax.broadcasted_iota(jnp.int32, (1, keys), 1) < length_ref[molecule]
    lane = lax.broadcasted_iota(jnp.int32, (1, width), 1) // head_size
    lane_pair = lax.broadcasted_iota(jnp.int32, (1, 2 * width), 1) % width // head_size
    total = jnp.zeros((rows, 2 * width), F32)
    zero = jnp.zeros((), BF16)
    for c in range(0, heads, chunk):
        here = slice(c, c + chunk)
        spread = jnp.concatenate([jnp.where(lane == c + t, query, zero) for t in range(chunk)], 0)
        scores = against(spread, key) + pair_ref[0, here].reshape(chunk * rows, keys).astype(F32)
        pair_out_ref[0, here] = scores.astype(BF16).reshape(chunk, rows, keys)
        masked = jnp.where(valid, scores, MASKED)
        weights = jnp.exp(masked - jnp.max(masked, -1, keepdims=True)).astype(BF16)
        weights_ref[0, here] = weights.reshape(chunk, rows, keys)
        product = dot(weights, value)
        for t in range(chunk):
            total = jnp.where(lane_pair == c + t, product[t * rows : (t + 1) * rows], total)
    inverse = 1.0 / total[:, width:]
    inverse_ref[...] = inverse[None]
    mixed_ref[...] = (total[:, :width] * inverse)[None]


def attention_forward(head_size, chunk, lengths, atoms_all, atoms, pair_bias, parameters):
    spans, molecules, rows, model_width = atoms_all.shape
    keys = pair_bias.shape[3]
    groups = model_width // LANES
    heads = LANES // head_size
    pair_spec = pl.BlockSpec((1, heads, rows, keys), lambda m, g, n: (m, g, 0, 0))
    row_spec = pl.BlockSpec((1, rows, LANES), lambda m, g, n: (m, 0, g))
    all_spec = pl.BlockSpec((spans, 1, rows, model_width), lambda m, g, n: (0, m, 0, 0))
    fixed = [pl.BlockSpec(a.shape, lambda m, g, n: (0, 0)) for a in parameters]
    token_shape = (molecules, rows, model_width)
    return pl.pallas_call(
        functools.partial(forward_kernel, head_size, chunk),
        grid_spec=pltpu.PrefetchScalarGridSpec(
            num_scalar_prefetch=1,
            grid=(molecules, groups),
            in_specs=[
                all_spec,
                pl.BlockSpec((1, rows, model_width), lambda m, g, n: (m, 0, 0)),
                pair_spec,
            ]
            + fixed,
            out_specs=[
                pair_spec,
                pair_spec,
                row_spec,
                row_spec,
                all_spec,
                row_spec,
                pl.BlockSpec((1, keys, LANES), lambda m, g, n: (m, 0, g)),
                pl.BlockSpec((1, keys, 2 * LANES), lambda m, g, n: (m, 0, g)),
            ],
            scratch_shapes=[
                pltpu.VMEM((groups, rows, LANES), BF16),
                pltpu.VMEM((groups, keys, LANES), BF16),
                pltpu.VMEM((groups, keys, 2 * LANES), BF16),
            ],
        ),
        out_shape=[
            jax.ShapeDtypeStruct(pair_bias.shape, BF16),
            jax.ShapeDtypeStruct(pair_bias.shape, BF16),
            jax.ShapeDtypeStruct(token_shape, F32),
            jax.ShapeDtypeStruct(token_shape, F32),
            jax.ShapeDtypeStruct(atoms_all.shape, BF16),
            jax.ShapeDtypeStruct(token_shape, BF16),
            jax.ShapeDtypeStruct((molecules, keys, model_width), BF16),
            jax.ShapeDtypeStruct((molecules, keys, 2 * model_width), BF16),
        ],
        compiler_params=pltpu.CompilerParams(vmem_limit_bytes=40 << 20),
        name="attention_forward",
    )(lengths, atoms_all, atoms, pair_bias, *parameters)


def backward_kernel(
    head_size,
    chunk,
    weights_ref,
    cotangent_ref,
    grad_mixed_ref,
    mixed_ref,
    inverse_ref,
    query_ref,
    key_ref,
    value_ref,
    pair_grad_ref,
    grad_query_ref,
    grad_key_ref,
    grad_value_ref,
):
    rows, width = query_ref.shape[1:]
    keys = key_ref.shape[1]
    heads = width // head_size
    factor = head_size**-0.5
    query = query_ref[0]
    key = key_ref[0]
    value = value_ref[0]
    upstream = (grad_mixed_ref[0].astype(F32) * inverse_ref[0]).astype(BF16)
    offset = (-(upstream.astype(F32) * mixed_ref[0])).astype(BF16)
    both = jnp.concatenate([upstream, offset], 1)
    lane = lax.broadcasted_iota(jnp.int32, (1, width), 1) // head_size
    lane_pair = lax.broadcasted_iota(jnp.int32, (1, 2 * width), 1) % width // head_size
    query_turned = jnp.transpose(query.astype(F32)).astype(BF16)
    upstream_turned = jnp.transpose(upstream.astype(F32)).astype(BF16)
    query_turned = jnp.concatenate([query_turned] * chunk, 1)
    upstream_turned = jnp.concatenate([upstream_turned] * chunk, 1)
    turned_shape = (chunk * head_size, chunk * rows)
    same = (
        lax.broadcasted_iota(jnp.int32, turned_shape, 0) // head_size
        == lax.broadcasted_iota(jnp.int32, turned_shape, 1) // rows
    )
    zero = jnp.zeros((), BF16)
    total = jnp.zeros((rows, width), F32)
    key_parts = []
    value_parts = []
    for c in range(0, heads, chunk):
        here = slice(c, c + chunk)
        feature = slice(c * head_size, (c + chunk) * head_size)
        spread = jnp.concatenate([jnp.where(lane_pair == c + t, both, zero) for t in range(chunk)], 0)
        centred = against(spread, value)
        weights = weights_ref[0, here].reshape(chunk * rows, keys)
        cotangent = cotangent_ref[0, here].reshape(chunk * rows, keys)
        grad = (weights.astype(F32) * centred + cotangent.astype(F32)).astype(BF16)
        pair_grad_ref[0, here] = grad.reshape(chunk, rows, keys)
        product = dot(grad, key)
        for t in range(chunk):
            total = jnp.where(lane == c + t, product[t * rows : (t + 1) * rows], total)
        key_parts.append(dot(jnp.where(same, query_turned[feature], zero), grad))
        value_parts.append(dot(jnp.where(same, upstream_turned[feature], zero), weights))
    grad_query_ref[...] = (total * factor).astype(BF16)[None]
    grad_key = jnp.transpose(jnp.concatenate(key_parts, 0)).astype(BF16)
    grad_value = jnp.transpose(jnp.concatenate(value_parts, 0)).astype(BF16)
    grad_key_ref[...] = grad_key.reshape(grad_key_ref.shape)
    grad_value_ref[...] = grad_value.reshape(grad_value_ref.shape)


def attention_backward(
    head_size, chunk, spans, weights, cotangent, grad_mixed, mixed, inverse, query, key, value
):
    molecules, _, rows, keys = weights.shape
    model_width = query.shape[2]
    groups = model_width // LANES
    heads = LANES // head_size
    pair_spec = pl.BlockSpec((1, heads, rows, keys), lambda m, g: (m, g, 0, 0))
    row_spec = pl.BlockSpec((1, rows, LANES), lambda m, g: (m, 0, g))
    span_spec = pl.BlockSpec((spans, 1, rows, LANES), lambda m, g: (0, m, 0, g))
    span_shape = jax.ShapeDtypeStruct((spans, molecules, rows, model_width), BF16)
    return pl.pallas_call(
        functools.partial(backward_kernel, head_size, chunk),
        grid=(molecules, groups),
        in_specs=[
            pair_spec,
            pair_spec,
            row_spec,
            row_spec,
            row_spec,
            row_spec,
            pl.BlockSpec((1, keys, LANES), lambda m, g: (m, 0, g)),
            pl.BlockSpec((1, keys, 2 * LANES), lambda m, g: (m, 0, g)),
        ],
        out_specs=[pair_spec, row_spec, span_spec, span_spec],
        out_shape=[
            jax.ShapeDtypeStruct(weights.shape, BF16),
            jax.ShapeDtypeStruct((molecules, rows, model_width), BF16),
            span_shape,
            span_shape,
        ],
        compiler_params=pltpu.CompilerParams(vmem_limit_bytes=40 << 20),
        name="attention_backward",
    )(weights, cotangent, grad_mixed, mixed, inverse, query, key, value)


def swap(value, axis, mask):
    size = lax.axis_size(axis)
    return lax.ppermute(value, axis, [(i, i ^ mask) for i in range(size)])


def gather_rows(value):
    size = lax.axis_size("rows")
    if size != 4:
        return lax.all_gather(value, "rows", axis=0, tiled=False)
    half = value.shape[0] // 2
    me = lax.axis_index("rows")
    one = swap(value, "rows", 1)
    three = swap(value, "rows", 3)
    two = jnp.concatenate([swap(one[:half], "rows", 3), swap(three[half:], "rows", 1)], 0)
    stacked = jnp.stack([value, one, two, three])
    return jnp.concatenate(
        [lax.dynamic_index_in_dim(stacked, me ^ i, 0, keepdims=True) for i in range(4)], 0
    )


def pick(value, index):
    return lax.dynamic_index_in_dim(value, index, 0, keepdims=False)


def scatter_rows(value):
    size = lax.axis_size("rows")
    if size != 4:
        return lax.psum_scatter(
            value, "rows", scatter_dimension=0, tiled=False
        ).astype(F32)
    me = lax.axis_index("rows")
    half = value.shape[1] // 2
    results = []
    for part, first, second in ((slice(0, half), 1, 3), (slice(half, None), 3, 1)):
        piece = value[:, part]
        sent = jnp.stack([pick(piece, me ^ first), pick(piece, me ^ 2)]).astype(BF16)
        came = swap(sent, "rows", first).astype(F32)
        mine = pick(piece, me) + came[0]
        other = (pick(piece, me ^ second) + came[1]).astype(BF16)
        results.append(mine + swap(other, "rows", second).astype(F32))
    return jnp.concatenate(results, 0)


def reduce_slices(value, flip):
    count = lax.axis_size("batch")
    spans = lax.axis_size("rows")
    bits = count.bit_length() - 1
    if count != 1 << bits or spans != 4:
        part = lax.psum_scatter(value, "batch", scatter_dimension=0, tiled=True)
        return lax.psum(part.astype(BF16), "rows").astype(F32)
    me = lax.axis_index("batch")
    shape = (count, value.shape[0] // count) + value.shape[1:]
    total = value.reshape(shape)
    order = [0] + (list(range(bits - 1, 0, -1)) if flip else list(range(1, bits)))
    left = list(range(bits - 1, -1, -1))
    total = total.reshape((2,) * bits + shape[1:])
    for bit in order:
        axis = left.index(bit)
        mine = (me >> bit) & 1
        sent = lax.dynamic_index_in_dim(total, 1 - mine, axis, keepdims=False).astype(BF16)
        kept = lax.dynamic_index_in_dim(total, mine, axis, keepdims=False).astype(F32)
        total = kept + swap(sent, "batch", 1 << bit).astype(F32)
        left.remove(bit)
    for mask in (3, 1) if flip else (1, 3):
        low = total.astype(BF16)
        total = low.astype(F32) + swap(low, "rows", mask).astype(F32)
    return total


def shards(
    atoms,
    pair_bias,
    lengths,
    first_gain,
    first_shift,
    query_weight,
    query_bias,
    key_weight,
    value_weight,
    value_bias,
    out_weight,
    out_bias,
    second_gain,
    second_shift,
    inner_weight,
    inner_bias,
    outer_weight,
    outer_bias,
    atoms_cotangent,
    pair_cotangent,
):
    molecules, rows, model_width = atoms.shape
    head_count = pair_bias.shape[1]
    head_size = model_width // head_count
    spans = lax.axis_size("rows")
    batch_count = lax.axis_size("batch")
    tokens = molecules * rows
    flat = lambda a: a.reshape(-1, model_width)
    atoms_all = gather_rows(atoms)
    pair_out, weights, mixed, inverse, hidden_all, query, key, value = attention_forward(
        head_size,
        4,
        lengths,
        atoms_all,
        atoms,
        pair_bias,
        (
            first_gain[None],
            first_shift[None],
            query_weight,
            query_bias[None],
            key_weight,
            value_weight,
            value_bias[None],
        ),
    )
    atoms_float = flat(atoms).astype(F32)
    mixed_low = flat(mixed).astype(BF16)
    middle = atoms_float + dot(mixed_low, out_weight) + out_bias.astype(F32)
    second_out, second_normed, second_inverse = norm_forward(
        middle, second_gain.astype(F32), second_shift.astype(F32)
    )
    second_low = second_out.astype(BF16)
    inner_pre = dot(second_low, inner_weight) + inner_bias.astype(F32)
    activated, gelu_pull = jax.vjp(jax.nn.gelu, inner_pre)
    activated_low = activated.astype(BF16)
    result_rows = middle + dot(activated_low, outer_weight) + outer_bias.astype(F32)
    atoms_out = result_rows.astype(BF16).reshape(atoms.shape)
    grad_outer = flat(atoms_cotangent)
    outer_weight_grad = across(activated_low, grad_outer)
    outer_bias_grad = column_sum(grad_outer)
    grad_activated = against(grad_outer, outer_weight)
    grad_inner = gelu_pull(grad_activated)[0].astype(BF16)
    inner_weight_grad = across(second_low, grad_inner)
    inner_bias_grad = column_sum(grad_inner)
    grad_second = against(grad_inner, inner_weight)
    second_gain_grad = jnp.sum(grad_second * second_normed, 0)
    second_shift_grad = jnp.sum(grad_second, 0)
    grad_middle = grad_outer.astype(F32) + norm_backward(
        grad_second, second_normed, second_inverse, second_gain.astype(F32)
    )
    grad_branch = grad_middle.astype(BF16)
    out_weight_grad = across(mixed_low, grad_branch)
    out_bias_grad = column_sum(grad_branch)
    grad_mixed = against(grad_branch, out_weight).astype(BF16)

    outer_weight_grad = reduce_slices(outer_weight_grad, False)
    inner_weight_grad = reduce_slices(inner_weight_grad, True)
    out_weight_grad = reduce_slices(out_weight_grad, True)

    pair_grad, query_grad, key_grad, value_grad = attention_backward(
        head_size,
        4,
        spans,
        weights,
        pair_cotangent,
        grad_mixed.reshape(atoms.shape),
        mixed,
        inverse,
        query,
        key,
        value,
    )
    query_flat, key_flat, value_flat = flat(query_grad), flat(key_grad), flat(value_grad)
    hidden_flat = flat(hidden_all)
    _, normed_all, _ = norm_forward(
        flat(atoms_all).astype(F32), first_gain.astype(F32), first_shift.astype(F32)
    )
    _, first_normed, first_inverse = norm_forward(
        atoms_float, first_gain.astype(F32), first_shift.astype(F32)
    )
    grad_shared = against(key_flat, key_weight) + against(value_flat, value_weight)
    grad_local = against(query_flat, query_weight)
    grad_first = (
        scatter_rows(grad_shared.reshape((spans,) + atoms.shape)).reshape(tokens, model_width)
        + grad_local
    )
    hidden_own = flat(lax.dynamic_index_in_dim(hidden_all, lax.axis_index("rows"), 0))
    query_weight_grad = reduce_slices(across(hidden_own, query_flat), False)
    key_weight_grad = reduce_slices(across(hidden_flat, key_flat), False)
    value_weight_grad = reduce_slices(across(hidden_flat, value_flat), True)
    vectors = [
        jnp.sum(grad_shared * normed_all, 0) + jnp.sum(grad_local * first_normed, 0),
        jnp.sum(grad_shared, 0) + jnp.sum(grad_local, 0),
        column_sum(query_flat),
        column_sum(value_flat),
        out_bias_grad,
        second_gain_grad,
        second_shift_grad,
        inner_bias_grad,
        outer_bias_grad,
    ]
    packed = jnp.concatenate([v.reshape(batch_count, -1) for v in vectors], 1)
    packed = reduce_slices(packed, True)[0]
    small = []
    start = 0
    for v in vectors:
        size = v.shape[0] // batch_count
        small.append(packed[start : start + size])
        start += size
    atoms_grad = grad_middle + norm_backward(
        grad_first, first_normed, first_inverse, first_gain.astype(F32)
    )
    return (
        atoms_out,
        pair_out,
        atoms_grad.astype(BF16).reshape(atoms.shape),
        pair_grad,
        small[0],
        small[1],
        query_weight_grad,
        small[2],
        key_weight_grad,
        value_weight_grad,
        small[3],
        out_weight_grad,
        small[4],
        small[5],
        small[6],
        inner_weight_grad,
        small[7],
        outer_weight_grad,
        small[8],
    )


def solution(mesh):
    tokens = P("batch", "rows", None)
    pairs = P("batch", None, "rows", None)
    vector = P("batch")
    matrix = P("batch", None)
    return jax.shard_map(
        shards,
        mesh=mesh,
        in_specs=(tokens, pairs, P("batch")) + (P(),) * 15 + (tokens, pairs),
        out_specs=(
            tokens,
            pairs,
            tokens,
            pairs,
            vector,
            vector,
            matrix,
            vector,
            matrix,
            matrix,
            vector,
            matrix,
            vector,
            vector,
            vector,
            matrix,
            vector,
            matrix,
            vector,
        ),
        check_vma=False,
    )
```

```python
import functools
import math

import jax
import jax.numpy as jnp
from jax import lax
from jax.experimental import pallas as pl
from jax.experimental.pallas import tpu as pltpu
from jax.sharding import PartitionSpec as P

EPSILON = 1e-05
MASKED = -1000000000.0
F32 = jnp.float32
BF16 = jnp.bfloat16
LANES = 128
STAGES = 2
VMEM_LIMIT = 56 << 20


def shape_of(shape, dtype):
    return jax.ShapeDtypeStruct(tuple(shape), dtype)


def norm_forward(values_in, gain, shift):
    centre = values_in - jnp.mean(values_in, -1, keepdims=True)
    inverse = lax.rsqrt(jnp.mean(centre * centre, -1, keepdims=True) + EPSILON)
    normed = centre * inverse
    return (normed * gain + shift, normed, inverse)


def norm_backward(upstream, normed, inverse, gain):
    scaled = upstream * gain
    return inverse * (
        scaled
        - jnp.mean(scaled, -1, keepdims=True)
        - normed * jnp.mean(scaled * normed, -1, keepdims=True)
    )


def dot(left, right):
    return jnp.dot(left, right, preferred_element_type=F32)


def across(left, right):
    return lax.dot_general(left, right, (((0,), (0,)), ((), ())), preferred_element_type=F32)


def against(left, right):
    return lax.dot_general(left, right, (((1,), (1,)), ((), ())), preferred_element_type=F32)


def column_sum(values_in):
    return jnp.sum(values_in.astype(F32), 0, keepdims=True)


def whole(array):
    return pl.BlockSpec(array.shape, lambda *_: (0,) * array.ndim)


def params(**extra):
    return pltpu.CompilerParams(vmem_limit_bytes=VMEM_LIMIT, **extra)


def forward_kernel(
    head_size,
    chunk,
    place_ref,
    length_ref,
    own_ref,
    one_ref,
    two_ref,
    three_ref,
    pair_ref,
    gain_ref,
    shift_ref,
    query_weight_ref,
    query_bias_ref,
    key_weight_ref,
    value_weight_ref,
    value_bias_ref,
    _,
    pair_out_ref,
    weights_ref,
    mixed_ref,
    inverse_ref,
    hidden_ref,
    normed_ref,
    query_ref,
    key_ref,
    value_ref,
    atoms_scratch,
    query_scratch,
    key_scratch,
    value_scratch,
    *,
    first,
):
    molecule = pl.program_id(0)
    group = pl.program_id(1)
    groups, keys, width = key_scratch.shape
    heads = width // head_size
    rows = own_ref.shape[1]
    factor = head_size**-0.5
    row = place_ref[1]

    @pl.when(group == 0)
    def _():
        for i, piece in enumerate((own_ref, one_ref, two_ref, three_ref)):
            start = pl.multiple_of((row ^ i) * rows, rows)
            atoms_scratch[pl.ds(start, rows)] = piece[0]
        gain = gain_ref[...].astype(F32)
        shift = shift_ref[...].astype(F32)
        hidden, normed, _ = norm_forward(atoms_scratch[...].astype(F32), gain, shift)
        hidden = hidden.astype(BF16)
        hidden_ref[0] = hidden
        normed_ref[0] = normed.astype(BF16)
        key_rows = dot(hidden, key_weight_ref[...]).astype(BF16)
        value_rows = dot(hidden, value_weight_ref[...]) + value_bias_ref[...].astype(F32)
        value_rows = value_rows.astype(BF16)
        own = norm_forward(own_ref[0].astype(F32), gain, shift)[0].astype(BF16)
        query_rows = dot(own, query_weight_ref[...]) + query_bias_ref[...].astype(F32)
        query_rows = (query_rows * factor).astype(BF16)
        ones = jnp.ones((keys, width), BF16)
        for t in range(groups):
            lanes = slice(t * width, (t + 1) * width)
            key_scratch[t] = key_rows[:, lanes]
            query_scratch[t] = query_rows[:, lanes]
            value_scratch[t, :, :width] = value_rows[:, lanes]
            value_scratch[t, :, width:] = ones

    query = query_scratch[group]
    key = key_scratch[group]
    value = value_scratch[group]
    query_ref[...] = query[None]
    key_ref[...] = key[None]
    value_ref[...] = value[None]
    valid = lax.broadcasted_iota(jnp.int32, (1, keys), 1) < length_ref[molecule + first]
    lane = lax.broadcasted_iota(jnp.int32, (1, width), 1) // head_size
    lane_pair = lax.broadcasted_iota(jnp.int32, (1, 2 * width), 1) % width // head_size
    total = jnp.zeros((rows, 2 * width), F32)
    zero = jnp.zeros((), BF16)
    for c in range(0, heads, chunk):
        here = slice(c, c + chunk)
        spread = jnp.concatenate([jnp.where(lane == c + t, query, zero) for t in range(chunk)], 0)
        scores = against(spread, key) + pair_ref[0, here].reshape(chunk * rows, keys).astype(F32)
        pair_out_ref[0, here] = scores.astype(BF16).reshape(chunk, rows, keys)
        masked = jnp.where(valid, scores, MASKED)
        weights = jnp.exp(masked - jnp.max(masked, -1, keepdims=True)).astype(BF16)
        weights_ref[0, here] = weights.reshape(chunk, rows, keys)
        product = dot(weights, value)
        for t in range(chunk):
            total = jnp.where(lane_pair == c + t, product[t * rows : (t + 1) * rows], total)
    inverse = 1.0 / total[:, width:]
    inverse_ref[...] = inverse[None]
    mixed_ref[...] = (total[:, :width] * inverse)[None]


def attention_forward(head_size, first, count, place, lengths, pieces, pair_bias, parameters, held):
    _, _, rows, keys = pair_bias.shape
    model_width = pieces[0].shape[2]
    groups = model_width // LANES
    heads = LANES // head_size
    pair_spec = pl.BlockSpec((1, heads, rows, keys), lambda m, g, *_: (m + first, g, 0, 0))
    stage_spec = pl.BlockSpec((1, heads, rows, keys), lambda m, g, *_: (m, g, 0, 0))
    row_spec = pl.BlockSpec((1, rows, LANES), lambda m, g, *_: (m, 0, g))
    all_spec = pl.BlockSpec((1, keys, model_width), lambda m, g, *_: (m, 0, 0))
    piece_specs = [
        pl.BlockSpec(
            (1, rows, model_width), lambda m, g, *_, base=first if i == 0 else 0: (m + base, 0, 0)
        )
        for i in range(len(pieces))
    ]
    token_shape = (count, rows, model_width)
    key_shape = (count, keys, model_width)
    elements = count * pair_bias.shape[1] * rows * keys
    operands = (place, lengths, *pieces, pair_bias, *parameters, held)
    return pl.pallas_call(
        functools.partial(forward_kernel, head_size, 4, first=first),
        grid_spec=pltpu.PrefetchScalarGridSpec(
            num_scalar_prefetch=2,
            grid=(count, groups),
            in_specs=piece_specs
            + [pair_spec]
            + [whole(a) for a in parameters]
            + [pl.BlockSpec(memory_space=pl.ANY)],
            out_specs=[
                pair_spec,
                stage_spec,
                row_spec,
                row_spec,
                all_spec,
                all_spec,
                row_spec,
                pl.BlockSpec((1, keys, LANES), lambda m, g, *_: (m, 0, g)),
                pl.BlockSpec((1, keys, 2 * LANES), lambda m, g, *_: (m, 0, g)),
            ],
            scratch_shapes=[
                pltpu.VMEM((keys, model_width), BF16),
                pltpu.VMEM((groups, rows, LANES), BF16),
                pltpu.VMEM((groups, keys, LANES), BF16),
                pltpu.VMEM((groups, keys, 2 * LANES), BF16),
            ],
        ),
        out_shape=[
            shape_of(pair_bias.shape, BF16),
            shape_of((count,) + pair_bias.shape[1:], BF16),
            shape_of(token_shape, F32),
            shape_of(token_shape, F32),
            shape_of(key_shape, BF16),
            shape_of(key_shape, BF16),
            shape_of(token_shape, BF16),
            shape_of(key_shape, BF16),
            shape_of((count, keys, 2 * model_width), BF16),
        ],
        input_output_aliases={} if held.ndim == 1 else {len(operands) - 1: 0},
        compiler_params=params(),
        cost_estimate=pl.CostEstimate(
            flops=elements * 2 * 384, transcendentals=elements, bytes_accessed=elements * 6
        ),
        name="attention_forward",
    )(*operands)


def dense_kernel(
    mixed_count,
    place_ref,
    *refs,
):
    mixed_refs = refs[:mixed_count]
    (
        atoms_ref,
        cotangent_ref,
        out_weight_ref,
        out_bias_ref,
        gain_ref,
        shift_ref,
        inner_weight_ref,
        inner_bias_ref,
        outer_weight_ref,
        outer_bias_ref,
        atoms_out_ref,
        outer_send_ref,
        outer_keep_ref,
        inner_send_ref,
        inner_keep_ref,
        out_send_ref,
        out_keep_ref,
        grad_middle_ref,
        grad_mixed_ref,
        vectors_ref,
        hidden_scratch,
        turned_scratch,
        normed_scratch,
        inverse_scratch,
        result_scratch,
        upstream_scratch,
        outer_scratch,
        inner_scratch,
    ) = refs[mixed_count:]
    step = pl.program_id(0)
    steps = pl.num_programs(0)
    core = place_ref[2]
    tokens, model_width = hidden_scratch.shape
    cotangent = cotangent_ref[...].reshape(tokens, model_width)

    def mixed_rows():
        return jnp.concatenate([m[...].reshape(-1, model_width) for m in mixed_refs], 0)

    @pl.when(step == 0)
    def _():
        mixed_low = mixed_rows().astype(BF16)
        middle = (
            atoms_ref[...].reshape(tokens, model_width).astype(F32)
            + dot(mixed_low, out_weight_ref[...])
            + out_bias_ref[...].astype(F32)
        )
        hidden, normed, inverse = norm_forward(
            middle, gain_ref[...].astype(F32), shift_ref[...].astype(F32)
        )
        hidden_scratch[...] = hidden.astype(BF16)
        turned_scratch[...] = jnp.transpose(hidden).astype(BF16)
        normed_scratch[...] = normed
        inverse_scratch[...] = inverse
        result_scratch[...] = middle + outer_bias_ref[...].astype(F32)
        upstream_scratch[...] = jnp.zeros_like(upstream_scratch)
        vectors_ref[0:1] = column_sum(cotangent)

    hidden = hidden_scratch[...]
    pre = dot(hidden, inner_weight_ref[...]) + inner_bias_ref[...].astype(F32)
    slope = math.sqrt(2.0 / math.pi)
    square = pre * pre
    tanh = jnp.tanh(slope * (pre + 0.044715 * (pre * square)))
    half = 0.5 * (1.0 + tanh)
    active = (pre * half).astype(BF16)
    result_scratch[...] += dot(active, outer_weight_ref[...])
    derivative = half + (0.5 * slope) * pre * (1.0 - tanh * tanh) * (1.0 + 0.134145 * square)
    grad_pre = against(cotangent, outer_weight_ref[...]) * derivative
    vectors_ref[pl.ds(4 + step, 1)] = column_sum(grad_pre.astype(BF16))
    grad_pre = grad_pre.astype(BF16)
    outer_scratch[...] = across(active, cotangent).reshape(outer_scratch.shape)
    outer_send_ref[...] = outer_scratch[:, 1 - core].astype(BF16).reshape(outer_send_ref.shape)
    outer_keep_ref[...] = outer_scratch[:, core].astype(BF16).reshape(outer_keep_ref.shape)
    inner_scratch[...] = dot(turned_scratch[...], grad_pre).reshape(inner_scratch.shape)
    inner_send_ref[:, 0] = inner_scratch[:, 1 - core].astype(BF16)
    inner_keep_ref[:, 0] = inner_scratch[:, core].astype(BF16)
    upstream_scratch[...] += against(grad_pre, inner_weight_ref[...])

    @pl.when(step == steps - 1)
    def _():
        atoms_out_ref[...] = result_scratch[...].astype(BF16).reshape(atoms_out_ref.shape)
        upstream = upstream_scratch[...]
        normed = normed_scratch[...]
        vectors_ref[1:2] = column_sum(upstream * normed)
        vectors_ref[2:3] = column_sum(upstream)
        grad_middle = cotangent.astype(F32) + norm_backward(
            upstream, normed, inverse_scratch[...], gain_ref[...].astype(F32)
        )
        grad_middle_ref[...] = grad_middle.reshape(grad_middle_ref.shape)
        branch = grad_middle.astype(BF16)
        vectors_ref[3:4] = column_sum(branch)
        grad_mixed = against(branch, out_weight_ref[...]).astype(BF16)
        grad_mixed_ref[...] = grad_mixed.reshape(grad_mixed_ref.shape)
        turned = jnp.transpose(mixed_rows()).astype(BF16)
        inner_scratch[...] = dot(turned, branch).reshape(inner_scratch.shape)
        out_send_ref[...] = inner_scratch[:, 1 - core].astype(BF16)
        out_keep_ref[...] = inner_scratch[:, core].astype(BF16)


def dense(place, mixed, atoms, cotangent, parameters, batch_count):
    (
        out_weight,
        out_bias,
        gain,
        shift,
        inner_weight,
        inner_bias,
        outer_weight,
        outer_bias,
    ) = parameters
    model_width, inner_width = inner_weight.shape
    tokens = atoms.shape[0] * atoms.shape[1]
    width = model_width
    steps = inner_width // width
    pairs = batch_count // 2
    outer_rows = inner_width // batch_count
    outer_pairs = width // (2 * outer_rows)
    own_rows = model_width // batch_count
    operands = (
        place,
        *mixed,
        atoms,
        cotangent,
        out_weight,
        out_bias,
        gain,
        shift,
        inner_weight,
        inner_bias,
        outer_weight,
        outer_bias,
    )
    outer_spec = pl.BlockSpec((outer_pairs, outer_rows, model_width), lambda s, *_: (s, 0, 0))
    inner_spec = pl.BlockSpec((pairs, 1, own_rows, width), lambda s, *_: (0, s, 0, 0))
    outer_shape = shape_of((pairs, outer_rows, model_width), BF16)
    inner_shape = shape_of((pairs, steps, own_rows, width), BF16)
    out_shape = shape_of((pairs, own_rows, model_width), BF16)
    out_shapes = [
        shape_of(atoms.shape, BF16),
        outer_shape,
        outer_shape,
        inner_shape,
        inner_shape,
        out_shape,
        out_shape,
        shape_of(atoms.shape, F32),
        shape_of(atoms.shape, BF16),
        shape_of((4 + steps, model_width), F32),
    ]
    fixed = lambda s: pl.BlockSpec(s.shape, lambda *_: (0,) * len(s.shape))
    out_specs = [fixed(s) for s in out_shapes]
    out_specs[1:5] = [outer_spec, outer_spec, inner_spec, inner_spec]
    in_specs = [whole(a) for a in operands[1:]]
    in_specs[-4] = pl.BlockSpec((model_width, width), lambda s, *_: (0, s))
    in_specs[-3] = pl.BlockSpec((1, width), lambda s, *_: (0, s))
    in_specs[-2] = pl.BlockSpec((width, model_width), lambda s, *_: (s, 0))
    return pl.pallas_call(
        functools.partial(dense_kernel, len(mixed)),
        grid_spec=pltpu.PrefetchScalarGridSpec(
            num_scalar_prefetch=1,
            grid=(steps,),
            in_specs=in_specs,
            out_specs=out_specs,
            scratch_shapes=[
                pltpu.VMEM((tokens, model_width), BF16),
                pltpu.VMEM((model_width, tokens), BF16),
                pltpu.VMEM((tokens, model_width), F32),
                pltpu.VMEM((tokens, 1), F32),
                pltpu.VMEM((tokens, model_width), F32),
                pltpu.VMEM((tokens, model_width), F32),
                pltpu.VMEM((outer_pairs, 2, outer_rows, model_width), F32),
                pltpu.VMEM((pairs, 2, own_rows, width), F32),
            ],
        ),
        out_shape=out_shapes,
        compiler_params=params(),
        cost_estimate=pl.CostEstimate(
            flops=12 * tokens * model_width * inner_width,
            transcendentals=tokens * inner_width,
            bytes_accessed=12 * model_width * inner_width,
        ),
        name="dense",
    )(*operands)


def backward_kernel(
    head_size,
    chunk,
    place_ref,
    weights_ref,
    cotangent_ref,
    grad_mixed_ref,
    mixed_ref,
    inverse_ref,
    query_ref,
    key_ref,
    value_ref,
    hidden_ref,
    normed_ref,
    query_weight_ref,
    key_weight_ref,
    value_weight_ref,
    _after,
    _held,
    pair_grad_ref,
    near_ref,
    cross_ref,
    own_ref,
    send_ref,
    keep_ref,
    vectors_ref,
    grad_query_scratch,
    grad_key_scratch,
    grad_value_scratch,
    total_scratch,
    grad_scratch,
):
    molecule = pl.program_id(0)
    group = pl.program_id(1)
    rows, width = query_ref.shape[1:]
    keys = key_ref.shape[1]
    groups = grad_key_scratch.shape[0]
    heads = width // head_size
    factor = head_size**-0.5
    query = query_ref[0]
    key = key_ref[0]
    value = value_ref[0]
    upstream = (grad_mixed_ref[0].astype(F32) * inverse_ref[0]).astype(BF16)
    offset = (-(upstream.astype(F32) * mixed_ref[0])).astype(BF16)
    both = jnp.concatenate([upstream, offset], 1)
    lane = lax.broadcasted_iota(jnp.int32, (1, width), 1) // head_size
    lane_pair = lax.broadcasted_iota(jnp.int32, (1, 2 * width), 1) % width // head_size
    query_turned = jnp.transpose(query.astype(F32)).astype(BF16)
    upstream_turned = jnp.transpose(upstream.astype(F32)).astype(BF16)
    query_turned = jnp.concatenate([query_turned] * chunk, 1)
    upstream_turned = jnp.concatenate([upstream_turned] * chunk, 1)
    turned_shape = (chunk * head_size, chunk * rows)
    same = (
        lax.broadcasted_iota(jnp.int32, turned_shape, 0) // head_size
        == lax.broadcasted_iota(jnp.int32, turned_shape, 1) // rows
    )
    zero = jnp.zeros((), BF16)
    total = jnp.zeros((rows, width), F32)
    key_parts = []
    value_parts = []
    for c in range(0, heads, chunk):
        here = slice(c, c + chunk)
        feature = slice(c * head_size, (c + chunk) * head_size)
        spread = jnp.concatenate([jnp.where(lane_pair == c + t, both, zero) for t in range(chunk)], 0)
        centred = against(spread, value)
        weights = weights_ref[0, here].reshape(chunk * rows, keys)
        cotangent = cotangent_ref[0, here].reshape(chunk * rows, keys)
        grad = (weights.astype(F32) * centred + cotangent.astype(F32)).astype(BF16)
        pair_grad_ref[0, here] = grad.reshape(chunk, rows, keys)
        product = dot(grad, key)
        for t in range(chunk):
            total = jnp.where(lane == c + t, product[t * rows : (t + 1) * rows], total)
        key_parts.append(dot(jnp.where(same, query_turned[feature], zero), grad))
        value_parts.append(dot(jnp.where(same, upstream_turned[feature], zero), weights))
    grad_query_scratch[group] = (total * factor).astype(BF16)
    grad_key_scratch[group] = jnp.transpose(jnp.concatenate(key_parts, 0)).astype(BF16)
    grad_value_scratch[group] = jnp.transpose(jnp.concatenate(value_parts, 0)).astype(BF16)

    @pl.when((molecule == 0) & (group == 0))
    def _():
        total_scratch[...] = jnp.zeros_like(total_scratch)
        vectors_ref[...] = jnp.zeros_like(vectors_ref)

    @pl.when(group == groups - 1)
    def _():
        row = place_ref[1]
        mine = pl.ds(pl.multiple_of(row * rows, rows), rows)
        join = lambda ref: jnp.concatenate([ref[t] for t in range(groups)], 1)
        grad_query = join(grad_query_scratch)
        grad_key = join(grad_key_scratch)
        grad_value = join(grad_value_scratch)
        hidden_turned = jnp.transpose(hidden_ref[0].astype(F32)).astype(BF16)
        own_turned = jnp.transpose(hidden_ref[0, mine].astype(F32)).astype(BF16)
        part_shape = (total_scratch.shape[0],) + total_scratch.shape[2:]
        total_scratch[:, 0] += dot(own_turned, grad_query).reshape(part_shape)
        total_scratch[:, 1] += dot(hidden_turned, grad_key).reshape(part_shape)
        total_scratch[:, 2] += dot(hidden_turned, grad_value).reshape(part_shape)
        grad_scratch[...] = against(grad_key, key_weight_ref[...]) + against(
            grad_value, value_weight_ref[...]
        )
        grad_scratch[mine] += against(grad_query, query_weight_ref[...])
        grad = grad_scratch[...]
        vectors_ref[0:1] += column_sum(grad * normed_ref[0].astype(F32))
        vectors_ref[1:2] += column_sum(grad)
        vectors_ref[2:3] += column_sum(grad_query)
        vectors_ref[3:4] += column_sum(grad_value)
        at = lambda other: pl.ds(pl.multiple_of((row ^ other) * rows, rows), rows)
        near_ref[0, 0] = grad_scratch[at(1)].astype(BF16)
        near_ref[1, 0] = grad_scratch[at(3)].astype(BF16)
        cross_ref[0] = grad_scratch[at(2)].astype(BF16)
        own_ref[0] = grad_scratch[mine]

    @pl.when((molecule == pl.num_programs(0) - 1) & (group == groups - 1))
    def _():
        core = place_ref[2]
        pairs, parts, count = send_ref.shape[0], send_ref.shape[1], 2
        for i in range(pairs):
            for j in range(parts):
                send_ref[i, j] = total_scratch[i * count + (1 - core), j].astype(BF16)
                keep_ref[i, j] = total_scratch[i * count + core, j].astype(BF16)


def attention_backward(
    head_size,
    first,
    place,
    stage,
    cotangent,
    grad_mixed,
    parameters,
    held,
    batch_count,
    after,
):
    weights, mixed, inverse, hidden, normed, query, key, value = stage
    count, _, rows, keys = weights.shape
    model_width = query.shape[2]
    groups = model_width // LANES
    heads = LANES // head_size
    pairs = batch_count // 2
    own_rows = model_width // batch_count
    stage_spec = pl.BlockSpec((1, heads, rows, keys), lambda m, g, *_: (m, g, 0, 0))
    pair_spec = pl.BlockSpec((1, heads, rows, keys), lambda m, g, *_: (m + first, g, 0, 0))
    row_spec = pl.BlockSpec((1, rows, LANES), lambda m, g, *_: (m, 0, g))
    all_spec = pl.BlockSpec((1, keys, model_width), lambda m, g, *_: (m, 0, 0))
    part_shape = shape_of((pairs, 3, own_rows, model_width), BF16)
    part_spec = pl.BlockSpec(part_shape.shape, lambda m, g, *_: (0, 0, 0, 0))
    token_spec = pl.BlockSpec((1, rows, model_width), lambda m, g, *_: (m, 0, 0))
    elements = math.prod(weights.shape)
    operands = (
        place,
        weights,
        cotangent,
        grad_mixed,
        mixed,
        inverse,
        query,
        key,
        value,
        hidden,
        normed,
        *parameters,
        after,
        held,
    )
    return pl.pallas_call(
        functools.partial(backward_kernel, head_size, 4),
        grid_spec=pltpu.PrefetchScalarGridSpec(
            num_scalar_prefetch=1,
            grid=(count, groups),
            in_specs=[
                stage_spec,
                pair_spec,
                pl.BlockSpec((1, rows, LANES), lambda m, g, *_: (m + first, 0, g)),
                row_spec,
                row_spec,
                row_spec,
                pl.BlockSpec((1, keys, LANES), lambda m, g, *_: (m, 0, g)),
                pl.BlockSpec((1, keys, 2 * LANES), lambda m, g, *_: (m, 0, g)),
                all_spec,
                all_spec,
            ]
            + [whole(a) for a in parameters]
            + [pl.BlockSpec(memory_space=pl.ANY)] * 2,
            out_specs=[
                pair_spec,
                pl.BlockSpec((2, 1, rows, model_width), lambda m, g, *_: (0, m, 0, 0)),
                token_spec,
                token_spec,
                part_spec,
                part_spec,
                pl.BlockSpec((8, model_width), lambda m, g, *_: (0, 0)),
            ],
            scratch_shapes=[
                pltpu.VMEM((groups, rows, LANES), BF16),
                pltpu.VMEM((groups, keys, LANES), BF16),
                pltpu.VMEM((groups, keys, LANES), BF16),
                pltpu.VMEM((batch_count, 3, own_rows, model_width), F32),
                pltpu.VMEM((keys, model_width), F32),
            ],
        ),
        out_shape=[
            shape_of(cotangent.shape, BF16),
            shape_of((2, count, rows, model_width), BF16),
            shape_of((count, rows, model_width), BF16),
            shape_of((count, rows, model_width), F32),
            part_shape,
            part_shape,
            shape_of((8, model_width), F32),
        ],
        input_output_aliases={} if held.ndim == 1 else {len(operands) - 1: 0},
        compiler_params=params(),
        cost_estimate=pl.CostEstimate(
            flops=elements * 2 * 768, transcendentals=0, bytes_accessed=elements * 6
        ),
        name="attention_backward",
    )(*operands)


def swap(value, axis, mask):
    size = lax.axis_size(axis)
    return lax.ppermute(value, axis, [(i, i ^ mask) for i in range(size)])


def first_sum_kernel(counts, place_ref, *refs):
    terms = sum(counts)
    mine_ref, other_ref = refs[terms : terms + 2]
    along_x_ref, along_y_ref, keep_x_ref, keep_y_ref, vectors_ref = refs[terms + 2 :]
    x, y = place_ref[3], place_ref[4]
    half = along_x_ref.shape[2]
    slots = keep_x_ref.shape[1]
    slot = 0
    start = 0
    for count in counts:
        group = refs[start : start + count]
        start += count
        for s in range(group[0].shape[1]):

            def total(at, lanes):
                values = [r[at, s, :, lanes].astype(F32) for r in group]
                return functools.reduce(lambda a, b: a + b, values)

            low, high = slice(0, half), slice(half, None)
            for k in range(2):
                along_x_ref[k * slots + slot] = total(2 * k + (1 - x), low).astype(BF16)
                keep_x_ref[k, slot] = total(2 * k + x, low)
                along_y_ref[k * slots + slot] = total(2 * (1 - y) + k, high).astype(BF16)
                keep_y_ref[k, slot] = total(2 * y + k, high)
            slot += 1
    vectors = (mine_ref[...] + other_ref[...]).astype(BF16)
    vectors_ref[...] = vectors
    put_vectors(vectors, along_x_ref, along_y_ref)


def put_vectors(vectors, low_ref, high_ref):
    count = vectors.shape[0]
    for ref, lanes in ((low_ref, vectors[:, : vectors.shape[1] // 2]), (high_ref, vectors[:, vectors.shape[1] // 2 :])):
        last = ref.shape[0] - 1
        ref[last] = jnp.zeros(ref.shape[1:], ref.dtype)
        ref[last, :count] = lanes


def get_vectors(low_ref, high_ref, count):
    last = low_ref.shape[0] - 1
    return jnp.concatenate([low_ref[last, :count], high_ref[last, :count]], 1).astype(F32)


def second_sum_kernel(
    place_ref,
    keep_x_ref,
    came_x_ref,
    keep_y_ref,
    came_y_ref,
    vectors_ref,
    send_y_ref,
    send_x_ref,
    left_x_ref,
    left_y_ref,
    vectors_out_ref,
):
    slots = keep_x_ref.shape[1]
    for keep, came, send, left, me in (
        (keep_x_ref, came_x_ref, send_y_ref, left_x_ref, place_ref[4]),
        (keep_y_ref, came_y_ref, send_x_ref, left_y_ref, place_ref[3]),
    ):
        for s in range(slots):
            send[s] = (keep[1 - me, s] + came[(1 - me) * slots + s].astype(F32)).astype(BF16)
            left[s] = keep[me, s] + came[me * slots + s].astype(F32)
    count = vectors_ref.shape[0]
    vectors = vectors_ref[...].astype(F32) + get_vectors(came_x_ref, came_y_ref, count)
    vectors = vectors.astype(BF16)
    vectors_out_ref[...] = vectors
    put_vectors(vectors, send_y_ref, send_x_ref)


def third_sum_kernel(left_x_ref, came_x_ref, left_y_ref, came_y_ref, vectors_ref, total_ref):
    slots = left_x_ref.shape[0]
    half = left_x_ref.shape[2]
    for s in range(slots):
        total_ref[s, :, :half] = (left_x_ref[s] + came_x_ref[s].astype(F32)).astype(BF16)
        total_ref[s, :, half:] = (left_y_ref[s] + came_y_ref[s].astype(F32)).astype(BF16)
    count = vectors_ref.shape[0]
    vectors = vectors_ref[...].astype(F32) + get_vectors(came_x_ref, came_y_ref, count)
    total_ref[slots] = jnp.zeros(total_ref.shape[1:], BF16)
    total_ref[slots, :count] = vectors.astype(BF16)


def small_call(kernel, place, operands, out_shapes, name, after=()):
    ahead = 0 if place is None else 1
    count = len(operands)

    def body(*refs):
        kernel(*refs[: ahead + count], *refs[ahead + count + len(after) :])

    fixed = lambda s: pl.BlockSpec(s.shape, lambda *_: (0,) * len(s.shape))
    size = sum(math.prod(a.shape) * a.dtype.itemsize for a in list(operands) + list(out_shapes))
    return pl.pallas_call(
        body,
        grid_spec=pltpu.PrefetchScalarGridSpec(
            num_scalar_prefetch=ahead,
            grid=(1,),
            in_specs=[fixed(a) for a in operands] + [pl.BlockSpec(memory_space=pl.ANY)] * len(after),
            out_specs=[fixed(s) for s in out_shapes],
        ),
        out_shape=out_shapes,
        compiler_params=params(),
        cost_estimate=pl.CostEstimate(flops=0, transcendentals=0, bytes_accessed=size),
        name=name,
    )(*(() if place is None else (place,)), *operands, *after)


def sum_core(place, groups, vectors, name, after=()):
    groups = [list(g) + [swap(a, "batch", 1) for a in sent] for g, sent in groups]
    vectors_other = swap(vectors, "batch", 1)
    slots = sum(g[0].shape[1] for g in groups)
    _, _, rows, width = groups[0][0].shape
    half = width // 2
    counts = tuple(len(g) for g in groups)
    message = shape_of((2 * slots + 1, rows, half), BF16)
    kept = shape_of((2, slots, rows, half), F32)
    along_x, along_y, keep_x, keep_y, vectors = small_call(
        functools.partial(first_sum_kernel, counts),
        place,
        [a for g in groups for a in g] + [vectors, vectors_other],
        [message, message, kept, kept, shape_of(vectors.shape, BF16)],
        name + "_sum_core",
        after,
    )
    came_x, came_y = swap(along_x, "batch", 2), swap(along_y, "batch", 4)
    return (keep_x, came_x, keep_y, came_y, vectors), along_x


def sum_first(place, pieces, name, after=()):
    keep_x, _, _, _, vectors = pieces
    _, slots, rows, half = keep_x.shape
    message = shape_of((slots + 1, rows, half), BF16)
    kept = shape_of((slots, rows, half), F32)
    send_y, send_x, left_x, left_y, vectors = small_call(
        second_sum_kernel,
        place,
        pieces,
        [message, message, kept, kept, shape_of(vectors.shape, BF16)],
        name + "_sum_first",
        after,
    )
    came_x, came_y = swap(send_y, "batch", 4), swap(send_x, "batch", 2)
    return (left_x, came_x, left_y, came_y, vectors), send_y


def sum_second(pieces, name, after=()):
    slots, rows, half = pieces[0].shape
    shape = shape_of((slots + 1, rows, 2 * half), BF16)
    return small_call(third_sum_kernel, None, pieces, [shape], name + "_sum_second", after)[0]


def batch_slices_any(groups, vectors):
    me = lax.axis_index("batch")
    bits = lax.axis_size("batch").bit_length() - 1
    pieces = []
    for kept, sent in groups:
        values = [a.astype(F32) for a in kept] + [swap(a, "batch", 1).astype(F32) for a in sent]
        pieces.append(functools.reduce(lambda a, b: a + b, values))
    total = jnp.concatenate(pieces, 1)
    total = total.reshape((2,) * (bits - 1) + total.shape[1:])
    for bit in range(bits - 1, 0, -1):
        mine = (me >> bit) & 1
        sent = lax.dynamic_index_in_dim(total, 1 - mine, 0, keepdims=False).astype(BF16)
        total = lax.dynamic_index_in_dim(total, mine, 0, keepdims=False)
        total = total + swap(sent, "batch", 1 << bit).astype(F32)
    total = lax.psum(total.astype(BF16), "rows").astype(F32)
    return total, lax.psum(vectors, ("batch", "rows"))


def rows_sum(total):
    for mask in (1, 2):
        total = (total.astype(F32) + swap(total, "rows", mask).astype(F32)).astype(
            BF16 if mask == 1 else F32
        )
    return total


def rows_sum_halving(total):
    me = lax.axis_index("rows")
    low_bit, high_bit = me & 1, me >> 1
    slots, rows, _ = total.shape
    half, part = slots // 2, rows // 2
    cut = lambda a, i, axis, n: lax.dynamic_slice_in_dim(a, i * n, n, axis)
    kept = cut(total, low_bit, 0, half).astype(F32)
    kept = kept + swap(cut(total, 1 - low_bit, 0, half), "rows", 1).astype(F32)
    sent = cut(kept, 1 - high_bit, 1, part).astype(BF16)
    kept = (cut(kept, high_bit, 1, part) + swap(sent, "rows", 2).astype(F32)).astype(BF16)
    other = swap(kept, "rows", 2)
    join = lambda bit, a, b, axis: jnp.concatenate(
        [jnp.where(bit == 0, a, b), jnp.where(bit == 0, b, a)], axis
    )
    kept = join(high_bit, kept, other, 1)
    other = swap(kept, "rows", 1)
    return join(low_bit, kept, other, 0).astype(F32)


def final_kernel(own_count, *refs):
    terms = refs[:own_count]
    atoms_ref, gain_ref, shift_ref, grad_middle_ref, out_ref = refs[own_count:]
    rows, width = terms[0].shape[1:]
    gain = gain_ref[...].astype(F32)
    for stage in range(own_count // 3):
        own_ref, near_ref, cross_ref = terms[3 * stage : 3 * stage + 3]
        count = own_ref.shape[0]
        grad = own_ref[...] + near_ref[0].astype(F32) + cross_ref[...].astype(F32)
        grad = grad.reshape(count * rows, width)
        at = slice(stage * count, (stage + 1) * count)
        atoms = atoms_ref[at].reshape(count * rows, width).astype(F32)
        _, normed, inverse = norm_forward(atoms, gain, shift_ref[...].astype(F32))
        middle = grad_middle_ref[at].reshape(count * rows, width)
        result = middle + norm_backward(grad, normed, inverse, gain)
        out_ref[at] = result.astype(BF16).reshape(count, rows, width)


def shards(
    atoms,
    pair_bias,
    lengths,
    first_gain,
    first_shift,
    query_weight,
    query_bias,
    key_weight,
    value_weight,
    value_bias,
    out_weight,
    out_bias,
    second_gain,
    second_shift,
    inner_weight,
    inner_bias,
    outer_weight,
    outer_bias,
    atoms_cotangent,
    pair_cotangent,
):
    molecules, rows, model_width = atoms.shape
    head_count = pair_bias.shape[1]
    head_size = model_width // head_count
    batch_count = lax.axis_size("batch")
    batch_index = lax.axis_index("batch")
    row = lax.axis_index("rows")
    place = jnp.stack(
        [batch_index, row, batch_index & 1, (batch_index >> 1) & 1, (batch_index >> 2) & 1]
    ).astype(jnp.int32)
    line = lambda v: v[None]
    count = molecules // STAGES
    stages = []
    pair_out = jnp.zeros((1,), BF16)
    for stage in range(STAGES):
        first = stage * count
        mine = atoms[first : first + count]
        pieces = [atoms] + [swap(mine, "rows", mask) for mask in (1, 2, 3)]
        pair_out, *kept = attention_forward(
            head_size,
            first,
            count,
            place,
            lengths,
            pieces,
            pair_bias,
            (
                line(first_gain),
                line(first_shift),
                query_weight,
                line(query_bias),
                key_weight,
                value_weight,
                line(value_bias),
            ),
            pair_out,
        )
        stages.append(kept)
    (
        atoms_out,
        outer_send,
        outer_keep,
        inner_send,
        inner_keep,
        out_send,
        out_keep,
        grad_middle,
        grad_mixed,
        dense_vectors,
    ) = dense(
        place,
        [s[1] for s in stages],
        atoms,
        atoms_cotangent,
        (
            out_weight,
            line(out_bias),
            line(second_gain),
            line(second_shift),
            inner_weight,
            line(inner_bias),
            outer_weight,
            line(outer_bias),
        ),
        batch_count,
    )
    pairs = batch_count // 2
    own_rows = model_width // batch_count
    slots = lambda a: a.reshape(pairs, -1, own_rows, model_width)
    dense_groups = [
        ([slots(outer_keep)], [slots(outer_send)]),
        ([inner_keep], [inner_send]),
        ([slots(out_keep)], [slots(out_send)]),
    ]
    usual = batch_count == 8
    held = pair_bias
    if usual:
        dense_pieces, held = sum_core(place, dense_groups, dense_vectors, "dense")
    else:
        dense_total, dense_vectors = batch_slices_any(dense_groups, dense_vectors)

    pair_grad = jnp.zeros((1,), BF16)
    sent, kept, vectors, terms = [], [], [], []
    for stage in range(STAGES):
        pair_grad, near, cross, own, send, keep, vector = attention_backward(
            head_size,
            stage * count,
            place,
            (stages[stage][0],) + tuple(stages[stage][1:]),
            pair_cotangent,
            grad_mixed,
            (query_weight, key_weight, value_weight),
            pair_grad,
            batch_count,
            held,
        )
        if usual and stage == 0:
            dense_pieces, held = sum_first(place, dense_pieces, "dense", (near,))
        near = swap(near, "rows", 1)
        cross = (cross.astype(F32) + near[1].astype(F32)).astype(BF16)
        terms += [own, near, swap(cross, "rows", 2)]
        sent.append(send)
        kept.append(keep)
        vectors.append(vector)
    groups = [(kept, sent)]
    tail_vectors = functools.reduce(lambda a, b: a + b, vectors)
    if usual:
        dense_total = sum_second(dense_pieces, "dense", (near,))
        dense_total = rows_sum_halving(dense_total)
        dense_vectors = dense_total[-1, : dense_vectors.shape[0]]
        pieces, _ = sum_core(place, groups, tail_vectors, "tail")
        pieces, _ = sum_first(place, pieces, "tail")
        total = rows_sum(sum_second(pieces, "tail"))
        tail_vectors = total[-1, : tail_vectors.shape[0]]
    else:
        total, tail_vectors = batch_slices_any(groups, tail_vectors)
    atoms_grad = small_call(
        functools.partial(final_kernel, len(terms)),
        None,
        terms + [atoms, line(first_gain), line(first_shift), grad_middle],
        [shape_of(atoms.shape, BF16)],
        "first_norm_backward",
    )[0]
    part = lambda v: lax.dynamic_slice_in_dim(
        v, batch_index * (v.shape[0] // batch_count), v.shape[0] // batch_count
    )
    ratio = inner_weight.shape[1] // model_width
    outer_grad = dense_total[:ratio].reshape(-1, model_width)
    inner_grad = dense_total[ratio : 2 * ratio].transpose(1, 0, 2).reshape(own_rows, -1)
    return (
        atoms_out,
        pair_out,
        atoms_grad,
        pair_grad,
        part(tail_vectors[0]),
        part(tail_vectors[1]),
        total[0],
        part(tail_vectors[2]),
        total[1],
        total[2],
        part(tail_vectors[3]),
        dense_total[2 * ratio],
        part(dense_vectors[3]),
        part(dense_vectors[1]),
        part(dense_vectors[2]),
        inner_grad,
        part(dense_vectors[4:].reshape(-1)),
        outer_grad,
        part(dense_vectors[0]),
    )


def solution(mesh):
    tokens = P("batch", "rows", None)
    pairs = P("batch", None, "rows", None)
    vector = P("batch")
    matrix = P("batch", None)
    return jax.shard_map(
        shards,
        mesh=mesh,
        in_specs=(tokens, pairs, P("batch")) + (P(),) * 15 + (tokens, pairs),
        out_specs=(
            tokens,
            pairs,
            tokens,
            pairs,
            vector,
            vector,
            matrix,
            vector,
            matrix,
            matrix,
            vector,
            matrix,
            vector,
            vector,
            vector,
            matrix,
            vector,
            matrix,
            vector,
        ),
        check_vma=False,
    )
```

```python
import functools
import math

import jax
import jax.numpy as jnp
from jax import lax
from jax.experimental import pallas as pl
from jax.experimental.pallas import tpu as pltpu
from jax.sharding import PartitionSpec as P

EPSILON = 1e-05
MASKED = -1000000000.0
F32 = jnp.float32
BF16 = jnp.bfloat16
LANES = 128
STAGES = 2
VMEM_LIMIT = 18 << 20


def shape_of(shape, dtype):
    return jax.ShapeDtypeStruct(tuple(shape), dtype)


def norm_forward(values_in, gain, shift):
    centre = values_in - jnp.mean(values_in, -1, keepdims=True)
    inverse = lax.rsqrt(jnp.mean(centre * centre, -1, keepdims=True) + EPSILON)
    normed = centre * inverse
    return (normed * gain + shift, normed, inverse)


def norm_backward(upstream, normed, inverse, gain):
    scaled = upstream * gain
    return inverse * (
        scaled
        - jnp.mean(scaled, -1, keepdims=True)
        - normed * jnp.mean(scaled * normed, -1, keepdims=True)
    )


def dot(left, right):
    return jnp.dot(left, right, preferred_element_type=F32)


def across(left, right):
    return lax.dot_general(left, right, (((0,), (0,)), ((), ())), preferred_element_type=F32)


def against(left, right):
    return lax.dot_general(left, right, (((1,), (1,)), ((), ())), preferred_element_type=F32)


def column_sum(values_in):
    return jnp.sum(values_in.astype(F32), 0, keepdims=True)


def near(shape, dtype):
    return pltpu.VMEM(tuple(shape), dtype)


def near_spec():
    return pl.BlockSpec(memory_space=pltpu.VMEM)


def as_row(ref):
    return ref[...].astype(F32).reshape(1, -1)


def whole(array):
    return pl.BlockSpec(array.shape, lambda *_: (0,) * array.ndim)


def params(mib=10):
    return pltpu.CompilerParams(vmem_limit_bytes=mib << 20)


def load_kernel(count, *refs):
    sources, targets, semaphores = refs[:count], refs[count : 2 * count], refs[2 * count]
    copies = [
        pltpu.make_async_copy(source, target, semaphores.at[i])
        for i, (source, target) in enumerate(zip(sources, targets))
    ]
    for copy in copies:
        copy.start()
    for copy in copies:
        copy.wait()


def load(arrays, name):
    return pl.pallas_call(
        functools.partial(load_kernel, len(arrays)),
        in_specs=[pl.BlockSpec(memory_space=pltpu.HBM)] * len(arrays),
        out_specs=[near_spec()] * len(arrays),
        out_shape=[near(a.shape, a.dtype) for a in arrays],
        scratch_shapes=[pltpu.SemaphoreType.DMA((len(arrays),))],
        compiler_params=params(),
        name=name,
    )(*arrays)


def forward_kernel(
    head_size,
    chunk,
    first,
    place_ref,
    length_ref,
    own_ref,
    one_ref,
    two_ref,
    three_ref,
    pair_ref,
    gain_ref,
    shift_ref,
    query_weight_ref,
    query_bias_ref,
    key_weight_ref,
    value_weight_ref,
    value_bias_ref,
    _,
    pair_out_ref,
    weights_ref,
    mixed_ref,
    inverse_ref,
    hidden_ref,
    normed_ref,
    query_ref,
    key_ref,
    value_ref,
    atoms_scratch,
    pair_scratch,
    semaphores,
):
    molecule = pl.program_id(0)
    group = pl.program_id(1)
    count, groups, keys, width = key_ref.shape
    heads = width // head_size
    rows, model_width = own_ref.shape[1:]
    factor = head_size**-0.5

    def pair_copy(m, g):
        span = pl.ds(g * heads, heads)
        return pltpu.make_async_copy(
            pair_ref.at[m + first, span], pair_scratch.at[m, span], semaphores.at[m, g]
        )

    @pl.when((molecule == 0) & (group == 0))
    def _():
        for m in range(count):
            for g in range(groups):
                pair_copy(m, g).start()
        row = place_ref[1]
        gain = as_row(gain_ref)
        shift = as_row(shift_ref)
        query_bias = as_row(query_bias_ref)
        value_bias = as_row(value_bias_ref)
        ones = jnp.ones((keys, width), BF16)
        for m in range(count):
            for i, piece in enumerate((own_ref, one_ref, two_ref, three_ref)):
                start = pl.multiple_of((row ^ i) * rows, rows)
                atoms_scratch[pl.ds(start, rows)] = piece[m]
            hidden, normed, _ = norm_forward(atoms_scratch[...].astype(F32), gain, shift)
            hidden = hidden.astype(BF16)
            hidden_ref[m] = hidden
            normed_ref[m] = normed.astype(BF16)
            key_rows = dot(hidden, key_weight_ref[...]).astype(BF16)
            value_rows = (dot(hidden, value_weight_ref[...]) + value_bias).astype(BF16)
            for t in range(groups):
                lanes = slice(t * width, (t + 1) * width)
                key_ref[m, t] = key_rows[:, lanes]
                value_ref[m, t, :, :width] = value_rows[:, lanes]
                value_ref[m, t, :, width:] = ones
        own = own_ref[...].reshape(count * rows, model_width).astype(F32)
        own = norm_forward(own, gain, shift)[0].astype(BF16)
        query_rows = (dot(own, query_weight_ref[...]) + query_bias) * factor
        query_rows = query_rows.astype(BF16).reshape(count, rows, model_width)
        for t in range(groups):
            query_ref[:, t] = query_rows[:, :, t * width : (t + 1) * width]

    pair_copy(molecule, group).wait()
    query = query_ref[molecule, group]
    key = key_ref[molecule, group]
    value = value_ref[molecule, group]
    valid = lax.broadcasted_iota(jnp.int32, (1, keys), 1) < length_ref[molecule + first]
    lane = lax.broadcasted_iota(jnp.int32, (1, width), 1) // head_size
    lane_pair = lax.broadcasted_iota(jnp.int32, (1, 2 * width), 1) % width // head_size
    total = jnp.zeros((rows, 2 * width), F32)
    zero = jnp.zeros((), BF16)
    for c in range(0, heads, chunk):
        here = slice(c, c + chunk)
        there = pl.ds(group * heads + c, chunk)
        spread = jnp.concatenate([jnp.where(lane == c + t, query, zero) for t in range(chunk)], 0)
        pair = pair_scratch[molecule, there].reshape(chunk * rows, keys)
        scores = against(spread, key) + pair.astype(F32)
        pair_out_ref[0, here] = scores.astype(BF16).reshape(chunk, rows, keys)
        masked = jnp.where(valid, scores, MASKED)
        weights = jnp.exp(masked - jnp.max(masked, -1, keepdims=True)).astype(BF16)
        weights_ref[molecule, there] = weights.reshape(chunk, rows, keys)
        product = dot(weights, value)
        for t in range(chunk):
            total = jnp.where(lane_pair == c + t, product[t * rows : (t + 1) * rows], total)
    inverse = 1.0 / total[:, width:]
    inverse_ref[molecule, group] = inverse
    mixed_ref[molecule, group] = total[:, :width] * inverse


def attention_forward(head_size, first, count, place, lengths, pieces, pair_bias, parameters, held):
    _, head_count, rows, keys = pair_bias.shape
    model_width = pieces[0].shape[2]
    groups = model_width // LANES
    heads = LANES // head_size
    pair_spec = pl.BlockSpec((1, heads, rows, keys), lambda m, g, *_: (m + first, g, 0, 0))
    elements = count * head_count * rows * keys
    own_spec = pl.BlockSpec((count, rows, model_width), lambda *_: (first // count, 0, 0))
    operands = (place, lengths, *pieces, pair_bias, *parameters, held)
    return pl.pallas_call(
        functools.partial(forward_kernel, head_size, 8, first),
        grid_spec=pltpu.PrefetchScalarGridSpec(
            num_scalar_prefetch=2,
            grid=(count, groups),
            in_specs=[own_spec]
            + [near_spec()] * (len(pieces) - 1)
            + [pl.BlockSpec(memory_space=pltpu.HBM)]
            + [whole(a) for a in parameters]
            + [pl.BlockSpec(memory_space=pl.ANY)],
            out_specs=[pair_spec] + [near_spec()] * 8,
            scratch_shapes=[
                pltpu.VMEM((keys, model_width), BF16),
                pltpu.VMEM((count, head_count, rows, keys), BF16),
                pltpu.SemaphoreType.DMA((count, groups)),
            ],
        ),
        out_shape=[
            shape_of(pair_bias.shape, BF16),
            near((count, head_count, rows, keys), BF16),
            near((count, groups, rows, LANES), F32),
            near((count, groups, rows, LANES), F32),
            near((count, keys, model_width), BF16),
            near((count, keys, model_width), BF16),
            near((count, groups, rows, LANES), BF16),
            near((count, groups, keys, LANES), BF16),
            near((count, groups, keys, 2 * LANES), BF16),
        ],
        input_output_aliases={} if held.ndim == 1 else {len(operands) - 1: 0},
        compiler_params=params(16),
        cost_estimate=pl.CostEstimate(
            flops=elements * 2 * 384, transcendentals=elements, bytes_accessed=elements * 6
        ),
        name="attention_forward",
    )(*operands)


def dense_kernel(
    mixed_count,
    place_ref,
    *refs,
):
    mixed_refs = refs[:mixed_count]
    (
        atoms_ref,
        cotangent_ref,
        out_weight_ref,
        out_bias_ref,
        gain_ref,
        shift_ref,
        inner_weight_ref,
        inner_bias_ref,
        outer_weight_ref,
        outer_bias_ref,
        atoms_out_ref,
        outer_send_ref,
        outer_keep_ref,
        inner_send_ref,
        inner_keep_ref,
        out_send_ref,
        out_keep_ref,
        grad_middle_ref,
        grad_mixed_ref,
        vectors_ref,
        hidden_scratch,
        turned_scratch,
        normed_scratch,
        inverse_scratch,
        result_scratch,
        upstream_scratch,
        outer_scratch,
        inner_scratch,
    ) = refs[mixed_count:]
    step = pl.program_id(0)
    steps = pl.num_programs(0)
    core = place_ref[2]
    tokens, model_width = hidden_scratch.shape
    cotangent = cotangent_ref[...].reshape(tokens, model_width)

    def mixed_rows():
        parts = []
        for ref in mixed_refs:
            count, groups, rows, width = ref.shape
            join = [ref[:, t].reshape(count * rows, width) for t in range(groups)]
            parts.append(jnp.concatenate(join, 1))
        return jnp.concatenate(parts, 0)

    @pl.when(step == 0)
    def _():
        mixed_low = mixed_rows().astype(BF16)
        middle = (
            atoms_ref[...].reshape(tokens, model_width).astype(F32)
            + dot(mixed_low, out_weight_ref[...])
            + as_row(out_bias_ref)
        )
        hidden, normed, inverse = norm_forward(
            middle, as_row(gain_ref), as_row(shift_ref)
        )
        hidden_scratch[...] = hidden.astype(BF16)
        turned_scratch[...] = jnp.transpose(hidden).astype(BF16)
        normed_scratch[...] = normed
        inverse_scratch[...] = inverse
        result_scratch[...] = middle + as_row(outer_bias_ref)
        upstream_scratch[...] = jnp.zeros_like(upstream_scratch)
        vectors_ref[0:1] = column_sum(cotangent)

    hidden = hidden_scratch[...]
    pre = dot(hidden, inner_weight_ref[...]) + as_row(inner_bias_ref)
    slope = math.sqrt(2.0 / math.pi)
    square = pre * pre
    tanh = jnp.tanh(slope * (pre + 0.044715 * (pre * square)))
    half = 0.5 * (1.0 + tanh)
    active = (pre * half).astype(BF16)
    result_scratch[...] += dot(active, outer_weight_ref[...])
    derivative = half + (0.5 * slope) * pre * (1.0 - tanh * tanh) * (1.0 + 0.134145 * square)
    grad_pre = against(cotangent, outer_weight_ref[...]) * derivative
    vectors_ref[pl.ds(4 + step, 1)] = column_sum(grad_pre.astype(BF16))
    grad_pre = grad_pre.astype(BF16)
    outer_scratch[...] = across(active, cotangent).reshape(outer_scratch.shape)
    outer_send_ref[...] = outer_scratch[:, 1 - core].astype(BF16).reshape(outer_send_ref.shape)
    outer_keep_ref[...] = outer_scratch[:, core].astype(BF16).reshape(outer_keep_ref.shape)
    inner_scratch[...] = dot(turned_scratch[...], grad_pre).reshape(inner_scratch.shape)
    inner_send_ref[:, 0] = inner_scratch[:, 1 - core].astype(BF16)
    inner_keep_ref[:, 0] = inner_scratch[:, core].astype(BF16)
    upstream_scratch[...] += against(grad_pre, inner_weight_ref[...])

    @pl.when(step == steps - 1)
    def _():
        atoms_out_ref[...] = result_scratch[...].astype(BF16).reshape(atoms_out_ref.shape)
        upstream = upstream_scratch[...]
        normed = normed_scratch[...]
        vectors_ref[1:2] = column_sum(upstream * normed)
        vectors_ref[2:3] = column_sum(upstream)
        grad_middle = cotangent.astype(F32) + norm_backward(
            upstream, normed, inverse_scratch[...], as_row(gain_ref)
        )
        grad_middle_ref[...] = grad_middle.reshape(grad_middle_ref.shape)
        branch = grad_middle.astype(BF16)
        vectors_ref[3:4] = column_sum(branch)
        grad_mixed = against(branch, out_weight_ref[...]).astype(BF16)
        molecules, groups, rows, lanes = grad_mixed_ref.shape
        grad_mixed = grad_mixed.reshape(molecules, rows, model_width)
        for t in range(groups):
            grad_mixed_ref[:, t] = grad_mixed[:, :, t * lanes : (t + 1) * lanes]
        turned = jnp.transpose(mixed_rows()).astype(BF16)
        inner_scratch[...] = dot(turned, branch).reshape(inner_scratch.shape)
        out_send_ref[...] = inner_scratch[:, 1 - core].astype(BF16)
        out_keep_ref[...] = inner_scratch[:, core].astype(BF16)


def dense(place, mixed, atoms, cotangent, parameters, batch_count):
    (
        out_weight,
        out_bias,
        gain,
        shift,
        inner_weight,
        inner_bias,
        outer_weight,
        outer_bias,
    ) = parameters
    model_width, inner_width = inner_weight.shape
    tokens = atoms.shape[0] * atoms.shape[1]
    width = model_width
    steps = inner_width // width
    pairs = batch_count // 2
    outer_rows = inner_width // batch_count
    outer_pairs = width // (2 * outer_rows)
    own_rows = model_width // batch_count
    operands = (
        place,
        *mixed,
        atoms,
        cotangent,
        out_weight,
        out_bias,
        gain,
        shift,
        inner_weight,
        inner_bias,
        outer_weight,
        outer_bias,
    )
    outer_spec = pl.BlockSpec((outer_pairs, outer_rows, model_width), lambda s, *_: (s, 0, 0))
    inner_spec = pl.BlockSpec((pairs, 1, own_rows, width), lambda s, *_: (0, s, 0, 0))
    outer_shape = shape_of((pairs, outer_rows, model_width), BF16)
    inner_shape = shape_of((pairs, steps, own_rows, width), BF16)
    out_shape = shape_of((pairs, own_rows, model_width), BF16)
    out_shapes = [
        shape_of(atoms.shape, BF16),
        outer_shape,
        outer_shape,
        inner_shape,
        inner_shape,
        out_shape,
        out_shape,
        near(atoms.shape, F32),
        near((atoms.shape[0], model_width // LANES, atoms.shape[1], LANES), BF16),
        shape_of((4 + steps, model_width), F32),
    ]
    fixed = lambda s: pl.BlockSpec(s.shape, lambda *_: (0,) * len(s.shape))
    out_specs = [fixed(s) for s in out_shapes]
    out_specs[1:5] = [outer_spec, outer_spec, inner_spec, inner_spec]
    out_specs[7:9] = [near_spec(), near_spec()]
    in_specs = [whole(a) for a in operands[1:]]
    in_specs[: len(mixed)] = [near_spec() for _ in mixed]
    in_specs[-4] = pl.BlockSpec((model_width, width), lambda s, *_: (0, s))
    in_specs[-3] = pl.BlockSpec((width,), lambda s, *_: (s,))
    in_specs[-2] = pl.BlockSpec((width, model_width), lambda s, *_: (s, 0))
    return pl.pallas_call(
        functools.partial(dense_kernel, len(mixed)),
        grid_spec=pltpu.PrefetchScalarGridSpec(
            num_scalar_prefetch=1,
            grid=(steps,),
            in_specs=in_specs,
            out_specs=out_specs,
            scratch_shapes=[
                pltpu.VMEM((tokens, model_width), BF16),
                pltpu.VMEM((model_width, tokens), BF16),
                pltpu.VMEM((tokens, model_width), F32),
                pltpu.VMEM((tokens, 1), F32),
                pltpu.VMEM((tokens, model_width), F32),
                pltpu.VMEM((tokens, model_width), F32),
                pltpu.VMEM((outer_pairs, 2, outer_rows, model_width), F32),
                pltpu.VMEM((pairs, 2, own_rows, width), F32),
            ],
        ),
        out_shape=out_shapes,
        compiler_params=params(18),
        cost_estimate=pl.CostEstimate(
            flops=12 * tokens * model_width * inner_width,
            transcendentals=tokens * inner_width,
            bytes_accessed=12 * model_width * inner_width,
        ),
        name="dense",
    )(*operands)


def backward_kernel(
    head_size,
    chunk,
    first,
    base,
    start,
    fresh,
    place_ref,
    weights_ref,
    cotangent_ref,
    grad_mixed_ref,
    mixed_ref,
    inverse_ref,
    query_ref,
    key_ref,
    value_ref,
    normed_ref,
    query_weight_ref,
    key_weight_ref,
    value_weight_ref,
    *refs,
):
    refs = refs[start:]
    pair_grad_ref, near_ref, cross_ref, own_ref, vectors_ref = refs[:5]
    query_grad_ref, key_grad_ref, value_grad_ref = refs[5:8]
    grad_query_scratch, grad_key_scratch, grad_value_scratch, grad_scratch = refs[-4:]
    molecule = pl.program_id(0) + base
    group = pl.program_id(1)
    _, groups, rows, width = query_ref.shape
    keys = key_ref.shape[2]
    heads = width // head_size
    factor = head_size**-0.5
    query = query_ref[molecule, group]
    key = key_ref[molecule, group]
    value = value_ref[molecule, group]
    upstream = grad_mixed_ref[molecule + first, group].astype(F32) * inverse_ref[molecule, group]
    upstream = upstream.astype(BF16)
    offset = (-(upstream.astype(F32) * mixed_ref[molecule, group])).astype(BF16)
    both = jnp.concatenate([upstream, offset], 1)
    lane = lax.broadcasted_iota(jnp.int32, (1, width), 1) // head_size
    lane_pair = lax.broadcasted_iota(jnp.int32, (1, 2 * width), 1) % width // head_size
    query_turned = jnp.transpose(query.astype(F32)).astype(BF16)
    upstream_turned = jnp.transpose(upstream.astype(F32)).astype(BF16)
    query_turned = jnp.concatenate([query_turned] * chunk, 1)
    upstream_turned = jnp.concatenate([upstream_turned] * chunk, 1)
    turned_shape = (chunk * head_size, chunk * rows)
    same = (
        lax.broadcasted_iota(jnp.int32, turned_shape, 0) // head_size
        == lax.broadcasted_iota(jnp.int32, turned_shape, 1) // rows
    )
    zero = jnp.zeros((), BF16)
    total = jnp.zeros((rows, width), F32)
    key_parts = []
    value_parts = []
    for c in range(0, heads, chunk):
        here = slice(c, c + chunk)
        feature = slice(c * head_size, (c + chunk) * head_size)
        spread = jnp.concatenate([jnp.where(lane_pair == c + t, both, zero) for t in range(chunk)], 0)
        centred = against(spread, value)
        there = pl.ds(group * heads + c, chunk)
        weights = weights_ref[molecule, there].reshape(chunk * rows, keys)
        cotangent = cotangent_ref[0, here].reshape(chunk * rows, keys)
        grad = (weights.astype(F32) * centred + cotangent.astype(F32)).astype(BF16)
        pair_grad_ref[0, here] = grad.reshape(chunk, rows, keys)
        product = dot(grad, key)
        for t in range(chunk):
            total = jnp.where(lane == c + t, product[t * rows : (t + 1) * rows], total)
        key_parts.append(dot(jnp.where(same, query_turned[feature], zero), grad))
        value_parts.append(dot(jnp.where(same, upstream_turned[feature], zero), weights))
    grad_query_scratch[group] = (total * factor).astype(BF16)
    grad_key_scratch[group] = jnp.transpose(jnp.concatenate(key_parts, 0)).astype(BF16)
    grad_value_scratch[group] = jnp.transpose(jnp.concatenate(value_parts, 0)).astype(BF16)

    if fresh:

        @pl.when((pl.program_id(0) == 0) & (group == 0))
        def _():
            vectors_ref[...] = jnp.zeros_like(vectors_ref)

    @pl.when(group == groups - 1)
    def _():
        row = place_ref[1]
        mine = pl.ds(pl.multiple_of(row * rows, rows), rows)
        join = lambda ref: jnp.concatenate([ref[t] for t in range(groups)], 1)
        grad_query = join(grad_query_scratch)
        grad_key = join(grad_key_scratch)
        grad_value = join(grad_value_scratch)
        at = pl.program_id(0)
        query_grad_ref[at] = grad_query
        key_grad_ref[at] = grad_key
        value_grad_ref[at] = grad_value
        grad_scratch[...] = against(grad_key, key_weight_ref[...]) + against(
            grad_value, value_weight_ref[...]
        )
        grad_scratch[mine] += against(grad_query, query_weight_ref[...])
        grad = grad_scratch[...]
        vectors_ref[0:1] += column_sum(grad * normed_ref[molecule].astype(F32))
        vectors_ref[1:2] += column_sum(grad)
        vectors_ref[2:3] += column_sum(grad_query)
        vectors_ref[3:4] += column_sum(grad_value)
        at = lambda other: pl.ds(pl.multiple_of((row ^ other) * rows, rows), rows)
        near_ref[0, 0] = grad_scratch[at(1)].astype(BF16)
        near_ref[1, 0] = grad_scratch[at(3)].astype(BF16)
        cross_ref[0] = grad_scratch[at(2)].astype(BF16)
        own_ref[pl.program_id(0)] = grad_scratch[mine]

def attention_backward(
    head_size, first, span, place, stage, cotangent, grad_mixed, parameters, held, sums, after
):
    weights, mixed, inverse, _, normed, query, key, value = stage
    _, head_count, rows, keys = weights.shape
    base, count = span[0], span[1] - span[0]
    groups = query.shape[1]
    model_width = groups * LANES
    heads = LANES // head_size
    pair_spec = pl.BlockSpec((1, heads, rows, keys), lambda m, g, *_: (m + first + base, g, 0, 0))
    elements = count * head_count * rows * keys
    operands = [
        place,
        weights,
        cotangent,
        grad_mixed,
        mixed,
        inverse,
        query,
        key,
        value,
        normed,
        *parameters,
    ]
    in_specs = [near_spec()] * (len(operands) - 1)
    in_specs[1] = pair_spec
    in_specs[-3:] = [whole(a) for a in parameters]
    aliases = {}
    start = len(operands)
    if sums is not None:
        aliases = {start: 0, start + 1: 4}
        operands += [held, sums]
        in_specs += [pl.BlockSpec(memory_space=pl.ANY), near_spec()]
    operands += list(after)
    in_specs += [pl.BlockSpec(memory_space=pl.ANY)] * len(after)
    out_shape = [
        shape_of(cotangent.shape, BF16),
        shape_of((2, count, rows, model_width), BF16),
        shape_of((count, rows, model_width), BF16),
        near((count, rows, model_width), F32),
        near((8, model_width), F32),
        near((count, rows, model_width), BF16),
        near((count, keys, model_width), BF16),
        near((count, keys, model_width), BF16),
    ]
    out_specs = [
        pair_spec,
        pl.BlockSpec((2, 1, rows, model_width), lambda m, g, *_: (0, m, 0, 0)),
        pl.BlockSpec((1, rows, model_width), lambda m, g, *_: (m, 0, 0)),
        near_spec(),
        near_spec(),
        near_spec(),
        near_spec(),
        near_spec(),
    ]
    return pl.pallas_call(
        functools.partial(
            backward_kernel, head_size, 4, first, base, len(operands) - start, sums is None
        ),
        grid_spec=pltpu.PrefetchScalarGridSpec(
            num_scalar_prefetch=1,
            grid=(count, groups),
            in_specs=in_specs,
            out_specs=out_specs,
            scratch_shapes=[
                pltpu.VMEM((groups, rows, LANES), BF16),
                pltpu.VMEM((groups, keys, LANES), BF16),
                pltpu.VMEM((groups, keys, LANES), BF16),
                pltpu.VMEM((keys, model_width), F32),
            ],
        ),
        out_shape=out_shape,
        input_output_aliases=aliases,
        compiler_params=params(14),
        cost_estimate=pl.CostEstimate(
            flops=elements * 2 * 768, transcendentals=0, bytes_accessed=elements * 6
        ),
        name="attention_backward",
    )(*operands)


def weight_kernel(calls, stages, place_ref, *refs):
    hidden_refs = refs[:stages]
    grads = refs[stages : stages + 3 * calls]
    out_refs = refs[stages + 3 * calls : -1]
    total_ref = refs[-1]
    rows = grads[0].shape[1]
    row = place_ref[1]
    core = place_ref[2]
    mine = pl.ds(pl.multiple_of(row * rows, rows), rows)
    hidden = [(ref, m) for ref in hidden_refs for m in range(ref.shape[0])]
    width = hidden_refs[0].shape[2]
    own = jnp.concatenate([ref[m, mine] for ref, m in hidden], 0)
    every = jnp.concatenate([ref[m] for ref, m in hidden], 0)
    own = jnp.transpose(own.astype(F32)).astype(BF16)
    every = jnp.transpose(every.astype(F32)).astype(BF16)
    for j, left in enumerate((own, every, every)):
        right = jnp.concatenate([grads[3 * c + j][...].reshape(-1, width) for c in range(calls)], 0)
        total_ref[...] = dot(left, right).reshape(total_ref.shape)
        send_ref, keep_ref = out_refs[2 * j : 2 * j + 2]
        send_ref[:, 0] = total_ref[:, 1 - core].astype(BF16)
        keep_ref[:, 0] = total_ref[:, core].astype(BF16)


def swap(value, axis, mask):
    size = lax.axis_size(axis)
    return lax.ppermute(value, axis, [(i, i ^ mask) for i in range(size)])


VECTOR_ROWS = 8


def first_sum_kernel(counts, place_ref, *refs):
    terms = sum(counts)
    mine_ref, other_ref = refs[terms : terms + 2]
    along_x_ref, along_y_ref, keep_x_ref, keep_y_ref, vectors_ref = refs[terms + 2 :]
    x, y = place_ref[3], place_ref[4]
    half = along_x_ref.shape[1]
    size = keep_x_ref.shape[1]
    low, high = slice(0, half), slice(half, None)
    row = 0
    start = 0
    for count in counts:
        group = refs[start : start + count]
        start += count
        for s in range(group[0].shape[1]):
            rows = group[0].shape[2]

            def total(at, lanes):
                values = [r[at, s, :, lanes].astype(F32) for r in group]
                return functools.reduce(lambda a, b: a + b, values)

            for k in range(2):
                to = slice(k * size + row, k * size + row + rows)
                here = slice(row, row + rows)
                along_x_ref[to] = total(2 * k + (1 - x), low).astype(BF16)
                keep_x_ref[k, here] = total(2 * k + x, low)
                along_y_ref[to] = total(2 * (1 - y) + k, high).astype(BF16)
                keep_y_ref[k, here] = total(2 * y + k, high)
            row += rows
    vectors = (mine_ref[...] + other_ref[...]).astype(BF16)
    vectors_ref[...] = vectors
    put_vectors(vectors, along_x_ref, along_y_ref)


def put_vectors(vectors, low_ref, high_ref):
    half = vectors.shape[1] // 2
    low_ref[low_ref.shape[0] - VECTOR_ROWS :] = vectors[:, :half]
    high_ref[high_ref.shape[0] - VECTOR_ROWS :] = vectors[:, half:]


def get_vectors(low_ref, high_ref):
    low = low_ref[low_ref.shape[0] - VECTOR_ROWS :]
    return jnp.concatenate([low, high_ref[high_ref.shape[0] - VECTOR_ROWS :]], 1).astype(F32)


def second_sum_kernel(
    place_ref,
    keep_x_ref,
    came_x_ref,
    keep_y_ref,
    came_y_ref,
    vectors_ref,
    send_y_ref,
    send_x_ref,
    left_x_ref,
    left_y_ref,
    vectors_out_ref,
):
    size = keep_x_ref.shape[1]
    for keep, came, send, left, me in (
        (keep_x_ref, came_x_ref, send_y_ref, left_x_ref, place_ref[4]),
        (keep_y_ref, came_y_ref, send_x_ref, left_y_ref, place_ref[3]),
    ):
        at = lambda i: pl.ds(pl.multiple_of(i * size, size), size)
        send[:size] = (keep[1 - me] + came[at(1 - me)].astype(F32)).astype(BF16)
        left[...] = keep[me] + came[at(me)].astype(F32)
    vectors = vectors_ref[...].astype(F32) + get_vectors(came_x_ref, came_y_ref)
    vectors = vectors.astype(BF16)
    vectors_out_ref[...] = vectors
    put_vectors(vectors, send_y_ref, send_x_ref)


def third_sum_kernel(left_x_ref, came_x_ref, left_y_ref, came_y_ref, vectors_ref, total_ref):
    size, half = left_x_ref.shape
    total_ref[:size, :half] = (left_x_ref[...] + came_x_ref[:size].astype(F32)).astype(BF16)
    total_ref[:size, half:] = (left_y_ref[...] + came_y_ref[:size].astype(F32)).astype(BF16)
    vectors = vectors_ref[...].astype(F32) + get_vectors(came_x_ref, came_y_ref)
    total_ref[size : size + VECTOR_ROWS] = vectors.astype(BF16)


def third_cut_kernel(place_ref, *refs):
    third_sum_kernel(*refs[:-1])
    total_ref, sent_ref = refs[-2:]
    filled = refs[0].shape[0] + VECTOR_ROWS
    if filled < total_ref.shape[0]:
        total_ref[filled:] = jnp.zeros((total_ref.shape[0] - filled, total_ref.shape[1]), BF16)
    half = sent_ref.shape[0]
    away = pl.multiple_of((1 - (place_ref[1] & 1)) * half, half)
    sent_ref[...] = total_ref[pl.ds(away, half)]


def near_sum_kernel(place_ref, total_ref, came_ref, sent_ref, kept_ref):
    half, part = came_ref.shape[0], sent_ref.shape[0]
    row = place_ref[1]
    here = (row & 1) * half

    def total(other):
        start = other * part
        mine = total_ref[pl.ds(pl.multiple_of(here + start, part), part)]
        return mine.astype(F32) + came_ref[pl.ds(pl.multiple_of(start, part), part)].astype(F32)

    kept_ref[...] = total(row >> 1)
    sent_ref[...] = total(1 - (row >> 1)).astype(BF16)


def add_kernel(left_ref, right_ref, out_ref):
    out_ref[...] = (left_ref[...].astype(F32) + right_ref[...].astype(F32)).astype(out_ref.dtype)


def join_rows(place, mine_ref, other_ref, out_ref):
    part = mine_ref.shape[0]
    out_ref[pl.ds(pl.multiple_of(place * part, part), part)] = mine_ref[...]
    out_ref[pl.ds(pl.multiple_of((1 - place) * part, part), part)] = other_ref[...]


def join_kernel(place_ref, mine_ref, other_ref, out_ref):
    join_rows(place_ref[1] >> 1, mine_ref, other_ref, out_ref)


def finish_dense_kernel(
    ratio, place_ref, mine_ref, other_ref, outer_ref, inner_ref, out_ref, vectors_ref, total_scratch
):
    rows, width = out_ref.shape
    join_rows(place_ref[1] & 1, mine_ref, other_ref, total_scratch)
    outer_ref[...] = total_scratch[: ratio * rows].astype(F32)
    for s in range(ratio):
        at = (ratio + s) * rows
        inner_ref[:, s * width : (s + 1) * width] = total_scratch[at : at + rows].astype(F32)
    at = 2 * ratio * rows
    out_ref[...] = total_scratch[at : at + rows].astype(F32)
    vectors_ref[...] = total_scratch[at + rows : at + rows + VECTOR_ROWS].astype(F32)


def finish_tail_kernel(low_ref, came_ref, query_ref, key_ref, value_ref, vectors_ref):
    rows = query_ref.shape[0]
    for s, ref in enumerate((query_ref, key_ref, value_ref, vectors_ref)):
        at = slice(s * rows, s * rows + ref.shape[0])
        ref[...] = low_ref[at].astype(F32) + came_ref[at].astype(F32)


def small_call(kernel, place, operands, out_shapes, name, after=(), inside=True, scratch=(), mib=4):
    ahead = 0 if place is None else 1
    count = len(operands)

    def body(*refs):
        kernel(*refs[: ahead + count], *refs[ahead + count + len(after) :])

    size = sum(math.prod(a.shape) * a.dtype.itemsize for a in list(operands) + list(out_shapes))
    return pl.pallas_call(
        body,
        grid_spec=pltpu.PrefetchScalarGridSpec(
            num_scalar_prefetch=ahead,
            grid=(1,),
            in_specs=[near_spec() for a in operands] + [pl.BlockSpec(memory_space=pl.ANY)] * len(after),
            out_specs=[near_spec() for s in out_shapes],
            scratch_shapes=list(scratch),
        ),
        out_shape=[near(s.shape, s.dtype) if inside else s for s in out_shapes],
        compiler_params=params(mib),
        cost_estimate=pl.CostEstimate(flops=0, transcendentals=0, bytes_accessed=size),
        name=name,
    )(*(() if place is None else (place,)), *operands, *after)


def sum_core(place, groups, vectors, name, after=()):
    groups = [list(g) + [swap(a, "batch", 1) for a in sent] for g, sent in groups]
    vectors_other = swap(vectors, "batch", 1)
    _, _, rows, width = groups[0][0].shape
    size = sum(g[0].shape[1] for g in groups) * rows
    half = width // 2
    counts = tuple(len(g) for g in groups)
    message = shape_of((2 * size + VECTOR_ROWS, half), BF16)
    kept = shape_of((2, size, half), F32)
    along_x, along_y, keep_x, keep_y, vectors = small_call(
        functools.partial(first_sum_kernel, counts),
        place,
        [a for g in groups for a in g] + [vectors, vectors_other],
        [message, message, kept, kept, shape_of(vectors.shape, BF16)],
        name + "_sum_core",
        after,
    )
    came_x, came_y = swap(along_x, "batch", 2), swap(along_y, "batch", 4)
    return (keep_x, came_x, keep_y, came_y, vectors), along_x


def sum_first(place, pieces, name, after=()):
    keep_x, _, _, _, vectors = pieces
    _, size, half = keep_x.shape
    message = shape_of((size + VECTOR_ROWS, half), BF16)
    kept = shape_of((size, half), F32)
    send_y, send_x, left_x, left_y, vectors = small_call(
        second_sum_kernel,
        place,
        pieces,
        [message, message, kept, kept, shape_of(vectors.shape, BF16)],
        name + "_sum_first",
        after,
    )
    came_x, came_y = swap(send_y, "batch", 4), swap(send_x, "batch", 2)
    return (left_x, came_x, left_y, came_y, vectors), send_y


def sum_second(pieces, name, after=()):
    size, half = pieces[0].shape
    shape = shape_of((size + VECTOR_ROWS, 2 * half), BF16)
    return small_call(third_sum_kernel, None, pieces, [shape], name + "_sum_second", after)[0]


def sum_second_cut(place, pieces, name, after=()):
    size, half = pieces[0].shape
    rows = -(-(size + VECTOR_ROWS) // 32) * 32
    total, sent = small_call(
        third_cut_kernel,
        place,
        pieces,
        [shape_of((rows, 2 * half), BF16), shape_of((rows // 2, 2 * half), BF16)],
        name + "_sum_second",
        after,
    )
    return total, swap(sent, "rows", 1)


def batch_slices_any(groups, vectors):
    me = lax.axis_index("batch")
    bits = lax.axis_size("batch").bit_length() - 1
    pieces = []
    for kept, sent in groups:
        values = [a.astype(F32) for a in kept] + [swap(a, "batch", 1).astype(F32) for a in sent]
        pieces.append(functools.reduce(lambda a, b: a + b, values))
    total = jnp.concatenate(pieces, 1)
    total = total.reshape((2,) * (bits - 1) + total.shape[1:])
    for bit in range(bits - 1, 0, -1):
        mine = (me >> bit) & 1
        sent = lax.dynamic_index_in_dim(total, 1 - mine, 0, keepdims=False).astype(BF16)
        total = lax.dynamic_index_in_dim(total, mine, 0, keepdims=False)
        total = total + swap(sent, "batch", 1 << bit).astype(F32)
    total = lax.psum(total.astype(BF16), "rows").astype(F32)
    return total, lax.psum(vectors, ("batch", "rows"))


def cross_kernel(count, *refs):
    out_ref = refs[-1]
    start = 0
    for term, came in zip(refs[:count], refs[count : 2 * count]):
        end = start + term.shape[0]
        out_ref[start:end] = (term[...].astype(F32) + came[1].astype(F32)).astype(BF16)
        start = end


def cross_sum(terms, came, name, after=()):
    shape = (sum(t.shape[0] for t in terms),) + terms[0].shape[1:]
    return small_call(
        functools.partial(cross_kernel, len(terms)),
        None,
        list(terms) + list(came),
        [shape_of(shape, BF16)],
        name,
        after,
    )[0]


def final_kernel(calls, crosses, *refs):
    own_refs, near_refs = refs[:calls], refs[calls : 2 * calls]
    cross_refs = refs[2 * calls : 2 * calls + crosses]
    atoms_ref, gain_ref, shift_ref, grad_middle_ref, out_ref = refs[2 * calls + crosses :]
    rows, width = own_refs[0].shape[1:]
    gain = as_row(gain_ref)
    shift = as_row(shift_ref)
    crosses = [(ref, i) for ref in cross_refs for i in range(ref.shape[0])]
    m = 0
    for own_ref, near_ref in zip(own_refs, near_refs):
        for i in range(own_ref.shape[0]):
            cross_ref, at = crosses[m]
            grad = own_ref[i] + near_ref[0, i].astype(F32) + cross_ref[at].astype(F32)
            _, normed, inverse = norm_forward(atoms_ref[m].astype(F32), gain, shift)
            result = grad_middle_ref[m] + norm_backward(grad, normed, inverse, gain)
            out_ref[m] = result.astype(BF16)
            m += 1


def first_norm_backward(owns, nears, crosses, others, after=()):
    return small_call(
        functools.partial(final_kernel, len(owns), len(crosses)),
        None,
        owns + nears + crosses + list(others),
        [shape_of(others[0].shape, BF16)],
        "first_norm_backward",
        after,
        inside=False,
    )[0]


def shards(
    atoms,
    pair_bias,
    lengths,
    first_gain,
    first_shift,
    query_weight,
    query_bias,
    key_weight,
    value_weight,
    value_bias,
    out_weight,
    out_bias,
    second_gain,
    second_shift,
    inner_weight,
    inner_bias,
    outer_weight,
    outer_bias,
    atoms_cotangent,
    pair_cotangent,
):
    molecules, rows, model_width = atoms.shape
    head_count = pair_bias.shape[1]
    head_size = model_width // head_count
    batch_count = lax.axis_size("batch")
    batch_index = lax.axis_index("batch")
    row = lax.axis_index("rows")
    (
        atoms_far,
        pair_bias,
        first_gain,
        first_shift,
        query_weight,
        query_bias,
        key_weight,
        value_weight,
        value_bias,
        out_weight,
        out_bias,
        second_gain,
        second_shift,
        inner_weight,
        inner_bias,
        outer_weight,
        outer_bias,
        atoms_cotangent,
        pair_cotangent,
    ) = [
        pltpu.with_memory_space_constraint(a, pltpu.HBM)
        for a in (
            atoms,
            pair_bias,
            first_gain,
            first_shift,
            query_weight,
            query_bias,
            key_weight,
            value_weight,
            value_bias,
            out_weight,
            out_bias,
            second_gain,
            second_shift,
            inner_weight,
            inner_bias,
            outer_weight,
            outer_bias,
            atoms_cotangent,
            pair_cotangent,
        )
    ]
    place = jnp.stack(
        [batch_index, row, batch_index & 1, (batch_index >> 1) & 1, (batch_index >> 2) & 1]
    ).astype(jnp.int32)
    line = lambda v: v
    count = molecules // STAGES
    stages = []
    pair_out = jnp.zeros((1,), BF16)
    gathered = []
    for stage in range(STAGES):
        mine = atoms[stage * count : (stage + 1) * count]
        gathered.append([swap(mine, "rows", mask) for mask in (1, 2, 3)])
    pair_near, query_near, key_near, value_near = pair_bias, query_weight, key_weight, value_weight
    for stage in range(STAGES):
        first = stage * count
        pieces = [atoms_far] + gathered[stage]
        pair_out, *kept = attention_forward(
            head_size,
            first,
            count,
            place,
            lengths,
            pieces,
            pair_near,
            (
                line(first_gain),
                line(first_shift),
                query_near,
                line(query_bias),
                key_near,
                value_near,
                line(value_bias),
            ),
            pair_out,
        )
        stages.append(kept)
    (
        atoms_out,
        outer_send,
        outer_keep,
        inner_send,
        inner_keep,
        out_send,
        out_keep,
        grad_middle,
        grad_mixed,
        dense_vectors,
    ) = dense(
        place,
        [s[1] for s in stages],
        atoms,
        atoms_cotangent,
        (
            out_weight,
            line(out_bias),
            line(second_gain),
            line(second_shift),
            inner_weight,
            line(inner_bias),
            outer_weight,
            line(outer_bias),
        ),
        batch_count,
    )
    pairs = batch_count // 2
    own_rows = model_width // batch_count
    slots = lambda a: a.reshape(pairs, -1, own_rows, model_width)
    dense_groups = [
        ([slots(outer_keep)], [slots(outer_send)]),
        ([inner_keep], [inner_send]),
        ([slots(out_keep)], [slots(out_send)]),
    ]
    usual = batch_count == 8
    if usual:
        dense_pieces, held = sum_core(place, dense_groups, dense_vectors, "dense")
        after = [held]
    else:
        dense_total, dense_vectors = batch_slices_any(dense_groups, dense_vectors)
        after = []

    def backward(stage, span, held, sums, after):
        return attention_backward(
            head_size,
            stage * count,
            span,
            place,
            stages[stage],
            pair_cotangent,
            grad_mixed,
            (query_near, key_near, value_near),
            held,
            sums,
            after,
        )

    pair_grad, near0, cross0, own0, sums, *grads0 = backward(0, (0, count), None, None, after)
    near0 = swap(near0, "rows", 1)
    after = []
    if usual:
        dense_pieces, held = sum_first(place, dense_pieces, "dense", (own0,))
        after = [held]
    half = count // 2
    pair_grad, near1, cross1, own1, sums, *grads1 = backward(1, (0, half), pair_grad, sums, after)
    near1 = swap(near1, "rows", 1)
    after = [own1]
    came = near1
    if usual:
        dense_total, came = sum_second_cut(place, dense_pieces, "dense", after)
        after = [dense_total]
    cross0 = cross_sum([cross0], [near0], "cross_first", after)
    far0 = swap(cross0, "rows", 2)
    pair_grad, near2, cross2, own2, tail_vectors, *grads2 = backward(
        1, (half, count), pair_grad, sums, [cross0]
    )
    near2 = swap(near2, "rows", 1)
    part = shape_of((pairs, 1, own_rows, model_width), BF16)
    parts = small_call(
        functools.partial(weight_kernel, 3, STAGES),
        place,
        [s[3] for s in stages] + grads0 + grads1 + grads2,
        [part] * 6,
        "attention_weights",
        (far0, near1, came),
        scratch=[pltpu.VMEM((pairs, 2, own_rows, model_width), F32)],
        mib=14,
    )
    groups = [([parts[2 * i + 1]], [parts[2 * i]]) for i in range(3)]
    matrix = shape_of((own_rows, model_width), F32)
    ratio = inner_weight.shape[1] // model_width
    vectors_shape = shape_of((8, model_width), F32)
    finish = (atoms, line(first_gain), line(first_shift), grad_middle)
    if usual:
        pieces, held = sum_core(place, groups, tail_vectors, "tail")
        part = shape_of((came.shape[0] // 2, model_width), BF16)
        sent, kept = small_call(
            near_sum_kernel,
            place,
            [dense_total, came],
            [part, shape_of(part.shape, F32)],
            "dense_near_sum",
            (held,),
        )
        came = swap(sent, "rows", 2)
        cross1 = cross_sum([cross1, cross2], [near1, near2], "cross_second", (sent,))
        far1 = swap(cross1, "rows", 2)
        pieces, held = sum_first(place, pieces, "tail", (cross1,))
        total = sum_second(pieces, "tail", (held,))
        tail_came = swap(total, "rows", 1)
        mine = small_call(add_kernel, None, [kept, came], [part], "dense_far_sum", (total,))[0]
        came = swap(mine, "rows", 2)
        atoms_grad = first_norm_backward(
            [own0, own1, own2], [near0, near1, near2], [far0, far1], finish, (mine,)
        )
        total = small_call(
            add_kernel, None, [total, tail_came], [total], "tail_near_sum", (atoms_grad,)
        )[0]
        tail_came = swap(total, "rows", 2)
        half_shape = shape_of((2 * part.shape[0], model_width), BF16)
        mine = small_call(
            join_kernel, place, [mine, came], [half_shape], "dense_join", (total,)
        )[0]
        came = swap(mine, "rows", 1)
        outer_grad, inner_grad, out_grad, dense_vectors = small_call(
            functools.partial(finish_dense_kernel, ratio),
            place,
            [mine, came],
            [
                shape_of((ratio * own_rows, model_width), F32),
                shape_of((own_rows, ratio * model_width), F32),
                matrix,
                vectors_shape,
            ],
            "finish_dense",
            (total,),
            inside=False,
            scratch=[pltpu.VMEM((4 * part.shape[0], model_width), BF16)],
        )
        query_grad, key_grad, value_grad, tail_vectors = small_call(
            finish_tail_kernel,
            None,
            [total, tail_came],
            [matrix, matrix, matrix, vectors_shape],
            "finish_tail",
            (out_grad,),
            inside=False,
        )
    else:
        far1 = swap(cross_sum([cross1, cross2], [near1, near2], "cross_second"), "rows", 2)
        atoms_grad = first_norm_backward(
            [own0, own1, own2], [near0, near1, near2], [far0, far1], finish
        )
        total, tail_vectors = batch_slices_any(groups, tail_vectors)
        query_grad, key_grad, value_grad = total[0], total[1], total[2]
        outer_grad = dense_total[:ratio].reshape(-1, model_width)
        inner_grad = dense_total[ratio : 2 * ratio].transpose(1, 0, 2).reshape(own_rows, -1)
        out_grad = dense_total[2 * ratio]
    part = lambda v: lax.dynamic_slice_in_dim(
        v, batch_index * (v.shape[0] // batch_count), v.shape[0] // batch_count
    )
    return (
        atoms_out,
        pair_out,
        atoms_grad,
        pair_grad,
        part(tail_vectors[0]),
        part(tail_vectors[1]),
        query_grad,
        part(tail_vectors[2]),
        key_grad,
        value_grad,
        part(tail_vectors[3]),
        out_grad,
        part(dense_vectors[3]),
        part(dense_vectors[1]),
        part(dense_vectors[2]),
        inner_grad,
        part(dense_vectors[4:].reshape(-1)),
        outer_grad,
        part(dense_vectors[0]),
    )


def solution(mesh):
    tokens = P("batch", "rows", None)
    pairs = P("batch", None, "rows", None)
    vector = P("batch")
    matrix = P("batch", None)
    return jax.shard_map(
        shards,
        mesh=mesh,
        in_specs=(tokens, pairs, P("batch")) + (P(),) * 15 + (tokens, pairs),
        out_specs=(
            tokens,
            pairs,
            tokens,
            pairs,
            vector,
            vector,
            matrix,
            vector,
            matrix,
            matrix,
            vector,
            matrix,
            vector,
            vector,
            vector,
            matrix,
            vector,
            matrix,
            vector,
        ),
        check_vma=False,
    )
```

```python
import functools
import math

import jax
import jax.numpy as jnp
from jax import lax
from jax.experimental import pallas as pl
from jax.experimental.pallas import tpu as pltpu
from jax.sharding import PartitionSpec as P

EPSILON = 1e-05
MASKED = -1000000000.0
F32 = jnp.float32
BF16 = jnp.bfloat16
LANES = 128
STAGES = 2
VMEM_LIMIT = 18 << 20


def shape_of(shape, dtype):
    return jax.ShapeDtypeStruct(tuple(shape), dtype)


def norm_forward(values_in, gain, shift):
    centre = values_in - jnp.mean(values_in, -1, keepdims=True)
    inverse = lax.rsqrt(jnp.mean(centre * centre, -1, keepdims=True) + EPSILON)
    normed = centre * inverse
    return (normed * gain + shift, normed, inverse)


def norm_backward(upstream, normed, inverse, gain):
    scaled = upstream * gain
    return inverse * (
        scaled
        - jnp.mean(scaled, -1, keepdims=True)
        - normed * jnp.mean(scaled * normed, -1, keepdims=True)
    )


def dot(left, right):
    return jnp.dot(left, right, preferred_element_type=F32)


def across(left, right):
    return lax.dot_general(left, right, (((0,), (0,)), ((), ())), preferred_element_type=F32)


def against(left, right):
    return lax.dot_general(left, right, (((1,), (1,)), ((), ())), preferred_element_type=F32)


def column_sum(values_in):
    return jnp.sum(values_in.astype(F32), 0, keepdims=True)


def near(shape, dtype):
    return pltpu.VMEM(tuple(shape), dtype)


def near_spec():
    return pl.BlockSpec(memory_space=pltpu.VMEM)


def as_row(ref):
    return ref[...].astype(F32).reshape(1, -1)


def whole(array):
    return pl.BlockSpec(array.shape, lambda *_: (0,) * array.ndim)


def params(mib=10):
    return pltpu.CompilerParams(vmem_limit_bytes=mib << 20)


def load_kernel(count, starts, *refs):
    sources, targets, semaphores = refs[:count], refs[-count - 1 : -1], refs[-1]
    copies = [
        pltpu.make_async_copy(source.at[pl.ds(start, target.shape[0])], target, semaphores.at[i])
        for i, (source, target, start) in enumerate(zip(sources, targets, starts))
    ]
    for copy in copies:
        copy.start()
    for copy in copies:
        copy.wait()


def copies_beside(sources, targets, semaphores):
    return [
        pltpu.make_async_copy(source, target, semaphores.at[i])
        for i, (source, target) in enumerate(zip(sources, targets))
    ]


def load(arrays, name, starts=None, after=()):
    count = len(arrays)
    starts = starts or (0,) * count
    return pl.pallas_call(
        functools.partial(load_kernel, count, starts),
        in_specs=[pl.BlockSpec(memory_space=pltpu.HBM)] * count
        + [pl.BlockSpec(memory_space=pl.ANY)] * len(after),
        out_specs=[near_spec()] * count,
        out_shape=[
            near((a.shape[0] - start,) + a.shape[1:], a.dtype) for a, start in zip(arrays, starts)
        ],
        scratch_shapes=[pltpu.SemaphoreType.DMA((count,))],
        compiler_params=params(),
        name=name,
    )(*arrays, *after)


def project(pieces, first, parameters, row, refs, atoms_scratch):
    gain_ref, shift_ref, key_weight_ref, value_weight_ref, value_bias_ref = parameters
    hidden_ref, normed_ref, key_ref, value_ref = refs
    count = hidden_ref.shape[0]
    _, groups, keys, width = key_ref.shape
    rows = keys // 4
    half = 2 * rows
    model_width = hidden_ref.shape[2]
    for m in range(count):
        for i, piece in enumerate(pieces):
            start = pl.multiple_of(m * half + ((row ^ i) & 1) * rows, rows)
            atoms_scratch[pl.ds(start, rows)] = piece[m + first]
    hidden, normed, _ = norm_forward(
        atoms_scratch[...].astype(F32), as_row(gain_ref), as_row(shift_ref)
    )
    hidden = hidden.astype(BF16)
    normed = normed.astype(BF16)
    key_rows = dot(hidden, key_weight_ref[...]).astype(BF16)
    value_rows = (dot(hidden, value_weight_ref[...]) + as_row(value_bias_ref)).astype(BF16)
    return [a.reshape(count, half, model_width) for a in (hidden, normed, key_rows, value_rows)]


def put_half(values, at, refs):
    hidden, normed, key_rows, value_rows = values
    hidden_ref, normed_ref, key_ref, value_ref = refs
    count, groups, _, width = key_ref.shape
    half = hidden.shape[1]
    ones = jnp.ones((count, half, width), BF16)
    hidden_ref[:, at] = hidden
    normed_ref[:, at] = normed
    for t in range(groups):
        lanes = slice(t * width, (t + 1) * width)
        key_ref[:, t, at] = key_rows[:, :, lanes]
        value_ref[:, t, at, :width] = value_rows[:, :, lanes]
        value_ref[:, t, at, width:] = ones


def half_rows(row, other, rows):
    which = row >> 1
    which = 1 - which if other else which
    return pl.ds(pl.multiple_of(which * 2 * rows, 2 * rows), 2 * rows)


def near_half_kernel(
    head_size,
    stages,
    ahead,
    place_ref,
    own_ref,
    one_ref,
    gain_ref,
    shift_ref,
    query_weight_ref,
    query_bias_ref,
    key_weight_ref,
    value_weight_ref,
    value_bias_ref,
    *refs,
):
    refs = refs[ahead:]
    atoms_scratch = refs[-1]
    row = place_ref[1]
    rows, model_width = own_ref.shape[1:]
    factor = head_size**-0.5
    parameters = (gain_ref, shift_ref, key_weight_ref, value_weight_ref, value_bias_ref)
    for stage in range(stages):
        hidden_ref, normed_ref, key_ref, value_ref, query_ref = refs[5 * stage : 5 * stage + 5]
        outs = (hidden_ref, normed_ref, key_ref, value_ref)
        count, groups, _, width = key_ref.shape
        values = project((own_ref, one_ref), stage * count, parameters, row, outs, atoms_scratch)
        put_half(values, half_rows(row, False, rows), outs)
        mine = pl.ds(pl.multiple_of(row * rows, rows), rows)
        own = jnp.concatenate([hidden_ref[m, mine] for m in range(count)], 0)
        query_rows = (dot(own, query_weight_ref[...]) + as_row(query_bias_ref)) * factor
        query_rows = query_rows.astype(BF16).reshape(count, rows, model_width)
        for t in range(groups):
            query_ref[:, t] = query_rows[:, :, t * width : (t + 1) * width]


def near_half(head_size, stages, place, atoms, one, parameters, after):
    molecules, rows, model_width = atoms.shape
    keys = 4 * rows
    count = molecules // stages
    groups = model_width // LANES
    operands = (place, atoms, one, *parameters, *after)
    return pl.pallas_call(
        functools.partial(near_half_kernel, head_size, stages, len(after)),
        grid_spec=pltpu.PrefetchScalarGridSpec(
            num_scalar_prefetch=1,
            grid=(1,),
            in_specs=[whole(atoms), near_spec()]
            + [near_spec() if a.ndim > 1 else whole(a) for a in parameters]
            + [pl.BlockSpec(memory_space=pl.ANY)] * len(after),
            out_specs=[near_spec()] * (5 * stages),
            scratch_shapes=[pltpu.VMEM((count * 2 * rows, model_width), BF16)],
        ),
        out_shape=[
            near((count, keys, model_width), BF16),
            near((count, keys, model_width), BF16),
            near((count, groups, keys, LANES), BF16),
            near((count, groups, keys, 2 * LANES), BF16),
            near((count, groups, rows, LANES), BF16),
        ]
        * stages,
        compiler_params=params(10),
        name="near_half",
    )(*operands)


def forward_kernel(
    head_size,
    chunk,
    first,
    extra,
    place_ref,
    length_ref,
    two_ref,
    three_ref,
    pair_ref,
    query_ref,
    gain_ref,
    shift_ref,
    key_weight_ref,
    value_weight_ref,
    value_bias_ref,
    *refs,
):
    (
        pair_out_ref,
        weights_ref,
        mixed_ref,
        inverse_ref,
        hidden_ref,
        normed_ref,
        key_ref,
        value_ref,
    ) = refs[5 + extra : 13 + extra]
    atoms_scratch, semaphores = refs[-2:]
    copies = copies_beside(refs[5 : 5 + extra], refs[13 + extra : 13 + 2 * extra], semaphores)
    molecule = pl.program_id(0)
    group = pl.program_id(1)
    count, groups, keys, width = key_ref.shape
    heads = width // head_size
    rows = query_ref.shape[2]

    @pl.when((molecule == 0) & (group == 0))
    def _():
        for copy in copies:
            copy.start()
        row = place_ref[1]
        outs = (hidden_ref, normed_ref, key_ref, value_ref)
        parameters = (gain_ref, shift_ref, key_weight_ref, value_weight_ref, value_bias_ref)
        values = project((two_ref, three_ref), 0, parameters, row, outs, atoms_scratch)
        put_half(values, half_rows(row, True, rows), outs)

    query = query_ref[molecule, group]
    key = key_ref[molecule, group]
    value = value_ref[molecule, group]
    valid = lax.broadcasted_iota(jnp.int32, (1, keys), 1) < length_ref[molecule + first]
    lane = lax.broadcasted_iota(jnp.int32, (1, width), 1) // head_size
    lane_pair = lax.broadcasted_iota(jnp.int32, (1, 2 * width), 1) % width // head_size
    total = jnp.zeros((rows, 2 * width), F32)
    zero = jnp.zeros((), BF16)
    for c in range(0, heads, chunk):
        here = slice(c, c + chunk)
        there = pl.ds(group * heads + c, chunk)
        spread = jnp.concatenate([jnp.where(lane == c + t, query, zero) for t in range(chunk)], 0)
        pair = pair_ref[molecule + first, there].reshape(chunk * rows, keys)
        scores = against(spread, key) + pair.astype(F32)
        pair_out_ref[0, here] = scores.astype(BF16).reshape(chunk, rows, keys)
        masked = jnp.where(valid, scores, MASKED)
        weights = jnp.exp(masked - jnp.max(masked, -1, keepdims=True)).astype(BF16)
        weights_ref[molecule, there] = weights.reshape(chunk, rows, keys)
        product = dot(weights, value)
        for t in range(chunk):
            total = jnp.where(lane_pair == c + t, product[t * rows : (t + 1) * rows], total)
    inverse = 1.0 / total[:, width:]
    inverse_ref[molecule, group] = inverse
    mixed_ref[molecule, group] = total[:, :width] * inverse

    @pl.when((molecule == count - 1) & (group == groups - 1))
    def _():
        for copy in copies:
            copy.wait()


def attention_forward(
    head_size, first, place, lengths, pieces, pair_bias, parameters, projected, held, extra
):
    _, head_count, rows, keys = pair_bias.shape
    hidden, normed, key, value, query = projected
    count, groups = key.shape[:2]
    model_width = groups * LANES
    heads = LANES // head_size
    pair_spec = pl.BlockSpec((1, heads, rows, keys), lambda m, g, *_: (m + first, g, 0, 0))
    elements = count * head_count * rows * keys
    operands = [place, lengths, *pieces, pair_bias, query, *parameters]
    in_specs = [near_spec()] * (len(pieces) + 2)
    in_specs += [near_spec() if a.ndim > 1 else whole(a) for a in parameters]
    start = len(operands)
    operands += [hidden, normed, key, value, held]
    in_specs += [near_spec()] * 4 + [pl.BlockSpec(memory_space=pl.ANY)]
    aliases = {start + i: 4 + i for i in range(4)}
    if held.ndim > 1:
        aliases[start + 4] = 0
    operands += extra
    in_specs += [pl.BlockSpec(memory_space=pltpu.HBM)] * len(extra)
    outs = pl.pallas_call(
        functools.partial(forward_kernel, head_size, 8, first, len(extra)),
        grid_spec=pltpu.PrefetchScalarGridSpec(
            num_scalar_prefetch=2,
            grid=(count, groups),
            in_specs=in_specs,
            out_specs=[pair_spec] + [near_spec()] * (7 + len(extra)),
            scratch_shapes=[
                pltpu.VMEM((count * 2 * rows, model_width), BF16),
                pltpu.SemaphoreType.DMA((max(len(extra), 1),)),
            ],
        ),
        out_shape=[
            shape_of(pair_bias.shape, BF16),
            near((count, head_count, rows, keys), BF16),
            near((count, groups, rows, LANES), F32),
            near((count, groups, rows, LANES), F32),
            near(hidden.shape, BF16),
            near(normed.shape, BF16),
            near(key.shape, BF16),
            near(value.shape, BF16),
        ]
        + [near(a.shape, a.dtype) for a in extra],
        input_output_aliases=aliases,
        compiler_params=params(10),
        cost_estimate=pl.CostEstimate(
            flops=elements * 2 * 384, transcendentals=elements, bytes_accessed=elements * 6
        ),
        name="attention_forward",
    )(*operands)
    pair_out, weights, mixed, inverse, hidden, normed, key, value = outs[:8]
    return pair_out, (weights, mixed, inverse, hidden, normed, query, key, value), outs[8:]


def dense_kernel(
    mixed_count,
    place_ref,
    *refs,
):
    mixed_refs = refs[:mixed_count]
    (
        atoms_ref,
        cotangent_ref,
        out_weight_ref,
        out_bias_ref,
        gain_ref,
        shift_ref,
        inner_weight_ref,
        inner_bias_ref,
        outer_weight_ref,
        outer_bias_ref,
        far_ref,
        atoms_out_ref,
        outer_send_ref,
        outer_keep_ref,
        inner_send_ref,
        inner_keep_ref,
        out_send_ref,
        out_keep_ref,
        grad_middle_ref,
        grad_mixed_ref,
        vectors_ref,
        copied_ref,
        hidden_scratch,
        turned_scratch,
        normed_scratch,
        inverse_scratch,
        result_scratch,
        upstream_scratch,
        outer_scratch,
        inner_scratch,
        semaphores,
    ) = refs[mixed_count:]
    (copy,) = copies_beside([far_ref], [copied_ref], semaphores)
    step = pl.program_id(0)
    steps = pl.num_programs(0)
    core = place_ref[2]
    tokens, model_width = hidden_scratch.shape
    cotangent = cotangent_ref[...].reshape(tokens, model_width)

    def mixed_rows():
        parts = []
        for ref in mixed_refs:
            count, groups, rows, width = ref.shape
            join = [ref[:, t].reshape(count * rows, width) for t in range(groups)]
            parts.append(jnp.concatenate(join, 1))
        return jnp.concatenate(parts, 0)

    @pl.when(step == 0)
    def _():
        copy.start()
        mixed_low = mixed_rows().astype(BF16)
        middle = (
            atoms_ref[...].reshape(tokens, model_width).astype(F32)
            + dot(mixed_low, out_weight_ref[...])
            + as_row(out_bias_ref)
        )
        hidden, normed, inverse = norm_forward(
            middle, as_row(gain_ref), as_row(shift_ref)
        )
        hidden_scratch[...] = hidden.astype(BF16)
        turned_scratch[...] = jnp.transpose(hidden).astype(BF16)
        normed_scratch[...] = normed
        inverse_scratch[...] = inverse
        result_scratch[...] = middle + as_row(outer_bias_ref)
        upstream_scratch[...] = jnp.zeros_like(upstream_scratch)
        vectors_ref[0:1] = column_sum(cotangent)

    hidden = hidden_scratch[...]
    width = outer_weight_ref.shape[1]
    at = pl.ds(pl.multiple_of(step * width, width), width)
    inner_weight = inner_weight_ref[:, at]
    outer_weight = outer_weight_ref[at]
    pre = dot(hidden, inner_weight) + as_row(inner_bias_ref)
    slope = math.sqrt(2.0 / math.pi)
    square = pre * pre
    tanh = jnp.tanh(slope * (pre + 0.044715 * (pre * square)))
    half = 0.5 * (1.0 + tanh)
    active = (pre * half).astype(BF16)
    result_scratch[...] += dot(active, outer_weight)
    derivative = half + (0.5 * slope) * pre * (1.0 - tanh * tanh) * (1.0 + 0.134145 * square)
    grad_pre = against(cotangent, outer_weight) * derivative
    vectors_ref[pl.ds(4 + step, 1)] = column_sum(grad_pre.astype(BF16))
    grad_pre = grad_pre.astype(BF16)
    outer_scratch[...] = across(active, cotangent).reshape(outer_scratch.shape)
    outer_send_ref[...] = outer_scratch[:, 1 - core].astype(BF16).reshape(outer_send_ref.shape)
    outer_keep_ref[...] = outer_scratch[:, core].astype(BF16).reshape(outer_keep_ref.shape)
    inner_scratch[...] = dot(turned_scratch[...], grad_pre).reshape(inner_scratch.shape)
    inner_send_ref[:, 0] = inner_scratch[:, 1 - core].astype(BF16)
    inner_keep_ref[:, 0] = inner_scratch[:, core].astype(BF16)
    upstream_scratch[...] += against(grad_pre, inner_weight)

    @pl.when(step == steps - 1)
    def _():
        atoms_out_ref[...] = result_scratch[...].astype(BF16).reshape(atoms_out_ref.shape)
        upstream = upstream_scratch[...]
        normed = normed_scratch[...]
        vectors_ref[1:2] = column_sum(upstream * normed)
        vectors_ref[2:3] = column_sum(upstream)
        grad_middle = cotangent.astype(F32) + norm_backward(
            upstream, normed, inverse_scratch[...], as_row(gain_ref)
        )
        grad_middle_ref[...] = grad_middle.reshape(grad_middle_ref.shape)
        branch = grad_middle.astype(BF16)
        vectors_ref[3:4] = column_sum(branch)
        grad_mixed = against(branch, out_weight_ref[...]).astype(BF16)
        molecules, groups, rows, lanes = grad_mixed_ref.shape
        grad_mixed = grad_mixed.reshape(molecules, rows, model_width)
        for t in range(groups):
            grad_mixed_ref[:, t] = grad_mixed[:, :, t * lanes : (t + 1) * lanes]
        turned = jnp.transpose(mixed_rows()).astype(BF16)
        inner_scratch[...] = dot(turned, branch).reshape(inner_scratch.shape)
        out_send_ref[...] = inner_scratch[:, 1 - core].astype(BF16)
        out_keep_ref[...] = inner_scratch[:, core].astype(BF16)
        copy.wait()


def dense(place, mixed, atoms, cotangent, parameters, batch_count, extra):
    (
        out_weight,
        out_bias,
        gain,
        shift,
        inner_weight,
        inner_bias,
        outer_weight,
        outer_bias,
    ) = parameters
    model_width, inner_width = inner_weight.shape
    tokens = atoms.shape[0] * atoms.shape[1]
    width = model_width
    steps = inner_width // width
    pairs = batch_count // 2
    outer_rows = inner_width // batch_count
    outer_pairs = width // (2 * outer_rows)
    own_rows = model_width // batch_count
    operands = (
        place,
        *mixed,
        atoms,
        cotangent,
        out_weight,
        out_bias,
        gain,
        shift,
        inner_weight,
        inner_bias,
        outer_weight,
        outer_bias,
        extra,
    )
    outer_spec = pl.BlockSpec((outer_pairs, outer_rows, model_width), lambda s, *_: (s, 0, 0))
    inner_spec = pl.BlockSpec((pairs, 1, own_rows, width), lambda s, *_: (0, s, 0, 0))
    outer_shape = shape_of((pairs, outer_rows, model_width), BF16)
    inner_shape = shape_of((pairs, steps, own_rows, width), BF16)
    out_shape = shape_of((pairs, own_rows, model_width), BF16)
    out_shapes = [
        shape_of(atoms.shape, BF16),
        outer_shape,
        outer_shape,
        inner_shape,
        inner_shape,
        out_shape,
        out_shape,
        near(atoms.shape, F32),
        near((atoms.shape[0], model_width // LANES, atoms.shape[1], LANES), BF16),
        shape_of((4 + steps, model_width), F32),
        near(extra.shape, extra.dtype),
    ]
    fixed = lambda s: pl.BlockSpec(s.shape, lambda *_: (0,) * len(s.shape))
    out_specs = [fixed(s) for s in out_shapes]
    out_specs[1:5] = [outer_spec, outer_spec, inner_spec, inner_spec]
    out_specs[7:9] = [near_spec(), near_spec()]
    out_specs[10] = near_spec()
    in_specs = [whole(a) for a in operands[1:]]
    for i, a in enumerate(operands[1:]):
        if a.ndim > 1 and i != len(mixed):
            in_specs[i] = near_spec()
    in_specs[-4] = pl.BlockSpec((width,), lambda s, *_: (s,))
    in_specs[-1] = pl.BlockSpec(memory_space=pltpu.HBM)
    return pl.pallas_call(
        functools.partial(dense_kernel, len(mixed)),
        grid_spec=pltpu.PrefetchScalarGridSpec(
            num_scalar_prefetch=1,
            grid=(steps,),
            in_specs=in_specs,
            out_specs=out_specs,
            scratch_shapes=[
                pltpu.VMEM((tokens, model_width), BF16),
                pltpu.VMEM((model_width, tokens), BF16),
                pltpu.VMEM((tokens, model_width), F32),
                pltpu.VMEM((tokens, 1), F32),
                pltpu.VMEM((tokens, model_width), F32),
                pltpu.VMEM((tokens, model_width), F32),
                pltpu.VMEM((outer_pairs, 2, outer_rows, model_width), F32),
                pltpu.VMEM((pairs, 2, own_rows, width), F32),
                pltpu.SemaphoreType.DMA((1,)),
            ],
        ),
        out_shape=out_shapes,
        compiler_params=params(14),
        cost_estimate=pl.CostEstimate(
            flops=12 * tokens * model_width * inner_width,
            transcendentals=tokens * inner_width,
            bytes_accessed=12 * model_width * inner_width,
        ),
        name="dense",
    )(*operands)


def backward_kernel(
    head_size,
    chunk,
    first,
    base,
    start,
    fresh,
    joined,
    place_ref,
    weights_ref,
    cotangent_ref,
    grad_mixed_ref,
    mixed_ref,
    inverse_ref,
    query_ref,
    key_ref,
    value_ref,
    normed_ref,
    query_weight_ref,
    key_weight_ref,
    value_weight_ref,
    *refs,
):
    before_ref = refs[start - 1] if joined else None
    refs = refs[start:]
    pair_grad_ref, near_ref, cross_ref, own_ref, vectors_ref = refs[:5]
    query_grad_ref, key_grad_ref, value_grad_ref = refs[5:8]
    grad_query_scratch, grad_key_scratch, grad_value_scratch, grad_scratch = refs[-4:]
    molecule = pl.program_id(0) + base
    group = pl.program_id(1)
    _, groups, rows, width = query_ref.shape
    keys = key_ref.shape[2]
    heads = width // head_size
    factor = head_size**-0.5
    query = query_ref[molecule, group]
    key = key_ref[molecule, group]
    value = value_ref[molecule, group]
    upstream = grad_mixed_ref[molecule + first, group].astype(F32) * inverse_ref[molecule, group]
    upstream = upstream.astype(BF16)
    offset = (-(upstream.astype(F32) * mixed_ref[molecule, group])).astype(BF16)
    both = jnp.concatenate([upstream, offset], 1)
    lane = lax.broadcasted_iota(jnp.int32, (1, width), 1) // head_size
    lane_pair = lax.broadcasted_iota(jnp.int32, (1, 2 * width), 1) % width // head_size
    query_turned = jnp.transpose(query.astype(F32)).astype(BF16)
    upstream_turned = jnp.transpose(upstream.astype(F32)).astype(BF16)
    query_turned = jnp.concatenate([query_turned] * chunk, 1)
    upstream_turned = jnp.concatenate([upstream_turned] * chunk, 1)
    turned_shape = (chunk * head_size, chunk * rows)
    same = (
        lax.broadcasted_iota(jnp.int32, turned_shape, 0) // head_size
        == lax.broadcasted_iota(jnp.int32, turned_shape, 1) // rows
    )
    zero = jnp.zeros((), BF16)
    total = jnp.zeros((rows, width), F32)
    key_parts = []
    value_parts = []
    for c in range(0, heads, chunk):
        here = slice(c, c + chunk)
        feature = slice(c * head_size, (c + chunk) * head_size)
        spread = jnp.concatenate([jnp.where(lane_pair == c + t, both, zero) for t in range(chunk)], 0)
        centred = against(spread, value)
        there = pl.ds(group * heads + c, chunk)
        weights = weights_ref[molecule, there].reshape(chunk * rows, keys)
        cotangent = cotangent_ref[molecule + first, there].reshape(chunk * rows, keys)
        grad = (weights.astype(F32) * centred + cotangent.astype(F32)).astype(BF16)
        pair_grad_ref[0, here] = grad.reshape(chunk, rows, keys)
        product = dot(grad, key)
        for t in range(chunk):
            total = jnp.where(lane == c + t, product[t * rows : (t + 1) * rows], total)
        key_parts.append(dot(jnp.where(same, query_turned[feature], zero), grad))
        value_parts.append(dot(jnp.where(same, upstream_turned[feature], zero), weights))
    grad_query_scratch[group] = (total * factor).astype(BF16)
    grad_key_scratch[group] = jnp.transpose(jnp.concatenate(key_parts, 0)).astype(BF16)
    grad_value_scratch[group] = jnp.transpose(jnp.concatenate(value_parts, 0)).astype(BF16)

    if fresh:

        @pl.when((pl.program_id(0) == 0) & (group == 0))
        def _():
            vectors_ref[...] = jnp.zeros_like(vectors_ref)

    @pl.when(group == groups - 1)
    def _():
        row = place_ref[1]
        mine = pl.ds(pl.multiple_of(row * rows, rows), rows)
        join = lambda ref: jnp.concatenate([ref[t] for t in range(groups)], 1)
        grad_query = join(grad_query_scratch)
        grad_key = join(grad_key_scratch)
        grad_value = join(grad_value_scratch)
        query_grad_ref[0] = grad_query
        key_grad_ref[0] = grad_key
        value_grad_ref[0] = grad_value
        grad_scratch[...] = against(grad_key, key_weight_ref[...]) + against(
            grad_value, value_weight_ref[...]
        )
        grad_scratch[mine] += against(grad_query, query_weight_ref[...])
        grad = grad_scratch[...]
        vectors_ref[0:1] += column_sum(grad * normed_ref[molecule].astype(F32))
        vectors_ref[1:2] += column_sum(grad)
        vectors_ref[2:3] += column_sum(grad_query)
        vectors_ref[3:4] += column_sum(grad_value)
        at = lambda other: pl.ds(pl.multiple_of((row ^ other) * rows, rows), rows)
        slot = near_ref.shape[1] - 1
        near_ref[0, slot] = grad_scratch[at(1)].astype(BF16)
        near_ref[1, slot] = grad_scratch[at(3)].astype(BF16)
        if joined:
            near_ref[:, 0] = before_ref[:, 0]
        cross_ref[0] = grad_scratch[at(2)].astype(BF16)
        own_ref[0] = grad_scratch[mine]


def attention_backward(
    head_size, first, base, place, stage, cotangent, grad_mixed, parameters, held, sums, after, before
):
    weights, mixed, inverse, _, normed, query, key, value = stage
    _, head_count, rows, keys = weights.shape
    count = 1
    groups = query.shape[1]
    model_width = groups * LANES
    heads = LANES // head_size
    pair_spec = pl.BlockSpec((1, heads, rows, keys), lambda m, g, *_: (m + first + base, g, 0, 0))
    elements = count * head_count * rows * keys
    operands = [
        place,
        weights,
        cotangent,
        grad_mixed,
        mixed,
        inverse,
        query,
        key,
        value,
        normed,
        *parameters,
    ]
    in_specs = [near_spec()] * (len(operands) - 1)
    aliases = {}
    start = len(operands)
    if sums is not None:
        aliases = {start: 0, start + 1: 4}
        operands += [held, sums]
        in_specs += [pl.BlockSpec(memory_space=pl.ANY), near_spec()]
    operands += list(after)
    in_specs += [pl.BlockSpec(memory_space=pl.ANY)] * len(after)
    joined = before is not None
    if joined:
        operands.append(before)
        in_specs.append(near_spec())
    out_shape = [
        shape_of(cotangent.shape, BF16),
        near((2, 1 + joined, rows, model_width), BF16),
        near((count, rows, model_width), BF16),
        near((count, rows, model_width), F32),
        near((8, model_width), F32),
        near((count, rows, model_width), BF16),
        near((count, keys, model_width), BF16),
        near((count, keys, model_width), BF16),
    ]
    out_specs = [
        pair_spec,
        near_spec(),
        near_spec(),
        near_spec(),
        near_spec(),
        near_spec(),
        near_spec(),
        near_spec(),
    ]
    return pl.pallas_call(
        functools.partial(
            backward_kernel, head_size, 4, first, base, len(operands) - start, sums is None, joined
        ),
        grid_spec=pltpu.PrefetchScalarGridSpec(
            num_scalar_prefetch=1,
            grid=(count, groups),
            in_specs=in_specs,
            out_specs=out_specs,
            scratch_shapes=[
                pltpu.VMEM((groups, rows, LANES), BF16),
                pltpu.VMEM((groups, keys, LANES), BF16),
                pltpu.VMEM((groups, keys, LANES), BF16),
                pltpu.VMEM((keys, model_width), F32),
            ],
        ),
        out_shape=out_shape,
        input_output_aliases=aliases,
        compiler_params=params(8),
        cost_estimate=pl.CostEstimate(
            flops=elements * 2 * 768, transcendentals=0, bytes_accessed=elements * 6
        ),
        name="attention_backward",
    )(*operands)


def weight_kernel(calls, stages, place_ref, *refs):
    hidden_refs = refs[:stages]
    grads = refs[stages : stages + 3 * calls]
    out_refs = refs[stages + 3 * calls : -1]
    total_ref = refs[-1]
    rows = grads[0].shape[1]
    row = place_ref[1]
    core = place_ref[2]
    mine = pl.ds(pl.multiple_of(row * rows, rows), rows)
    hidden = [(ref, m) for ref in hidden_refs for m in range(ref.shape[0])]
    width = hidden_refs[0].shape[2]
    own = jnp.concatenate([ref[m, mine] for ref, m in hidden], 0)
    every = jnp.concatenate([ref[m] for ref, m in hidden], 0)
    own = jnp.transpose(own.astype(F32)).astype(BF16)
    every = jnp.transpose(every.astype(F32)).astype(BF16)
    for j, left in enumerate((own, every, every)):
        right = jnp.concatenate([grads[3 * c + j][...].reshape(-1, width) for c in range(calls)], 0)
        total_ref[...] = dot(left, right).reshape(total_ref.shape)
        send_ref, keep_ref = out_refs[2 * j : 2 * j + 2]
        send_ref[:, 0] = total_ref[:, 1 - core].astype(BF16)
        keep_ref[:, 0] = total_ref[:, core].astype(BF16)


def swap(value, axis, mask):
    size = lax.axis_size(axis)
    return lax.ppermute(value, axis, [(i, i ^ mask) for i in range(size)])


VECTOR_ROWS = 8


def first_sum_kernel(counts, place_ref, *refs):
    terms = sum(counts)
    mine_ref, other_ref = refs[terms : terms + 2]
    along_x_ref, along_y_ref, keep_x_ref, keep_y_ref, vectors_ref = refs[terms + 2 :]
    x, y = place_ref[3], place_ref[4]
    half = along_x_ref.shape[1]
    size = keep_x_ref.shape[1]
    low, high = slice(0, half), slice(half, None)
    row = 0
    start = 0
    for count in counts:
        group = refs[start : start + count]
        start += count
        for s in range(group[0].shape[1]):
            rows = group[0].shape[2]

            def total(at, lanes):
                values = [r[at, s, :, lanes].astype(F32) for r in group]
                return functools.reduce(lambda a, b: a + b, values)

            for k in range(2):
                to = slice(k * size + row, k * size + row + rows)
                here = slice(row, row + rows)
                along_x_ref[to] = total(2 * k + (1 - x), low).astype(BF16)
                keep_x_ref[k, here] = total(2 * k + x, low)
                along_y_ref[to] = total(2 * (1 - y) + k, high).astype(BF16)
                keep_y_ref[k, here] = total(2 * y + k, high)
            row += rows
    vectors = (mine_ref[...] + other_ref[...]).astype(BF16)
    vectors_ref[...] = vectors
    put_vectors(vectors, along_x_ref, along_y_ref)


def put_vectors(vectors, low_ref, high_ref):
    half = vectors.shape[1] // 2
    low_ref[low_ref.shape[0] - VECTOR_ROWS :] = vectors[:, :half]
    high_ref[high_ref.shape[0] - VECTOR_ROWS :] = vectors[:, half:]


def get_vectors(low_ref, high_ref):
    low = low_ref[low_ref.shape[0] - VECTOR_ROWS :]
    return jnp.concatenate([low, high_ref[high_ref.shape[0] - VECTOR_ROWS :]], 1).astype(F32)


def second_sum_kernel(
    place_ref,
    keep_x_ref,
    came_x_ref,
    keep_y_ref,
    came_y_ref,
    vectors_ref,
    send_y_ref,
    send_x_ref,
    left_x_ref,
    left_y_ref,
    vectors_out_ref,
):
    size = keep_x_ref.shape[1]
    for keep, came, send, left, me in (
        (keep_x_ref, came_x_ref, send_y_ref, left_x_ref, place_ref[4]),
        (keep_y_ref, came_y_ref, send_x_ref, left_y_ref, place_ref[3]),
    ):
        at = lambda i: pl.ds(pl.multiple_of(i * size, size), size)
        send[:size] = (keep[1 - me] + came[at(1 - me)].astype(F32)).astype(BF16)
        left[...] = keep[me] + came[at(me)].astype(F32)
    vectors = vectors_ref[...].astype(F32) + get_vectors(came_x_ref, came_y_ref)
    vectors = vectors.astype(BF16)
    vectors_out_ref[...] = vectors
    put_vectors(vectors, send_y_ref, send_x_ref)


def third_sum_kernel(left_x_ref, came_x_ref, left_y_ref, came_y_ref, vectors_ref, total_ref):
    size, half = left_x_ref.shape
    total_ref[:size, :half] = (left_x_ref[...] + came_x_ref[:size].astype(F32)).astype(BF16)
    total_ref[:size, half:] = (left_y_ref[...] + came_y_ref[:size].astype(F32)).astype(BF16)
    vectors = vectors_ref[...].astype(F32) + get_vectors(came_x_ref, came_y_ref)
    total_ref[size : size + VECTOR_ROWS] = vectors.astype(BF16)


def third_cut_kernel(place_ref, *refs):
    third_sum_kernel(*refs[:-1])
    total_ref, sent_ref = refs[-2:]
    filled = refs[0].shape[0] + VECTOR_ROWS
    if filled < total_ref.shape[0]:
        total_ref[filled:] = jnp.zeros((total_ref.shape[0] - filled, total_ref.shape[1]), BF16)
    half = sent_ref.shape[0]
    away = pl.multiple_of((1 - (place_ref[1] & 1)) * half, half)
    sent_ref[...] = total_ref[pl.ds(away, half)]


def near_sum_kernel(place_ref, total_ref, came_ref, out_ref):
    half = came_ref.shape[0]
    mine = total_ref[pl.ds(pl.multiple_of((place_ref[1] & 1) * half, half), half)]
    out_ref[...] = (mine.astype(F32) + came_ref[...].astype(F32)).astype(BF16)


def add_kernel(left_ref, right_ref, out_ref):
    out_ref[...] = (left_ref[...].astype(F32) + right_ref[...].astype(F32)).astype(out_ref.dtype)


def join_rows(place, mine_ref, other_ref, out_ref):
    part = mine_ref.shape[0]
    out_ref[pl.ds(pl.multiple_of(place * part, part), part)] = mine_ref[...]
    out_ref[pl.ds(pl.multiple_of((1 - place) * part, part), part)] = other_ref[...]


def finish_dense_kernel(
    ratio, place_ref, mine_ref, other_ref, outer_ref, inner_ref, out_ref, *refs
):
    vector_refs, wide_ref, total_scratch, row_scratch = refs[:4], refs[4], refs[5], refs[6]
    rows, width = out_ref.shape
    join_rows(place_ref[1] & 1, mine_ref, other_ref, total_scratch)
    outer_ref[...] = total_scratch[: ratio * rows].astype(F32)
    for s in range(ratio):
        at = (ratio + s) * rows
        inner_ref[:, s * width : (s + 1) * width] = total_scratch[at : at + rows].astype(F32)
    at = 2 * ratio * rows
    out_ref[...] = total_scratch[at : at + rows].astype(F32)
    vectors = total_scratch[at + rows : at + rows + VECTOR_ROWS].astype(F32)
    put_slices(vectors, place_ref[0], vector_refs)
    row_scratch[...] = vectors
    size = wide_ref.shape[0]
    start = place_ref[0] * size
    row = row_scratch[pl.ds(len(vector_refs) + start // width, 1)]
    wide_ref[...] = pltpu.roll(row, lax.rem(width - lax.rem(start, width), width), 1)[0, :size]


def put_slices(vectors, index, refs):
    width, size = vectors.shape[1], refs[0].shape[0]
    turned = pltpu.roll(vectors, lax.rem(width - index * size, width), 1)
    for i, ref in enumerate(refs):
        ref[...] = turned[i, :size]


def finish_tail_kernel(place_ref, low_ref, came_ref, query_ref, key_ref, value_ref, *vector_refs):
    rows = query_ref.shape[0]
    total = lambda at: low_ref[at].astype(F32) + came_ref[at].astype(F32)
    for s, ref in enumerate((query_ref, key_ref, value_ref)):
        ref[...] = total(slice(s * rows, (s + 1) * rows))
    put_slices(total(slice(3 * rows, 3 * rows + VECTOR_ROWS)), place_ref[0], vector_refs)


def small_call(kernel, place, operands, out_shapes, name, after=(), inside=True, scratch=(), mib=4):
    ahead = 0 if place is None else 1
    count = len(operands)

    def body(*refs):
        kernel(*refs[: ahead + count], *refs[ahead + count + len(after) :])

    size = sum(math.prod(a.shape) * a.dtype.itemsize for a in list(operands) + list(out_shapes))
    return pl.pallas_call(
        body,
        grid_spec=pltpu.PrefetchScalarGridSpec(
            num_scalar_prefetch=ahead,
            grid=(1,),
            in_specs=[near_spec() for a in operands] + [pl.BlockSpec(memory_space=pl.ANY)] * len(after),
            out_specs=[near_spec() for s in out_shapes],
            scratch_shapes=list(scratch),
        ),
        out_shape=[near(s.shape, s.dtype) if inside else s for s in out_shapes],
        compiler_params=params(mib),
        cost_estimate=pl.CostEstimate(flops=0, transcendentals=0, bytes_accessed=size),
        name=name,
    )(*(() if place is None else (place,)), *operands, *after)


def sum_core(place, groups, vectors, name, after=()):
    groups = [list(g) + [swap(a, "batch", 1) for a in sent] for g, sent in groups]
    vectors_other = swap(vectors, "batch", 1)
    _, _, rows, width = groups[0][0].shape
    size = sum(g[0].shape[1] for g in groups) * rows
    half = width // 2
    counts = tuple(len(g) for g in groups)
    message = shape_of((2 * size + VECTOR_ROWS, half), BF16)
    kept = shape_of((2, size, half), F32)
    along_x, along_y, keep_x, keep_y, vectors = small_call(
        functools.partial(first_sum_kernel, counts),
        place,
        [a for g in groups for a in g] + [vectors, vectors_other],
        [message, message, kept, kept, shape_of(vectors.shape, BF16)],
        name + "_sum_core",
        after,
    )
    came_x, came_y = swap(along_x, "batch", 2), swap(along_y, "batch", 4)
    return (keep_x, came_x, keep_y, came_y, vectors), along_x


def sum_first(place, pieces, name, after=()):
    keep_x, _, _, _, vectors = pieces
    _, size, half = keep_x.shape
    message = shape_of((size + VECTOR_ROWS, half), BF16)
    kept = shape_of((size, half), F32)
    send_y, send_x, left_x, left_y, vectors = small_call(
        second_sum_kernel,
        place,
        pieces,
        [message, message, kept, kept, shape_of(vectors.shape, BF16)],
        name + "_sum_first",
        after,
    )
    came_x, came_y = swap(send_y, "batch", 4), swap(send_x, "batch", 2)
    return (left_x, came_x, left_y, came_y, vectors), send_y


def sum_second(pieces, name, after=()):
    size, half = pieces[0].shape
    shape = shape_of((size + VECTOR_ROWS, 2 * half), BF16)
    return small_call(third_sum_kernel, None, pieces, [shape], name + "_sum_second", after)[0]


def sum_second_cut(place, pieces, name, after=()):
    size, half = pieces[0].shape
    rows = -(-(size + VECTOR_ROWS) // 32) * 32
    total, sent = small_call(
        third_cut_kernel,
        place,
        pieces,
        [shape_of((rows, 2 * half), BF16), shape_of((rows // 2, 2 * half), BF16)],
        name + "_sum_second",
        after,
    )
    return total, swap(sent, "rows", 1)


def batch_slices_any(groups, vectors):
    me = lax.axis_index("batch")
    bits = lax.axis_size("batch").bit_length() - 1
    pieces = []
    for kept, sent in groups:
        values = [a.astype(F32) for a in kept] + [swap(a, "batch", 1).astype(F32) for a in sent]
        pieces.append(functools.reduce(lambda a, b: a + b, values))
    total = jnp.concatenate(pieces, 1)
    total = total.reshape((2,) * (bits - 1) + total.shape[1:])
    for bit in range(bits - 1, 0, -1):
        mine = (me >> bit) & 1
        sent = lax.dynamic_index_in_dim(total, 1 - mine, 0, keepdims=False).astype(BF16)
        total = lax.dynamic_index_in_dim(total, mine, 0, keepdims=False)
        total = total + swap(sent, "batch", 1 << bit).astype(F32)
    total = lax.psum(total.astype(BF16), "rows").astype(F32)
    return total, lax.psum(vectors, ("batch", "rows"))


def cross_kernel(count, *refs):
    out_ref = refs[-1]
    came = [(ref, i) for ref in refs[count:-1] for i in range(ref.shape[1])]
    for m, (term, (ref, i)) in enumerate(zip(refs[:count], came)):
        out_ref[m] = (term[0].astype(F32) + ref[1, i].astype(F32)).astype(BF16)


def cross_sum(terms, came, name, after=()):
    shape = (len(terms),) + terms[0].shape[1:]
    return small_call(
        functools.partial(cross_kernel, len(terms)),
        None,
        list(terms) + list(came),
        [shape_of(shape, BF16)],
        name,
        after,
    )[0]


def final_kernel(counts, *refs):
    owns, nears, crosses = [refs[sum(counts[:i]) : sum(counts[: i + 1])] for i in range(3)]
    atoms_ref, gain_ref, shift_ref, grad_middle_ref, out_ref = refs[sum(counts) :]
    gain = as_row(gain_ref)
    shift = as_row(shift_ref)
    nears = [(ref, i) for ref in nears for i in range(ref.shape[1])]
    crosses = [(ref, i) for ref in crosses for i in range(ref.shape[0])]
    for m, own_ref in enumerate(owns):
        near_ref, i = nears[m]
        cross_ref, at = crosses[m]
        grad = own_ref[0] + near_ref[0, i].astype(F32) + cross_ref[at].astype(F32)
        _, normed, inverse = norm_forward(atoms_ref[m].astype(F32), gain, shift)
        result = grad_middle_ref[m] + norm_backward(grad, normed, inverse, gain)
        out_ref[m] = result.astype(BF16)


def first_norm_backward(owns, nears, crosses, others, after=()):
    return small_call(
        functools.partial(final_kernel, (len(owns), len(nears), len(crosses))),
        None,
        owns + nears + crosses + list(others),
        [shape_of(others[0].shape, BF16)],
        "first_norm_backward",
        after,
        inside=False,
    )[0]


def shards(
    atoms,
    pair_bias,
    lengths,
    first_gain,
    first_shift,
    query_weight,
    query_bias,
    key_weight,
    value_weight,
    value_bias,
    out_weight,
    out_bias,
    second_gain,
    second_shift,
    inner_weight,
    inner_bias,
    outer_weight,
    outer_bias,
    atoms_cotangent,
    pair_cotangent,
):
    molecules, rows, model_width = atoms.shape
    head_count = pair_bias.shape[1]
    head_size = model_width // head_count
    batch_count = lax.axis_size("batch")
    batch_index = lax.axis_index("batch")
    row = lax.axis_index("rows")
    (
        atoms_far,
        pair_bias,
        first_gain,
        first_shift,
        query_weight,
        query_bias,
        key_weight,
        value_weight,
        value_bias,
        out_weight,
        out_bias,
        second_gain,
        second_shift,
        inner_weight,
        inner_bias,
        outer_weight,
        outer_bias,
        atoms_cotangent,
        pair_cotangent,
    ) = [
        pltpu.with_memory_space_constraint(a, pltpu.HBM)
        for a in (
            atoms,
            pair_bias,
            first_gain,
            first_shift,
            query_weight,
            query_bias,
            key_weight,
            value_weight,
            value_bias,
            out_weight,
            out_bias,
            second_gain,
            second_shift,
            inner_weight,
            inner_bias,
            outer_weight,
            outer_bias,
            atoms_cotangent,
            pair_cotangent,
        )
    ]
    place = jnp.stack(
        [batch_index, row, batch_index & 1, (batch_index >> 1) & 1, (batch_index >> 2) & 1]
    ).astype(jnp.int32)
    line = lambda v: v
    count = molecules // STAGES
    stages = []
    pair_out = jnp.zeros((1,), BF16)
    one = swap(atoms, "rows", 1)
    mine = [atoms[:count]]
    pair_near, query_near, key_near, value_near, later = load(
        [pair_bias, query_weight, key_weight, value_weight, atoms_far],
        "load_first",
        (0, 0, 0, 0, count),
        (place,),
    )
    mine.append(later)
    gathered = [[swap(a, "rows", mask) for mask in (2, 3)] for a in mine]
    projected = near_half(
        head_size,
        STAGES,
        place,
        atoms_far,
        one,
        (
            first_gain,
            first_shift,
            query_near,
            query_bias,
            key_near,
            value_near,
            value_bias,
        ),
        (),
    )
    for stage in range(STAGES):
        pair_out, kept, loaded = attention_forward(
            head_size,
            stage * count,
            place,
            lengths,
            gathered[stage],
            pair_near,
            (first_gain, first_shift, key_near, value_near, value_bias),
            projected[5 * stage : 5 * stage + 5],
            pair_out,
            [out_weight, inner_weight, outer_weight, atoms_cotangent] if stage else [],
        )
        stages.append(kept)
    out_weight, inner_weight, outer_weight, atoms_cotangent = loaded
    (
        atoms_out,
        outer_send,
        outer_keep,
        inner_send,
        inner_keep,
        out_send,
        out_keep,
        grad_middle,
        grad_mixed,
        dense_vectors,
        pair_cotangent,
    ) = dense(
        place,
        [s[1] for s in stages],
        atoms,
        atoms_cotangent,
        (
            out_weight,
            line(out_bias),
            line(second_gain),
            line(second_shift),
            inner_weight,
            line(inner_bias),
            outer_weight,
            line(outer_bias),
        ),
        batch_count,
        pair_cotangent,
    )
    pairs = batch_count // 2
    own_rows = model_width // batch_count
    slots = lambda a: a.reshape(pairs, -1, own_rows, model_width)
    dense_groups = [
        ([slots(outer_keep)], [slots(outer_send)]),
        ([inner_keep], [inner_send]),
        ([slots(out_keep)], [slots(out_send)]),
    ]
    usual = batch_count == 8

    def backward(molecule, held, sums, after, before=None):
        stage = molecule // count
        return attention_backward(
            head_size,
            stage * count,
            molecule % count,
            place,
            stages[stage],
            pair_cotangent,
            grad_mixed,
            (query_near, key_near, value_near),
            held,
            sums,
            after,
            before,
        )

    pair_grad, near0, cross0, own0, sums, *grads0 = backward(0, None, None, [])
    after = []
    if usual:
        dense_pieces, held = sum_core(place, dense_groups, dense_vectors, "dense", (own0,))
        after = [held]
    else:
        dense_total, dense_vectors = batch_slices_any(dense_groups, dense_vectors)
    pair_grad, near1, cross1, own1, sums, *grads1 = backward(1, pair_grad, sums, after, near0)
    near1 = swap(near1, "rows", 1)
    pair_grad, near2, cross2, own2, sums, *grads2 = backward(2, pair_grad, sums, [own1])
    near2 = swap(near2, "rows", 1)
    after = [own2]
    if usual:
        dense_pieces, held = sum_first(place, dense_pieces, "dense", after)
        after = [held]
    cross0 = cross_sum([cross0, cross1], [near1], "cross_first", after)
    far0 = swap(cross0, "rows", 2)
    pair_grad, near3, cross3, own3, tail_vectors, *grads3 = backward(3, pair_grad, sums, [cross0])
    near3 = swap(near3, "rows", 1)
    after = [own3]
    if usual:
        dense_total, came = sum_second_cut(place, dense_pieces, "dense", after)
        after = [dense_total]
    cross2 = cross_sum([cross2], [near2], "cross_second", after)
    far2 = swap(cross2, "rows", 2)
    after = [far0, cross2]
    part = shape_of((pairs, 1, own_rows, model_width), BF16)
    parts = small_call(
        functools.partial(weight_kernel, 4, STAGES),
        place,
        [s[3] for s in stages] + grads0 + grads1 + grads2 + grads3,
        [part] * 6,
        "attention_weights",
        after,
        scratch=[pltpu.VMEM((pairs, 2, own_rows, model_width), F32)],
        mib=14,
    )
    groups = [([parts[2 * i + 1]], [parts[2 * i]]) for i in range(3)]
    matrix = shape_of((own_rows, model_width), F32)
    ratio = inner_weight.shape[1] // model_width
    vector = shape_of((own_rows,), F32)
    finish = (atoms, line(first_gain), line(first_shift), grad_middle)
    if usual:
        pieces, _ = sum_core(place, groups, tail_vectors, "tail")
        pieces, held = sum_first(place, pieces, "tail")
        part = shape_of(came.shape, BF16)
        mine = small_call(
            near_sum_kernel, place, [dense_total, came], [part], "dense_near_sum", (held, far2)
        )[0]
        came = swap(mine, "rows", 2)
        cross3 = cross_sum([cross3], [near3], "cross_third", (mine,))
        far3 = swap(cross3, "rows", 2)
        total = sum_second(pieces, "tail", (cross3,))
        tail_came = swap(total, "rows", 1)
        mine = small_call(add_kernel, None, [mine, came], [part], "dense_far_sum", (total,))[0]
        came = swap(mine, "rows", 1)
        total = small_call(
            add_kernel, None, [total, tail_came], [total], "tail_near_sum", (mine, far3)
        )[0]
        tail_came = swap(total, "rows", 2)
        atoms_grad = first_norm_backward(
            [own0, own1, own2, own3], [near1, near2, near3], [far0, far2, far3], finish, (total,)
        )
        outer_grad, inner_grad, out_grad, *dense_parts = small_call(
            functools.partial(finish_dense_kernel, ratio),
            place,
            [mine, came],
            [
                shape_of((ratio * own_rows, model_width), F32),
                shape_of((own_rows, ratio * model_width), F32),
                matrix,
                vector,
                vector,
                vector,
                vector,
                shape_of((ratio * own_rows,), F32),
            ],
            "finish_dense",
            (atoms_grad,),
            inside=False,
            scratch=[
                pltpu.VMEM((2 * part.shape[0], model_width), BF16),
                pltpu.VMEM((VECTOR_ROWS, model_width), F32),
            ],
        )
        query_grad, key_grad, value_grad, *tail_parts = small_call(
            finish_tail_kernel,
            place,
            [total, tail_came],
            [matrix, matrix, matrix, vector, vector, vector, vector],
            "finish_tail",
            (out_grad,),
            inside=False,
        )
    else:
        far3 = swap(cross_sum([cross3], [near3], "cross_third"), "rows", 2)
        atoms_grad = first_norm_backward(
            [own0, own1, own2, own3], [near1, near2, near3], [far0, far2, far3], finish
        )
        total, tail_vectors = batch_slices_any(groups, tail_vectors)
        query_grad, key_grad, value_grad = total[0], total[1], total[2]
        outer_grad = dense_total[:ratio].reshape(-1, model_width)
        inner_grad = dense_total[ratio : 2 * ratio].transpose(1, 0, 2).reshape(own_rows, -1)
        out_grad = dense_total[2 * ratio]
        part = lambda v: lax.dynamic_slice_in_dim(
            v, batch_index * (v.shape[0] // batch_count), v.shape[0] // batch_count
        )
        tail_parts = [part(v) for v in tail_vectors[:4]]
        dense_parts = [part(v) for v in dense_vectors[:4]] + [part(dense_vectors[4:].reshape(-1))]
    return (
        atoms_out,
        pair_out,
        atoms_grad,
        pair_grad,
        tail_parts[0],
        tail_parts[1],
        query_grad,
        tail_parts[2],
        key_grad,
        value_grad,
        tail_parts[3],
        out_grad,
        dense_parts[3],
        dense_parts[1],
        dense_parts[2],
        inner_grad,
        dense_parts[4],
        outer_grad,
        dense_parts[0],
    )


def solution(mesh):
    tokens = P("batch", "rows", None)
    pairs = P("batch", None, "rows", None)
    vector = P("batch")
    matrix = P("batch", None)
    return jax.shard_map(
        shards,
        mesh=mesh,
        in_specs=(tokens, pairs, P("batch")) + (P(),) * 15 + (tokens, pairs),
        out_specs=(
            tokens,
            pairs,
            tokens,
            pairs,
            vector,
            vector,
            matrix,
            vector,
            matrix,
            matrix,
            vector,
            matrix,
            vector,
            vector,
            vector,
            matrix,
            vector,
            matrix,
            vector,
        ),
        check_vma=False,
    )
```

```python
import functools
import math

import jax
import jax.numpy as jnp
from jax import lax
from jax.experimental import pallas as pl
from jax.experimental.pallas import tpu as pltpu
from jax.sharding import PartitionSpec as P

EPSILON = 1e-05
MASKED = -1000000000.0
F32 = jnp.float32
BF16 = jnp.bfloat16
LANES = 128
STAGES = 2
VMEM_LIMIT = 18 << 20


def shape_of(shape, dtype):
    return jax.ShapeDtypeStruct(tuple(shape), dtype)


def norm_forward(values_in, gain, shift):
    centre = values_in - jnp.mean(values_in, -1, keepdims=True)
    inverse = lax.rsqrt(jnp.mean(centre * centre, -1, keepdims=True) + EPSILON)
    normed = centre * inverse
    return (normed * gain + shift, normed, inverse)


def norm_backward(upstream, normed, inverse, gain):
    scaled = upstream * gain
    return inverse * (
        scaled
        - jnp.mean(scaled, -1, keepdims=True)
        - normed * jnp.mean(scaled * normed, -1, keepdims=True)
    )


def dot(left, right):
    return jnp.dot(left, right, preferred_element_type=F32)


def across(left, right):
    return lax.dot_general(left, right, (((0,), (0,)), ((), ())), preferred_element_type=F32)


def against(left, right):
    return lax.dot_general(left, right, (((1,), (1,)), ((), ())), preferred_element_type=F32)


def column_sum(values_in):
    return jnp.sum(values_in.astype(F32), 0, keepdims=True)


def near(shape, dtype):
    return pltpu.VMEM(tuple(shape), dtype)


def near_spec():
    return pl.BlockSpec(memory_space=pltpu.VMEM)


def as_row(ref):
    return ref[...].astype(F32).reshape(1, -1)


def whole(array):
    return pl.BlockSpec(array.shape, lambda *_: (0,) * array.ndim)


def params(mib=10):
    return pltpu.CompilerParams(vmem_limit_bytes=mib << 20)


def load_kernel(count, starts, *refs):
    sources, targets, semaphores = refs[:count], refs[-count - 1 : -1], refs[-1]
    copies = [
        pltpu.make_async_copy(source.at[pl.ds(start, target.shape[0])], target, semaphores.at[i])
        for i, (source, target, start) in enumerate(zip(sources, targets, starts))
    ]
    for copy in copies:
        copy.start()
    for copy in copies:
        copy.wait()


def copies_beside(sources, targets, semaphores):
    return [
        pltpu.make_async_copy(source, target, semaphores.at[i])
        for i, (source, target) in enumerate(zip(sources, targets))
    ]


def load(arrays, name, starts=None, after=()):
    count = len(arrays)
    starts = starts or (0,) * count
    return pl.pallas_call(
        functools.partial(load_kernel, count, starts),
        in_specs=[pl.BlockSpec(memory_space=pltpu.HBM)] * count
        + [pl.BlockSpec(memory_space=pl.ANY)] * len(after),
        out_specs=[near_spec()] * count,
        out_shape=[
            near((a.shape[0] - start,) + a.shape[1:], a.dtype) for a, start in zip(arrays, starts)
        ],
        scratch_shapes=[pltpu.SemaphoreType.DMA((count,))],
        compiler_params=params(),
        name=name,
    )(*arrays, *after)


def project(pieces, first, parameters, row, refs, atoms_scratch):
    gain_ref, shift_ref, key_weight_ref, value_weight_ref, value_bias_ref = parameters
    hidden_ref, normed_ref, key_ref, value_ref = refs
    count = hidden_ref.shape[0]
    _, groups, keys, width = key_ref.shape
    rows = keys // 4
    half = 2 * rows
    model_width = hidden_ref.shape[2]
    for m in range(count):
        for i, piece in enumerate(pieces):
            start = pl.multiple_of(m * half + ((row ^ i) & 1) * rows, rows)
            atoms_scratch[pl.ds(start, rows)] = piece[m + first]
    hidden, normed, _ = norm_forward(
        atoms_scratch[...].astype(F32), as_row(gain_ref), as_row(shift_ref)
    )
    hidden = hidden.astype(BF16)
    normed = normed.astype(BF16)
    key_rows = dot(hidden, key_weight_ref[...]).astype(BF16)
    value_rows = (dot(hidden, value_weight_ref[...]) + as_row(value_bias_ref)).astype(BF16)
    return [a.reshape(count, half, model_width) for a in (hidden, normed, key_rows, value_rows)]


def put_half(values, at, refs):
    hidden, normed, key_rows, value_rows = values
    hidden_ref, normed_ref, key_ref, value_ref = refs
    count, groups, _, width = key_ref.shape
    half = hidden.shape[1]
    ones = jnp.ones((count, half, width), BF16)
    hidden_ref[:, at] = hidden
    normed_ref[:, at] = normed
    for t in range(groups):
        lanes = slice(t * width, (t + 1) * width)
        key_ref[:, t, at] = key_rows[:, :, lanes]
        value_ref[:, t, at, :width] = value_rows[:, :, lanes]
        value_ref[:, t, at, width:] = ones


def half_rows(row, other, rows):
    which = row >> 1
    which = 1 - which if other else which
    return pl.ds(pl.multiple_of(which * 2 * rows, 2 * rows), 2 * rows)


def near_half_kernel(
    head_size,
    stages,
    ahead,
    place_ref,
    own_ref,
    one_ref,
    gain_ref,
    shift_ref,
    query_weight_ref,
    query_bias_ref,
    key_weight_ref,
    value_weight_ref,
    value_bias_ref,
    *refs,
):
    refs = refs[ahead:]
    atoms_scratch = refs[-1]
    row = place_ref[1]
    rows, model_width = own_ref.shape[1:]
    factor = head_size**-0.5
    parameters = (gain_ref, shift_ref, key_weight_ref, value_weight_ref, value_bias_ref)
    for stage in range(stages):
        hidden_ref, normed_ref, key_ref, value_ref, query_ref = refs[5 * stage : 5 * stage + 5]
        outs = (hidden_ref, normed_ref, key_ref, value_ref)
        count, groups, _, width = key_ref.shape
        values = project((own_ref, one_ref), stage * count, parameters, row, outs, atoms_scratch)
        put_half(values, half_rows(row, False, rows), outs)
        mine = pl.ds(pl.multiple_of(row * rows, rows), rows)
        own = jnp.concatenate([hidden_ref[m, mine] for m in range(count)], 0)
        query_rows = (dot(own, query_weight_ref[...]) + as_row(query_bias_ref)) * factor
        query_rows = query_rows.astype(BF16).reshape(count, rows, model_width)
        for t in range(groups):
            query_ref[:, t] = query_rows[:, :, t * width : (t + 1) * width]


def near_half(head_size, stages, place, atoms, one, parameters, after):
    molecules, rows, model_width = atoms.shape
    keys = 4 * rows
    count = molecules // stages
    groups = model_width // LANES
    operands = (place, atoms, one, *parameters, *after)
    return pl.pallas_call(
        functools.partial(near_half_kernel, head_size, stages, len(after)),
        grid_spec=pltpu.PrefetchScalarGridSpec(
            num_scalar_prefetch=1,
            grid=(1,),
            in_specs=[whole(atoms), near_spec()]
            + [near_spec() for a in parameters]
            + [pl.BlockSpec(memory_space=pl.ANY)] * len(after),
            out_specs=[near_spec()] * (5 * stages),
            scratch_shapes=[pltpu.VMEM((count * 2 * rows, model_width), BF16)],
        ),
        out_shape=[
            near((count, keys, model_width), BF16),
            near((count, keys, model_width), BF16),
            near((count, groups, keys, LANES), BF16),
            near((count, groups, keys, 2 * LANES), BF16),
            near((count, groups, rows, LANES), BF16),
        ]
        * stages,
        compiler_params=params(10),
        name="near_half",
    )(*operands)


def forward_kernel(
    head_size,
    chunk,
    first,
    extra,
    place_ref,
    length_ref,
    two_ref,
    three_ref,
    pair_ref,
    query_ref,
    gain_ref,
    shift_ref,
    key_weight_ref,
    value_weight_ref,
    value_bias_ref,
    *refs,
):
    (
        pair_out_ref,
        weights_ref,
        mixed_ref,
        inverse_ref,
        hidden_ref,
        normed_ref,
        key_ref,
        value_ref,
    ) = refs[5 + extra : 13 + extra]
    atoms_scratch, semaphores = refs[-2:]
    copies = copies_beside(refs[5 : 5 + extra], refs[13 + extra : 13 + 2 * extra], semaphores)
    molecule = pl.program_id(0)
    group = pl.program_id(1)
    count, groups, keys, width = key_ref.shape
    heads = width // head_size
    rows = query_ref.shape[2]

    @pl.when((molecule == 0) & (group == 0))
    def _():
        for copy in copies:
            copy.start()
        row = place_ref[1]
        outs = (hidden_ref, normed_ref, key_ref, value_ref)
        parameters = (gain_ref, shift_ref, key_weight_ref, value_weight_ref, value_bias_ref)
        values = project((two_ref, three_ref), 0, parameters, row, outs, atoms_scratch)
        put_half(values, half_rows(row, True, rows), outs)

    query = query_ref[molecule, group]
    key = key_ref[molecule, group]
    value = value_ref[molecule, group]
    valid = lax.broadcasted_iota(jnp.int32, (1, keys), 1) < length_ref[molecule + first]
    lane = lax.broadcasted_iota(jnp.int32, (1, width), 1) // head_size
    lane_pair = lax.broadcasted_iota(jnp.int32, (1, 2 * width), 1) % width // head_size
    total = jnp.zeros((rows, 2 * width), F32)
    zero = jnp.zeros((), BF16)
    for c in range(0, heads, chunk):
        here = slice(c, c + chunk)
        there = pl.ds(group * heads + c, chunk)
        spread = jnp.concatenate([jnp.where(lane == c + t, query, zero) for t in range(chunk)], 0)
        pair = pair_ref[molecule + first, there].reshape(chunk * rows, keys)
        scores = against(spread, key) + pair.astype(F32)
        pair_out_ref[0, here] = scores.astype(BF16).reshape(chunk, rows, keys)
        masked = jnp.where(valid, scores, MASKED)
        weights = jnp.exp(masked - jnp.max(masked, -1, keepdims=True)).astype(BF16)
        weights_ref[molecule, there] = weights.reshape(chunk, rows, keys)
        product = dot(weights, value)
        for t in range(chunk):
            total = jnp.where(lane_pair == c + t, product[t * rows : (t + 1) * rows], total)
    inverse = 1.0 / total[:, width:]
    inverse_ref[molecule, group] = inverse
    mixed_ref[molecule, group] = total[:, :width] * inverse

    @pl.when((molecule == count - 1) & (group == groups - 1))
    def _():
        for copy in copies:
            copy.wait()


def attention_forward(
    head_size, first, place, lengths, pieces, pair_bias, parameters, projected, held, extra
):
    _, head_count, rows, keys = pair_bias.shape
    hidden, normed, key, value, query = projected
    count, groups = key.shape[:2]
    model_width = groups * LANES
    heads = LANES // head_size
    pair_spec = pl.BlockSpec((1, heads, rows, keys), lambda m, g, *_: (m + first, g, 0, 0))
    elements = count * head_count * rows * keys
    operands = [place, lengths, *pieces, pair_bias, query, *parameters]
    in_specs = [near_spec()] * (len(pieces) + 2)
    in_specs += [near_spec() for a in parameters]
    start = len(operands)
    operands += [hidden, normed, key, value, held]
    in_specs += [near_spec()] * 4 + [pl.BlockSpec(memory_space=pl.ANY)]
    aliases = {start + i: 4 + i for i in range(4)}
    if held.ndim > 1:
        aliases[start + 4] = 0
    operands += extra
    in_specs += [pl.BlockSpec(memory_space=pltpu.HBM)] * len(extra)
    outs = pl.pallas_call(
        functools.partial(forward_kernel, head_size, 8, first, len(extra)),
        grid_spec=pltpu.PrefetchScalarGridSpec(
            num_scalar_prefetch=2,
            grid=(count, groups),
            in_specs=in_specs,
            out_specs=[pair_spec] + [near_spec()] * (7 + len(extra)),
            scratch_shapes=[
                pltpu.VMEM((count * 2 * rows, model_width), BF16),
                pltpu.SemaphoreType.DMA((max(len(extra), 1),)),
            ],
        ),
        out_shape=[
            shape_of(pair_bias.shape, BF16),
            near((count, head_count, rows, keys), BF16),
            near((count, groups, rows, LANES), F32),
            near((count, groups, rows, LANES), F32),
            near(hidden.shape, BF16),
            near(normed.shape, BF16),
            near(key.shape, BF16),
            near(value.shape, BF16),
        ]
        + [near(a.shape, a.dtype) for a in extra],
        input_output_aliases=aliases,
        compiler_params=params(10),
        cost_estimate=pl.CostEstimate(
            flops=elements * 2 * 384, transcendentals=elements, bytes_accessed=elements * 6
        ),
        name="attention_forward",
    )(*operands)
    pair_out, weights, mixed, inverse, hidden, normed, key, value = outs[:8]
    return pair_out, (weights, mixed, inverse, hidden, normed, query, key, value), outs[8:]


def dense_kernel(
    mixed_count,
    place_ref,
    *refs,
):
    mixed_refs = refs[:mixed_count]
    (
        atoms_ref,
        cotangent_ref,
        out_weight_ref,
        out_bias_ref,
        gain_ref,
        shift_ref,
        inner_weight_ref,
        inner_bias_ref,
        outer_weight_ref,
        outer_bias_ref,
        far_ref,
        atoms_out_ref,
        outer_send_ref,
        outer_keep_ref,
        inner_send_ref,
        inner_keep_ref,
        out_send_ref,
        out_keep_ref,
        grad_middle_ref,
        grad_mixed_ref,
        vectors_ref,
        copied_ref,
        hidden_scratch,
        turned_scratch,
        normed_scratch,
        inverse_scratch,
        result_scratch,
        upstream_scratch,
        outer_scratch,
        inner_scratch,
        semaphores,
    ) = refs[mixed_count:]
    (copy,) = copies_beside([far_ref], [copied_ref], semaphores)
    step = pl.program_id(0)
    steps = pl.num_programs(0)
    core = place_ref[2]
    tokens, model_width = hidden_scratch.shape
    cotangent = cotangent_ref[...].reshape(tokens, model_width)

    def mixed_rows():
        parts = []
        for ref in mixed_refs:
            count, groups, rows, width = ref.shape
            join = [ref[:, t].reshape(count * rows, width) for t in range(groups)]
            parts.append(jnp.concatenate(join, 1))
        return jnp.concatenate(parts, 0)

    @pl.when(step == 0)
    def _():
        copy.start()
        mixed_low = mixed_rows().astype(BF16)
        middle = (
            atoms_ref[...].reshape(tokens, model_width).astype(F32)
            + dot(mixed_low, out_weight_ref[...])
            + as_row(out_bias_ref)
        )
        hidden, normed, inverse = norm_forward(
            middle, as_row(gain_ref), as_row(shift_ref)
        )
        hidden_scratch[...] = hidden.astype(BF16)
        turned_scratch[...] = jnp.transpose(hidden).astype(BF16)
        normed_scratch[...] = normed
        inverse_scratch[...] = inverse
        result_scratch[...] = middle + as_row(outer_bias_ref)
        upstream_scratch[...] = jnp.zeros_like(upstream_scratch)
        vectors_ref[0:1] = column_sum(cotangent)

    hidden = hidden_scratch[...]
    width = outer_weight_ref.shape[1]
    at = pl.ds(pl.multiple_of(step * width, width), width)
    inner_weight = inner_weight_ref[:, at]
    outer_weight = outer_weight_ref[at]
    pre = dot(hidden, inner_weight) + inner_bias_ref[at].astype(F32).reshape(1, -1)
    slope = math.sqrt(2.0 / math.pi)
    square = pre * pre
    tanh = jnp.tanh(slope * (pre + 0.044715 * (pre * square)))
    half = 0.5 * (1.0 + tanh)
    active = (pre * half).astype(BF16)
    result_scratch[...] += dot(active, outer_weight)
    derivative = half + (0.5 * slope) * pre * (1.0 - tanh * tanh) * (1.0 + 0.134145 * square)
    grad_pre = against(cotangent, outer_weight) * derivative
    vectors_ref[pl.ds(4 + step, 1)] = column_sum(grad_pre.astype(BF16))
    grad_pre = grad_pre.astype(BF16)
    outer_scratch[...] = across(active, cotangent).reshape(outer_scratch.shape)
    outer_send_ref[...] = outer_scratch[:, 1 - core].astype(BF16).reshape(outer_send_ref.shape)
    outer_keep_ref[...] = outer_scratch[:, core].astype(BF16).reshape(outer_keep_ref.shape)
    inner_scratch[...] = dot(turned_scratch[...], grad_pre).reshape(inner_scratch.shape)
    inner_send_ref[:, 0] = inner_scratch[:, 1 - core].astype(BF16)
    inner_keep_ref[:, 0] = inner_scratch[:, core].astype(BF16)
    upstream_scratch[...] += against(grad_pre, inner_weight)

    @pl.when(step == steps - 1)
    def _():
        atoms_out_ref[...] = result_scratch[...].astype(BF16).reshape(atoms_out_ref.shape)
        upstream = upstream_scratch[...]
        normed = normed_scratch[...]
        vectors_ref[1:2] = column_sum(upstream * normed)
        vectors_ref[2:3] = column_sum(upstream)
        grad_middle = cotangent.astype(F32) + norm_backward(
            upstream, normed, inverse_scratch[...], as_row(gain_ref)
        )
        grad_middle_ref[...] = grad_middle.reshape(grad_middle_ref.shape)
        branch = grad_middle.astype(BF16)
        vectors_ref[3:4] = column_sum(branch)
        grad_mixed = against(branch, out_weight_ref[...]).astype(BF16)
        molecules, groups, rows, lanes = grad_mixed_ref.shape
        grad_mixed = grad_mixed.reshape(molecules, rows, model_width)
        for t in range(groups):
            grad_mixed_ref[:, t] = grad_mixed[:, :, t * lanes : (t + 1) * lanes]
        turned = jnp.transpose(mixed_rows()).astype(BF16)
        inner_scratch[...] = dot(turned, branch).reshape(inner_scratch.shape)
        out_send_ref[...] = inner_scratch[:, 1 - core].astype(BF16)
        out_keep_ref[...] = inner_scratch[:, core].astype(BF16)
        copy.wait()


def dense(place, mixed, atoms, cotangent, parameters, batch_count, extra):
    (
        out_weight,
        out_bias,
        gain,
        shift,
        inner_weight,
        inner_bias,
        outer_weight,
        outer_bias,
    ) = parameters
    model_width, inner_width = inner_weight.shape
    tokens = atoms.shape[0] * atoms.shape[1]
    width = model_width
    steps = inner_width // width
    pairs = batch_count // 2
    outer_rows = inner_width // batch_count
    outer_pairs = width // (2 * outer_rows)
    own_rows = model_width // batch_count
    operands = (
        place,
        *mixed,
        atoms,
        cotangent,
        out_weight,
        out_bias,
        gain,
        shift,
        inner_weight,
        inner_bias,
        outer_weight,
        outer_bias,
        extra,
    )
    outer_spec = pl.BlockSpec((outer_pairs, outer_rows, model_width), lambda s, *_: (s, 0, 0))
    inner_spec = pl.BlockSpec((pairs, 1, own_rows, width), lambda s, *_: (0, s, 0, 0))
    outer_shape = shape_of((pairs, outer_rows, model_width), BF16)
    inner_shape = shape_of((pairs, steps, own_rows, width), BF16)
    out_shape = shape_of((pairs, own_rows, model_width), BF16)
    out_shapes = [
        shape_of(atoms.shape, BF16),
        outer_shape,
        outer_shape,
        inner_shape,
        inner_shape,
        out_shape,
        out_shape,
        near(atoms.shape, F32),
        near((atoms.shape[0], model_width // LANES, atoms.shape[1], LANES), BF16),
        shape_of((4 + steps, model_width), F32),
        near(extra.shape, extra.dtype),
    ]
    fixed = lambda s: pl.BlockSpec(s.shape, lambda *_: (0,) * len(s.shape))
    out_specs = [fixed(s) for s in out_shapes]
    out_specs[1:5] = [outer_spec, outer_spec, inner_spec, inner_spec]
    out_specs[7:9] = [near_spec(), near_spec()]
    out_specs[10] = near_spec()
    in_specs = [whole(a) for a in operands[1:]]
    for i, a in enumerate(operands[1:]):
        if i != len(mixed):
            in_specs[i] = near_spec()
    in_specs[-1] = pl.BlockSpec(memory_space=pltpu.HBM)
    return pl.pallas_call(
        functools.partial(dense_kernel, len(mixed)),
        grid_spec=pltpu.PrefetchScalarGridSpec(
            num_scalar_prefetch=1,
            grid=(steps,),
            in_specs=in_specs,
            out_specs=out_specs,
            scratch_shapes=[
                pltpu.VMEM((tokens, model_width), BF16),
                pltpu.VMEM((model_width, tokens), BF16),
                pltpu.VMEM((tokens, model_width), F32),
                pltpu.VMEM((tokens, 1), F32),
                pltpu.VMEM((tokens, model_width), F32),
                pltpu.VMEM((tokens, model_width), F32),
                pltpu.VMEM((outer_pairs, 2, outer_rows, model_width), F32),
                pltpu.VMEM((pairs, 2, own_rows, width), F32),
                pltpu.SemaphoreType.DMA((1,)),
            ],
        ),
        out_shape=out_shapes,
        compiler_params=params(14),
        cost_estimate=pl.CostEstimate(
            flops=12 * tokens * model_width * inner_width,
            transcendentals=tokens * inner_width,
            bytes_accessed=12 * model_width * inner_width,
        ),
        name="dense",
    )(*operands)


def backward_kernel(
    head_size,
    chunk,
    first,
    base,
    start,
    fresh,
    joined,
    place_ref,
    weights_ref,
    cotangent_ref,
    grad_mixed_ref,
    mixed_ref,
    inverse_ref,
    query_ref,
    key_ref,
    value_ref,
    normed_ref,
    query_weight_ref,
    key_weight_ref,
    value_weight_ref,
    *refs,
):
    before_ref = refs[start - 1] if joined else None
    refs = refs[start:]
    pair_grad_ref, near_ref, cross_ref, own_ref, vectors_ref = refs[:5]
    query_grad_ref, key_grad_ref, value_grad_ref = refs[5:8]
    grad_query_scratch, grad_key_scratch, grad_value_scratch, grad_scratch = refs[-4:]
    molecule = pl.program_id(0) + base
    group = pl.program_id(1)
    _, groups, rows, width = query_ref.shape
    keys = key_ref.shape[2]
    heads = width // head_size
    factor = head_size**-0.5
    query = query_ref[molecule, group]
    key = key_ref[molecule, group]
    value = value_ref[molecule, group]
    upstream = grad_mixed_ref[molecule + first, group].astype(F32) * inverse_ref[molecule, group]
    upstream = upstream.astype(BF16)
    offset = (-(upstream.astype(F32) * mixed_ref[molecule, group])).astype(BF16)
    both = jnp.concatenate([upstream, offset], 1)
    lane = lax.broadcasted_iota(jnp.int32, (1, width), 1) // head_size
    lane_pair = lax.broadcasted_iota(jnp.int32, (1, 2 * width), 1) % width // head_size
    query_turned = jnp.transpose(query.astype(F32)).astype(BF16)
    upstream_turned = jnp.transpose(upstream.astype(F32)).astype(BF16)
    query_turned = jnp.concatenate([query_turned] * chunk, 1)
    upstream_turned = jnp.concatenate([upstream_turned] * chunk, 1)
    turned_shape = (chunk * head_size, chunk * rows)
    same = (
        lax.broadcasted_iota(jnp.int32, turned_shape, 0) // head_size
        == lax.broadcasted_iota(jnp.int32, turned_shape, 1) // rows
    )
    zero = jnp.zeros((), BF16)
    total = jnp.zeros((rows, width), F32)
    key_parts = []
    value_parts = []
    for c in range(0, heads, chunk):
        here = slice(c, c + chunk)
        feature = slice(c * head_size, (c + chunk) * head_size)
        spread = jnp.concatenate([jnp.where(lane_pair == c + t, both, zero) for t in range(chunk)], 0)
        centred = against(spread, value)
        there = pl.ds(group * heads + c, chunk)
        weights = weights_ref[molecule, there].reshape(chunk * rows, keys)
        cotangent = cotangent_ref[molecule + first, there].reshape(chunk * rows, keys)
        grad = (weights.astype(F32) * centred + cotangent.astype(F32)).astype(BF16)
        pair_grad_ref[0, here] = grad.reshape(chunk, rows, keys)
        product = dot(grad, key)
        for t in range(chunk):
            total = jnp.where(lane == c + t, product[t * rows : (t + 1) * rows], total)
        key_parts.append(dot(jnp.where(same, query_turned[feature], zero), grad))
        value_parts.append(dot(jnp.where(same, upstream_turned[feature], zero), weights))
    grad_query_scratch[group] = (total * factor).astype(BF16)
    grad_key_scratch[group] = jnp.transpose(jnp.concatenate(key_parts, 0)).astype(BF16)
    grad_value_scratch[group] = jnp.transpose(jnp.concatenate(value_parts, 0)).astype(BF16)

    if fresh:

        @pl.when((pl.program_id(0) == 0) & (group == 0))
        def _():
            vectors_ref[...] = jnp.zeros_like(vectors_ref)

    @pl.when(group == groups - 1)
    def _():
        row = place_ref[1]
        mine = pl.ds(pl.multiple_of(row * rows, rows), rows)
        join = lambda ref: jnp.concatenate([ref[t] for t in range(groups)], 1)
        grad_query = join(grad_query_scratch)
        grad_key = join(grad_key_scratch)
        grad_value = join(grad_value_scratch)
        query_grad_ref[0] = grad_query
        key_grad_ref[0] = grad_key
        value_grad_ref[0] = grad_value
        grad_scratch[...] = against(grad_key, key_weight_ref[...]) + against(
            grad_value, value_weight_ref[...]
        )
        grad_scratch[mine] += against(grad_query, query_weight_ref[...])
        grad = grad_scratch[...]
        vectors_ref[0:1] += column_sum(grad * normed_ref[molecule].astype(F32))
        vectors_ref[1:2] += column_sum(grad)
        vectors_ref[2:3] += column_sum(grad_query)
        vectors_ref[3:4] += column_sum(grad_value)
        at = lambda other: pl.ds(pl.multiple_of((row ^ other) * rows, rows), rows)
        slot = near_ref.shape[1] - 1
        near_ref[0, slot] = grad_scratch[at(1)].astype(BF16)
        near_ref[1, slot] = grad_scratch[at(3)].astype(BF16)
        if joined:
            near_ref[:, 0] = before_ref[:, 0]
        cross_ref[0] = grad_scratch[at(2)].astype(BF16)
        own_ref[0] = grad_scratch[mine]


def attention_backward(
    head_size, first, base, place, stage, cotangent, grad_mixed, parameters, held, sums, after, before
):
    weights, mixed, inverse, _, normed, query, key, value = stage
    _, head_count, rows, keys = weights.shape
    count = 1
    groups = query.shape[1]
    model_width = groups * LANES
    heads = LANES // head_size
    pair_spec = pl.BlockSpec((1, heads, rows, keys), lambda m, g, *_: (m + first + base, g, 0, 0))
    elements = count * head_count * rows * keys
    operands = [
        place,
        weights,
        cotangent,
        grad_mixed,
        mixed,
        inverse,
        query,
        key,
        value,
        normed,
        *parameters,
    ]
    in_specs = [near_spec()] * (len(operands) - 1)
    aliases = {}
    start = len(operands)
    if sums is not None:
        aliases = {start: 0, start + 1: 4}
        operands += [held, sums]
        in_specs += [pl.BlockSpec(memory_space=pl.ANY), near_spec()]
    operands += list(after)
    in_specs += [pl.BlockSpec(memory_space=pl.ANY)] * len(after)
    joined = before is not None
    if joined:
        operands.append(before)
        in_specs.append(near_spec())
    out_shape = [
        shape_of(cotangent.shape, BF16),
        near((2, 1 + joined, rows, model_width), BF16),
        near((count, rows, model_width), BF16),
        near((count, rows, model_width), F32),
        near((8, model_width), F32),
        near((count, rows, model_width), BF16),
        near((count, keys, model_width), BF16),
        near((count, keys, model_width), BF16),
    ]
    out_specs = [
        pair_spec,
        near_spec(),
        near_spec(),
        near_spec(),
        near_spec(),
        near_spec(),
        near_spec(),
        near_spec(),
    ]
    return pl.pallas_call(
        functools.partial(
            backward_kernel, head_size, 4, first, base, len(operands) - start, sums is None, joined
        ),
        grid_spec=pltpu.PrefetchScalarGridSpec(
            num_scalar_prefetch=1,
            grid=(count, groups),
            in_specs=in_specs,
            out_specs=out_specs,
            scratch_shapes=[
                pltpu.VMEM((groups, rows, LANES), BF16),
                pltpu.VMEM((groups, keys, LANES), BF16),
                pltpu.VMEM((groups, keys, LANES), BF16),
                pltpu.VMEM((keys, model_width), F32),
            ],
        ),
        out_shape=out_shape,
        input_output_aliases=aliases,
        compiler_params=params(8),
        cost_estimate=pl.CostEstimate(
            flops=elements * 2 * 768, transcendentals=0, bytes_accessed=elements * 6
        ),
        name="attention_backward",
    )(*operands)


def weight_kernel(calls, stages, place_ref, *refs):
    hidden_refs = refs[:stages]
    grads = refs[stages : stages + 3 * calls]
    out_refs = refs[stages + 3 * calls : -1]
    total_ref = refs[-1]
    rows = grads[0].shape[1]
    row = place_ref[1]
    core = place_ref[2]
    mine = pl.ds(pl.multiple_of(row * rows, rows), rows)
    hidden = [(ref, m) for ref in hidden_refs for m in range(ref.shape[0])]
    width = hidden_refs[0].shape[2]
    own = jnp.concatenate([ref[m, mine] for ref, m in hidden], 0)
    every = jnp.concatenate([ref[m] for ref, m in hidden], 0)
    own = jnp.transpose(own.astype(F32)).astype(BF16)
    every = jnp.transpose(every.astype(F32)).astype(BF16)
    for j, left in enumerate((own, every, every)):
        right = jnp.concatenate([grads[3 * c + j][...].reshape(-1, width) for c in range(calls)], 0)
        total_ref[...] = dot(left, right).reshape(total_ref.shape)
        send_ref, keep_ref = out_refs[2 * j : 2 * j + 2]
        send_ref[:, 0] = total_ref[:, 1 - core].astype(BF16)
        keep_ref[:, 0] = total_ref[:, core].astype(BF16)


def swap(value, axis, mask):
    size = lax.axis_size(axis)
    return lax.ppermute(value, axis, [(i, i ^ mask) for i in range(size)])


VECTOR_ROWS = 8


def first_sum_kernel(counts, place_ref, *refs):
    terms = sum(counts)
    mine_ref, other_ref = refs[terms : terms + 2]
    along_x_ref, along_y_ref, keep_x_ref, keep_y_ref, vectors_ref = refs[terms + 2 :]
    x, y = place_ref[3], place_ref[4]
    half = along_x_ref.shape[1]
    size = keep_x_ref.shape[1]
    low, high = slice(0, half), slice(half, None)
    row = 0
    start = 0
    for count in counts:
        group = refs[start : start + count]
        start += count
        for s in range(group[0].shape[1]):
            rows = group[0].shape[2]

            def total(at, lanes):
                values = [r[at, s, :, lanes].astype(F32) for r in group]
                return functools.reduce(lambda a, b: a + b, values)

            for k in range(2):
                to = slice(k * size + row, k * size + row + rows)
                here = slice(row, row + rows)
                along_x_ref[to] = total(2 * k + (1 - x), low).astype(BF16)
                keep_x_ref[k, here] = total(2 * k + x, low)
                along_y_ref[to] = total(2 * (1 - y) + k, high).astype(BF16)
                keep_y_ref[k, here] = total(2 * y + k, high)
            row += rows
    vectors = (mine_ref[...] + other_ref[...]).astype(BF16)
    vectors_ref[...] = vectors
    put_vectors(vectors, along_x_ref, along_y_ref)


def put_vectors(vectors, low_ref, high_ref):
    half = vectors.shape[1] // 2
    low_ref[low_ref.shape[0] - VECTOR_ROWS :] = vectors[:, :half]
    high_ref[high_ref.shape[0] - VECTOR_ROWS :] = vectors[:, half:]


def get_vectors(low_ref, high_ref):
    low = low_ref[low_ref.shape[0] - VECTOR_ROWS :]
    return jnp.concatenate([low, high_ref[high_ref.shape[0] - VECTOR_ROWS :]], 1).astype(F32)


def second_sum_kernel(
    place_ref,
    keep_x_ref,
    came_x_ref,
    keep_y_ref,
    came_y_ref,
    vectors_ref,
    send_y_ref,
    send_x_ref,
    left_x_ref,
    left_y_ref,
    vectors_out_ref,
):
    size = keep_x_ref.shape[1]
    for keep, came, send, left, me in (
        (keep_x_ref, came_x_ref, send_y_ref, left_x_ref, place_ref[4]),
        (keep_y_ref, came_y_ref, send_x_ref, left_y_ref, place_ref[3]),
    ):
        at = lambda i: pl.ds(pl.multiple_of(i * size, size), size)
        send[:size] = (keep[1 - me] + came[at(1 - me)].astype(F32)).astype(BF16)
        left[...] = keep[me] + came[at(me)].astype(F32)
    vectors = vectors_ref[...].astype(F32) + get_vectors(came_x_ref, came_y_ref)
    vectors = vectors.astype(BF16)
    vectors_out_ref[...] = vectors
    put_vectors(vectors, send_y_ref, send_x_ref)


def third_sum_kernel(left_x_ref, came_x_ref, left_y_ref, came_y_ref, vectors_ref, total_ref):
    size, half = left_x_ref.shape
    total_ref[:size, :half] = (left_x_ref[...] + came_x_ref[:size].astype(F32)).astype(BF16)
    total_ref[:size, half:] = (left_y_ref[...] + came_y_ref[:size].astype(F32)).astype(BF16)
    vectors = vectors_ref[...].astype(F32) + get_vectors(came_x_ref, came_y_ref)
    total_ref[size : size + VECTOR_ROWS] = vectors.astype(BF16)


def third_cut_kernel(place_ref, left_x_ref, came_x_ref, left_y_ref, came_y_ref, vectors_ref, *refs):
    more_ref, total_ref, sent_ref = refs
    third_sum_kernel(left_x_ref, came_x_ref, left_y_ref, came_y_ref, vectors_ref, total_ref)
    filled = left_x_ref.shape[0] + VECTOR_ROWS
    if filled < total_ref.shape[0]:
        total_ref[filled:] = jnp.zeros((total_ref.shape[0] - filled, total_ref.shape[1]), BF16)
    half = total_ref.shape[0] // 2
    rows = more_ref.shape[2]
    away = pl.multiple_of((1 - (place_ref[1] & 1)) * half, half)
    sent_ref[:half] = total_ref[pl.ds(away, half)]
    for i in range(2):
        sent_ref[half + i * rows : half + (i + 1) * rows] = more_ref[i, 0]


def near_sum_kernel(place_ref, total_ref, came_ref, second_ref, out_ref):
    half = total_ref.shape[0] // 2
    rows = second_ref.shape[1]
    mine = total_ref[pl.ds(pl.multiple_of((place_ref[1] & 1) * half, half), half)]
    out_ref[:half] = (mine.astype(F32) + came_ref[:half].astype(F32)).astype(BF16)
    second = second_ref[0].astype(F32) + came_ref[half + rows : half + 2 * rows].astype(F32)
    out_ref[half : half + rows] = second.astype(BF16)


def far_sum_kernel(left_ref, right_ref, out_ref):
    at = slice(0, out_ref.shape[0])
    out_ref[...] = (left_ref[at].astype(F32) + right_ref[at].astype(F32)).astype(BF16)


def add_kernel(left_ref, right_ref, out_ref):
    out_ref[...] = (left_ref[...].astype(F32) + right_ref[...].astype(F32)).astype(out_ref.dtype)


def join_rows(place, mine_ref, other_ref, out_ref):
    part = mine_ref.shape[0]
    out_ref[pl.ds(pl.multiple_of(place * part, part), part)] = mine_ref[...]
    out_ref[pl.ds(pl.multiple_of((1 - place) * part, part), part)] = other_ref[...]


def finish_kernel(ratio, place_ref, low_ref, came_ref, mine_ref, other_ref, *refs):
    query_ref, key_ref, value_ref, outer_ref, inner_ref, out_ref = refs[:6]
    tail_refs, dense_refs, wide_ref, total_scratch, row_scratch = refs[6:10], refs[10:14], *refs[14:]
    rows, width = out_ref.shape
    total = lambda at: low_ref[at].astype(F32) + came_ref[at].astype(F32)
    for s, ref in enumerate((query_ref, key_ref, value_ref)):
        ref[...] = total(slice(s * rows, (s + 1) * rows))
    put_slices(total(slice(3 * rows, 3 * rows + VECTOR_ROWS)), place_ref[0], tail_refs)
    join_rows(place_ref[1] & 1, mine_ref, other_ref, total_scratch)
    outer_ref[...] = total_scratch[: ratio * rows].astype(F32)
    for s in range(ratio):
        at = (ratio + s) * rows
        inner_ref[:, s * width : (s + 1) * width] = total_scratch[at : at + rows].astype(F32)
    at = 2 * ratio * rows
    out_ref[...] = total_scratch[at : at + rows].astype(F32)
    vectors = total_scratch[at + rows : at + rows + VECTOR_ROWS].astype(F32)
    put_slices(vectors, place_ref[0], dense_refs)
    row_scratch[...] = vectors
    size = wide_ref.shape[0]
    start = place_ref[0] * size
    row = row_scratch[pl.ds(len(dense_refs) + start // width, 1)]
    wide_ref[...] = pltpu.roll(row, lax.rem(width - lax.rem(start, width), width), 1)[0, :size]


def put_slices(vectors, index, refs):
    width, size = vectors.shape[1], refs[0].shape[0]
    turned = pltpu.roll(vectors, lax.rem(width - index * size, width), 1)
    for i, ref in enumerate(refs):
        ref[...] = turned[i, :size]


def small_call(kernel, place, operands, out_shapes, name, after=(), inside=True, scratch=(), mib=4, size=None):
    ahead = 0 if place is None else 1
    count = len(operands)

    def body(*refs):
        kernel(*refs[: ahead + count], *refs[ahead + count + len(after) :])

    if size is None:
        size = sum(math.prod(a.shape) * a.dtype.itemsize for a in list(operands) + list(out_shapes))
    return pl.pallas_call(
        body,
        grid_spec=pltpu.PrefetchScalarGridSpec(
            num_scalar_prefetch=ahead,
            grid=(1,),
            in_specs=[near_spec() for a in operands] + [pl.BlockSpec(memory_space=pl.ANY)] * len(after),
            out_specs=[near_spec() for s in out_shapes],
            scratch_shapes=list(scratch),
        ),
        out_shape=[near(s.shape, s.dtype) if inside else s for s in out_shapes],
        compiler_params=params(mib),
        cost_estimate=pl.CostEstimate(flops=0, transcendentals=0, bytes_accessed=size),
        name=name,
    )(*(() if place is None else (place,)), *operands, *after)


def sum_core(place, groups, vectors, name, after=()):
    groups = [list(g) + [swap(a, "batch", 1) for a in sent] for g, sent in groups]
    vectors_other = swap(vectors, "batch", 1)
    _, _, rows, width = groups[0][0].shape
    size = sum(g[0].shape[1] for g in groups) * rows
    half = width // 2
    counts = tuple(len(g) for g in groups)
    message = shape_of((2 * size + VECTOR_ROWS, half), BF16)
    kept = shape_of((2, size, half), F32)
    along_x, along_y, keep_x, keep_y, vectors = small_call(
        functools.partial(first_sum_kernel, counts),
        place,
        [a for g in groups for a in g] + [vectors, vectors_other],
        [message, message, kept, kept, shape_of(vectors.shape, BF16)],
        name + "_sum_core",
        after,
    )
    came_x, came_y = swap(along_x, "batch", 2), swap(along_y, "batch", 4)
    return (keep_x, came_x, keep_y, came_y, vectors), along_x


def sum_first(place, pieces, name, after=()):
    keep_x, _, _, _, vectors = pieces
    _, size, half = keep_x.shape
    message = shape_of((size + VECTOR_ROWS, half), BF16)
    kept = shape_of((size, half), F32)
    send_y, send_x, left_x, left_y, vectors = small_call(
        second_sum_kernel,
        place,
        pieces,
        [message, message, kept, kept, shape_of(vectors.shape, BF16)],
        name + "_sum_first",
        after,
    )
    came_x, came_y = swap(send_y, "batch", 4), swap(send_x, "batch", 2)
    return (left_x, came_x, left_y, came_y, vectors), send_y


def sum_second(pieces, name, after=()):
    size, half = pieces[0].shape
    shape = shape_of((size + VECTOR_ROWS, 2 * half), BF16)
    return small_call(third_sum_kernel, None, pieces, [shape], name + "_sum_second", after)[0]


def sum_second_cut(place, pieces, more, name, after=()):
    size, half = pieces[0].shape
    rows = -(-(size + VECTOR_ROWS) // 32) * 32
    total, sent = small_call(
        third_cut_kernel,
        place,
        list(pieces) + [more],
        [
            shape_of((rows, 2 * half), BF16),
            shape_of((rows // 2 + 2 * more.shape[2], 2 * half), BF16),
        ],
        name + "_sum_second",
        after,
    )
    return total, swap(sent, "rows", 1)


def batch_slices_any(groups, vectors):
    me = lax.axis_index("batch")
    bits = lax.axis_size("batch").bit_length() - 1
    pieces = []
    for kept, sent in groups:
        values = [a.astype(F32) for a in kept] + [swap(a, "batch", 1).astype(F32) for a in sent]
        pieces.append(functools.reduce(lambda a, b: a + b, values))
    total = jnp.concatenate(pieces, 1)
    total = total.reshape((2,) * (bits - 1) + total.shape[1:])
    for bit in range(bits - 1, 0, -1):
        mine = (me >> bit) & 1
        sent = lax.dynamic_index_in_dim(total, 1 - mine, 0, keepdims=False).astype(BF16)
        total = lax.dynamic_index_in_dim(total, mine, 0, keepdims=False)
        total = total + swap(sent, "batch", 1 << bit).astype(F32)
    total = lax.psum(total.astype(BF16), "rows").astype(F32)
    return total, lax.psum(vectors, ("batch", "rows"))


def cross_kernel(count, *refs):
    out_ref = refs[-1]
    came = [(ref, i) for ref in refs[count:-1] for i in range(ref.shape[1])]
    for m, (term, (ref, i)) in enumerate(zip(refs[:count], came)):
        out_ref[m] = (term[0].astype(F32) + ref[1, i].astype(F32)).astype(BF16)


def cross_sum(terms, came, name, after=()):
    shape = (len(terms),) + terms[0].shape[1:]
    return small_call(
        functools.partial(cross_kernel, len(terms)),
        None,
        list(terms) + list(came),
        [shape_of(shape, BF16)],
        name,
        after,
    )[0]


def final_kernel(count, *refs):
    owns, nears, crosses = refs[:count], refs[count : 2 * count], refs[2 * count : 3 * count]
    atoms_ref, gain_ref, shift_ref, grad_middle_ref, out_ref = refs[3 * count :]
    gain = as_row(gain_ref)
    shift = as_row(shift_ref)
    for m in range(count):
        grad = owns[m][0] + nears[m][...].astype(F32) + crosses[m][...].astype(F32)
        _, normed, inverse = norm_forward(atoms_ref[m].astype(F32), gain, shift)
        result = grad_middle_ref[m] + norm_backward(grad, normed, inverse, gain)
        out_ref[m] = result.astype(BF16)


def first_norm_backward(owns, nears, crosses, others, after=()):
    count = len(owns)
    arrays = [a for a, _ in nears + crosses]
    spots = [at for _, at in nears + crosses]

    def kernel(*refs):
        picked = [r.at[at] for r, at in zip(refs[count : 3 * count], spots)]
        final_kernel(count, *refs[:count], *picked, *refs[3 * count :])

    return small_call(
        kernel,
        None,
        list(owns) + arrays + list(others),
        [shape_of(others[0].shape, BF16)],
        "first_norm_backward",
        after,
        inside=False,
    )[0]


def shards(
    atoms,
    pair_bias,
    lengths,
    first_gain,
    first_shift,
    query_weight,
    query_bias,
    key_weight,
    value_weight,
    value_bias,
    out_weight,
    out_bias,
    second_gain,
    second_shift,
    inner_weight,
    inner_bias,
    outer_weight,
    outer_bias,
    atoms_cotangent,
    pair_cotangent,
):
    molecules, rows, model_width = atoms.shape
    head_count = pair_bias.shape[1]
    head_size = model_width // head_count
    batch_count = lax.axis_size("batch")
    batch_index = lax.axis_index("batch")
    row = lax.axis_index("rows")
    (
        atoms_far,
        pair_bias,
        first_gain,
        first_shift,
        query_weight,
        query_bias,
        key_weight,
        value_weight,
        value_bias,
        out_weight,
        out_bias,
        second_gain,
        second_shift,
        inner_weight,
        inner_bias,
        outer_weight,
        outer_bias,
        atoms_cotangent,
        pair_cotangent,
    ) = [
        pltpu.with_memory_space_constraint(a, pltpu.HBM)
        for a in (
            atoms,
            pair_bias,
            first_gain,
            first_shift,
            query_weight,
            query_bias,
            key_weight,
            value_weight,
            value_bias,
            out_weight,
            out_bias,
            second_gain,
            second_shift,
            inner_weight,
            inner_bias,
            outer_weight,
            outer_bias,
            atoms_cotangent,
            pair_cotangent,
        )
    ]
    place = jnp.stack(
        [batch_index, row, batch_index & 1, (batch_index >> 1) & 1, (batch_index >> 2) & 1]
    ).astype(jnp.int32)
    line = lambda v: v
    count = molecules // STAGES
    stages = []
    pair_out = jnp.zeros((1,), BF16)
    one = swap(atoms, "rows", 1)
    mine = [atoms[:count]]
    (
        pair_near,
        query_near,
        key_near,
        value_near,
        later,
        first_gain,
        first_shift,
        query_bias,
        value_bias,
        out_bias,
        second_gain,
        second_shift,
        inner_bias,
        outer_bias,
    ) = load(
        [
            pair_bias,
            query_weight,
            key_weight,
            value_weight,
            atoms_far,
            first_gain,
            first_shift,
            query_bias,
            value_bias,
            out_bias,
            second_gain,
            second_shift,
            inner_bias,
            outer_bias,
        ],
        "load_first",
        (0, 0, 0, 0, count) + (0,) * 9,
        (place,),
    )
    mine.append(later)
    gathered = [[swap(a, "rows", mask) for mask in (2, 3)] for a in mine]
    projected = near_half(
        head_size,
        STAGES,
        place,
        atoms_far,
        one,
        (
            first_gain,
            first_shift,
            query_near,
            query_bias,
            key_near,
            value_near,
            value_bias,
        ),
        (),
    )
    for stage in range(STAGES):
        pair_out, kept, loaded = attention_forward(
            head_size,
            stage * count,
            place,
            lengths,
            gathered[stage],
            pair_near,
            (first_gain, first_shift, key_near, value_near, value_bias),
            projected[5 * stage : 5 * stage + 5],
            pair_out,
            [out_weight, inner_weight, outer_weight, atoms_cotangent] if stage else [],
        )
        stages.append(kept)
    out_weight, inner_weight, outer_weight, atoms_cotangent = loaded
    (
        atoms_out,
        outer_send,
        outer_keep,
        inner_send,
        inner_keep,
        out_send,
        out_keep,
        grad_middle,
        grad_mixed,
        dense_vectors,
        pair_cotangent,
    ) = dense(
        place,
        [s[1] for s in stages],
        atoms,
        atoms_cotangent,
        (
            out_weight,
            line(out_bias),
            line(second_gain),
            line(second_shift),
            inner_weight,
            line(inner_bias),
            outer_weight,
            line(outer_bias),
        ),
        batch_count,
        pair_cotangent,
    )
    pairs = batch_count // 2
    own_rows = model_width // batch_count
    slots = lambda a: a.reshape(pairs, -1, own_rows, model_width)
    dense_groups = [
        ([slots(outer_keep)], [slots(outer_send)]),
        ([inner_keep], [inner_send]),
        ([slots(out_keep)], [slots(out_send)]),
    ]
    usual = batch_count == 8

    def backward(molecule, held, sums, after, before=None):
        stage = molecule // count
        return attention_backward(
            head_size,
            stage * count,
            molecule % count,
            place,
            stages[stage],
            pair_cotangent,
            grad_mixed,
            (query_near, key_near, value_near),
            held,
            sums,
            after,
            before,
        )

    pair_grad, near0, cross0, own0, sums, *grads0 = backward(0, None, None, [])
    after = []
    if usual:
        dense_pieces, held = sum_core(place, dense_groups, dense_vectors, "dense", (own0,))
        after = [held]
    else:
        dense_total, dense_vectors = batch_slices_any(dense_groups, dense_vectors)
    pair_grad, near1, cross1, own1, sums, *grads1 = backward(1, pair_grad, sums, after, near0)
    near1 = swap(near1, "rows", 1)
    pair_grad, near2, cross2, own2, sums, *grads2 = backward(2, pair_grad, sums, [own1])
    near2 = swap(near2, "rows", 1)
    after = [own2]
    if usual:
        dense_pieces, held = sum_first(place, dense_pieces, "dense", after)
        after = [held]
    cross0 = cross_sum([cross0, cross1], [near1], "cross_first", after)
    far0 = swap(cross0, "rows", 2)
    pair_grad, near3, cross3, own3, tail_vectors, *grads3 = backward(3, pair_grad, sums, [cross0])
    owns = [own0, own1, own2, own3]
    after = [far0, near2]
    if usual:
        dense_total, came = sum_second_cut(place, dense_pieces, near3, "dense", (own3,))
        after.append(dense_total)
    cross2 = cross_sum([cross2], [near2], "cross_second", after[-1:])
    far2 = swap(cross2, "rows", 2)
    after = [far0, cross2]
    part = shape_of((pairs, 1, own_rows, model_width), BF16)
    parts = small_call(
        functools.partial(weight_kernel, 4, STAGES),
        place,
        [s[3] for s in stages] + grads0 + grads1 + grads2 + grads3,
        [part] * 6,
        "attention_weights",
        after,
        scratch=[pltpu.VMEM((pairs, 2, own_rows, model_width), F32)],
        mib=14,
    )
    groups = [([parts[2 * i + 1]], [parts[2 * i]]) for i in range(3)]
    matrix = shape_of((own_rows, model_width), F32)
    ratio = inner_weight.shape[1] // model_width
    vector = shape_of((own_rows,), F32)
    finish = (atoms, line(first_gain), line(first_shift), grad_middle)
    if usual:
        pieces, _ = sum_core(place, groups, tail_vectors, "tail")
        pieces, held = sum_first(place, pieces, "tail")
        start = dense_total.shape[0] // 2
        first_rows = slice(start, start + rows)
        mine = small_call(
            near_sum_kernel,
            place,
            [dense_total, came, cross3],
            [shape_of((start + rows, model_width), BF16)],
            "dense_near_sum",
            (held, far2),
        )[0]
        far = swap(mine, "rows", 2)
        total = sum_second(pieces, "tail", (mine,))
        tail_came = swap(total, "rows", 1)
        total = small_call(add_kernel, None, [total, tail_came], [total], "tail_near_sum")[0]
        tail_came = swap(total, "rows", 2)
        part = shape_of((start, model_width), BF16)
        mine = small_call(far_sum_kernel, None, [mine, far], [part], "dense_far_sum", (total,))[0]
        other = swap(mine, "rows", 1)
        atoms_grad = first_norm_backward(
            owns,
            [(near1, (0, 0)), (near1, (0, 1)), (near2, (0, 0)), (came, first_rows)],
            [(far0, 0), (far0, 1), (far2, 0), (far, first_rows)],
            finish,
            (mine,),
        )
        outs = small_call(
            functools.partial(finish_kernel, ratio),
            place,
            [total, tail_came, mine, other],
            [matrix] * 3
            + [
                shape_of((ratio * own_rows, model_width), F32),
                shape_of((own_rows, ratio * model_width), F32),
                matrix,
            ]
            + [vector] * 8
            + [shape_of((ratio * own_rows,), F32)],
            "finish",
            inside=False,
            scratch=[
                pltpu.VMEM((2 * part.shape[0], model_width), BF16),
                pltpu.VMEM((VECTOR_ROWS, model_width), F32),
            ],
        )
        query_grad, key_grad, value_grad, outer_grad, inner_grad, out_grad = outs[:6]
        tail_parts, dense_parts = outs[6:10], outs[10:]
    else:
        near3 = swap(near3, "rows", 1)
        far3 = swap(cross_sum([cross3], [near3], "cross_third"), "rows", 2)
        atoms_grad = first_norm_backward(
            owns,
            [(near1, (0, 0)), (near1, (0, 1)), (near2, (0, 0)), (near3, (0, 0))],
            [(far0, 0), (far0, 1), (far2, 0), (far3, 0)],
            finish,
        )
        total, tail_vectors = batch_slices_any(groups, tail_vectors)
        query_grad, key_grad, value_grad = total[0], total[1], total[2]
        outer_grad = dense_total[:ratio].reshape(-1, model_width)
        inner_grad = dense_total[ratio : 2 * ratio].transpose(1, 0, 2).reshape(own_rows, -1)
        out_grad = dense_total[2 * ratio]
        part = lambda v: lax.dynamic_slice_in_dim(
            v, batch_index * (v.shape[0] // batch_count), v.shape[0] // batch_count
        )
        tail_parts = [part(v) for v in tail_vectors[:4]]
        dense_parts = [part(v) for v in dense_vectors[:4]] + [part(dense_vectors[4:].reshape(-1))]
    return (
        atoms_out,
        pair_out,
        atoms_grad,
        pair_grad,
        tail_parts[0],
        tail_parts[1],
        query_grad,
        tail_parts[2],
        key_grad,
        value_grad,
        tail_parts[3],
        out_grad,
        dense_parts[3],
        dense_parts[1],
        dense_parts[2],
        inner_grad,
        dense_parts[4],
        outer_grad,
        dense_parts[0],
    )


def solution(mesh):
    tokens = P("batch", "rows", None)
    pairs = P("batch", None, "rows", None)
    vector = P("batch")
    matrix = P("batch", None)
    return jax.shard_map(
        shards,
        mesh=mesh,
        in_specs=(tokens, pairs, P("batch")) + (P(),) * 15 + (tokens, pairs),
        out_specs=(
            tokens,
            pairs,
            tokens,
            pairs,
            vector,
            vector,
            matrix,
            vector,
            matrix,
            matrix,
            vector,
            matrix,
            vector,
            vector,
            vector,
            matrix,
            vector,
            matrix,
            vector,
        ),
        check_vma=False,
    )
```

```python
import functools
import math

import jax
import jax.numpy as jnp
from jax import lax
from jax.experimental import pallas as pl
from jax.experimental.pallas import tpu as pltpu
from jax.sharding import PartitionSpec as P

EPSILON = 1e-05
MASKED = -1000000000.0
F32 = jnp.float32
BF16 = jnp.bfloat16
LANES = 128
STAGES = 2
VMEM_LIMIT = 18 << 20


def shape_of(shape, dtype):
    return jax.ShapeDtypeStruct(tuple(shape), dtype)


def norm_forward(values_in, gain, shift):
    centre = values_in - jnp.mean(values_in, -1, keepdims=True)
    inverse = lax.rsqrt(jnp.mean(centre * centre, -1, keepdims=True) + EPSILON)
    normed = centre * inverse
    return (normed * gain + shift, normed, inverse)


def norm_backward(upstream, normed, inverse, gain):
    scaled = upstream * gain
    return inverse * (
        scaled
        - jnp.mean(scaled, -1, keepdims=True)
        - normed * jnp.mean(scaled * normed, -1, keepdims=True)
    )


def dot(left, right):
    return jnp.dot(left, right, preferred_element_type=F32)


def across(left, right):
    return lax.dot_general(left, right, (((0,), (0,)), ((), ())), preferred_element_type=F32)


def against(left, right):
    return lax.dot_general(left, right, (((1,), (1,)), ((), ())), preferred_element_type=F32)


def column_sum(values_in):
    return jnp.sum(values_in.astype(F32), 0, keepdims=True)


def near(shape, dtype):
    return pltpu.VMEM(tuple(shape), dtype)


def near_spec():
    return pl.BlockSpec(memory_space=pltpu.VMEM)


def as_row(ref):
    return ref[...].astype(F32).reshape(1, -1)


def whole(array):
    return pl.BlockSpec(array.shape, lambda *_: (0,) * array.ndim)


def params(mib=10):
    return pltpu.CompilerParams(vmem_limit_bytes=mib << 20)


def load_kernel(count, starts, *refs):
    sources, targets, semaphores = refs[:count], refs[-count - 1 : -1], refs[-1]
    copies = [
        pltpu.make_async_copy(source.at[pl.ds(start, target.shape[0])], target, semaphores.at[i])
        for i, (source, target, start) in enumerate(zip(sources, targets, starts))
    ]
    for copy in copies:
        copy.start()
    for copy in copies:
        copy.wait()


def copies_beside(sources, targets, semaphores):
    return [
        pltpu.make_async_copy(source, target, semaphores.at[i])
        for i, (source, target) in enumerate(zip(sources, targets))
    ]


def load(arrays, name, starts=None, after=()):
    count = len(arrays)
    starts = starts or (0,) * count
    return pl.pallas_call(
        functools.partial(load_kernel, count, starts),
        in_specs=[pl.BlockSpec(memory_space=pltpu.HBM)] * count
        + [pl.BlockSpec(memory_space=pl.ANY)] * len(after),
        out_specs=[near_spec()] * count,
        out_shape=[
            near((a.shape[0] - start,) + a.shape[1:], a.dtype) for a, start in zip(arrays, starts)
        ],
        scratch_shapes=[pltpu.SemaphoreType.DMA((count,))],
        compiler_params=params(),
        name=name,
    )(*arrays, *after)


def project(pieces, first, parameters, row, refs, atoms_scratch):
    gain_ref, shift_ref, key_weight_ref, value_weight_ref, value_bias_ref = parameters
    hidden_ref, normed_ref, key_ref, value_ref = refs
    count = hidden_ref.shape[0]
    _, groups, keys, width = key_ref.shape
    rows = keys // 4
    half = 2 * rows
    model_width = hidden_ref.shape[2]
    for m in range(count):
        for i, piece in enumerate(pieces):
            start = pl.multiple_of(m * half + ((row ^ i) & 1) * rows, rows)
            atoms_scratch[pl.ds(start, rows)] = piece[m + first]
    hidden, normed, _ = norm_forward(
        atoms_scratch[...].astype(F32), as_row(gain_ref), as_row(shift_ref)
    )
    hidden = hidden.astype(BF16)
    normed = normed.astype(BF16)
    key_rows = dot(hidden, key_weight_ref[...]).astype(BF16)
    value_rows = (dot(hidden, value_weight_ref[...]) + as_row(value_bias_ref)).astype(BF16)
    return [a.reshape(count, half, model_width) for a in (hidden, normed, key_rows, value_rows)]


def put_half(values, at, refs):
    hidden, normed, key_rows, value_rows = values
    hidden_ref, normed_ref, key_ref, value_ref = refs
    count, groups, _, width = key_ref.shape
    half = hidden.shape[1]
    ones = jnp.ones((count, half, width), BF16)
    hidden_ref[:, at] = hidden
    normed_ref[:, at] = normed
    for t in range(groups):
        lanes = slice(t * width, (t + 1) * width)
        key_ref[:, t, at] = key_rows[:, :, lanes]
        value_ref[:, t, at, :width] = value_rows[:, :, lanes]
        value_ref[:, t, at, width:] = ones


def half_rows(row, other, rows):
    which = row >> 1
    which = 1 - which if other else which
    return pl.ds(pl.multiple_of(which * 2 * rows, 2 * rows), 2 * rows)


def near_half_kernel(
    head_size,
    stages,
    ahead,
    place_ref,
    own_ref,
    one_ref,
    gain_ref,
    shift_ref,
    query_weight_ref,
    query_bias_ref,
    key_weight_ref,
    value_weight_ref,
    value_bias_ref,
    *refs,
):
    refs = refs[ahead:]
    later_ref, atoms_scratch = refs[-2:]
    later_ref[...] = own_ref[own_ref.shape[0] - later_ref.shape[0] :]
    row = place_ref[1]
    rows, model_width = own_ref.shape[1:]
    factor = head_size**-0.5
    parameters = (gain_ref, shift_ref, key_weight_ref, value_weight_ref, value_bias_ref)
    for stage in range(stages):
        hidden_ref, normed_ref, key_ref, value_ref, query_ref = refs[5 * stage : 5 * stage + 5]
        outs = (hidden_ref, normed_ref, key_ref, value_ref)
        count, groups, _, width = key_ref.shape
        values = project((own_ref, one_ref), stage * count, parameters, row, outs, atoms_scratch)
        put_half(values, half_rows(row, False, rows), outs)
        mine = pl.ds(pl.multiple_of(row * rows, rows), rows)
        own = jnp.concatenate([hidden_ref[m, mine] for m in range(count)], 0)
        query_rows = (dot(own, query_weight_ref[...]) + as_row(query_bias_ref)) * factor
        query_rows = query_rows.astype(BF16).reshape(count, rows, model_width)
        for t in range(groups):
            query_ref[:, t] = query_rows[:, :, t * width : (t + 1) * width]


def near_half(head_size, stages, place, atoms, one, parameters, after):
    molecules, rows, model_width = atoms.shape
    keys = 4 * rows
    count = molecules // stages
    groups = model_width // LANES
    operands = (place, atoms, one, *parameters, *after)
    return pl.pallas_call(
        functools.partial(near_half_kernel, head_size, stages, len(after)),
        grid_spec=pltpu.PrefetchScalarGridSpec(
            num_scalar_prefetch=1,
            grid=(1,),
            in_specs=[whole(atoms), near_spec()]
            + [near_spec() for a in parameters]
            + [pl.BlockSpec(memory_space=pl.ANY)] * len(after),
            out_specs=[near_spec()] * (5 * stages + 1),
            scratch_shapes=[pltpu.VMEM((count * 2 * rows, model_width), BF16)],
        ),
        out_shape=[
            near((count, keys, model_width), BF16),
            near((count, keys, model_width), BF16),
            near((count, groups, keys, LANES), BF16),
            near((count, groups, keys, 2 * LANES), BF16),
            near((count, groups, rows, LANES), BF16),
        ]
        * stages
        + [near((molecules - count, rows, model_width), BF16)],
        compiler_params=params(10),
        name="near_half",
    )(*operands)


def forward_kernel(
    head_size,
    chunk,
    first,
    extra,
    place_ref,
    length_ref,
    two_ref,
    three_ref,
    pair_ref,
    query_ref,
    gain_ref,
    shift_ref,
    key_weight_ref,
    value_weight_ref,
    value_bias_ref,
    *refs,
):
    (
        pair_out_ref,
        weights_ref,
        mixed_ref,
        inverse_ref,
        hidden_ref,
        normed_ref,
        key_ref,
        value_ref,
    ) = refs[5 + extra : 13 + extra]
    atoms_scratch, semaphores = refs[-2:]
    copies = copies_beside(refs[5 : 5 + extra], refs[13 + extra : 13 + 2 * extra], semaphores)
    molecule = pl.program_id(0)
    group = pl.program_id(1)
    count, groups, keys, width = key_ref.shape
    heads = width // head_size
    rows = query_ref.shape[2]

    @pl.when((molecule == 0) & (group == 0))
    def _():
        for copy in copies:
            copy.start()
        row = place_ref[1]
        outs = (hidden_ref, normed_ref, key_ref, value_ref)
        parameters = (gain_ref, shift_ref, key_weight_ref, value_weight_ref, value_bias_ref)
        values = project((two_ref, three_ref), 0, parameters, row, outs, atoms_scratch)
        put_half(values, half_rows(row, True, rows), outs)

    query = query_ref[molecule, group]
    key = key_ref[molecule, group]
    value = value_ref[molecule, group]
    valid = lax.broadcasted_iota(jnp.int32, (1, keys), 1) < length_ref[molecule + first]
    lane = lax.broadcasted_iota(jnp.int32, (1, width), 1) // head_size
    lane_pair = lax.broadcasted_iota(jnp.int32, (1, 2 * width), 1) % width // head_size
    total = jnp.zeros((rows, 2 * width), F32)
    zero = jnp.zeros((), BF16)
    for c in range(0, heads, chunk):
        here = slice(c, c + chunk)
        there = pl.ds(group * heads + c, chunk)
        spread = jnp.concatenate([jnp.where(lane == c + t, query, zero) for t in range(chunk)], 0)
        pair = pair_ref[molecule + first, there].reshape(chunk * rows, keys)
        scores = against(spread, key) + pair.astype(F32)
        pair_out_ref[0, here] = scores.astype(BF16).reshape(chunk, rows, keys)
        masked = jnp.where(valid, scores, MASKED)
        weights = jnp.exp(masked - jnp.max(masked, -1, keepdims=True)).astype(BF16)
        weights_ref[molecule, there] = weights.reshape(chunk, rows, keys)
        product = dot(weights, value)
        for t in range(chunk):
            total = jnp.where(lane_pair == c + t, product[t * rows : (t + 1) * rows], total)
    inverse = 1.0 / total[:, width:]
    inverse_ref[molecule, group] = inverse
    mixed_ref[molecule, group] = total[:, :width] * inverse

    @pl.when((molecule == count - 1) & (group == groups - 1))
    def _():
        for copy in copies:
            copy.wait()


def attention_forward(
    head_size, first, place, lengths, pieces, pair_bias, parameters, projected, held, extra
):
    _, head_count, rows, keys = pair_bias.shape
    hidden, normed, key, value, query = projected
    count, groups = key.shape[:2]
    model_width = groups * LANES
    heads = LANES // head_size
    pair_spec = pl.BlockSpec((1, heads, rows, keys), lambda m, g, *_: (m + first, g, 0, 0))
    elements = count * head_count * rows * keys
    operands = [place, lengths, *pieces, pair_bias, query, *parameters]
    in_specs = [near_spec()] * (len(pieces) + 2)
    in_specs += [near_spec() for a in parameters]
    start = len(operands)
    operands += [hidden, normed, key, value, held]
    in_specs += [near_spec()] * 4 + [pl.BlockSpec(memory_space=pl.ANY)]
    aliases = {start + i: 4 + i for i in range(4)}
    if held.ndim > 1:
        aliases[start + 4] = 0
    operands += extra
    in_specs += [pl.BlockSpec(memory_space=pltpu.HBM)] * len(extra)
    outs = pl.pallas_call(
        functools.partial(forward_kernel, head_size, 8, first, len(extra)),
        grid_spec=pltpu.PrefetchScalarGridSpec(
            num_scalar_prefetch=2,
            grid=(count, groups),
            in_specs=in_specs,
            out_specs=[pair_spec] + [near_spec()] * (7 + len(extra)),
            scratch_shapes=[
                pltpu.VMEM((count * 2 * rows, model_width), BF16),
                pltpu.SemaphoreType.DMA((max(len(extra), 1),)),
            ],
        ),
        out_shape=[
            shape_of(pair_bias.shape, BF16),
            near((count, head_count, rows, keys), BF16),
            near((count, groups, rows, LANES), F32),
            near((count, groups, rows, LANES), F32),
            near(hidden.shape, BF16),
            near(normed.shape, BF16),
            near(key.shape, BF16),
            near(value.shape, BF16),
        ]
        + [near(a.shape, a.dtype) for a in extra],
        input_output_aliases=aliases,
        compiler_params=params(10),
        cost_estimate=pl.CostEstimate(
            flops=elements * 2 * 384, transcendentals=elements, bytes_accessed=elements * 6
        ),
        name="attention_forward",
    )(*operands)
    pair_out, weights, mixed, inverse, hidden, normed, key, value = outs[:8]
    return pair_out, (weights, mixed, inverse, hidden, normed, query, key, value), outs[8:]


def dense_kernel(
    mixed_count,
    place_ref,
    *refs,
):
    mixed_refs = refs[:mixed_count]
    (
        atoms_ref,
        cotangent_ref,
        out_weight_ref,
        out_bias_ref,
        gain_ref,
        shift_ref,
        inner_weight_ref,
        inner_bias_ref,
        outer_weight_ref,
        outer_bias_ref,
        far_ref,
        atoms_out_ref,
        outer_send_ref,
        outer_keep_ref,
        inner_send_ref,
        inner_keep_ref,
        out_send_ref,
        out_keep_ref,
        grad_middle_ref,
        grad_mixed_ref,
        vectors_ref,
        copied_ref,
        hidden_scratch,
        turned_scratch,
        normed_scratch,
        inverse_scratch,
        result_scratch,
        upstream_scratch,
        outer_scratch,
        inner_scratch,
        semaphores,
    ) = refs[mixed_count:]
    (copy,) = copies_beside([far_ref], [copied_ref], semaphores)
    step = pl.program_id(0)
    steps = pl.num_programs(0)
    core = place_ref[2]
    tokens, model_width = hidden_scratch.shape
    cotangent = cotangent_ref[...].reshape(tokens, model_width)

    def mixed_rows():
        parts = []
        for ref in mixed_refs:
            count, groups, rows, width = ref.shape
            join = [ref[:, t].reshape(count * rows, width) for t in range(groups)]
            parts.append(jnp.concatenate(join, 1))
        return jnp.concatenate(parts, 0)

    @pl.when(step == 0)
    def _():
        copy.start()
        mixed_low = mixed_rows().astype(BF16)
        middle = (
            atoms_ref[...].reshape(tokens, model_width).astype(F32)
            + dot(mixed_low, out_weight_ref[...])
            + as_row(out_bias_ref)
        )
        hidden, normed, inverse = norm_forward(
            middle, as_row(gain_ref), as_row(shift_ref)
        )
        hidden_scratch[...] = hidden.astype(BF16)
        turned_scratch[...] = jnp.transpose(hidden).astype(BF16)
        normed_scratch[...] = normed
        inverse_scratch[...] = inverse
        result_scratch[...] = middle + as_row(outer_bias_ref)
        upstream_scratch[...] = jnp.zeros_like(upstream_scratch)
        vectors_ref[0:1] = column_sum(cotangent)

    hidden = hidden_scratch[...]
    width = outer_weight_ref.shape[1]
    at = pl.ds(pl.multiple_of(step * width, width), width)
    inner_weight = inner_weight_ref[:, at]
    outer_weight = outer_weight_ref[at]
    pre = dot(hidden, inner_weight) + inner_bias_ref[at].astype(F32).reshape(1, -1)
    slope = math.sqrt(2.0 / math.pi)
    square = pre * pre
    tanh = jnp.tanh(slope * (pre + 0.044715 * (pre * square)))
    half = 0.5 * (1.0 + tanh)
    active = (pre * half).astype(BF16)
    result_scratch[...] += dot(active, outer_weight)
    derivative = half + (0.5 * slope) * pre * (1.0 - tanh * tanh) * (1.0 + 0.134145 * square)
    grad_pre = against(cotangent, outer_weight) * derivative
    vectors_ref[pl.ds(4 + step, 1)] = column_sum(grad_pre.astype(BF16))
    grad_pre = grad_pre.astype(BF16)
    outer_scratch[...] = across(active, cotangent).reshape(outer_scratch.shape)
    outer_send_ref[...] = outer_scratch[:, 1 - core].astype(BF16).reshape(outer_send_ref.shape)
    outer_keep_ref[...] = outer_scratch[:, core].astype(BF16).reshape(outer_keep_ref.shape)
    inner_scratch[...] = dot(turned_scratch[...], grad_pre).reshape(inner_scratch.shape)
    inner_send_ref[:, 0] = inner_scratch[:, 1 - core].astype(BF16)
    inner_keep_ref[:, 0] = inner_scratch[:, core].astype(BF16)
    upstream_scratch[...] += against(grad_pre, inner_weight)

    @pl.when(step == steps - 1)
    def _():
        atoms_out_ref[...] = result_scratch[...].astype(BF16).reshape(atoms_out_ref.shape)
        upstream = upstream_scratch[...]
        normed = normed_scratch[...]
        vectors_ref[1:2] = column_sum(upstream * normed)
        vectors_ref[2:3] = column_sum(upstream)
        grad_middle = cotangent.astype(F32) + norm_backward(
            upstream, normed, inverse_scratch[...], as_row(gain_ref)
        )
        grad_middle_ref[...] = grad_middle.reshape(grad_middle_ref.shape)
        branch = grad_middle.astype(BF16)
        vectors_ref[3:4] = column_sum(branch)
        grad_mixed = against(branch, out_weight_ref[...]).astype(BF16)
        molecules, groups, rows, lanes = grad_mixed_ref.shape
        grad_mixed = grad_mixed.reshape(molecules, rows, model_width)
        for t in range(groups):
            grad_mixed_ref[:, t] = grad_mixed[:, :, t * lanes : (t + 1) * lanes]
        turned = jnp.transpose(mixed_rows()).astype(BF16)
        inner_scratch[...] = dot(turned, branch).reshape(inner_scratch.shape)
        out_send_ref[...] = inner_scratch[:, 1 - core].astype(BF16)
        out_keep_ref[...] = inner_scratch[:, core].astype(BF16)
        copy.wait()


def dense(place, mixed, atoms, cotangent, parameters, batch_count, extra):
    (
        out_weight,
        out_bias,
        gain,
        shift,
        inner_weight,
        inner_bias,
        outer_weight,
        outer_bias,
    ) = parameters
    model_width, inner_width = inner_weight.shape
    tokens = atoms.shape[0] * atoms.shape[1]
    width = model_width
    steps = inner_width // width
    pairs = batch_count // 2
    outer_rows = inner_width // batch_count
    outer_pairs = width // (2 * outer_rows)
    own_rows = model_width // batch_count
    operands = (
        place,
        *mixed,
        atoms,
        cotangent,
        out_weight,
        out_bias,
        gain,
        shift,
        inner_weight,
        inner_bias,
        outer_weight,
        outer_bias,
        extra,
    )
    outer_spec = pl.BlockSpec((outer_pairs, outer_rows, model_width), lambda s, *_: (s, 0, 0))
    inner_spec = pl.BlockSpec((pairs, 1, own_rows, width), lambda s, *_: (0, s, 0, 0))
    outer_shape = shape_of((pairs, outer_rows, model_width), BF16)
    inner_shape = shape_of((pairs, steps, own_rows, width), BF16)
    out_shape = shape_of((pairs, own_rows, model_width), BF16)
    out_shapes = [
        shape_of(atoms.shape, BF16),
        outer_shape,
        outer_shape,
        inner_shape,
        inner_shape,
        out_shape,
        out_shape,
        near(atoms.shape, F32),
        near((atoms.shape[0], model_width // LANES, atoms.shape[1], LANES), BF16),
        shape_of((4 + steps, model_width), F32),
        near(extra.shape, extra.dtype),
    ]
    fixed = lambda s: pl.BlockSpec(s.shape, lambda *_: (0,) * len(s.shape))
    out_specs = [fixed(s) for s in out_shapes]
    out_specs[1:5] = [outer_spec, outer_spec, inner_spec, inner_spec]
    out_specs[7:9] = [near_spec(), near_spec()]
    out_specs[10] = near_spec()
    in_specs = [whole(a) for a in operands[1:]]
    for i, a in enumerate(operands[1:]):
        if i != len(mixed):
            in_specs[i] = near_spec()
    in_specs[-1] = pl.BlockSpec(memory_space=pltpu.HBM)
    return pl.pallas_call(
        functools.partial(dense_kernel, len(mixed)),
        grid_spec=pltpu.PrefetchScalarGridSpec(
            num_scalar_prefetch=1,
            grid=(steps,),
            in_specs=in_specs,
            out_specs=out_specs,
            scratch_shapes=[
                pltpu.VMEM((tokens, model_width), BF16),
                pltpu.VMEM((model_width, tokens), BF16),
                pltpu.VMEM((tokens, model_width), F32),
                pltpu.VMEM((tokens, 1), F32),
                pltpu.VMEM((tokens, model_width), F32),
                pltpu.VMEM((tokens, model_width), F32),
                pltpu.VMEM((outer_pairs, 2, outer_rows, model_width), F32),
                pltpu.VMEM((pairs, 2, own_rows, width), F32),
                pltpu.SemaphoreType.DMA((1,)),
            ],
        ),
        out_shape=out_shapes,
        compiler_params=params(14),
        cost_estimate=pl.CostEstimate(
            flops=12 * tokens * model_width * inner_width,
            transcendentals=tokens * inner_width,
            bytes_accessed=12 * model_width * inner_width,
        ),
        name="dense",
    )(*operands)


def backward_kernel(
    head_size,
    chunk,
    first,
    base,
    start,
    fresh,
    joined,
    place_ref,
    weights_ref,
    cotangent_ref,
    grad_mixed_ref,
    mixed_ref,
    inverse_ref,
    query_ref,
    key_ref,
    value_ref,
    normed_ref,
    query_weight_ref,
    key_weight_ref,
    value_weight_ref,
    *refs,
):
    before_ref = refs[start - 1] if joined else None
    refs = refs[start:]
    pair_grad_ref, near_ref, cross_ref, own_ref, vectors_ref = refs[:5]
    query_grad_ref, key_grad_ref, value_grad_ref = refs[5:8]
    grad_query_scratch, grad_key_scratch, grad_value_scratch, grad_scratch = refs[-4:]
    molecule = pl.program_id(0) + base
    group = pl.program_id(1)
    _, groups, rows, width = query_ref.shape
    keys = key_ref.shape[2]
    heads = width // head_size
    factor = head_size**-0.5
    query = query_ref[molecule, group]
    key = key_ref[molecule, group]
    value = value_ref[molecule, group]
    upstream = grad_mixed_ref[molecule + first, group].astype(F32) * inverse_ref[molecule, group]
    upstream = upstream.astype(BF16)
    offset = (-(upstream.astype(F32) * mixed_ref[molecule, group])).astype(BF16)
    both = jnp.concatenate([upstream, offset], 1)
    lane = lax.broadcasted_iota(jnp.int32, (1, width), 1) // head_size
    lane_pair = lax.broadcasted_iota(jnp.int32, (1, 2 * width), 1) % width // head_size
    query_turned = jnp.transpose(query.astype(F32)).astype(BF16)
    upstream_turned = jnp.transpose(upstream.astype(F32)).astype(BF16)
    query_turned = jnp.concatenate([query_turned] * chunk, 1)
    upstream_turned = jnp.concatenate([upstream_turned] * chunk, 1)
    turned_shape = (chunk * head_size, chunk * rows)
    same = (
        lax.broadcasted_iota(jnp.int32, turned_shape, 0) // head_size
        == lax.broadcasted_iota(jnp.int32, turned_shape, 1) // rows
    )
    zero = jnp.zeros((), BF16)
    total = jnp.zeros((rows, width), F32)
    key_parts = []
    value_parts = []
    for c in range(0, heads, chunk):
        here = slice(c, c + chunk)
        feature = slice(c * head_size, (c + chunk) * head_size)
        spread = jnp.concatenate([jnp.where(lane_pair == c + t, both, zero) for t in range(chunk)], 0)
        centred = against(spread, value)
        there = pl.ds(group * heads + c, chunk)
        weights = weights_ref[molecule, there].reshape(chunk * rows, keys)
        cotangent = cotangent_ref[molecule + first, there].reshape(chunk * rows, keys)
        grad = (weights.astype(F32) * centred + cotangent.astype(F32)).astype(BF16)
        pair_grad_ref[0, here] = grad.reshape(chunk, rows, keys)
        product = dot(grad, key)
        for t in range(chunk):
            total = jnp.where(lane == c + t, product[t * rows : (t + 1) * rows], total)
        key_parts.append(dot(jnp.where(same, query_turned[feature], zero), grad))
        value_parts.append(dot(jnp.where(same, upstream_turned[feature], zero), weights))
    grad_query_scratch[group] = (total * factor).astype(BF16)
    grad_key_scratch[group] = jnp.transpose(jnp.concatenate(key_parts, 0)).astype(BF16)
    grad_value_scratch[group] = jnp.transpose(jnp.concatenate(value_parts, 0)).astype(BF16)

    if fresh:

        @pl.when((pl.program_id(0) == 0) & (group == 0))
        def _():
            vectors_ref[...] = jnp.zeros_like(vectors_ref)

    @pl.when(group == groups - 1)
    def _():
        row = place_ref[1]
        mine = pl.ds(pl.multiple_of(row * rows, rows), rows)
        join = lambda ref: jnp.concatenate([ref[t] for t in range(groups)], 1)
        grad_query = join(grad_query_scratch)
        grad_key = join(grad_key_scratch)
        grad_value = join(grad_value_scratch)
        query_grad_ref[0] = grad_query
        key_grad_ref[0] = grad_key
        value_grad_ref[0] = grad_value
        grad_scratch[...] = against(grad_key, key_weight_ref[...]) + against(
            grad_value, value_weight_ref[...]
        )
        grad_scratch[mine] += against(grad_query, query_weight_ref[...])
        grad = grad_scratch[...]
        vectors_ref[0:1] += column_sum(grad * normed_ref[molecule].astype(F32))
        vectors_ref[1:2] += column_sum(grad)
        vectors_ref[2:3] += column_sum(grad_query)
        vectors_ref[3:4] += column_sum(grad_value)
        at = lambda other: pl.ds(pl.multiple_of((row ^ other) * rows, rows), rows)
        slot = near_ref.shape[1] - 1
        near_ref[0, slot] = grad_scratch[at(1)].astype(BF16)
        near_ref[1, slot] = grad_scratch[at(3)].astype(BF16)
        if joined:
            near_ref[:, 0] = before_ref[:, 0]
        cross_ref[0] = grad_scratch[at(2)].astype(BF16)
        own_ref[0] = grad_scratch[mine]


def attention_backward(
    head_size, first, base, place, stage, cotangent, grad_mixed, parameters, held, sums, after, before
):
    weights, mixed, inverse, _, normed, query, key, value = stage
    _, head_count, rows, keys = weights.shape
    count = 1
    groups = query.shape[1]
    model_width = groups * LANES
    heads = LANES // head_size
    pair_spec = pl.BlockSpec((1, heads, rows, keys), lambda m, g, *_: (m + first + base, g, 0, 0))
    elements = count * head_count * rows * keys
    operands = [
        place,
        weights,
        cotangent,
        grad_mixed,
        mixed,
        inverse,
        query,
        key,
        value,
        normed,
        *parameters,
    ]
    in_specs = [near_spec()] * (len(operands) - 1)
    aliases = {}
    start = len(operands)
    if sums is not None:
        aliases = {start: 0, start + 1: 4}
        operands += [held, sums]
        in_specs += [pl.BlockSpec(memory_space=pl.ANY), near_spec()]
    operands += list(after)
    in_specs += [pl.BlockSpec(memory_space=pl.ANY)] * len(after)
    joined = before is not None
    if joined:
        operands.append(before)
        in_specs.append(near_spec())
    out_shape = [
        shape_of(cotangent.shape, BF16),
        near((2, 1 + joined, rows, model_width), BF16),
        near((count, rows, model_width), BF16),
        near((count, rows, model_width), F32),
        near((8, model_width), F32),
        near((count, rows, model_width), BF16),
        near((count, keys, model_width), BF16),
        near((count, keys, model_width), BF16),
    ]
    out_specs = [
        pair_spec,
        near_spec(),
        near_spec(),
        near_spec(),
        near_spec(),
        near_spec(),
        near_spec(),
        near_spec(),
    ]
    return pl.pallas_call(
        functools.partial(
            backward_kernel, head_size, 4, first, base, len(operands) - start, sums is None, joined
        ),
        grid_spec=pltpu.PrefetchScalarGridSpec(
            num_scalar_prefetch=1,
            grid=(count, groups),
            in_specs=in_specs,
            out_specs=out_specs,
            scratch_shapes=[
                pltpu.VMEM((groups, rows, LANES), BF16),
                pltpu.VMEM((groups, keys, LANES), BF16),
                pltpu.VMEM((groups, keys, LANES), BF16),
                pltpu.VMEM((keys, model_width), F32),
            ],
        ),
        out_shape=out_shape,
        input_output_aliases=aliases,
        compiler_params=params(8),
        cost_estimate=pl.CostEstimate(
            flops=elements * 2 * 768, transcendentals=0, bytes_accessed=elements * 6
        ),
        name="attention_backward",
    )(*operands)


def weight_kernel(calls, stages, place_ref, *refs):
    hidden_refs = refs[:stages]
    grads = refs[stages : stages + 3 * calls]
    out_refs = refs[stages + 3 * calls : -1]
    total_ref = refs[-1]
    rows = grads[0].shape[1]
    row = place_ref[1]
    core = place_ref[2]
    mine = pl.ds(pl.multiple_of(row * rows, rows), rows)
    hidden = [(ref, m) for ref in hidden_refs for m in range(ref.shape[0])]
    width = hidden_refs[0].shape[2]
    own = jnp.concatenate([ref[m, mine] for ref, m in hidden], 0)
    every = jnp.concatenate([ref[m] for ref, m in hidden], 0)
    own = jnp.transpose(own.astype(F32)).astype(BF16)
    every = jnp.transpose(every.astype(F32)).astype(BF16)
    for j, left in enumerate((own, every, every)):
        right = jnp.concatenate([grads[3 * c + j][...].reshape(-1, width) for c in range(calls)], 0)
        total_ref[...] = dot(left, right).reshape(total_ref.shape)
        send_ref, keep_ref = out_refs[2 * j : 2 * j + 2]
        send_ref[:, 0] = total_ref[:, 1 - core].astype(BF16)
        keep_ref[:, 0] = total_ref[:, core].astype(BF16)


def swap(value, axis, mask):
    size = lax.axis_size(axis)
    return lax.ppermute(value, axis, [(i, i ^ mask) for i in range(size)])


VECTOR_ROWS = 8


def first_sum_kernel(counts, place_ref, *refs):
    terms = sum(counts)
    mine_ref, other_ref = refs[terms : terms + 2]
    along_x_ref, along_y_ref, keep_x_ref, keep_y_ref, vectors_ref = refs[terms + 2 :]
    x, y = place_ref[3], place_ref[4]
    half = along_x_ref.shape[1]
    size = keep_x_ref.shape[1]
    low, high = slice(0, half), slice(half, None)
    row = 0
    start = 0
    for count in counts:
        group = refs[start : start + count]
        start += count
        for s in range(group[0].shape[1]):
            rows = group[0].shape[2]

            def total(at, lanes):
                values = [r[at, s, :, lanes].astype(F32) for r in group]
                return functools.reduce(lambda a, b: a + b, values)

            for k in range(2):
                to = slice(k * size + row, k * size + row + rows)
                here = slice(row, row + rows)
                along_x_ref[to] = total(2 * k + (1 - x), low).astype(BF16)
                keep_x_ref[k, here] = total(2 * k + x, low)
                along_y_ref[to] = total(2 * (1 - y) + k, high).astype(BF16)
                keep_y_ref[k, here] = total(2 * y + k, high)
            row += rows
    vectors = (mine_ref[...] + other_ref[...]).astype(BF16)
    vectors_ref[...] = vectors
    put_vectors(vectors, along_x_ref, along_y_ref)


def put_vectors(vectors, low_ref, high_ref):
    half = vectors.shape[1] // 2
    low_ref[low_ref.shape[0] - VECTOR_ROWS :] = vectors[:, :half]
    high_ref[high_ref.shape[0] - VECTOR_ROWS :] = vectors[:, half:]


def get_vectors(low_ref, high_ref):
    low = low_ref[low_ref.shape[0] - VECTOR_ROWS :]
    return jnp.concatenate([low, high_ref[high_ref.shape[0] - VECTOR_ROWS :]], 1).astype(F32)


def second_sum_kernel(
    place_ref,
    keep_x_ref,
    came_x_ref,
    keep_y_ref,
    came_y_ref,
    vectors_ref,
    send_y_ref,
    send_x_ref,
    left_x_ref,
    left_y_ref,
    vectors_out_ref,
):
    size = keep_x_ref.shape[1]
    for keep, came, send, left, me in (
        (keep_x_ref, came_x_ref, send_y_ref, left_x_ref, place_ref[4]),
        (keep_y_ref, came_y_ref, send_x_ref, left_y_ref, place_ref[3]),
    ):
        at = lambda i: pl.ds(pl.multiple_of(i * size, size), size)
        send[:size] = (keep[1 - me] + came[at(1 - me)].astype(F32)).astype(BF16)
        left[...] = keep[me] + came[at(me)].astype(F32)
    vectors = vectors_ref[...].astype(F32) + get_vectors(came_x_ref, came_y_ref)
    vectors = vectors.astype(BF16)
    vectors_out_ref[...] = vectors
    put_vectors(vectors, send_y_ref, send_x_ref)


def third_sum_kernel(left_x_ref, came_x_ref, left_y_ref, came_y_ref, vectors_ref, total_ref):
    size, half = left_x_ref.shape
    total_ref[:size, :half] = (left_x_ref[...] + came_x_ref[:size].astype(F32)).astype(BF16)
    total_ref[:size, half:] = (left_y_ref[...] + came_y_ref[:size].astype(F32)).astype(BF16)
    vectors = vectors_ref[...].astype(F32) + get_vectors(came_x_ref, came_y_ref)
    total_ref[size : size + VECTOR_ROWS] = vectors.astype(BF16)


def third_cut_kernel(place_ref, left_x_ref, came_x_ref, left_y_ref, came_y_ref, vectors_ref, *refs):
    more_ref, total_ref, sent_ref = refs
    third_sum_kernel(left_x_ref, came_x_ref, left_y_ref, came_y_ref, vectors_ref, total_ref)
    filled = left_x_ref.shape[0] + VECTOR_ROWS
    if filled < total_ref.shape[0]:
        total_ref[filled:] = jnp.zeros((total_ref.shape[0] - filled, total_ref.shape[1]), BF16)
    half = total_ref.shape[0] // 2
    rows = more_ref.shape[2]
    away = pl.multiple_of((1 - (place_ref[1] & 1)) * half, half)
    sent_ref[:half] = total_ref[pl.ds(away, half)]
    for i in range(2):
        sent_ref[half + i * rows : half + (i + 1) * rows] = more_ref[i, 0]


def near_sum_kernel(place_ref, total_ref, came_ref, second_ref, out_ref):
    half = total_ref.shape[0] // 2
    rows = second_ref.shape[1]
    mine = total_ref[pl.ds(pl.multiple_of((place_ref[1] & 1) * half, half), half)]
    out_ref[:half] = (mine.astype(F32) + came_ref[:half].astype(F32)).astype(BF16)
    second = second_ref[0].astype(F32) + came_ref[half + rows : half + 2 * rows].astype(F32)
    out_ref[half : half + rows] = second.astype(BF16)


def far_sum_kernel(left_ref, right_ref, out_ref):
    at = slice(0, out_ref.shape[0])
    out_ref[...] = (left_ref[at].astype(F32) + right_ref[at].astype(F32)).astype(BF16)


def add_kernel(left_ref, right_ref, out_ref):
    out_ref[...] = (left_ref[...].astype(F32) + right_ref[...].astype(F32)).astype(out_ref.dtype)


def join_rows(place, mine_ref, other_ref, out_ref):
    part = mine_ref.shape[0]
    out_ref[pl.ds(pl.multiple_of(place * part, part), part)] = mine_ref[...]
    out_ref[pl.ds(pl.multiple_of((1 - place) * part, part), part)] = other_ref[...]


def finish_kernel(ratio, place_ref, low_ref, came_ref, mine_ref, other_ref, *refs):
    query_ref, key_ref, value_ref, outer_ref, inner_ref, out_ref = refs[:6]
    tail_refs, dense_refs, wide_ref, total_scratch, row_scratch = refs[6:10], refs[10:14], *refs[14:]
    rows, width = out_ref.shape
    total = lambda at: low_ref[at].astype(F32) + came_ref[at].astype(F32)
    for s, ref in enumerate((query_ref, key_ref, value_ref)):
        ref[...] = total(slice(s * rows, (s + 1) * rows))
    put_slices(total(slice(3 * rows, 3 * rows + VECTOR_ROWS)), place_ref[0], tail_refs)
    join_rows(place_ref[1] & 1, mine_ref, other_ref, total_scratch)
    outer_ref[...] = total_scratch[: ratio * rows].astype(F32)
    for s in range(ratio):
        at = (ratio + s) * rows
        inner_ref[:, s * width : (s + 1) * width] = total_scratch[at : at + rows].astype(F32)
    at = 2 * ratio * rows
    out_ref[...] = total_scratch[at : at + rows].astype(F32)
    vectors = total_scratch[at + rows : at + rows + VECTOR_ROWS].astype(F32)
    put_slices(vectors, place_ref[0], dense_refs)
    row_scratch[...] = vectors
    size = wide_ref.shape[0]
    start = place_ref[0] * size
    row = row_scratch[pl.ds(len(dense_refs) + start // width, 1)]
    wide_ref[...] = pltpu.roll(row, lax.rem(width - lax.rem(start, width), width), 1)[0, :size]


def put_slices(vectors, index, refs):
    width, size = vectors.shape[1], refs[0].shape[0]
    turned = pltpu.roll(vectors, lax.rem(width - index * size, width), 1)
    for i, ref in enumerate(refs):
        ref[...] = turned[i, :size]


def small_call(kernel, place, operands, out_shapes, name, after=(), inside=True, scratch=(), mib=4, size=None):
    ahead = 0 if place is None else 1
    count = len(operands)

    def body(*refs):
        kernel(*refs[: ahead + count], *refs[ahead + count + len(after) :])

    if size is None:
        size = sum(math.prod(a.shape) * a.dtype.itemsize for a in list(operands) + list(out_shapes))
    return pl.pallas_call(
        body,
        grid_spec=pltpu.PrefetchScalarGridSpec(
            num_scalar_prefetch=ahead,
            grid=(1,),
            in_specs=[near_spec() for a in operands] + [pl.BlockSpec(memory_space=pl.ANY)] * len(after),
            out_specs=[near_spec() for s in out_shapes],
            scratch_shapes=list(scratch),
        ),
        out_shape=[near(s.shape, s.dtype) if inside else s for s in out_shapes],
        compiler_params=params(mib),
        cost_estimate=pl.CostEstimate(flops=0, transcendentals=0, bytes_accessed=size),
        name=name,
    )(*(() if place is None else (place,)), *operands, *after)


def sum_core(place, groups, vectors, name, after=()):
    groups = [list(g) + [swap(a, "batch", 1) for a in sent] for g, sent in groups]
    vectors_other = swap(vectors, "batch", 1)
    _, _, rows, width = groups[0][0].shape
    size = sum(g[0].shape[1] for g in groups) * rows
    half = width // 2
    counts = tuple(len(g) for g in groups)
    message = shape_of((2 * size + VECTOR_ROWS, half), BF16)
    kept = shape_of((2, size, half), F32)
    along_x, along_y, keep_x, keep_y, vectors = small_call(
        functools.partial(first_sum_kernel, counts),
        place,
        [a for g in groups for a in g] + [vectors, vectors_other],
        [message, message, kept, kept, shape_of(vectors.shape, BF16)],
        name + "_sum_core",
        after,
    )
    came_x, came_y = swap(along_x, "batch", 2), swap(along_y, "batch", 4)
    return (keep_x, came_x, keep_y, came_y, vectors), along_x


def sum_first(place, pieces, name, after=()):
    keep_x, _, _, _, vectors = pieces
    _, size, half = keep_x.shape
    message = shape_of((size + VECTOR_ROWS, half), BF16)
    kept = shape_of((size, half), F32)
    send_y, send_x, left_x, left_y, vectors = small_call(
        second_sum_kernel,
        place,
        pieces,
        [message, message, kept, kept, shape_of(vectors.shape, BF16)],
        name + "_sum_first",
        after,
    )
    came_x, came_y = swap(send_y, "batch", 4), swap(send_x, "batch", 2)
    return (left_x, came_x, left_y, came_y, vectors), send_y


def sum_second(pieces, name, after=()):
    size, half = pieces[0].shape
    shape = shape_of((size + VECTOR_ROWS, 2 * half), BF16)
    return small_call(third_sum_kernel, None, pieces, [shape], name + "_sum_second", after)[0]


def sum_second_cut(place, pieces, more, name, after=()):
    size, half = pieces[0].shape
    rows = -(-(size + VECTOR_ROWS) // 32) * 32
    total, sent = small_call(
        third_cut_kernel,
        place,
        list(pieces) + [more],
        [
            shape_of((rows, 2 * half), BF16),
            shape_of((rows // 2 + 2 * more.shape[2], 2 * half), BF16),
        ],
        name + "_sum_second",
        after,
    )
    return total, swap(sent, "rows", 1)


def batch_slices_any(groups, vectors):
    me = lax.axis_index("batch")
    bits = lax.axis_size("batch").bit_length() - 1
    pieces = []
    for kept, sent in groups:
        values = [a.astype(F32) for a in kept] + [swap(a, "batch", 1).astype(F32) for a in sent]
        pieces.append(functools.reduce(lambda a, b: a + b, values))
    total = jnp.concatenate(pieces, 1)
    total = total.reshape((2,) * (bits - 1) + total.shape[1:])
    for bit in range(bits - 1, 0, -1):
        mine = (me >> bit) & 1
        sent = lax.dynamic_index_in_dim(total, 1 - mine, 0, keepdims=False).astype(BF16)
        total = lax.dynamic_index_in_dim(total, mine, 0, keepdims=False)
        total = total + swap(sent, "batch", 1 << bit).astype(F32)
    total = lax.psum(total.astype(BF16), "rows").astype(F32)
    return total, lax.psum(vectors, ("batch", "rows"))


def cross_kernel(count, *refs):
    out_ref = refs[-1]
    came = [(ref, i) for ref in refs[count:-1] for i in range(ref.shape[1])]
    for m, (term, (ref, i)) in enumerate(zip(refs[:count], came)):
        out_ref[m] = (term[0].astype(F32) + ref[1, i].astype(F32)).astype(BF16)


def cross_sum(terms, came, name, after=()):
    shape = (len(terms),) + terms[0].shape[1:]
    return small_call(
        functools.partial(cross_kernel, len(terms)),
        None,
        list(terms) + list(came),
        [shape_of(shape, BF16)],
        name,
        after,
    )[0]


def final_kernel(count, *refs):
    owns, nears, crosses = refs[:count], refs[count : 2 * count], refs[2 * count : 3 * count]
    atoms_ref, gain_ref, shift_ref, grad_middle_ref, out_ref = refs[3 * count :]
    gain = as_row(gain_ref)
    shift = as_row(shift_ref)
    for m in range(count):
        grad = owns[m][0] + nears[m][...].astype(F32) + crosses[m][...].astype(F32)
        _, normed, inverse = norm_forward(atoms_ref[m].astype(F32), gain, shift)
        result = grad_middle_ref[m] + norm_backward(grad, normed, inverse, gain)
        out_ref[m] = result.astype(BF16)


def first_norm_backward(owns, nears, crosses, others, after=()):
    count = len(owns)
    arrays = [a for a, _ in nears + crosses]
    spots = [at for _, at in nears + crosses]

    def kernel(*refs):
        picked = [r.at[at] for r, at in zip(refs[count : 3 * count], spots)]
        final_kernel(count, *refs[:count], *picked, *refs[3 * count :])

    return small_call(
        kernel,
        None,
        list(owns) + arrays + list(others),
        [shape_of(others[0].shape, BF16)],
        "first_norm_backward",
        after,
        inside=False,
    )[0]


def shards(
    atoms,
    pair_bias,
    lengths,
    first_gain,
    first_shift,
    query_weight,
    query_bias,
    key_weight,
    value_weight,
    value_bias,
    out_weight,
    out_bias,
    second_gain,
    second_shift,
    inner_weight,
    inner_bias,
    outer_weight,
    outer_bias,
    atoms_cotangent,
    pair_cotangent,
):
    molecules, rows, model_width = atoms.shape
    head_count = pair_bias.shape[1]
    head_size = model_width // head_count
    batch_count = lax.axis_size("batch")
    batch_index = lax.axis_index("batch")
    row = lax.axis_index("rows")
    (
        atoms_far,
        pair_bias,
        first_gain,
        first_shift,
        query_weight,
        query_bias,
        key_weight,
        value_weight,
        value_bias,
        out_weight,
        out_bias,
        second_gain,
        second_shift,
        inner_weight,
        inner_bias,
        outer_weight,
        outer_bias,
        atoms_cotangent,
        pair_cotangent,
    ) = [
        pltpu.with_memory_space_constraint(a, pltpu.HBM)
        for a in (
            atoms,
            pair_bias,
            first_gain,
            first_shift,
            query_weight,
            query_bias,
            key_weight,
            value_weight,
            value_bias,
            out_weight,
            out_bias,
            second_gain,
            second_shift,
            inner_weight,
            inner_bias,
            outer_weight,
            outer_bias,
            atoms_cotangent,
            pair_cotangent,
        )
    ]
    place = jnp.stack(
        [batch_index, row, batch_index & 1, (batch_index >> 1) & 1, (batch_index >> 2) & 1]
    ).astype(jnp.int32)
    line = lambda v: v
    count = molecules // STAGES
    stages = []
    pair_out = jnp.zeros((1,), BF16)
    one = swap(atoms, "rows", 1)
    (
        pair_near,
        query_near,
        key_near,
        value_near,
        first_gain,
        first_shift,
        query_bias,
        value_bias,
        out_bias,
        second_gain,
        second_shift,
        inner_bias,
        outer_bias,
    ) = load(
        [
            pair_bias,
            query_weight,
            key_weight,
            value_weight,
            first_gain,
            first_shift,
            query_bias,
            value_bias,
            out_bias,
            second_gain,
            second_shift,
            inner_bias,
            outer_bias,
        ],
        "load_first",
        None,
        (place,),
    )
    projected = near_half(
        head_size,
        STAGES,
        place,
        atoms_far,
        one,
        (
            first_gain,
            first_shift,
            query_near,
            query_bias,
            key_near,
            value_near,
            value_bias,
        ),
        (),
    )
    mine = [atoms[:count], projected[-1]]
    gathered = [[swap(a, "rows", mask) for mask in (2, 3)] for a in mine]
    for stage in range(STAGES):
        pair_out, kept, loaded = attention_forward(
            head_size,
            stage * count,
            place,
            lengths,
            gathered[stage],
            pair_near,
            (first_gain, first_shift, key_near, value_near, value_bias),
            projected[5 * stage : 5 * stage + 5],
            pair_out,
            [out_weight, inner_weight, outer_weight, atoms_cotangent] if stage else [],
        )
        stages.append(kept)
    out_weight, inner_weight, outer_weight, atoms_cotangent = loaded
    (
        atoms_out,
        outer_send,
        outer_keep,
        inner_send,
        inner_keep,
        out_send,
        out_keep,
        grad_middle,
        grad_mixed,
        dense_vectors,
        pair_cotangent,
    ) = dense(
        place,
        [s[1] for s in stages],
        atoms,
        atoms_cotangent,
        (
            out_weight,
            line(out_bias),
            line(second_gain),
            line(second_shift),
            inner_weight,
            line(inner_bias),
            outer_weight,
            line(outer_bias),
        ),
        batch_count,
        pair_cotangent,
    )
    pairs = batch_count // 2
    own_rows = model_width // batch_count
    slots = lambda a: a.reshape(pairs, -1, own_rows, model_width)
    dense_groups = [
        ([slots(outer_keep)], [slots(outer_send)]),
        ([inner_keep], [inner_send]),
        ([slots(out_keep)], [slots(out_send)]),
    ]
    usual = batch_count == 8

    def backward(molecule, held, sums, after, before=None):
        stage = molecule // count
        return attention_backward(
            head_size,
            stage * count,
            molecule % count,
            place,
            stages[stage],
            pair_cotangent,
            grad_mixed,
            (query_near, key_near, value_near),
            held,
            sums,
            after,
            before,
        )

    pair_grad, near0, cross0, own0, sums, *grads0 = backward(0, None, None, [])
    after = []
    if usual:
        dense_pieces, held = sum_core(place, dense_groups, dense_vectors, "dense", (own0,))
        after = [held]
    else:
        dense_total, dense_vectors = batch_slices_any(dense_groups, dense_vectors)
    pair_grad, near1, cross1, own1, sums, *grads1 = backward(1, pair_grad, sums, after, near0)
    near1 = swap(near1, "rows", 1)
    pair_grad, near2, cross2, own2, sums, *grads2 = backward(2, pair_grad, sums, [own1])
    near2 = swap(near2, "rows", 1)
    after = [own2]
    if usual:
        dense_pieces, held = sum_first(place, dense_pieces, "dense", after)
        after = [held]
    cross0 = cross_sum([cross0, cross1], [near1], "cross_first", after)
    far0 = swap(cross0, "rows", 2)
    pair_grad, near3, cross3, own3, tail_vectors, *grads3 = backward(3, pair_grad, sums, [cross0])
    owns = [own0, own1, own2, own3]
    after = [far0, near2]
    if usual:
        dense_total, came = sum_second_cut(place, dense_pieces, near3, "dense", (own3,))
        after.append(dense_total)
    cross2 = cross_sum([cross2], [near2], "cross_second", after[-1:])
    far2 = swap(cross2, "rows", 2)
    after = [far0, cross2]
    part = shape_of((pairs, 1, own_rows, model_width), BF16)
    parts = small_call(
        functools.partial(weight_kernel, 4, STAGES),
        place,
        [s[3] for s in stages] + grads0 + grads1 + grads2 + grads3,
        [part] * 6,
        "attention_weights",
        after,
        scratch=[pltpu.VMEM((pairs, 2, own_rows, model_width), F32)],
        mib=14,
    )
    groups = [([parts[2 * i + 1]], [parts[2 * i]]) for i in range(3)]
    matrix = shape_of((own_rows, model_width), F32)
    ratio = inner_weight.shape[1] // model_width
    vector = shape_of((own_rows,), F32)
    finish = (atoms, line(first_gain), line(first_shift), grad_middle)
    if usual:
        pieces, _ = sum_core(place, groups, tail_vectors, "tail")
        pieces, held = sum_first(place, pieces, "tail")
        start = dense_total.shape[0] // 2
        first_rows = slice(start, start + rows)
        mine = small_call(
            near_sum_kernel,
            place,
            [dense_total, came, cross3],
            [shape_of((start + rows, model_width), BF16)],
            "dense_near_sum",
            (held, far2),
        )[0]
        far = swap(mine, "rows", 2)
        total = sum_second(pieces, "tail", (mine,))
        tail_came = swap(total, "rows", 1)
        total = small_call(add_kernel, None, [total, tail_came], [total], "tail_near_sum")[0]
        tail_came = swap(total, "rows", 2)
        part = shape_of((start, model_width), BF16)
        mine = small_call(far_sum_kernel, None, [mine, far], [part], "dense_far_sum", (total,))[0]
        other = swap(mine, "rows", 1)
        atoms_grad = first_norm_backward(
            owns,
            [(near1, (0, 0)), (near1, (0, 1)), (near2, (0, 0)), (came, first_rows)],
            [(far0, 0), (far0, 1), (far2, 0), (far, first_rows)],
            finish,
            (mine,),
        )
        outs = small_call(
            functools.partial(finish_kernel, ratio),
            place,
            [total, tail_came, mine, other],
            [matrix] * 3
            + [
                shape_of((ratio * own_rows, model_width), F32),
                shape_of((own_rows, ratio * model_width), F32),
                matrix,
            ]
            + [vector] * 8
            + [shape_of((ratio * own_rows,), F32)],
            "finish",
            inside=False,
            scratch=[
                pltpu.VMEM((2 * part.shape[0], model_width), BF16),
                pltpu.VMEM((VECTOR_ROWS, model_width), F32),
            ],
        )
        query_grad, key_grad, value_grad, outer_grad, inner_grad, out_grad = outs[:6]
        tail_parts, dense_parts = outs[6:10], outs[10:]
    else:
        near3 = swap(near3, "rows", 1)
        far3 = swap(cross_sum([cross3], [near3], "cross_third"), "rows", 2)
        atoms_grad = first_norm_backward(
            owns,
            [(near1, (0, 0)), (near1, (0, 1)), (near2, (0, 0)), (near3, (0, 0))],
            [(far0, 0), (far0, 1), (far2, 0), (far3, 0)],
            finish,
        )
        total, tail_vectors = batch_slices_any(groups, tail_vectors)
        query_grad, key_grad, value_grad = total[0], total[1], total[2]
        outer_grad = dense_total[:ratio].reshape(-1, model_width)
        inner_grad = dense_total[ratio : 2 * ratio].transpose(1, 0, 2).reshape(own_rows, -1)
        out_grad = dense_total[2 * ratio]
        part = lambda v: lax.dynamic_slice_in_dim(
            v, batch_index * (v.shape[0] // batch_count), v.shape[0] // batch_count
        )
        tail_parts = [part(v) for v in tail_vectors[:4]]
        dense_parts = [part(v) for v in dense_vectors[:4]] + [part(dense_vectors[4:].reshape(-1))]
    return (
        atoms_out,
        pair_out,
        atoms_grad,
        pair_grad,
        tail_parts[0],
        tail_parts[1],
        query_grad,
        tail_parts[2],
        key_grad,
        value_grad,
        tail_parts[3],
        out_grad,
        dense_parts[3],
        dense_parts[1],
        dense_parts[2],
        inner_grad,
        dense_parts[4],
        outer_grad,
        dense_parts[0],
    )


def solution(mesh):
    tokens = P("batch", "rows", None)
    pairs = P("batch", None, "rows", None)
    vector = P("batch")
    matrix = P("batch", None)
    return jax.shard_map(
        shards,
        mesh=mesh,
        in_specs=(tokens, pairs, P("batch")) + (P(),) * 15 + (tokens, pairs),
        out_specs=(
            tokens,
            pairs,
            tokens,
            pairs,
            vector,
            vector,
            matrix,
            vector,
            matrix,
            matrix,
            vector,
            matrix,
            vector,
            vector,
            vector,
            matrix,
            vector,
            matrix,
            vector,
        ),
        check_vma=False,
    )
```

```python
import functools
import math

import jax
import jax.numpy as jnp
from jax import lax
from jax.experimental import pallas as pl
from jax.experimental.pallas import tpu as pltpu
from jax.sharding import PartitionSpec as P

EPSILON = 1e-05
MASKED = -1000000000.0
F32 = jnp.float32
BF16 = jnp.bfloat16
LANES = 128
STAGES = 2
VMEM_LIMIT = 18 << 20


def shape_of(shape, dtype):
    return jax.ShapeDtypeStruct(tuple(shape), dtype)


def norm_forward(values_in, gain, shift):
    centre = values_in - jnp.mean(values_in, -1, keepdims=True)
    inverse = lax.rsqrt(jnp.mean(centre * centre, -1, keepdims=True) + EPSILON)
    normed = centre * inverse
    return (normed * gain + shift, normed, inverse)


def norm_backward(upstream, normed, inverse, gain):
    scaled = upstream * gain
    return inverse * (
        scaled
        - jnp.mean(scaled, -1, keepdims=True)
        - normed * jnp.mean(scaled * normed, -1, keepdims=True)
    )


def dot(left, right):
    return jnp.dot(left, right, preferred_element_type=F32)


def across(left, right):
    return lax.dot_general(left, right, (((0,), (0,)), ((), ())), preferred_element_type=F32)


def against(left, right):
    return lax.dot_general(left, right, (((1,), (1,)), ((), ())), preferred_element_type=F32)


def column_sum(values_in):
    return jnp.sum(values_in.astype(F32), 0, keepdims=True)


def near(shape, dtype):
    return pltpu.VMEM(tuple(shape), dtype)


def near_spec():
    return pl.BlockSpec(memory_space=pltpu.VMEM)


def as_row(ref):
    return ref[...].astype(F32).reshape(1, -1)


def whole(array):
    return pl.BlockSpec(array.shape, lambda *_: (0,) * array.ndim)


def params(mib=10):
    return pltpu.CompilerParams(vmem_limit_bytes=mib << 20)


def load_kernel(count, starts, *refs):
    sources, targets, semaphores = refs[:count], refs[-count - 1 : -1], refs[-1]
    copies = [
        pltpu.make_async_copy(source.at[pl.ds(start, target.shape[0])], target, semaphores.at[i])
        for i, (source, target, start) in enumerate(zip(sources, targets, starts))
    ]
    for copy in copies:
        copy.start()
    for copy in copies:
        copy.wait()


def copies_beside(sources, targets, semaphores):
    return [
        pltpu.make_async_copy(source, target, semaphores.at[i])
        for i, (source, target) in enumerate(zip(sources, targets))
    ]


def load(arrays, name, starts=None, after=()):
    count = len(arrays)
    starts = starts or (0,) * count
    return pl.pallas_call(
        functools.partial(load_kernel, count, starts),
        in_specs=[pl.BlockSpec(memory_space=pltpu.HBM)] * count
        + [pl.BlockSpec(memory_space=pl.ANY)] * len(after),
        out_specs=[near_spec()] * count,
        out_shape=[
            near((a.shape[0] - start,) + a.shape[1:], a.dtype) for a, start in zip(arrays, starts)
        ],
        scratch_shapes=[pltpu.SemaphoreType.DMA((count,))],
        compiler_params=params(),
        name=name,
    )(*arrays, *after)


def project(pieces, first, parameters, row, refs, atoms_scratch):
    gain_ref, shift_ref, key_weight_ref, value_weight_ref, value_bias_ref = parameters
    hidden_ref, normed_ref, key_ref, value_ref = refs
    count = hidden_ref.shape[0]
    _, groups, keys, width = key_ref.shape
    rows = keys // 4
    half = 2 * rows
    model_width = hidden_ref.shape[2]
    for m in range(count):
        for i, piece in enumerate(pieces):
            start = pl.multiple_of(m * half + ((row ^ i) & 1) * rows, rows)
            atoms_scratch[pl.ds(start, rows)] = piece[m + first]
    hidden, normed, _ = norm_forward(
        atoms_scratch[...].astype(F32), as_row(gain_ref), as_row(shift_ref)
    )
    hidden = hidden.astype(BF16)
    normed = normed.astype(BF16)
    key_rows = dot(hidden, key_weight_ref[...]).astype(BF16)
    value_rows = (dot(hidden, value_weight_ref[...]) + as_row(value_bias_ref)).astype(BF16)
    return [a.reshape(count, half, model_width) for a in (hidden, normed, key_rows, value_rows)]


def put_half(values, at, refs):
    hidden, normed, key_rows, value_rows = values
    hidden_ref, normed_ref, key_ref, value_ref = refs
    count, groups, _, width = key_ref.shape
    half = hidden.shape[1]
    ones = jnp.ones((count, half, width), BF16)
    hidden_ref[:, at] = hidden
    normed_ref[:, at] = normed
    for t in range(groups):
        lanes = slice(t * width, (t + 1) * width)
        key_ref[:, t, at] = key_rows[:, :, lanes]
        value_ref[:, t, at, :width] = value_rows[:, :, lanes]
        value_ref[:, t, at, width:] = ones


def half_rows(row, other, rows):
    which = row >> 1
    which = 1 - which if other else which
    return pl.ds(pl.multiple_of(which * 2 * rows, 2 * rows), 2 * rows)


def near_half_kernel(
    head_size,
    stages,
    ahead,
    place_ref,
    own_ref,
    one_ref,
    gain_ref,
    shift_ref,
    query_weight_ref,
    query_bias_ref,
    key_weight_ref,
    value_weight_ref,
    value_bias_ref,
    *refs,
):
    refs = refs[ahead:]
    later_ref, atoms_scratch = refs[-2:]
    later_ref[...] = own_ref[own_ref.shape[0] - later_ref.shape[0] :]
    row = place_ref[1]
    rows, model_width = own_ref.shape[1:]
    factor = head_size**-0.5
    parameters = (gain_ref, shift_ref, key_weight_ref, value_weight_ref, value_bias_ref)
    for stage in range(stages):
        hidden_ref, normed_ref, key_ref, value_ref, query_ref = refs[5 * stage : 5 * stage + 5]
        outs = (hidden_ref, normed_ref, key_ref, value_ref)
        count, groups, _, width = key_ref.shape
        values = project((own_ref, one_ref), stage * count, parameters, row, outs, atoms_scratch)
        put_half(values, half_rows(row, False, rows), outs)
        mine = pl.ds(pl.multiple_of(row * rows, rows), rows)
        own = jnp.concatenate([hidden_ref[m, mine] for m in range(count)], 0)
        query_rows = (dot(own, query_weight_ref[...]) + as_row(query_bias_ref)) * factor
        query_rows = query_rows.astype(BF16).reshape(count, rows, model_width)
        for t in range(groups):
            query_ref[:, t] = query_rows[:, :, t * width : (t + 1) * width]


def near_half(head_size, stages, place, atoms, one, parameters, after):
    molecules, rows, model_width = atoms.shape
    keys = 4 * rows
    count = molecules // stages
    groups = model_width // LANES
    operands = (place, atoms, one, *parameters, *after)
    return pl.pallas_call(
        functools.partial(near_half_kernel, head_size, stages, len(after)),
        grid_spec=pltpu.PrefetchScalarGridSpec(
            num_scalar_prefetch=1,
            grid=(1,),
            in_specs=[whole(atoms), near_spec()]
            + [near_spec() for a in parameters]
            + [pl.BlockSpec(memory_space=pl.ANY)] * len(after),
            out_specs=[near_spec()] * (5 * stages + 1),
            scratch_shapes=[pltpu.VMEM((count * 2 * rows, model_width), BF16)],
        ),
        out_shape=[
            near((count, keys, model_width), BF16),
            near((count, keys, model_width), BF16),
            near((count, groups, keys, LANES), BF16),
            near((count, groups, keys, 2 * LANES), BF16),
            near((count, groups, rows, LANES), BF16),
        ]
        * stages
        + [near((molecules - count, rows, model_width), BF16)],
        compiler_params=params(10),
        name="near_half",
    )(*operands)


def forward_kernel(
    head_size,
    chunk,
    first,
    extra,
    place_ref,
    length_ref,
    two_ref,
    three_ref,
    pair_ref,
    query_ref,
    gain_ref,
    shift_ref,
    key_weight_ref,
    value_weight_ref,
    value_bias_ref,
    *refs,
):
    (
        pair_out_ref,
        weights_ref,
        mixed_ref,
        inverse_ref,
        hidden_ref,
        normed_ref,
        key_ref,
        value_ref,
    ) = refs[5 + extra : 13 + extra]
    atoms_scratch, semaphores = refs[-2:]
    copies = copies_beside(refs[5 : 5 + extra], refs[13 + extra : 13 + 2 * extra], semaphores)
    molecule = pl.program_id(0)
    group = pl.program_id(1)
    count, groups, keys, width = key_ref.shape
    heads = width // head_size
    rows = query_ref.shape[2]

    @pl.when((molecule == 0) & (group == 0))
    def _():
        for copy in copies:
            copy.start()
        row = place_ref[1]
        outs = (hidden_ref, normed_ref, key_ref, value_ref)
        parameters = (gain_ref, shift_ref, key_weight_ref, value_weight_ref, value_bias_ref)
        values = project((two_ref, three_ref), 0, parameters, row, outs, atoms_scratch)
        put_half(values, half_rows(row, True, rows), outs)

    query = query_ref[molecule, group]
    key = key_ref[molecule, group]
    value = value_ref[molecule, group]
    valid = lax.broadcasted_iota(jnp.int32, (1, keys), 1) < length_ref[molecule + first]
    lane = lax.broadcasted_iota(jnp.int32, (1, width), 1) // head_size
    lane_pair = lax.broadcasted_iota(jnp.int32, (1, 2 * width), 1) % width // head_size
    total = jnp.zeros((rows, 2 * width), F32)
    zero = jnp.zeros((), BF16)
    for c in range(0, heads, chunk):
        here = slice(c, c + chunk)
        there = pl.ds(group * heads + c, chunk)
        spread = jnp.concatenate([jnp.where(lane == c + t, query, zero) for t in range(chunk)], 0)
        pair = pair_ref[molecule + first, there].reshape(chunk * rows, keys)
        scores = against(spread, key) + pair.astype(F32)
        pair_out_ref[0, here] = scores.astype(BF16).reshape(chunk, rows, keys)
        masked = jnp.where(valid, scores, MASKED)
        weights = jnp.exp(masked - jnp.max(masked, -1, keepdims=True)).astype(BF16)
        weights_ref[molecule, there] = weights.reshape(chunk, rows, keys)
        product = dot(weights, value)
        for t in range(chunk):
            total = jnp.where(lane_pair == c + t, product[t * rows : (t + 1) * rows], total)
    inverse = 1.0 / total[:, width:]
    inverse_ref[molecule, group] = inverse
    mixed_ref[molecule, group] = total[:, :width] * inverse

    @pl.when((molecule == count - 1) & (group == groups - 1))
    def _():
        for copy in copies:
            copy.wait()


def attention_forward(
    head_size, first, place, lengths, pieces, pair_bias, parameters, projected, held, extra
):
    _, head_count, rows, keys = pair_bias.shape
    hidden, normed, key, value, query = projected
    count, groups = key.shape[:2]
    model_width = groups * LANES
    heads = LANES // head_size
    pair_spec = pl.BlockSpec((1, heads, rows, keys), lambda m, g, *_: (m + first, g, 0, 0))
    elements = count * head_count * rows * keys
    operands = [place, lengths, *pieces, pair_bias, query, *parameters]
    in_specs = [near_spec()] * (len(pieces) + 2)
    in_specs += [near_spec() for a in parameters]
    start = len(operands)
    operands += [hidden, normed, key, value, held]
    in_specs += [near_spec()] * 4 + [pl.BlockSpec(memory_space=pl.ANY)]
    aliases = {start + i: 4 + i for i in range(4)}
    if held.ndim > 1:
        aliases[start + 4] = 0
    operands += extra
    in_specs += [pl.BlockSpec(memory_space=pltpu.HBM)] * len(extra)
    outs = pl.pallas_call(
        functools.partial(forward_kernel, head_size, 8, first, len(extra)),
        grid_spec=pltpu.PrefetchScalarGridSpec(
            num_scalar_prefetch=2,
            grid=(count, groups),
            in_specs=in_specs,
            out_specs=[pair_spec] + [near_spec()] * (7 + len(extra)),
            scratch_shapes=[
                pltpu.VMEM((count * 2 * rows, model_width), BF16),
                pltpu.SemaphoreType.DMA((max(len(extra), 1),)),
            ],
        ),
        out_shape=[
            shape_of(pair_bias.shape, BF16),
            near((count, head_count, rows, keys), BF16),
            near((count, groups, rows, LANES), F32),
            near((count, groups, rows, LANES), F32),
            near(hidden.shape, BF16),
            near(normed.shape, BF16),
            near(key.shape, BF16),
            near(value.shape, BF16),
        ]
        + [near(a.shape, a.dtype) for a in extra],
        input_output_aliases=aliases,
        compiler_params=params(10),
        cost_estimate=pl.CostEstimate(
            flops=elements * 2 * 384, transcendentals=elements, bytes_accessed=elements * 6
        ),
        name="attention_forward",
    )(*operands)
    pair_out, weights, mixed, inverse, hidden, normed, key, value = outs[:8]
    return pair_out, (weights, mixed, inverse, hidden, normed, query, key, value), outs[8:]


def dense_kernel(
    mixed_count,
    place_ref,
    *refs,
):
    mixed_refs = refs[:mixed_count]
    (
        atoms_ref,
        cotangent_ref,
        out_weight_ref,
        out_bias_ref,
        gain_ref,
        shift_ref,
        inner_weight_ref,
        inner_bias_ref,
        outer_weight_ref,
        outer_bias_ref,
        far_ref,
        atoms_out_ref,
        send_ref,
        keep_ref,
        grad_middle_ref,
        grad_mixed_ref,
        vectors_ref,
        copied_ref,
        hidden_scratch,
        turned_scratch,
        normed_scratch,
        inverse_scratch,
        result_scratch,
        upstream_scratch,
        outer_scratch,
        inner_scratch,
        semaphores,
    ) = refs[mixed_count:]
    (copy,) = copies_beside([far_ref], [copied_ref], semaphores)
    step = pl.program_id(0)
    steps = pl.num_programs(0)
    core = place_ref[2]
    tokens, model_width = hidden_scratch.shape
    cotangent = cotangent_ref[...].reshape(tokens, model_width)

    def mixed_rows():
        parts = []
        for ref in mixed_refs:
            count, groups, rows, width = ref.shape
            join = [ref[:, t].reshape(count * rows, width) for t in range(groups)]
            parts.append(jnp.concatenate(join, 1))
        return jnp.concatenate(parts, 0)

    @pl.when(step == 0)
    def _():
        copy.start()
        mixed_low = mixed_rows().astype(BF16)
        middle = (
            atoms_ref[...].reshape(tokens, model_width).astype(F32)
            + dot(mixed_low, out_weight_ref[...])
            + as_row(out_bias_ref)
        )
        hidden, normed, inverse = norm_forward(
            middle, as_row(gain_ref), as_row(shift_ref)
        )
        hidden_scratch[...] = hidden.astype(BF16)
        turned_scratch[...] = jnp.transpose(hidden).astype(BF16)
        normed_scratch[...] = normed
        inverse_scratch[...] = inverse
        result_scratch[...] = middle + as_row(outer_bias_ref)
        upstream_scratch[...] = jnp.zeros_like(upstream_scratch)
        vectors_ref[0:1] = column_sum(cotangent)

    hidden = hidden_scratch[...]
    width = outer_weight_ref.shape[1]
    at = pl.ds(pl.multiple_of(step * width, width), width)
    inner_weight = inner_weight_ref[:, at]
    outer_weight = outer_weight_ref[at]
    pre = dot(hidden, inner_weight) + inner_bias_ref[at].astype(F32).reshape(1, -1)
    slope = math.sqrt(2.0 / math.pi)
    square = pre * pre
    tanh = jnp.tanh(slope * (pre + 0.044715 * (pre * square)))
    half = 0.5 * (1.0 + tanh)
    active = (pre * half).astype(BF16)
    result_scratch[...] += dot(active, outer_weight)
    derivative = half + (0.5 * slope) * pre * (1.0 - tanh * tanh) * (1.0 + 0.134145 * square)
    grad_pre = against(cotangent, outer_weight) * derivative
    vectors_ref[pl.ds(4 + step, 1)] = column_sum(grad_pre.astype(BF16))
    grad_pre = grad_pre.astype(BF16)
    outer_scratch[...] = across(active, cotangent).reshape(outer_scratch.shape)
    ratio = send_ref.shape[1] // 2
    outer_pairs = outer_scratch.shape[0]
    outer_shape = (outer_pairs, ratio) + send_ref.shape[2:]
    outer_at = (pl.ds(step * outer_pairs, outer_pairs), slice(0, ratio))
    send_ref[outer_at] = outer_scratch[:, 1 - core].reshape(outer_shape).astype(BF16)
    keep_ref[outer_at] = outer_scratch[:, core].reshape(outer_shape).astype(BF16)
    inner_scratch[...] = dot(turned_scratch[...], grad_pre).reshape(inner_scratch.shape)
    send_ref[:, ratio + step] = inner_scratch[:, 1 - core].astype(BF16)
    keep_ref[:, ratio + step] = inner_scratch[:, core].astype(BF16)
    upstream_scratch[...] += against(grad_pre, inner_weight)

    @pl.when(step == steps - 1)
    def _():
        atoms_out_ref[...] = result_scratch[...].astype(BF16).reshape(atoms_out_ref.shape)
        upstream = upstream_scratch[...]
        normed = normed_scratch[...]
        vectors_ref[1:2] = column_sum(upstream * normed)
        vectors_ref[2:3] = column_sum(upstream)
        grad_middle = cotangent.astype(F32) + norm_backward(
            upstream, normed, inverse_scratch[...], as_row(gain_ref)
        )
        grad_middle_ref[...] = grad_middle.reshape(grad_middle_ref.shape)
        branch = grad_middle.astype(BF16)
        vectors_ref[3:4] = column_sum(branch)
        grad_mixed = against(branch, out_weight_ref[...]).astype(BF16)
        molecules, groups, rows, lanes = grad_mixed_ref.shape
        grad_mixed = grad_mixed.reshape(molecules, rows, model_width)
        for t in range(groups):
            grad_mixed_ref[:, t] = grad_mixed[:, :, t * lanes : (t + 1) * lanes]
        turned = jnp.transpose(mixed_rows()).astype(BF16)
        inner_scratch[...] = dot(turned, branch).reshape(inner_scratch.shape)
        send_ref[:, 2 * ratio] = inner_scratch[:, 1 - core].astype(BF16)
        keep_ref[:, 2 * ratio] = inner_scratch[:, core].astype(BF16)
        copy.wait()


def dense(place, mixed, atoms, cotangent, parameters, batch_count, extra):
    (
        out_weight,
        out_bias,
        gain,
        shift,
        inner_weight,
        inner_bias,
        outer_weight,
        outer_bias,
    ) = parameters
    model_width, inner_width = inner_weight.shape
    tokens = atoms.shape[0] * atoms.shape[1]
    width = model_width
    steps = inner_width // width
    pairs = batch_count // 2
    outer_rows = inner_width // batch_count
    outer_pairs = width // (2 * outer_rows)
    own_rows = model_width // batch_count
    operands = (
        place,
        *mixed,
        atoms,
        cotangent,
        out_weight,
        out_bias,
        gain,
        shift,
        inner_weight,
        inner_bias,
        outer_weight,
        outer_bias,
        extra,
    )
    part = near((pairs, 2 * steps + 1, own_rows, model_width), BF16)
    out_shapes = [
        shape_of(atoms.shape, BF16),
        part,
        part,
        near(atoms.shape, F32),
        near((atoms.shape[0], model_width // LANES, atoms.shape[1], LANES), BF16),
        shape_of((4 + steps, model_width), F32),
        near(extra.shape, extra.dtype),
    ]
    fixed = lambda s: pl.BlockSpec(s.shape, lambda *_: (0,) * len(s.shape))
    out_specs = [fixed(s) for s in out_shapes]
    out_specs[1:5] = [near_spec()] * 4
    out_specs[6] = near_spec()
    in_specs = [whole(a) for a in operands[1:]]
    for i, a in enumerate(operands[1:]):
        if i != len(mixed):
            in_specs[i] = near_spec()
    in_specs[-1] = pl.BlockSpec(memory_space=pltpu.HBM)
    return pl.pallas_call(
        functools.partial(dense_kernel, len(mixed)),
        grid_spec=pltpu.PrefetchScalarGridSpec(
            num_scalar_prefetch=1,
            grid=(steps,),
            in_specs=in_specs,
            out_specs=out_specs,
            scratch_shapes=[
                pltpu.VMEM((tokens, model_width), BF16),
                pltpu.VMEM((model_width, tokens), BF16),
                pltpu.VMEM((tokens, model_width), F32),
                pltpu.VMEM((tokens, 1), F32),
                pltpu.VMEM((tokens, model_width), F32),
                pltpu.VMEM((tokens, model_width), F32),
                pltpu.VMEM((outer_pairs, 2, outer_rows, model_width), F32),
                pltpu.VMEM((pairs, 2, own_rows, width), F32),
                pltpu.SemaphoreType.DMA((1,)),
            ],
        ),
        out_shape=out_shapes,
        compiler_params=params(14),
        cost_estimate=pl.CostEstimate(
            flops=12 * tokens * model_width * inner_width,
            transcendentals=tokens * inner_width,
            bytes_accessed=12 * model_width * inner_width,
        ),
        name="dense",
    )(*operands)


def backward_kernel(
    head_size,
    chunk,
    first,
    base,
    start,
    fresh,
    joined,
    place_ref,
    weights_ref,
    cotangent_ref,
    grad_mixed_ref,
    mixed_ref,
    inverse_ref,
    query_ref,
    key_ref,
    value_ref,
    normed_ref,
    query_weight_ref,
    key_weight_ref,
    value_weight_ref,
    *refs,
):
    before_ref = refs[start - 1] if joined else None
    refs = refs[start:]
    pair_grad_ref, near_ref, cross_ref, own_ref, vectors_ref = refs[:5]
    query_grad_ref, key_grad_ref, value_grad_ref = refs[5:8]
    grad_query_scratch, grad_key_scratch, grad_value_scratch, grad_scratch = refs[-4:]
    molecule = pl.program_id(0) + base
    group = pl.program_id(1)
    _, groups, rows, width = query_ref.shape
    keys = key_ref.shape[2]
    heads = width // head_size
    factor = head_size**-0.5
    query = query_ref[molecule, group]
    key = key_ref[molecule, group]
    value = value_ref[molecule, group]
    upstream = grad_mixed_ref[molecule + first, group].astype(F32) * inverse_ref[molecule, group]
    upstream = upstream.astype(BF16)
    offset = (-(upstream.astype(F32) * mixed_ref[molecule, group])).astype(BF16)
    both = jnp.concatenate([upstream, offset], 1)
    lane = lax.broadcasted_iota(jnp.int32, (1, width), 1) // head_size
    lane_pair = lax.broadcasted_iota(jnp.int32, (1, 2 * width), 1) % width // head_size
    query_turned = jnp.transpose(query.astype(F32)).astype(BF16)
    upstream_turned = jnp.transpose(upstream.astype(F32)).astype(BF16)
    query_turned = jnp.concatenate([query_turned] * chunk, 1)
    upstream_turned = jnp.concatenate([upstream_turned] * chunk, 1)
    turned_shape = (chunk * head_size, chunk * rows)
    same = (
        lax.broadcasted_iota(jnp.int32, turned_shape, 0) // head_size
        == lax.broadcasted_iota(jnp.int32, turned_shape, 1) // rows
    )
    zero = jnp.zeros((), BF16)
    total = jnp.zeros((rows, width), F32)
    key_parts = []
    value_parts = []
    for c in range(0, heads, chunk):
        here = slice(c, c + chunk)
        feature = slice(c * head_size, (c + chunk) * head_size)
        spread = jnp.concatenate([jnp.where(lane_pair == c + t, both, zero) for t in range(chunk)], 0)
        centred = against(spread, value)
        there = pl.ds(group * heads + c, chunk)
        weights = weights_ref[molecule, there].reshape(chunk * rows, keys)
        cotangent = cotangent_ref[molecule + first, there].reshape(chunk * rows, keys)
        grad = (weights.astype(F32) * centred + cotangent.astype(F32)).astype(BF16)
        pair_grad_ref[0, here] = grad.reshape(chunk, rows, keys)
        product = dot(grad, key)
        for t in range(chunk):
            total = jnp.where(lane == c + t, product[t * rows : (t + 1) * rows], total)
        key_parts.append(dot(jnp.where(same, query_turned[feature], zero), grad))
        value_parts.append(dot(jnp.where(same, upstream_turned[feature], zero), weights))
    grad_query_scratch[group] = (total * factor).astype(BF16)
    grad_key_scratch[group] = jnp.transpose(jnp.concatenate(key_parts, 0)).astype(BF16)
    grad_value_scratch[group] = jnp.transpose(jnp.concatenate(value_parts, 0)).astype(BF16)

    if fresh:

        @pl.when((pl.program_id(0) == 0) & (group == 0))
        def _():
            vectors_ref[...] = jnp.zeros_like(vectors_ref)

    @pl.when(group == groups - 1)
    def _():
        row = place_ref[1]
        mine = pl.ds(pl.multiple_of(row * rows, rows), rows)
        join = lambda ref: jnp.concatenate([ref[t] for t in range(groups)], 1)
        grad_query = join(grad_query_scratch)
        grad_key = join(grad_key_scratch)
        grad_value = join(grad_value_scratch)
        query_grad_ref[0] = grad_query
        key_grad_ref[0] = grad_key
        value_grad_ref[0] = grad_value
        grad_scratch[...] = against(grad_key, key_weight_ref[...]) + against(
            grad_value, value_weight_ref[...]
        )
        grad_scratch[mine] += against(grad_query, query_weight_ref[...])
        grad = grad_scratch[...]
        vectors_ref[0:1] += column_sum(grad * normed_ref[molecule].astype(F32))
        vectors_ref[1:2] += column_sum(grad)
        vectors_ref[2:3] += column_sum(grad_query)
        vectors_ref[3:4] += column_sum(grad_value)
        at = lambda other: pl.ds(pl.multiple_of((row ^ other) * rows, rows), rows)
        slot = near_ref.shape[1] - 1
        near_ref[0, slot] = grad_scratch[at(1)].astype(BF16)
        near_ref[1, slot] = grad_scratch[at(3)].astype(BF16)
        if joined:
            near_ref[:, 0] = before_ref[:, 0]
        cross_ref[0] = grad_scratch[at(2)].astype(BF16)
        own_ref[0] = grad_scratch[mine]


def attention_backward(
    head_size, first, base, place, stage, cotangent, grad_mixed, parameters, held, sums, after, before
):
    weights, mixed, inverse, _, normed, query, key, value = stage
    _, head_count, rows, keys = weights.shape
    count = 1
    groups = query.shape[1]
    model_width = groups * LANES
    heads = LANES // head_size
    pair_spec = pl.BlockSpec((1, heads, rows, keys), lambda m, g, *_: (m + first + base, g, 0, 0))
    elements = count * head_count * rows * keys
    operands = [
        place,
        weights,
        cotangent,
        grad_mixed,
        mixed,
        inverse,
        query,
        key,
        value,
        normed,
        *parameters,
    ]
    in_specs = [near_spec()] * (len(operands) - 1)
    aliases = {}
    start = len(operands)
    if sums is not None:
        aliases = {start: 0, start + 1: 4}
        operands += [held, sums]
        in_specs += [pl.BlockSpec(memory_space=pl.ANY), near_spec()]
    operands += list(after)
    in_specs += [pl.BlockSpec(memory_space=pl.ANY)] * len(after)
    joined = before is not None
    if joined:
        operands.append(before)
        in_specs.append(near_spec())
    out_shape = [
        shape_of(cotangent.shape, BF16),
        near((2, 1 + joined, rows, model_width), BF16),
        near((count, rows, model_width), BF16),
        near((count, rows, model_width), F32),
        near((8, model_width), F32),
        near((count, rows, model_width), BF16),
        near((count, keys, model_width), BF16),
        near((count, keys, model_width), BF16),
    ]
    out_specs = [
        pair_spec,
        near_spec(),
        near_spec(),
        near_spec(),
        near_spec(),
        near_spec(),
        near_spec(),
        near_spec(),
    ]
    return pl.pallas_call(
        functools.partial(
            backward_kernel, head_size, 4, first, base, len(operands) - start, sums is None, joined
        ),
        grid_spec=pltpu.PrefetchScalarGridSpec(
            num_scalar_prefetch=1,
            grid=(count, groups),
            in_specs=in_specs,
            out_specs=out_specs,
            scratch_shapes=[
                pltpu.VMEM((groups, rows, LANES), BF16),
                pltpu.VMEM((groups, keys, LANES), BF16),
                pltpu.VMEM((groups, keys, LANES), BF16),
                pltpu.VMEM((keys, model_width), F32),
            ],
        ),
        out_shape=out_shape,
        input_output_aliases=aliases,
        compiler_params=params(8),
        cost_estimate=pl.CostEstimate(
            flops=elements * 2 * 768, transcendentals=0, bytes_accessed=elements * 6
        ),
        name="attention_backward",
    )(*operands)


def weight_kernel(calls, stages, place_ref, *refs):
    hidden_refs = refs[:stages]
    grads = refs[stages : stages + 3 * calls]
    out_refs = refs[stages + 3 * calls : -1]
    total_ref = refs[-1]
    rows = grads[0].shape[1]
    row = place_ref[1]
    core = place_ref[2]
    mine = pl.ds(pl.multiple_of(row * rows, rows), rows)
    hidden = [(ref, m) for ref in hidden_refs for m in range(ref.shape[0])]
    width = hidden_refs[0].shape[2]
    own = jnp.concatenate([ref[m, mine] for ref, m in hidden], 0)
    every = jnp.concatenate([ref[m] for ref, m in hidden], 0)
    own = jnp.transpose(own.astype(F32)).astype(BF16)
    every = jnp.transpose(every.astype(F32)).astype(BF16)
    for j, left in enumerate((own, every, every)):
        right = jnp.concatenate([grads[3 * c + j][...].reshape(-1, width) for c in range(calls)], 0)
        total_ref[...] = dot(left, right).reshape(total_ref.shape)
        send_ref, keep_ref = out_refs
        send_ref[:, j] = total_ref[:, 1 - core].astype(BF16)
        keep_ref[:, j] = total_ref[:, core].astype(BF16)


def swap(value, axis, mask):
    size = lax.axis_size(axis)
    return lax.ppermute(value, axis, [(i, i ^ mask) for i in range(size)])


VECTOR_ROWS = 8


def first_sum_kernel(counts, place_ref, *refs):
    terms = sum(counts)
    mine_ref, other_ref = refs[terms : terms + 2]
    along_x_ref, along_y_ref, keep_x_ref, keep_y_ref, vectors_ref = refs[terms + 2 :]
    x, y = place_ref[3], place_ref[4]
    half = along_x_ref.shape[1]
    size = keep_x_ref.shape[1]
    low, high = slice(0, half), slice(half, None)
    row = 0
    start = 0
    for count in counts:
        group = refs[start : start + count]
        start += count
        for s in range(group[0].shape[1]):
            rows = group[0].shape[2]

            def total(at, lanes):
                values = [r[at, s, :, lanes].astype(F32) for r in group]
                return functools.reduce(lambda a, b: a + b, values)

            for k in range(2):
                to = slice(k * size + row, k * size + row + rows)
                here = slice(row, row + rows)
                along_x_ref[to] = total(2 * k + (1 - x), low).astype(BF16)
                keep_x_ref[k, here] = total(2 * k + x, low)
                along_y_ref[to] = total(2 * (1 - y) + k, high).astype(BF16)
                keep_y_ref[k, here] = total(2 * y + k, high)
            row += rows
    vectors = (mine_ref[...] + other_ref[...]).astype(BF16)
    vectors_ref[...] = vectors
    put_vectors(vectors, along_x_ref, along_y_ref)


def put_vectors(vectors, low_ref, high_ref):
    half = vectors.shape[1] // 2
    low_ref[low_ref.shape[0] - VECTOR_ROWS :] = vectors[:, :half]
    high_ref[high_ref.shape[0] - VECTOR_ROWS :] = vectors[:, half:]


def get_vectors(low_ref, high_ref):
    low = low_ref[low_ref.shape[0] - VECTOR_ROWS :]
    return jnp.concatenate([low, high_ref[high_ref.shape[0] - VECTOR_ROWS :]], 1).astype(F32)


def second_sum_kernel(
    place_ref,
    keep_x_ref,
    came_x_ref,
    keep_y_ref,
    came_y_ref,
    vectors_ref,
    send_y_ref,
    send_x_ref,
    left_x_ref,
    left_y_ref,
    vectors_out_ref,
):
    size = keep_x_ref.shape[1]
    for keep, came, send, left, me in (
        (keep_x_ref, came_x_ref, send_y_ref, left_x_ref, place_ref[4]),
        (keep_y_ref, came_y_ref, send_x_ref, left_y_ref, place_ref[3]),
    ):
        at = lambda i: pl.ds(pl.multiple_of(i * size, size), size)
        send[:size] = (keep[1 - me] + came[at(1 - me)].astype(F32)).astype(BF16)
        left[...] = keep[me] + came[at(me)].astype(F32)
    vectors = vectors_ref[...].astype(F32) + get_vectors(came_x_ref, came_y_ref)
    vectors = vectors.astype(BF16)
    vectors_out_ref[...] = vectors
    put_vectors(vectors, send_y_ref, send_x_ref)


def third_sum_kernel(left_x_ref, came_x_ref, left_y_ref, came_y_ref, vectors_ref, total_ref):
    size, half = left_x_ref.shape
    total_ref[:size, :half] = (left_x_ref[...] + came_x_ref[:size].astype(F32)).astype(BF16)
    total_ref[:size, half:] = (left_y_ref[...] + came_y_ref[:size].astype(F32)).astype(BF16)
    vectors = vectors_ref[...].astype(F32) + get_vectors(came_x_ref, came_y_ref)
    total_ref[size : size + VECTOR_ROWS] = vectors.astype(BF16)


def third_cut_kernel(place_ref, left_x_ref, came_x_ref, left_y_ref, came_y_ref, vectors_ref, *refs):
    more_ref, total_ref, sent_ref = refs
    third_sum_kernel(left_x_ref, came_x_ref, left_y_ref, came_y_ref, vectors_ref, total_ref)
    filled = left_x_ref.shape[0] + VECTOR_ROWS
    if filled < total_ref.shape[0]:
        total_ref[filled:] = jnp.zeros((total_ref.shape[0] - filled, total_ref.shape[1]), BF16)
    half = total_ref.shape[0] // 2
    rows = more_ref.shape[2]
    away = pl.multiple_of((1 - (place_ref[1] & 1)) * half, half)
    sent_ref[:half] = total_ref[pl.ds(away, half)]
    for i in range(2):
        sent_ref[half + i * rows : half + (i + 1) * rows] = more_ref[i, 0]


def near_sum_kernel(place_ref, total_ref, came_ref, second_ref, out_ref):
    half = total_ref.shape[0] // 2
    rows = second_ref.shape[1]
    mine = total_ref[pl.ds(pl.multiple_of((place_ref[1] & 1) * half, half), half)]
    out_ref[:half] = (mine.astype(F32) + came_ref[:half].astype(F32)).astype(BF16)
    second = second_ref[0].astype(F32) + came_ref[half + rows : half + 2 * rows].astype(F32)
    out_ref[half : half + rows] = second.astype(BF16)


def far_sum_kernel(left_ref, right_ref, out_ref):
    at = slice(0, out_ref.shape[0])
    out_ref[...] = (left_ref[at].astype(F32) + right_ref[at].astype(F32)).astype(BF16)


def add_kernel(left_ref, right_ref, out_ref):
    out_ref[...] = (left_ref[...].astype(F32) + right_ref[...].astype(F32)).astype(out_ref.dtype)


def join_rows(place, mine_ref, other_ref, out_ref):
    part = mine_ref.shape[0]
    out_ref[pl.ds(pl.multiple_of(place * part, part), part)] = mine_ref[...]
    out_ref[pl.ds(pl.multiple_of((1 - place) * part, part), part)] = other_ref[...]


def finish_kernel(ratio, place_ref, low_ref, came_ref, mine_ref, other_ref, *refs):
    query_ref, key_ref, value_ref, outer_ref, inner_ref, out_ref = refs[:6]
    tail_refs, dense_refs, wide_ref, total_scratch, row_scratch = refs[6:10], refs[10:14], *refs[14:]
    rows, width = out_ref.shape
    total = lambda at: low_ref[at].astype(F32) + came_ref[at].astype(F32)
    for s, ref in enumerate((query_ref, key_ref, value_ref)):
        ref[...] = total(slice(s * rows, (s + 1) * rows))
    put_slices(total(slice(3 * rows, 3 * rows + VECTOR_ROWS)), place_ref[0], tail_refs)
    join_rows(place_ref[1] & 1, mine_ref, other_ref, total_scratch)
    outer_ref[...] = total_scratch[: ratio * rows].astype(F32)
    for s in range(ratio):
        at = (ratio + s) * rows
        inner_ref[:, s * width : (s + 1) * width] = total_scratch[at : at + rows].astype(F32)
    at = 2 * ratio * rows
    out_ref[...] = total_scratch[at : at + rows].astype(F32)
    vectors = total_scratch[at + rows : at + rows + VECTOR_ROWS].astype(F32)
    put_slices(vectors, place_ref[0], dense_refs)
    row_scratch[...] = vectors
    size = wide_ref.shape[0]
    start = place_ref[0] * size
    row = row_scratch[pl.ds(len(dense_refs) + start // width, 1)]
    wide_ref[...] = pltpu.roll(row, lax.rem(width - lax.rem(start, width), width), 1)[0, :size]


def put_slices(vectors, index, refs):
    width, size = vectors.shape[1], refs[0].shape[0]
    turned = pltpu.roll(vectors, lax.rem(width - index * size, width), 1)
    for i, ref in enumerate(refs):
        ref[...] = turned[i, :size]


def small_call(kernel, place, operands, out_shapes, name, after=(), inside=True, scratch=(), mib=4, size=None):
    ahead = 0 if place is None else 1
    count = len(operands)

    def body(*refs):
        kernel(*refs[: ahead + count], *refs[ahead + count + len(after) :])

    if size is None:
        size = sum(math.prod(a.shape) * a.dtype.itemsize for a in list(operands) + list(out_shapes))
    return pl.pallas_call(
        body,
        grid_spec=pltpu.PrefetchScalarGridSpec(
            num_scalar_prefetch=ahead,
            grid=(1,),
            in_specs=[near_spec() for a in operands] + [pl.BlockSpec(memory_space=pl.ANY)] * len(after),
            out_specs=[near_spec() for s in out_shapes],
            scratch_shapes=list(scratch),
        ),
        out_shape=[near(s.shape, s.dtype) if inside else s for s in out_shapes],
        compiler_params=params(mib),
        cost_estimate=pl.CostEstimate(flops=0, transcendentals=0, bytes_accessed=size),
        name=name,
    )(*(() if place is None else (place,)), *operands, *after)


def sum_core(place, groups, vectors, name, after=()):
    groups = [list(g) + [swap(a, "batch", 1) for a in sent] for g, sent in groups]
    vectors_other = swap(vectors, "batch", 1)
    _, _, rows, width = groups[0][0].shape
    size = sum(g[0].shape[1] for g in groups) * rows
    half = width // 2
    counts = tuple(len(g) for g in groups)
    message = shape_of((2 * size + VECTOR_ROWS, half), BF16)
    kept = shape_of((2, size, half), F32)
    along_x, along_y, keep_x, keep_y, vectors = small_call(
        functools.partial(first_sum_kernel, counts),
        place,
        [a for g in groups for a in g] + [vectors, vectors_other],
        [message, message, kept, kept, shape_of(vectors.shape, BF16)],
        name + "_sum_core",
        after,
    )
    came_x, came_y = swap(along_x, "batch", 2), swap(along_y, "batch", 4)
    return (keep_x, came_x, keep_y, came_y, vectors), along_x


def sum_first(place, pieces, name, after=()):
    keep_x, _, _, _, vectors = pieces
    _, size, half = keep_x.shape
    message = shape_of((size + VECTOR_ROWS, half), BF16)
    kept = shape_of((size, half), F32)
    send_y, send_x, left_x, left_y, vectors = small_call(
        second_sum_kernel,
        place,
        pieces,
        [message, message, kept, kept, shape_of(vectors.shape, BF16)],
        name + "_sum_first",
        after,
    )
    came_x, came_y = swap(send_y, "batch", 4), swap(send_x, "batch", 2)
    return (left_x, came_x, left_y, came_y, vectors), send_y


def sum_second(pieces, name, after=()):
    size, half = pieces[0].shape
    shape = shape_of((size + VECTOR_ROWS, 2 * half), BF16)
    return small_call(third_sum_kernel, None, pieces, [shape], name + "_sum_second", after)[0]


def sum_second_cut(place, pieces, more, name, after=()):
    size, half = pieces[0].shape
    rows = -(-(size + VECTOR_ROWS) // 32) * 32
    total, sent = small_call(
        third_cut_kernel,
        place,
        list(pieces) + [more],
        [
            shape_of((rows, 2 * half), BF16),
            shape_of((rows // 2 + 2 * more.shape[2], 2 * half), BF16),
        ],
        name + "_sum_second",
        after,
    )
    return total, swap(sent, "rows", 1)


def batch_slices_any(groups, vectors):
    me = lax.axis_index("batch")
    bits = lax.axis_size("batch").bit_length() - 1
    pieces = []
    for kept, sent in groups:
        values = [a.astype(F32) for a in kept] + [swap(a, "batch", 1).astype(F32) for a in sent]
        pieces.append(functools.reduce(lambda a, b: a + b, values))
    total = jnp.concatenate(pieces, 1)
    total = total.reshape((2,) * (bits - 1) + total.shape[1:])
    for bit in range(bits - 1, 0, -1):
        mine = (me >> bit) & 1
        sent = lax.dynamic_index_in_dim(total, 1 - mine, 0, keepdims=False).astype(BF16)
        total = lax.dynamic_index_in_dim(total, mine, 0, keepdims=False)
        total = total + swap(sent, "batch", 1 << bit).astype(F32)
    total = lax.psum(total.astype(BF16), "rows").astype(F32)
    return total, lax.psum(vectors, ("batch", "rows"))


def cross_kernel(count, *refs):
    out_ref = refs[-1]
    came = [(ref, i) for ref in refs[count:-1] for i in range(ref.shape[1])]
    for m, (term, (ref, i)) in enumerate(zip(refs[:count], came)):
        out_ref[m] = (term[0].astype(F32) + ref[1, i].astype(F32)).astype(BF16)


def cross_sum(terms, came, name, after=()):
    shape = (len(terms),) + terms[0].shape[1:]
    return small_call(
        functools.partial(cross_kernel, len(terms)),
        None,
        list(terms) + list(came),
        [shape_of(shape, BF16)],
        name,
        after,
    )[0]


def final_kernel(count, *refs):
    owns, nears, crosses = refs[:count], refs[count : 2 * count], refs[2 * count : 3 * count]
    atoms_ref, gain_ref, shift_ref, grad_middle_ref, out_ref = refs[3 * count :]
    gain = as_row(gain_ref)
    shift = as_row(shift_ref)
    for m in range(count):
        grad = owns[m][0] + nears[m][...].astype(F32) + crosses[m][...].astype(F32)
        _, normed, inverse = norm_forward(atoms_ref[m].astype(F32), gain, shift)
        result = grad_middle_ref[m] + norm_backward(grad, normed, inverse, gain)
        out_ref[m] = result.astype(BF16)


def first_norm_backward(owns, nears, crosses, others, after=()):
    count = len(owns)
    arrays = [a for a, _ in nears + crosses]
    spots = [at for _, at in nears + crosses]

    def kernel(*refs):
        picked = [r.at[at] for r, at in zip(refs[count : 3 * count], spots)]
        final_kernel(count, *refs[:count], *picked, *refs[3 * count :])

    return small_call(
        kernel,
        None,
        list(owns) + arrays + list(others),
        [shape_of(others[0].shape, BF16)],
        "first_norm_backward",
        after,
        inside=False,
    )[0]


def shards(
    atoms,
    pair_bias,
    lengths,
    first_gain,
    first_shift,
    query_weight,
    query_bias,
    key_weight,
    value_weight,
    value_bias,
    out_weight,
    out_bias,
    second_gain,
    second_shift,
    inner_weight,
    inner_bias,
    outer_weight,
    outer_bias,
    atoms_cotangent,
    pair_cotangent,
):
    molecules, rows, model_width = atoms.shape
    head_count = pair_bias.shape[1]
    head_size = model_width // head_count
    batch_count = lax.axis_size("batch")
    batch_index = lax.axis_index("batch")
    row = lax.axis_index("rows")
    (
        atoms_far,
        pair_bias,
        first_gain,
        first_shift,
        query_weight,
        query_bias,
        key_weight,
        value_weight,
        value_bias,
        out_weight,
        out_bias,
        second_gain,
        second_shift,
        inner_weight,
        inner_bias,
        outer_weight,
        outer_bias,
        atoms_cotangent,
        pair_cotangent,
    ) = [
        pltpu.with_memory_space_constraint(a, pltpu.HBM)
        for a in (
            atoms,
            pair_bias,
            first_gain,
            first_shift,
            query_weight,
            query_bias,
            key_weight,
            value_weight,
            value_bias,
            out_weight,
            out_bias,
            second_gain,
            second_shift,
            inner_weight,
            inner_bias,
            outer_weight,
            outer_bias,
            atoms_cotangent,
            pair_cotangent,
        )
    ]
    place = jnp.stack(
        [batch_index, row, batch_index & 1, (batch_index >> 1) & 1, (batch_index >> 2) & 1]
    ).astype(jnp.int32)
    line = lambda v: v
    count = molecules // STAGES
    stages = []
    pair_out = jnp.zeros((1,), BF16)
    one = swap(atoms, "rows", 1)
    (
        pair_near,
        query_near,
        key_near,
        value_near,
        first_gain,
        first_shift,
        query_bias,
        value_bias,
        out_bias,
        second_gain,
        second_shift,
        inner_bias,
        outer_bias,
        out_weight,
        inner_weight,
        outer_weight,
        atoms_cotangent,
    ) = load(
        [
            pair_bias,
            query_weight,
            key_weight,
            value_weight,
            first_gain,
            first_shift,
            query_bias,
            value_bias,
            out_bias,
            second_gain,
            second_shift,
            inner_bias,
            outer_bias,
            out_weight,
            inner_weight,
            outer_weight,
            atoms_cotangent,
        ],
        "load_first",
        None,
        (place,),
    )
    projected = near_half(
        head_size,
        STAGES,
        place,
        atoms_far,
        one,
        (
            first_gain,
            first_shift,
            query_near,
            query_bias,
            key_near,
            value_near,
            value_bias,
        ),
        (),
    )
    mine = [atoms[:count], projected[-1]]
    gathered = [[swap(a, "rows", mask) for mask in (2, 3)] for a in mine]
    for stage in range(STAGES):
        pair_out, kept, _ = attention_forward(
            head_size,
            stage * count,
            place,
            lengths,
            gathered[stage],
            pair_near,
            (first_gain, first_shift, key_near, value_near, value_bias),
            projected[5 * stage : 5 * stage + 5],
            pair_out,
            [],
        )
        stages.append(kept)
    (
        atoms_out,
        send,
        keep,
        grad_middle,
        grad_mixed,
        dense_vectors,
        pair_cotangent,
    ) = dense(
        place,
        [s[1] for s in stages],
        atoms,
        atoms_cotangent,
        (
            out_weight,
            line(out_bias),
            line(second_gain),
            line(second_shift),
            inner_weight,
            line(inner_bias),
            outer_weight,
            line(outer_bias),
        ),
        batch_count,
        pair_cotangent,
    )
    pairs = batch_count // 2
    own_rows = model_width // batch_count
    dense_groups = [([keep], [send])]
    usual = batch_count == 8

    def backward(molecule, held, sums, after, before=None):
        stage = molecule // count
        return attention_backward(
            head_size,
            stage * count,
            molecule % count,
            place,
            stages[stage],
            pair_cotangent,
            grad_mixed,
            (query_near, key_near, value_near),
            held,
            sums,
            after,
            before,
        )

    pair_grad, near0, cross0, own0, sums, *grads0 = backward(0, None, None, [])
    after = []
    if usual:
        dense_pieces, held = sum_core(place, dense_groups, dense_vectors, "dense", (own0,))
        after = [held]
    else:
        dense_total, dense_vectors = batch_slices_any(dense_groups, dense_vectors)
    pair_grad, near1, cross1, own1, sums, *grads1 = backward(1, pair_grad, sums, after, near0)
    near1 = swap(near1, "rows", 1)
    pair_grad, near2, cross2, own2, sums, *grads2 = backward(2, pair_grad, sums, [own1])
    near2 = swap(near2, "rows", 1)
    after = [own2]
    if usual:
        dense_pieces, held = sum_first(place, dense_pieces, "dense", after)
        after = [held]
    cross0 = cross_sum([cross0, cross1], [near1], "cross_first", after)
    far0 = swap(cross0, "rows", 2)
    pair_grad, near3, cross3, own3, tail_vectors, *grads3 = backward(3, pair_grad, sums, [cross0])
    owns = [own0, own1, own2, own3]
    after = [far0, near2]
    if usual:
        dense_total, came = sum_second_cut(place, dense_pieces, near3, "dense", (own3,))
        after.append(dense_total)
    cross2 = cross_sum([cross2], [near2], "cross_second", after[-1:])
    far2 = swap(cross2, "rows", 2)
    after = [far0, cross2]
    part = shape_of((pairs, 3, own_rows, model_width), BF16)
    send, keep = small_call(
        functools.partial(weight_kernel, 4, STAGES),
        place,
        [s[3] for s in stages] + grads0 + grads1 + grads2 + grads3,
        [part] * 2,
        "attention_weights",
        after,
        scratch=[pltpu.VMEM((pairs, 2, own_rows, model_width), F32)],
        mib=14,
    )
    groups = [([keep], [send])]
    matrix = shape_of((own_rows, model_width), F32)
    ratio = inner_weight.shape[1] // model_width
    vector = shape_of((own_rows,), F32)
    finish = (atoms, line(first_gain), line(first_shift), grad_middle)
    if usual:
        pieces, _ = sum_core(place, groups, tail_vectors, "tail")
        pieces, held = sum_first(place, pieces, "tail")
        start = dense_total.shape[0] // 2
        first_rows = slice(start, start + rows)
        mine = small_call(
            near_sum_kernel,
            place,
            [dense_total, came, cross3],
            [shape_of((start + rows, model_width), BF16)],
            "dense_near_sum",
            (held, far2),
        )[0]
        far = swap(mine, "rows", 2)
        total = sum_second(pieces, "tail", (mine,))
        tail_came = swap(total, "rows", 1)
        total = small_call(add_kernel, None, [total, tail_came], [total], "tail_near_sum")[0]
        tail_came = swap(total, "rows", 2)
        part = shape_of((start, model_width), BF16)
        mine = small_call(far_sum_kernel, None, [mine, far], [part], "dense_far_sum", (total,))[0]
        other = swap(mine, "rows", 1)
        atoms_grad = first_norm_backward(
            owns,
            [(near1, (0, 0)), (near1, (0, 1)), (near2, (0, 0)), (came, first_rows)],
            [(far0, 0), (far0, 1), (far2, 0), (far, first_rows)],
            finish,
            (mine,),
        )
        outs = small_call(
            functools.partial(finish_kernel, ratio),
            place,
            [total, tail_came, mine, other],
            [matrix] * 3
            + [
                shape_of((ratio * own_rows, model_width), F32),
                shape_of((own_rows, ratio * model_width), F32),
                matrix,
            ]
            + [vector] * 8
            + [shape_of((ratio * own_rows,), F32)],
            "finish",
            inside=False,
            scratch=[
                pltpu.VMEM((2 * part.shape[0], model_width), BF16),
                pltpu.VMEM((VECTOR_ROWS, model_width), F32),
            ],
        )
        query_grad, key_grad, value_grad, outer_grad, inner_grad, out_grad = outs[:6]
        tail_parts, dense_parts = outs[6:10], outs[10:]
    else:
        near3 = swap(near3, "rows", 1)
        far3 = swap(cross_sum([cross3], [near3], "cross_third"), "rows", 2)
        atoms_grad = first_norm_backward(
            owns,
            [(near1, (0, 0)), (near1, (0, 1)), (near2, (0, 0)), (near3, (0, 0))],
            [(far0, 0), (far0, 1), (far2, 0), (far3, 0)],
            finish,
        )
        total, tail_vectors = batch_slices_any(groups, tail_vectors)
        query_grad, key_grad, value_grad = total[0], total[1], total[2]
        outer_grad = dense_total[:ratio].reshape(-1, model_width)
        inner_grad = dense_total[ratio : 2 * ratio].transpose(1, 0, 2).reshape(own_rows, -1)
        out_grad = dense_total[2 * ratio]
        part = lambda v: lax.dynamic_slice_in_dim(
            v, batch_index * (v.shape[0] // batch_count), v.shape[0] // batch_count
        )
        tail_parts = [part(v) for v in tail_vectors[:4]]
        dense_parts = [part(v) for v in dense_vectors[:4]] + [part(dense_vectors[4:].reshape(-1))]
    return (
        atoms_out,
        pair_out,
        atoms_grad,
        pair_grad,
        tail_parts[0],
        tail_parts[1],
        query_grad,
        tail_parts[2],
        key_grad,
        value_grad,
        tail_parts[3],
        out_grad,
        dense_parts[3],
        dense_parts[1],
        dense_parts[2],
        inner_grad,
        dense_parts[4],
        outer_grad,
        dense_parts[0],
    )


def solution(mesh):
    tokens = P("batch", "rows", None)
    pairs = P("batch", None, "rows", None)
    vector = P("batch")
    matrix = P("batch", None)
    return jax.shard_map(
        shards,
        mesh=mesh,
        in_specs=(tokens, pairs, P("batch")) + (P(),) * 15 + (tokens, pairs),
        out_specs=(
            tokens,
            pairs,
            tokens,
            pairs,
            vector,
            vector,
            matrix,
            vector,
            matrix,
            matrix,
            vector,
            matrix,
            vector,
            vector,
            vector,
            matrix,
            vector,
            matrix,
            vector,
        ),
        check_vma=False,
    )
```

```python
import functools
import math

import jax
import jax.numpy as jnp
from jax import lax
from jax.experimental import pallas as pl
from jax.experimental.pallas import tpu as pltpu
from jax.sharding import PartitionSpec as P

EPSILON = 1e-05
MASKED = -1000000000.0
F32 = jnp.float32
BF16 = jnp.bfloat16
LANES = 128
STAGES = 2
VMEM_LIMIT = 18 << 20


def shape_of(shape, dtype):
    return jax.ShapeDtypeStruct(tuple(shape), dtype)


def norm_forward(values_in, gain, shift):
    centre = values_in - jnp.mean(values_in, -1, keepdims=True)
    inverse = lax.rsqrt(jnp.mean(centre * centre, -1, keepdims=True) + EPSILON)
    normed = centre * inverse
    return (normed * gain + shift, normed, inverse)


def norm_backward(upstream, normed, inverse, gain):
    scaled = upstream * gain
    return inverse * (
        scaled
        - jnp.mean(scaled, -1, keepdims=True)
        - normed * jnp.mean(scaled * normed, -1, keepdims=True)
    )


def dot(left, right):
    return jnp.dot(left, right, preferred_element_type=F32)


def across(left, right):
    return lax.dot_general(left, right, (((0,), (0,)), ((), ())), preferred_element_type=F32)


def against(left, right):
    return lax.dot_general(left, right, (((1,), (1,)), ((), ())), preferred_element_type=F32)


def column_sum(values_in):
    return jnp.sum(values_in.astype(F32), 0, keepdims=True)


def near(shape, dtype):
    return pltpu.VMEM(tuple(shape), dtype)


def near_spec():
    return pl.BlockSpec(memory_space=pltpu.VMEM)


def as_row(ref):
    return ref[...].astype(F32).reshape(1, -1)


def whole(array):
    return pl.BlockSpec(array.shape, lambda *_: (0,) * array.ndim)


def params(mib=10):
    return pltpu.CompilerParams(vmem_limit_bytes=mib << 20)


def load_kernel(count, starts, *refs):
    sources, targets, semaphores = refs[:count], refs[-count - 1 : -1], refs[-1]
    copies = [
        pltpu.make_async_copy(source.at[pl.ds(start, target.shape[0])], target, semaphores.at[i])
        for i, (source, target, start) in enumerate(zip(sources, targets, starts))
    ]
    for copy in copies:
        copy.start()
    for copy in copies:
        copy.wait()


def copies_beside(sources, targets, semaphores):
    return [
        pltpu.make_async_copy(source, target, semaphores.at[i])
        for i, (source, target) in enumerate(zip(sources, targets))
    ]


def load(arrays, name, starts=None, after=()):
    count = len(arrays)
    starts = starts or (0,) * count
    return pl.pallas_call(
        functools.partial(load_kernel, count, starts),
        in_specs=[pl.BlockSpec(memory_space=pltpu.HBM)] * count
        + [pl.BlockSpec(memory_space=pl.ANY)] * len(after),
        out_specs=[near_spec()] * count,
        out_shape=[
            near((a.shape[0] - start,) + a.shape[1:], a.dtype) for a, start in zip(arrays, starts)
        ],
        scratch_shapes=[pltpu.SemaphoreType.DMA((count,))],
        compiler_params=params(),
        name=name,
    )(*arrays, *after)


def project(pieces, first, parameters, row, refs, atoms_scratch):
    gain_ref, shift_ref, key_weight_ref, value_weight_ref, value_bias_ref = parameters
    hidden_ref, normed_ref, key_ref, value_ref = refs
    count = hidden_ref.shape[0]
    _, groups, keys, width = key_ref.shape
    rows = keys // 4
    half = 2 * rows
    model_width = hidden_ref.shape[2]
    for m in range(count):
        for i, piece in enumerate(pieces):
            start = pl.multiple_of(m * half + ((row ^ i) & 1) * rows, rows)
            atoms_scratch[pl.ds(start, rows)] = piece[m + first]
    hidden, normed, _ = norm_forward(
        atoms_scratch[...].astype(F32), as_row(gain_ref), as_row(shift_ref)
    )
    hidden = hidden.astype(BF16)
    normed = normed.astype(BF16)
    key_rows = dot(hidden, key_weight_ref[...]).astype(BF16)
    value_rows = (dot(hidden, value_weight_ref[...]) + as_row(value_bias_ref)).astype(BF16)
    return [a.reshape(count, half, model_width) for a in (hidden, normed, key_rows, value_rows)]


def put_half(values, at, refs):
    hidden, normed, key_rows, value_rows = values
    hidden_ref, normed_ref, key_ref, value_ref = refs
    count, groups, _, width = key_ref.shape
    half = hidden.shape[1]
    ones = jnp.ones((count, half, width), BF16)
    hidden_ref[:, at] = hidden
    normed_ref[:, at] = normed
    for t in range(groups):
        lanes = slice(t * width, (t + 1) * width)
        key_ref[:, t, at] = key_rows[:, :, lanes]
        value_ref[:, t, at, :width] = value_rows[:, :, lanes]
        value_ref[:, t, at, width:] = ones


def half_rows(row, other, rows):
    which = row >> 1
    which = 1 - which if other else which
    return pl.ds(pl.multiple_of(which * 2 * rows, 2 * rows), 2 * rows)


def near_half_kernel(
    head_size,
    stages,
    ahead,
    place_ref,
    own_ref,
    one_ref,
    gain_ref,
    shift_ref,
    query_weight_ref,
    query_bias_ref,
    key_weight_ref,
    value_weight_ref,
    value_bias_ref,
    *refs,
):
    refs = refs[ahead:]
    later_ref, atoms_scratch = refs[-2:]
    later_ref[...] = own_ref[own_ref.shape[0] - later_ref.shape[0] :]
    row = place_ref[1]
    rows, model_width = own_ref.shape[1:]
    factor = head_size**-0.5
    parameters = (gain_ref, shift_ref, key_weight_ref, value_weight_ref, value_bias_ref)
    for stage in range(stages):
        hidden_ref, normed_ref, key_ref, value_ref, query_ref = refs[5 * stage : 5 * stage + 5]
        outs = (hidden_ref, normed_ref, key_ref, value_ref)
        count, groups, _, width = key_ref.shape
        values = project((own_ref, one_ref), stage * count, parameters, row, outs, atoms_scratch)
        put_half(values, half_rows(row, False, rows), outs)
        mine = pl.ds(pl.multiple_of(row * rows, rows), rows)
        own = jnp.concatenate([hidden_ref[m, mine] for m in range(count)], 0)
        query_rows = (dot(own, query_weight_ref[...]) + as_row(query_bias_ref)) * factor
        query_rows = query_rows.astype(BF16).reshape(count, rows, model_width)
        for t in range(groups):
            query_ref[:, t] = query_rows[:, :, t * width : (t + 1) * width]


def near_half(head_size, stages, place, atoms, one, parameters, after):
    molecules, rows, model_width = atoms.shape
    keys = 4 * rows
    count = molecules // stages
    groups = model_width // LANES
    operands = (place, atoms, one, *parameters, *after)
    return pl.pallas_call(
        functools.partial(near_half_kernel, head_size, stages, len(after)),
        grid_spec=pltpu.PrefetchScalarGridSpec(
            num_scalar_prefetch=1,
            grid=(1,),
            in_specs=[whole(atoms), near_spec()]
            + [near_spec() for a in parameters]
            + [pl.BlockSpec(memory_space=pl.ANY)] * len(after),
            out_specs=[near_spec()] * (5 * stages + 1),
            scratch_shapes=[pltpu.VMEM((count * 2 * rows, model_width), BF16)],
        ),
        out_shape=[
            near((count, keys, model_width), BF16),
            near((count, keys, model_width), BF16),
            near((count, groups, keys, LANES), BF16),
            near((count, groups, keys, 2 * LANES), BF16),
            near((count, groups, rows, LANES), BF16),
        ]
        * stages
        + [near((molecules - count, rows, model_width), BF16)],
        compiler_params=params(10),
        name="near_half",
    )(*operands)


def forward_kernel(
    head_size,
    chunk,
    first,
    extra,
    place_ref,
    length_ref,
    two_ref,
    three_ref,
    pair_ref,
    query_ref,
    gain_ref,
    shift_ref,
    key_weight_ref,
    value_weight_ref,
    value_bias_ref,
    *refs,
):
    (
        pair_out_ref,
        weights_ref,
        mixed_ref,
        inverse_ref,
        hidden_ref,
        normed_ref,
        key_ref,
        value_ref,
    ) = refs[5 + extra : 13 + extra]
    atoms_scratch, semaphores = refs[-2:]
    copies = copies_beside(refs[5 : 5 + extra], refs[13 + extra : 13 + 2 * extra], semaphores)
    molecule = pl.program_id(0)
    group = pl.program_id(1)
    count, groups, keys, width = key_ref.shape
    heads = width // head_size
    rows = query_ref.shape[2]

    @pl.when((molecule == 0) & (group == 0))
    def _():
        for copy in copies:
            copy.start()
        row = place_ref[1]
        outs = (hidden_ref, normed_ref, key_ref, value_ref)
        parameters = (gain_ref, shift_ref, key_weight_ref, value_weight_ref, value_bias_ref)
        values = project((two_ref, three_ref), 0, parameters, row, outs, atoms_scratch)
        put_half(values, half_rows(row, True, rows), outs)

    query = query_ref[molecule, group]
    key = key_ref[molecule, group]
    value = value_ref[molecule, group]
    valid = lax.broadcasted_iota(jnp.int32, (1, keys), 1) < length_ref[molecule + first]
    lane = lax.broadcasted_iota(jnp.int32, (1, width), 1) // head_size
    lane_pair = lax.broadcasted_iota(jnp.int32, (1, 2 * width), 1) % width // head_size
    total = jnp.zeros((rows, 2 * width), F32)
    zero = jnp.zeros((), BF16)
    for c in range(0, heads, chunk):
        here = slice(c, c + chunk)
        there = pl.ds(group * heads + c, chunk)
        spread = jnp.concatenate([jnp.where(lane == c + t, query, zero) for t in range(chunk)], 0)
        pair = pair_ref[molecule + first, there].reshape(chunk * rows, keys)
        scores = against(spread, key) + pair.astype(F32)
        pair_out_ref[0, here] = scores.astype(BF16).reshape(chunk, rows, keys)
        masked = jnp.where(valid, scores, MASKED)
        weights = jnp.exp(masked - jnp.max(masked, -1, keepdims=True)).astype(BF16)
        weights_ref[molecule, there] = weights.reshape(chunk, rows, keys)
        product = dot(weights, value)
        for t in range(chunk):
            total = jnp.where(lane_pair == c + t, product[t * rows : (t + 1) * rows], total)
    inverse = 1.0 / total[:, width:]
    inverse_ref[molecule, group] = inverse
    mixed_ref[molecule, group] = total[:, :width] * inverse

    @pl.when((molecule == count - 1) & (group == groups - 1))
    def _():
        for copy in copies:
            copy.wait()


def attention_forward(
    head_size, first, place, lengths, pieces, pair_bias, parameters, projected, held, extra
):
    _, head_count, rows, keys = pair_bias.shape
    hidden, normed, key, value, query = projected
    count, groups = key.shape[:2]
    model_width = groups * LANES
    heads = LANES // head_size
    pair_spec = pl.BlockSpec((1, heads, rows, keys), lambda m, g, *_: (m + first, g, 0, 0))
    elements = count * head_count * rows * keys
    operands = [place, lengths, *pieces, pair_bias, query, *parameters]
    in_specs = [near_spec()] * (len(pieces) + 2)
    in_specs += [near_spec() for a in parameters]
    start = len(operands)
    operands += [hidden, normed, key, value, held]
    in_specs += [near_spec()] * 4 + [pl.BlockSpec(memory_space=pl.ANY)]
    aliases = {start + i: 4 + i for i in range(4)}
    if held.ndim > 1:
        aliases[start + 4] = 0
    operands += extra
    in_specs += [pl.BlockSpec(memory_space=pltpu.HBM)] * len(extra)
    outs = pl.pallas_call(
        functools.partial(forward_kernel, head_size, 4, first, len(extra)),
        grid_spec=pltpu.PrefetchScalarGridSpec(
            num_scalar_prefetch=2,
            grid=(count, groups),
            in_specs=in_specs,
            out_specs=[pair_spec] + [near_spec()] * (7 + len(extra)),
            scratch_shapes=[
                pltpu.VMEM((count * 2 * rows, model_width), BF16),
                pltpu.SemaphoreType.DMA((max(len(extra), 1),)),
            ],
        ),
        out_shape=[
            shape_of(pair_bias.shape, BF16),
            near((count, head_count, rows, keys), BF16),
            near((count, groups, rows, LANES), F32),
            near((count, groups, rows, LANES), F32),
            near(hidden.shape, BF16),
            near(normed.shape, BF16),
            near(key.shape, BF16),
            near(value.shape, BF16),
        ]
        + [near(a.shape, a.dtype) for a in extra],
        input_output_aliases=aliases,
        compiler_params=params(10),
        cost_estimate=pl.CostEstimate(
            flops=elements * 2 * 384, transcendentals=elements, bytes_accessed=elements * 6
        ),
        name="attention_forward",
    )(*operands)
    pair_out, weights, mixed, inverse, hidden, normed, key, value = outs[:8]
    return pair_out, (weights, mixed, inverse, hidden, normed, query, key, value), outs[8:]


def dense_kernel(
    mixed_count,
    place_ref,
    *refs,
):
    mixed_refs = refs[:mixed_count]
    (
        atoms_ref,
        cotangent_ref,
        out_weight_ref,
        out_bias_ref,
        gain_ref,
        shift_ref,
        inner_weight_ref,
        inner_bias_ref,
        outer_weight_ref,
        outer_bias_ref,
        far_ref,
        atoms_out_ref,
        send_ref,
        keep_ref,
        grad_middle_ref,
        grad_mixed_ref,
        vectors_ref,
        copied_ref,
        hidden_scratch,
        turned_scratch,
        normed_scratch,
        inverse_scratch,
        result_scratch,
        upstream_scratch,
        outer_scratch,
        inner_scratch,
        semaphores,
    ) = refs[mixed_count:]
    (copy,) = copies_beside([far_ref], [copied_ref], semaphores)
    step = pl.program_id(0)
    steps = pl.num_programs(0)
    core = place_ref[2]
    tokens, model_width = hidden_scratch.shape
    cotangent = cotangent_ref[...].reshape(tokens, model_width)

    def mixed_rows():
        parts = []
        for ref in mixed_refs:
            count, groups, rows, width = ref.shape
            join = [ref[:, t].reshape(count * rows, width) for t in range(groups)]
            parts.append(jnp.concatenate(join, 1))
        return jnp.concatenate(parts, 0)

    @pl.when(step == 0)
    def _():
        copy.start()
        mixed_low = mixed_rows().astype(BF16)
        middle = (
            atoms_ref[...].reshape(tokens, model_width).astype(F32)
            + dot(mixed_low, out_weight_ref[...])
            + as_row(out_bias_ref)
        )
        hidden, normed, inverse = norm_forward(
            middle, as_row(gain_ref), as_row(shift_ref)
        )
        hidden_scratch[...] = hidden.astype(BF16)
        turned_scratch[...] = jnp.transpose(hidden).astype(BF16)
        normed_scratch[...] = normed
        inverse_scratch[...] = inverse
        result_scratch[...] = middle + as_row(outer_bias_ref)
        upstream_scratch[...] = jnp.zeros_like(upstream_scratch)
        vectors_ref[0:1] = column_sum(cotangent)

    hidden = hidden_scratch[...]
    width = outer_weight_ref.shape[1]
    at = pl.ds(pl.multiple_of(step * width, width), width)
    inner_weight = inner_weight_ref[:, at]
    outer_weight = outer_weight_ref[at]
    pre = dot(hidden, inner_weight) + inner_bias_ref[at].astype(F32).reshape(1, -1)
    slope = math.sqrt(2.0 / math.pi)
    square = pre * pre
    tanh = jnp.tanh(slope * (pre + 0.044715 * (pre * square)))
    half = 0.5 * (1.0 + tanh)
    active = (pre * half).astype(BF16)
    result_scratch[...] += dot(active, outer_weight)
    derivative = half + (0.5 * slope) * pre * (1.0 - tanh * tanh) * (1.0 + 0.134145 * square)
    grad_pre = against(cotangent, outer_weight) * derivative
    vectors_ref[pl.ds(4 + step, 1)] = column_sum(grad_pre.astype(BF16))
    grad_pre = grad_pre.astype(BF16)
    outer_scratch[...] = across(active, cotangent).reshape(outer_scratch.shape)
    ratio = send_ref.shape[1] // 2
    outer_pairs = outer_scratch.shape[0]
    outer_shape = (outer_pairs, ratio) + send_ref.shape[2:]
    outer_at = (pl.ds(step * outer_pairs, outer_pairs), slice(0, ratio))
    send_ref[outer_at] = outer_scratch[:, 1 - core].reshape(outer_shape).astype(BF16)
    keep_ref[outer_at] = outer_scratch[:, core].reshape(outer_shape).astype(BF16)
    inner_scratch[...] = dot(turned_scratch[...], grad_pre).reshape(inner_scratch.shape)
    send_ref[:, ratio + step] = inner_scratch[:, 1 - core].astype(BF16)
    keep_ref[:, ratio + step] = inner_scratch[:, core].astype(BF16)
    upstream_scratch[...] += against(grad_pre, inner_weight)

    @pl.when(step == steps - 1)
    def _():
        atoms_out_ref[...] = result_scratch[...].astype(BF16).reshape(atoms_out_ref.shape)
        upstream = upstream_scratch[...]
        normed = normed_scratch[...]
        vectors_ref[1:2] = column_sum(upstream * normed)
        vectors_ref[2:3] = column_sum(upstream)
        grad_middle = cotangent.astype(F32) + norm_backward(
            upstream, normed, inverse_scratch[...], as_row(gain_ref)
        )
        grad_middle_ref[...] = grad_middle.reshape(grad_middle_ref.shape)
        branch = grad_middle.astype(BF16)
        vectors_ref[3:4] = column_sum(branch)
        grad_mixed = against(branch, out_weight_ref[...]).astype(BF16)
        molecules, groups, rows, lanes = grad_mixed_ref.shape
        grad_mixed = grad_mixed.reshape(molecules, rows, model_width)
        for t in range(groups):
            grad_mixed_ref[:, t] = grad_mixed[:, :, t * lanes : (t + 1) * lanes]
        turned = jnp.transpose(mixed_rows()).astype(BF16)
        inner_scratch[...] = dot(turned, branch).reshape(inner_scratch.shape)
        send_ref[:, 2 * ratio] = inner_scratch[:, 1 - core].astype(BF16)
        keep_ref[:, 2 * ratio] = inner_scratch[:, core].astype(BF16)
        copy.wait()


def dense(place, mixed, atoms, cotangent, parameters, batch_count, extra):
    (
        out_weight,
        out_bias,
        gain,
        shift,
        inner_weight,
        inner_bias,
        outer_weight,
        outer_bias,
    ) = parameters
    model_width, inner_width = inner_weight.shape
    tokens = atoms.shape[0] * atoms.shape[1]
    width = model_width
    steps = inner_width // width
    pairs = batch_count // 2
    outer_rows = inner_width // batch_count
    outer_pairs = width // (2 * outer_rows)
    own_rows = model_width // batch_count
    operands = (
        place,
        *mixed,
        atoms,
        cotangent,
        out_weight,
        out_bias,
        gain,
        shift,
        inner_weight,
        inner_bias,
        outer_weight,
        outer_bias,
        extra,
    )
    part = near((pairs, 2 * steps + 1, own_rows, model_width), BF16)
    out_shapes = [
        shape_of(atoms.shape, BF16),
        part,
        part,
        near(atoms.shape, F32),
        near((atoms.shape[0], model_width // LANES, atoms.shape[1], LANES), BF16),
        shape_of((4 + steps, model_width), F32),
        near(extra.shape, extra.dtype),
    ]
    fixed = lambda s: pl.BlockSpec(s.shape, lambda *_: (0,) * len(s.shape))
    out_specs = [fixed(s) for s in out_shapes]
    out_specs[1:5] = [near_spec()] * 4
    out_specs[6] = near_spec()
    in_specs = [whole(a) for a in operands[1:]]
    for i, a in enumerate(operands[1:]):
        if i != len(mixed):
            in_specs[i] = near_spec()
    in_specs[-1] = pl.BlockSpec(memory_space=pltpu.HBM)
    return pl.pallas_call(
        functools.partial(dense_kernel, len(mixed)),
        grid_spec=pltpu.PrefetchScalarGridSpec(
            num_scalar_prefetch=1,
            grid=(steps,),
            in_specs=in_specs,
            out_specs=out_specs,
            scratch_shapes=[
                pltpu.VMEM((tokens, model_width), BF16),
                pltpu.VMEM((model_width, tokens), BF16),
                pltpu.VMEM((tokens, model_width), F32),
                pltpu.VMEM((tokens, 1), F32),
                pltpu.VMEM((tokens, model_width), F32),
                pltpu.VMEM((tokens, model_width), F32),
                pltpu.VMEM((outer_pairs, 2, outer_rows, model_width), F32),
                pltpu.VMEM((pairs, 2, own_rows, width), F32),
                pltpu.SemaphoreType.DMA((1,)),
            ],
        ),
        out_shape=out_shapes,
        compiler_params=params(14),
        cost_estimate=pl.CostEstimate(
            flops=12 * tokens * model_width * inner_width,
            transcendentals=tokens * inner_width,
            bytes_accessed=12 * model_width * inner_width,
        ),
        name="dense",
    )(*operands)


def backward_kernel(
    head_size,
    chunk,
    first,
    base,
    start,
    fresh,
    joined,
    place_ref,
    weights_ref,
    cotangent_ref,
    grad_mixed_ref,
    mixed_ref,
    inverse_ref,
    query_ref,
    key_ref,
    value_ref,
    normed_ref,
    query_weight_ref,
    key_weight_ref,
    value_weight_ref,
    *refs,
):
    before_ref = refs[start - 1] if joined else None
    refs = refs[start:]
    pair_grad_ref, near_ref, cross_ref, own_ref, vectors_ref = refs[:5]
    query_grad_ref, key_grad_ref, value_grad_ref = refs[5:8]
    grad_query_scratch, grad_key_scratch, grad_value_scratch, grad_scratch = refs[-4:]
    molecule = pl.program_id(0) + base
    group = pl.program_id(1)
    _, groups, rows, width = query_ref.shape
    keys = key_ref.shape[2]
    heads = width // head_size
    factor = head_size**-0.5
    query = query_ref[molecule, group]
    key = key_ref[molecule, group]
    value = value_ref[molecule, group]
    upstream = grad_mixed_ref[molecule + first, group].astype(F32) * inverse_ref[molecule, group]
    upstream = upstream.astype(BF16)
    offset = (-(upstream.astype(F32) * mixed_ref[molecule, group])).astype(BF16)
    both = jnp.concatenate([upstream, offset], 1)
    lane = lax.broadcasted_iota(jnp.int32, (1, width), 1) // head_size
    lane_pair = lax.broadcasted_iota(jnp.int32, (1, 2 * width), 1) % width // head_size
    query_turned = jnp.transpose(query.astype(F32)).astype(BF16)
    upstream_turned = jnp.transpose(upstream.astype(F32)).astype(BF16)
    query_turned = jnp.concatenate([query_turned] * chunk, 1)
    upstream_turned = jnp.concatenate([upstream_turned] * chunk, 1)
    turned_shape = (chunk * head_size, chunk * rows)
    same = (
        lax.broadcasted_iota(jnp.int32, turned_shape, 0) // head_size
        == lax.broadcasted_iota(jnp.int32, turned_shape, 1) // rows
    )
    zero = jnp.zeros((), BF16)
    total = jnp.zeros((rows, width), F32)
    key_parts = []
    value_parts = []
    for c in range(0, heads, chunk):
        here = slice(c, c + chunk)
        feature = slice(c * head_size, (c + chunk) * head_size)
        spread = jnp.concatenate([jnp.where(lane_pair == c + t, both, zero) for t in range(chunk)], 0)
        centred = against(spread, value)
        there = pl.ds(group * heads + c, chunk)
        weights = weights_ref[molecule, there].reshape(chunk * rows, keys)
        cotangent = cotangent_ref[molecule + first, there].reshape(chunk * rows, keys)
        grad = (weights.astype(F32) * centred + cotangent.astype(F32)).astype(BF16)
        pair_grad_ref[molecule + first, there] = grad.reshape(chunk, rows, keys)
        product = dot(grad, key)
        for t in range(chunk):
            total = jnp.where(lane == c + t, product[t * rows : (t + 1) * rows], total)
        key_parts.append(dot(jnp.where(same, query_turned[feature], zero), grad))
        value_parts.append(dot(jnp.where(same, upstream_turned[feature], zero), weights))
    grad_query_scratch[group] = (total * factor).astype(BF16)
    grad_key_scratch[group] = jnp.transpose(jnp.concatenate(key_parts, 0)).astype(BF16)
    grad_value_scratch[group] = jnp.transpose(jnp.concatenate(value_parts, 0)).astype(BF16)

    if fresh:

        @pl.when((pl.program_id(0) == 0) & (group == 0))
        def _():
            vectors_ref[...] = jnp.zeros_like(vectors_ref)

    @pl.when(group == groups - 1)
    def _():
        row = place_ref[1]
        mine = pl.ds(pl.multiple_of(row * rows, rows), rows)
        join = lambda ref: jnp.concatenate([ref[t] for t in range(groups)], 1)
        grad_query = join(grad_query_scratch)
        grad_key = join(grad_key_scratch)
        grad_value = join(grad_value_scratch)
        query_grad_ref[0] = grad_query
        key_grad_ref[0] = grad_key
        value_grad_ref[0] = grad_value
        grad_scratch[...] = against(grad_key, key_weight_ref[...]) + against(
            grad_value, value_weight_ref[...]
        )
        grad_scratch[mine] += against(grad_query, query_weight_ref[...])
        grad = grad_scratch[...]
        vectors_ref[0:1] += column_sum(grad * normed_ref[molecule].astype(F32))
        vectors_ref[1:2] += column_sum(grad)
        vectors_ref[2:3] += column_sum(grad_query)
        vectors_ref[3:4] += column_sum(grad_value)
        at = lambda other: pl.ds(pl.multiple_of((row ^ other) * rows, rows), rows)
        slot = near_ref.shape[1] - 1
        near_ref[0, slot] = grad_scratch[at(1)].astype(BF16)
        near_ref[1, slot] = grad_scratch[at(3)].astype(BF16)
        if joined:
            near_ref[:, 0] = before_ref[:, 0]
        cross_ref[0] = grad_scratch[at(2)].astype(BF16)
        own_ref[0] = grad_scratch[mine]


def attention_backward(
    head_size, first, base, place, stage, cotangent, grad_mixed, parameters, held, sums, after, before
):
    weights, mixed, inverse, _, normed, query, key, value = stage
    _, head_count, rows, keys = weights.shape
    count = 1
    groups = query.shape[1]
    model_width = groups * LANES
    elements = count * head_count * rows * keys
    operands = [
        place,
        weights,
        cotangent,
        grad_mixed,
        mixed,
        inverse,
        query,
        key,
        value,
        normed,
        *parameters,
    ]
    in_specs = [near_spec()] * (len(operands) - 1)
    aliases = {}
    start = len(operands)
    if sums is not None:
        aliases = {start: 0, start + 1: 4}
        operands += [held, sums]
        in_specs += [near_spec(), near_spec()]
    operands += list(after)
    in_specs += [pl.BlockSpec(memory_space=pl.ANY)] * len(after)
    joined = before is not None
    if joined:
        operands.append(before)
        in_specs.append(near_spec())
    out_shape = [
        near(cotangent.shape, BF16),
        near((2, 1 + joined, rows, model_width), BF16),
        near((count, rows, model_width), BF16),
        near((count, rows, model_width), F32),
        near((8, model_width), F32),
        near((count, rows, model_width), BF16),
        near((count, keys, model_width), BF16),
        near((count, keys, model_width), BF16),
    ]
    out_specs = [
        near_spec(),
        near_spec(),
        near_spec(),
        near_spec(),
        near_spec(),
        near_spec(),
        near_spec(),
        near_spec(),
    ]
    return pl.pallas_call(
        functools.partial(
            backward_kernel, head_size, 4, first, base, len(operands) - start, sums is None, joined
        ),
        grid_spec=pltpu.PrefetchScalarGridSpec(
            num_scalar_prefetch=1,
            grid=(count, groups),
            in_specs=in_specs,
            out_specs=out_specs,
            scratch_shapes=[
                pltpu.VMEM((groups, rows, LANES), BF16),
                pltpu.VMEM((groups, keys, LANES), BF16),
                pltpu.VMEM((groups, keys, LANES), BF16),
                pltpu.VMEM((keys, model_width), F32),
            ],
        ),
        out_shape=out_shape,
        input_output_aliases=aliases,
        compiler_params=params(8),
        cost_estimate=pl.CostEstimate(
            flops=elements * 2 * 768, transcendentals=0, bytes_accessed=elements * 6
        ),
        name="attention_backward",
    )(*operands)


def weight_kernel(calls, stages, place_ref, *refs):
    hidden_refs = refs[:stages]
    grads = refs[stages : stages + 3 * calls]
    out_refs = refs[stages + 3 * calls : -1]
    total_ref = refs[-1]
    rows = grads[0].shape[1]
    row = place_ref[1]
    core = place_ref[2]
    mine = pl.ds(pl.multiple_of(row * rows, rows), rows)
    hidden = [(ref, m) for ref in hidden_refs for m in range(ref.shape[0])]
    width = hidden_refs[0].shape[2]
    own = jnp.concatenate([ref[m, mine] for ref, m in hidden], 0)
    every = jnp.concatenate([ref[m] for ref, m in hidden], 0)
    own = jnp.transpose(own.astype(F32)).astype(BF16)
    every = jnp.transpose(every.astype(F32)).astype(BF16)
    for j, left in enumerate((own, every, every)):
        right = jnp.concatenate([grads[3 * c + j][...].reshape(-1, width) for c in range(calls)], 0)
        total_ref[...] = dot(left, right).reshape(total_ref.shape)
        send_ref, keep_ref = out_refs
        send_ref[:, j] = total_ref[:, 1 - core].astype(BF16)
        keep_ref[:, j] = total_ref[:, core].astype(BF16)


def store_kernel(source_ref, *refs):
    target_ref, semaphore = refs[-2:]
    copy = pltpu.make_async_copy(source_ref, target_ref, semaphore)
    copy.start()
    copy.wait()


def store(array, after):
    return pl.pallas_call(
        store_kernel,
        in_specs=[near_spec()] + [pl.BlockSpec(memory_space=pl.ANY)] * len(after),
        out_specs=pl.BlockSpec(memory_space=pltpu.HBM),
        out_shape=pltpu.HBM(array.shape, array.dtype),
        scratch_shapes=[pltpu.SemaphoreType.DMA],
        compiler_params=params(),
        name="store",
    )(array, *after)


def swap(value, axis, mask):
    size = lax.axis_size(axis)
    return lax.ppermute(value, axis, [(i, i ^ mask) for i in range(size)])


VECTOR_ROWS = 8


def first_sum_kernel(counts, place_ref, *refs):
    terms = sum(counts)
    mine_ref, other_ref = refs[terms : terms + 2]
    along_x_ref, along_y_ref, keep_x_ref, keep_y_ref, vectors_ref = refs[terms + 2 :]
    x, y = place_ref[3], place_ref[4]
    half = along_x_ref.shape[1]
    size = keep_x_ref.shape[1]
    low, high = slice(0, half), slice(half, None)
    row = 0
    start = 0
    for count in counts:
        group = refs[start : start + count]
        start += count
        for s in range(group[0].shape[1]):
            rows = group[0].shape[2]

            def total(at, lanes):
                values = [r[at, s, :, lanes].astype(F32) for r in group]
                return functools.reduce(lambda a, b: a + b, values)

            for k in range(2):
                to = slice(k * size + row, k * size + row + rows)
                here = slice(row, row + rows)
                along_x_ref[to] = total(2 * k + (1 - x), low).astype(BF16)
                keep_x_ref[k, here] = total(2 * k + x, low)
                along_y_ref[to] = total(2 * (1 - y) + k, high).astype(BF16)
                keep_y_ref[k, here] = total(2 * y + k, high)
            row += rows
    vectors = (mine_ref[...] + other_ref[...]).astype(BF16)
    vectors_ref[...] = vectors
    put_vectors(vectors, along_x_ref, along_y_ref)


def put_vectors(vectors, low_ref, high_ref):
    half = vectors.shape[1] // 2
    low_ref[low_ref.shape[0] - VECTOR_ROWS :] = vectors[:, :half]
    high_ref[high_ref.shape[0] - VECTOR_ROWS :] = vectors[:, half:]


def get_vectors(low_ref, high_ref):
    low = low_ref[low_ref.shape[0] - VECTOR_ROWS :]
    return jnp.concatenate([low, high_ref[high_ref.shape[0] - VECTOR_ROWS :]], 1).astype(F32)


def second_sum_kernel(
    place_ref,
    keep_x_ref,
    came_x_ref,
    keep_y_ref,
    came_y_ref,
    vectors_ref,
    send_y_ref,
    send_x_ref,
    left_x_ref,
    left_y_ref,
    vectors_out_ref,
):
    size = keep_x_ref.shape[1]
    for keep, came, send, left, me in (
        (keep_x_ref, came_x_ref, send_y_ref, left_x_ref, place_ref[4]),
        (keep_y_ref, came_y_ref, send_x_ref, left_y_ref, place_ref[3]),
    ):
        at = lambda i: pl.ds(pl.multiple_of(i * size, size), size)
        send[:size] = (keep[1 - me] + came[at(1 - me)].astype(F32)).astype(BF16)
        left[...] = keep[me] + came[at(me)].astype(F32)
    vectors = vectors_ref[...].astype(F32) + get_vectors(came_x_ref, came_y_ref)
    vectors = vectors.astype(BF16)
    vectors_out_ref[...] = vectors
    put_vectors(vectors, send_y_ref, send_x_ref)


def third_sum_kernel(left_x_ref, came_x_ref, left_y_ref, came_y_ref, vectors_ref, total_ref):
    size, half = left_x_ref.shape
    total_ref[:size, :half] = (left_x_ref[...] + came_x_ref[:size].astype(F32)).astype(BF16)
    total_ref[:size, half:] = (left_y_ref[...] + came_y_ref[:size].astype(F32)).astype(BF16)
    vectors = vectors_ref[...].astype(F32) + get_vectors(came_x_ref, came_y_ref)
    total_ref[size : size + VECTOR_ROWS] = vectors.astype(BF16)


def third_cut_kernel(place_ref, *refs):
    third_sum_kernel(*refs[:-1])
    total_ref, sent_ref = refs[-2:]
    filled = refs[0].shape[0] + VECTOR_ROWS
    if filled < total_ref.shape[0]:
        total_ref[filled:] = jnp.zeros((total_ref.shape[0] - filled, total_ref.shape[1]), BF16)
    half = sent_ref.shape[0]
    away = pl.multiple_of((1 - (place_ref[1] & 1)) * half, half)
    sent_ref[...] = total_ref[pl.ds(away, half)]


def near_sum_kernel(place_ref, total_ref, came_ref, out_ref):
    half = came_ref.shape[0]
    mine = total_ref[pl.ds(pl.multiple_of((place_ref[1] & 1) * half, half), half)]
    out_ref[...] = (mine.astype(F32) + came_ref[...].astype(F32)).astype(BF16)


def far_sum_kernel(left_ref, right_ref, out_ref):
    at = slice(0, out_ref.shape[0])
    out_ref[...] = (left_ref[at].astype(F32) + right_ref[at].astype(F32)).astype(BF16)


def add_kernel(left_ref, right_ref, out_ref):
    out_ref[...] = (left_ref[...].astype(F32) + right_ref[...].astype(F32)).astype(out_ref.dtype)


def join_rows(place, mine_ref, other_ref, out_ref):
    part = mine_ref.shape[0]
    out_ref[pl.ds(pl.multiple_of(place * part, part), part)] = mine_ref[...]
    out_ref[pl.ds(pl.multiple_of((1 - place) * part, part), part)] = other_ref[...]


def finish_kernel(ratio, place_ref, low_ref, came_ref, mine_ref, other_ref, *refs):
    query_ref, key_ref, value_ref, outer_ref, inner_ref, out_ref = refs[:6]
    tail_refs, dense_refs, wide_ref, total_scratch, row_scratch = refs[6:10], refs[10:14], *refs[14:]
    rows, width = out_ref.shape
    total = lambda at: low_ref[at].astype(F32) + came_ref[at].astype(F32)
    for s, ref in enumerate((query_ref, key_ref, value_ref)):
        ref[...] = total(slice(s * rows, (s + 1) * rows))
    put_slices(total(slice(3 * rows, 3 * rows + VECTOR_ROWS)), place_ref[0], tail_refs)
    join_rows(place_ref[1] & 1, mine_ref, other_ref, total_scratch)
    outer_ref[...] = total_scratch[: ratio * rows].astype(F32)
    for s in range(ratio):
        at = (ratio + s) * rows
        inner_ref[:, s * width : (s + 1) * width] = total_scratch[at : at + rows].astype(F32)
    at = 2 * ratio * rows
    out_ref[...] = total_scratch[at : at + rows].astype(F32)
    vectors = total_scratch[at + rows : at + rows + VECTOR_ROWS].astype(F32)
    put_slices(vectors, place_ref[0], dense_refs)
    row_scratch[...] = vectors
    size = wide_ref.shape[0]
    start = place_ref[0] * size
    row = row_scratch[pl.ds(len(dense_refs) + start // width, 1)]
    wide_ref[...] = pltpu.roll(row, lax.rem(width - lax.rem(start, width), width), 1)[0, :size]


def put_slices(vectors, index, refs):
    width, size = vectors.shape[1], refs[0].shape[0]
    turned = pltpu.roll(vectors, lax.rem(width - index * size, width), 1)
    for i, ref in enumerate(refs):
        ref[...] = turned[i, :size]


def small_call(kernel, place, operands, out_shapes, name, after=(), inside=True, scratch=(), mib=4, size=None):
    ahead = 0 if place is None else 1
    count = len(operands)

    def body(*refs):
        kernel(*refs[: ahead + count], *refs[ahead + count + len(after) :])

    if size is None:
        size = sum(math.prod(a.shape) * a.dtype.itemsize for a in list(operands) + list(out_shapes))
    return pl.pallas_call(
        body,
        grid_spec=pltpu.PrefetchScalarGridSpec(
            num_scalar_prefetch=ahead,
            grid=(1,),
            in_specs=[near_spec() for a in operands] + [pl.BlockSpec(memory_space=pl.ANY)] * len(after),
            out_specs=[near_spec() for s in out_shapes],
            scratch_shapes=list(scratch),
        ),
        out_shape=[near(s.shape, s.dtype) if inside else s for s in out_shapes],
        compiler_params=params(mib),
        cost_estimate=pl.CostEstimate(flops=0, transcendentals=0, bytes_accessed=size),
        name=name,
    )(*(() if place is None else (place,)), *operands, *after)


def sum_core(place, groups, vectors, name, after=()):
    groups = [list(g) + [swap(a, "batch", 1) for a in sent] for g, sent in groups]
    vectors_other = swap(vectors, "batch", 1)
    _, _, rows, width = groups[0][0].shape
    size = sum(g[0].shape[1] for g in groups) * rows
    half = width // 2
    counts = tuple(len(g) for g in groups)
    message = shape_of((2 * size + VECTOR_ROWS, half), BF16)
    kept = shape_of((2, size, half), F32)
    along_x, along_y, keep_x, keep_y, vectors = small_call(
        functools.partial(first_sum_kernel, counts),
        place,
        [a for g in groups for a in g] + [vectors, vectors_other],
        [message, message, kept, kept, shape_of(vectors.shape, BF16)],
        name + "_sum_core",
        after,
    )
    came_x, came_y = swap(along_x, "batch", 2), swap(along_y, "batch", 4)
    return (keep_x, came_x, keep_y, came_y, vectors), along_x


def sum_first(place, pieces, name, after=()):
    keep_x, _, _, _, vectors = pieces
    _, size, half = keep_x.shape
    message = shape_of((size + VECTOR_ROWS, half), BF16)
    kept = shape_of((size, half), F32)
    send_y, send_x, left_x, left_y, vectors = small_call(
        second_sum_kernel,
        place,
        pieces,
        [message, message, kept, kept, shape_of(vectors.shape, BF16)],
        name + "_sum_first",
        after,
    )
    came_x, came_y = swap(send_y, "batch", 4), swap(send_x, "batch", 2)
    return (left_x, came_x, left_y, came_y, vectors), send_y


def sum_second(pieces, name, after=()):
    size, half = pieces[0].shape
    shape = shape_of((size + VECTOR_ROWS, 2 * half), BF16)
    return small_call(third_sum_kernel, None, pieces, [shape], name + "_sum_second", after)[0]


def sum_second_cut(place, pieces, name, after=()):
    size, half = pieces[0].shape
    rows = -(-(size + VECTOR_ROWS) // 32) * 32
    total, sent = small_call(
        third_cut_kernel,
        place,
        pieces,
        [shape_of((rows, 2 * half), BF16), shape_of((rows // 2, 2 * half), BF16)],
        name + "_sum_second",
        after,
    )
    return total, swap(sent, "rows", 1)


def batch_slices_any(groups, vectors):
    me = lax.axis_index("batch")
    bits = lax.axis_size("batch").bit_length() - 1
    pieces = []
    for kept, sent in groups:
        values = [a.astype(F32) for a in kept] + [swap(a, "batch", 1).astype(F32) for a in sent]
        pieces.append(functools.reduce(lambda a, b: a + b, values))
    total = jnp.concatenate(pieces, 1)
    total = total.reshape((2,) * (bits - 1) + total.shape[1:])
    for bit in range(bits - 1, 0, -1):
        mine = (me >> bit) & 1
        sent = lax.dynamic_index_in_dim(total, 1 - mine, 0, keepdims=False).astype(BF16)
        total = lax.dynamic_index_in_dim(total, mine, 0, keepdims=False)
        total = total + swap(sent, "batch", 1 << bit).astype(F32)
    total = lax.psum(total.astype(BF16), "rows").astype(F32)
    return total, lax.psum(vectors, ("batch", "rows"))


def cross_kernel(count, *refs):
    out_ref = refs[-1]
    came = [(ref, i) for ref in refs[count:-1] for i in range(ref.shape[1])]
    for m, (term, (ref, i)) in enumerate(zip(refs[:count], came)):
        out_ref[m] = (term[0].astype(F32) + ref[1, i].astype(F32)).astype(BF16)


def cross_sum(terms, came, name, after=()):
    shape = (len(terms),) + terms[0].shape[1:]
    return small_call(
        functools.partial(cross_kernel, len(terms)),
        None,
        list(terms) + list(came),
        [shape_of(shape, BF16)],
        name,
        after,
    )[0]


def final_kernel(count, *refs):
    owns, nears, crosses = refs[:count], refs[count : 2 * count], refs[2 * count : 3 * count]
    atoms_ref, gain_ref, shift_ref, grad_middle_ref, out_ref = refs[3 * count :]
    gain = as_row(gain_ref)
    shift = as_row(shift_ref)
    for m in range(count):
        grad = owns[m][0] + nears[m][...].astype(F32) + crosses[m][...].astype(F32)
        _, normed, inverse = norm_forward(atoms_ref[m].astype(F32), gain, shift)
        result = grad_middle_ref[m] + norm_backward(grad, normed, inverse, gain)
        out_ref[m] = result.astype(BF16)


def first_norm_backward(owns, nears, crosses, others, after=()):
    count = len(owns)
    arrays = [a for a, _ in nears + crosses]
    spots = [at for _, at in nears + crosses]

    def kernel(*refs):
        picked = [r.at[at] for r, at in zip(refs[count : 3 * count], spots)]
        final_kernel(count, *refs[:count], *picked, *refs[3 * count :])

    return small_call(
        kernel,
        None,
        list(owns) + arrays + list(others),
        [shape_of(others[0].shape, BF16)],
        "first_norm_backward",
        after,
        inside=False,
    )[0]


def shards(
    atoms,
    pair_bias,
    lengths,
    first_gain,
    first_shift,
    query_weight,
    query_bias,
    key_weight,
    value_weight,
    value_bias,
    out_weight,
    out_bias,
    second_gain,
    second_shift,
    inner_weight,
    inner_bias,
    outer_weight,
    outer_bias,
    atoms_cotangent,
    pair_cotangent,
):
    molecules, rows, model_width = atoms.shape
    head_count = pair_bias.shape[1]
    head_size = model_width // head_count
    batch_count = lax.axis_size("batch")
    batch_index = lax.axis_index("batch")
    row = lax.axis_index("rows")
    (
        atoms_far,
        pair_bias,
        first_gain,
        first_shift,
        query_weight,
        query_bias,
        key_weight,
        value_weight,
        value_bias,
        out_weight,
        out_bias,
        second_gain,
        second_shift,
        inner_weight,
        inner_bias,
        outer_weight,
        outer_bias,
        atoms_cotangent,
        pair_cotangent,
    ) = [
        pltpu.with_memory_space_constraint(a, pltpu.HBM)
        for a in (
            atoms,
            pair_bias,
            first_gain,
            first_shift,
            query_weight,
            query_bias,
            key_weight,
            value_weight,
            value_bias,
            out_weight,
            out_bias,
            second_gain,
            second_shift,
            inner_weight,
            inner_bias,
            outer_weight,
            outer_bias,
            atoms_cotangent,
            pair_cotangent,
        )
    ]
    place = jnp.stack(
        [batch_index, row, batch_index & 1, (batch_index >> 1) & 1, (batch_index >> 2) & 1]
    ).astype(jnp.int32)
    line = lambda v: v
    count = molecules // STAGES
    stages = []
    pair_out = jnp.zeros((1,), BF16)
    one = swap(atoms, "rows", 1)
    (
        pair_near,
        query_near,
        key_near,
        value_near,
        first_gain,
        first_shift,
        query_bias,
        value_bias,
        out_bias,
        second_gain,
        second_shift,
        inner_bias,
        outer_bias,
        out_weight,
        inner_weight,
        outer_weight,
        atoms_cotangent,
    ) = load(
        [
            pair_bias,
            query_weight,
            key_weight,
            value_weight,
            first_gain,
            first_shift,
            query_bias,
            value_bias,
            out_bias,
            second_gain,
            second_shift,
            inner_bias,
            outer_bias,
            out_weight,
            inner_weight,
            outer_weight,
            atoms_cotangent,
        ],
        "load_first",
        None,
        (place,),
    )
    projected = near_half(
        head_size,
        STAGES,
        place,
        atoms_far,
        one,
        (
            first_gain,
            first_shift,
            query_near,
            query_bias,
            key_near,
            value_near,
            value_bias,
        ),
        (),
    )
    mine = [atoms[:count], projected[-1]]
    gathered = [[swap(a, "rows", mask) for mask in (2, 3)] for a in mine]
    for stage in range(STAGES):
        pair_out, kept, _ = attention_forward(
            head_size,
            stage * count,
            place,
            lengths,
            gathered[stage],
            pair_near,
            (first_gain, first_shift, key_near, value_near, value_bias),
            projected[5 * stage : 5 * stage + 5],
            pair_out,
            [],
        )
        stages.append(kept)
    (
        atoms_out,
        send,
        keep,
        grad_middle,
        grad_mixed,
        dense_vectors,
        pair_cotangent,
    ) = dense(
        place,
        [s[1] for s in stages],
        atoms,
        atoms_cotangent,
        (
            out_weight,
            line(out_bias),
            line(second_gain),
            line(second_shift),
            inner_weight,
            line(inner_bias),
            outer_weight,
            line(outer_bias),
        ),
        batch_count,
        pair_cotangent,
    )
    pairs = batch_count // 2
    own_rows = model_width // batch_count
    dense_groups = [([keep], [send])]
    usual = batch_count == 8

    def backward(molecule, held, sums, after, before=None):
        stage = molecule // count
        return attention_backward(
            head_size,
            stage * count,
            molecule % count,
            place,
            stages[stage],
            pair_cotangent,
            grad_mixed,
            (query_near, key_near, value_near),
            held,
            sums,
            after,
            before,
        )

    pair_grad, near0, cross0, own0, sums, *grads0 = backward(0, None, None, [])
    after = []
    if usual:
        dense_pieces, held = sum_core(place, dense_groups, dense_vectors, "dense", (own0,))
        after = [held]
    else:
        dense_total, dense_vectors = batch_slices_any(dense_groups, dense_vectors)
    pair_grad, near1, cross1, own1, sums, *grads1 = backward(1, pair_grad, sums, after, near0)
    near1 = swap(near1, "rows", 1)
    pair_grad, near2, cross2, own2, sums, *grads2 = backward(2, pair_grad, sums, [own1])
    near2 = swap(near2, "rows", 1)
    cross0 = cross_sum([cross0, cross1], [near1], "cross_first", (own2,))
    far0 = swap(cross0, "rows", 2)
    pair_grad, near3, cross3, own3, tail_vectors, *grads3 = backward(3, pair_grad, sums, [cross0])
    near3 = swap(near3, "rows", 1)
    owns = [own0, own1, own2, own3]
    after = [far0]
    if usual:
        dense_pieces, held = sum_first(place, dense_pieces, "dense", (own3,))
        after.append(held)
    part = shape_of((pairs, 3, own_rows, model_width), BF16)
    send, keep = small_call(
        functools.partial(weight_kernel, 4, STAGES),
        place,
        [s[3] for s in stages] + grads0 + grads1 + grads2 + grads3,
        [part] * 2,
        "attention_weights",
        after,
        scratch=[pltpu.VMEM((pairs, 2, own_rows, model_width), F32)],
        mib=14,
    )
    groups = [([keep], [send])]
    matrix = shape_of((own_rows, model_width), F32)
    ratio = inner_weight.shape[1] // model_width
    vector = shape_of((own_rows,), F32)
    finish = (atoms, line(first_gain), line(first_shift), grad_middle)
    if usual:
        pieces, held = sum_core(place, groups, tail_vectors, "tail")
        cross2 = cross_sum([cross2, cross3], [near2, near3], "cross_second", (held,))
        far2 = swap(cross2, "rows", 2)
        dense_total, came = sum_second_cut(place, dense_pieces, "dense", (cross2,))
        pieces, held = sum_first(place, pieces, "tail", (dense_total,))
        start = dense_total.shape[0] // 2
        mine = small_call(
            near_sum_kernel, place, [dense_total, came], [came], "dense_near_sum", (held, far2)
        )[0]
        far = swap(mine, "rows", 2)
        total = sum_second(pieces, "tail", (mine,))
        tail_came = swap(total, "rows", 1)
        total = small_call(add_kernel, None, [total, tail_came], [total], "tail_near_sum")[0]
        tail_came = swap(total, "rows", 2)
        part = shape_of((start, model_width), BF16)
        mine = small_call(far_sum_kernel, None, [mine, far], [part], "dense_far_sum", (total,))[0]
        other = swap(mine, "rows", 1)
        pair_grad = store(pair_grad, (mine,))
        atoms_grad = first_norm_backward(
            owns,
            [(near1, (0, 0)), (near1, (0, 1)), (near2, (0, 0)), (near3, (0, 0))],
            [(far0, 0), (far0, 1), (far2, 0), (far2, 1)],
            finish,
            (mine,),
        )
        outs = small_call(
            functools.partial(finish_kernel, ratio),
            place,
            [total, tail_came, mine, other],
            [matrix] * 3
            + [
                shape_of((ratio * own_rows, model_width), F32),
                shape_of((own_rows, ratio * model_width), F32),
                matrix,
            ]
            + [vector] * 8
            + [shape_of((ratio * own_rows,), F32)],
            "finish",
            inside=False,
            scratch=[
                pltpu.VMEM((2 * part.shape[0], model_width), BF16),
                pltpu.VMEM((VECTOR_ROWS, model_width), F32),
            ],
        )
        query_grad, key_grad, value_grad, outer_grad, inner_grad, out_grad = outs[:6]
        tail_parts, dense_parts = outs[6:10], outs[10:]
    else:
        pair_grad = store(pair_grad, ())
        far2 = swap(cross_sum([cross2, cross3], [near2, near3], "cross_second"), "rows", 2)
        atoms_grad = first_norm_backward(
            owns,
            [(near1, (0, 0)), (near1, (0, 1)), (near2, (0, 0)), (near3, (0, 0))],
            [(far0, 0), (far0, 1), (far2, 0), (far2, 1)],
            finish,
        )
        total, tail_vectors = batch_slices_any(groups, tail_vectors)
        query_grad, key_grad, value_grad = total[0], total[1], total[2]
        outer_grad = dense_total[:ratio].reshape(-1, model_width)
        inner_grad = dense_total[ratio : 2 * ratio].transpose(1, 0, 2).reshape(own_rows, -1)
        out_grad = dense_total[2 * ratio]
        part = lambda v: lax.dynamic_slice_in_dim(
            v, batch_index * (v.shape[0] // batch_count), v.shape[0] // batch_count
        )
        tail_parts = [part(v) for v in tail_vectors[:4]]
        dense_parts = [part(v) for v in dense_vectors[:4]] + [part(dense_vectors[4:].reshape(-1))]
    return (
        atoms_out,
        pair_out,
        atoms_grad,
        pair_grad,
        tail_parts[0],
        tail_parts[1],
        query_grad,
        tail_parts[2],
        key_grad,
        value_grad,
        tail_parts[3],
        out_grad,
        dense_parts[3],
        dense_parts[1],
        dense_parts[2],
        inner_grad,
        dense_parts[4],
        outer_grad,
        dense_parts[0],
    )


def solution(mesh):
    tokens = P("batch", "rows", None)
    pairs = P("batch", None, "rows", None)
    vector = P("batch")
    matrix = P("batch", None)
    return jax.shard_map(
        shards,
        mesh=mesh,
        in_specs=(tokens, pairs, P("batch")) + (P(),) * 15 + (tokens, pairs),
        out_specs=(
            tokens,
            pairs,
            tokens,
            pairs,
            vector,
            vector,
            matrix,
            vector,
            matrix,
            matrix,
            vector,
            matrix,
            vector,
            vector,
            vector,
            matrix,
            vector,
            matrix,
            vector,
        ),
        check_vma=False,
    )
```

```python
import functools
import math

import jax
import jax.numpy as jnp
from jax import lax
from jax.experimental import pallas as pl
from jax.experimental.pallas import tpu as pltpu
from jax.sharding import PartitionSpec as P

EPSILON = 1e-05
MASKED = -1000000000.0
F32 = jnp.float32
BF16 = jnp.bfloat16
LANES = 128
STAGES = 2
VMEM_LIMIT = 18 << 20


def shape_of(shape, dtype):
    return jax.ShapeDtypeStruct(tuple(shape), dtype)


def norm_forward(values_in, gain, shift):
    centre = values_in - jnp.mean(values_in, -1, keepdims=True)
    inverse = lax.rsqrt(jnp.mean(centre * centre, -1, keepdims=True) + EPSILON)
    normed = centre * inverse
    return (normed * gain + shift, normed, inverse)


def norm_backward(upstream, normed, inverse, gain):
    scaled = upstream * gain
    return inverse * (
        scaled
        - jnp.mean(scaled, -1, keepdims=True)
        - normed * jnp.mean(scaled * normed, -1, keepdims=True)
    )


def dot(left, right):
    return jnp.dot(left, right, preferred_element_type=F32)


def across(left, right):
    return lax.dot_general(left, right, (((0,), (0,)), ((), ())), preferred_element_type=F32)


def against(left, right):
    return lax.dot_general(left, right, (((1,), (1,)), ((), ())), preferred_element_type=F32)


def column_sum(values_in):
    return jnp.sum(values_in.astype(F32), 0, keepdims=True)


def near(shape, dtype):
    return pltpu.VMEM(tuple(shape), dtype)


def near_spec():
    return pl.BlockSpec(memory_space=pltpu.VMEM)


def as_row(ref):
    return ref[...].astype(F32).reshape(1, -1)


def whole(array):
    return pl.BlockSpec(array.shape, lambda *_: (0,) * array.ndim)


def params(mib=10):
    return pltpu.CompilerParams(vmem_limit_bytes=mib << 20)


def load_kernel(count, starts, *refs):
    sources, targets, semaphores = refs[:count], refs[-count - 1 : -1], refs[-1]
    copies = [
        pltpu.make_async_copy(source.at[pl.ds(start, target.shape[0])], target, semaphores.at[i])
        for i, (source, target, start) in enumerate(zip(sources, targets, starts))
    ]
    for copy in copies:
        copy.start()
    for copy in copies:
        copy.wait()


def copies_beside(sources, targets, semaphores):
    return [
        pltpu.make_async_copy(source, target, semaphores.at[i])
        for i, (source, target) in enumerate(zip(sources, targets))
    ]


def load(arrays, name, starts=None, after=()):
    count = len(arrays)
    starts = starts or (0,) * count
    return pl.pallas_call(
        functools.partial(load_kernel, count, starts),
        in_specs=[pl.BlockSpec(memory_space=pltpu.HBM)] * count
        + [pl.BlockSpec(memory_space=pl.ANY)] * len(after),
        out_specs=[near_spec()] * count,
        out_shape=[
            near((a.shape[0] - start,) + a.shape[1:], a.dtype) for a, start in zip(arrays, starts)
        ],
        scratch_shapes=[pltpu.SemaphoreType.DMA((count,))],
        compiler_params=params(),
        name=name,
    )(*arrays, *after)


def project(pieces, first, parameters, row, refs, atoms_scratch):
    gain_ref, shift_ref, key_weight_ref, value_weight_ref, value_bias_ref = parameters
    hidden_ref, normed_ref, key_ref, value_ref = refs
    count = hidden_ref.shape[0]
    _, groups, keys, width = key_ref.shape
    rows = keys // 4
    half = 2 * rows
    model_width = hidden_ref.shape[2]
    for m in range(count):
        for i, piece in enumerate(pieces):
            start = pl.multiple_of(m * half + ((row ^ i) & 1) * rows, rows)
            atoms_scratch[pl.ds(start, rows)] = piece[m + first]
    hidden, normed, _ = norm_forward(
        atoms_scratch[...].astype(F32), as_row(gain_ref), as_row(shift_ref)
    )
    hidden = hidden.astype(BF16)
    normed = normed.astype(BF16)
    key_rows = dot(hidden, key_weight_ref[...]).astype(BF16)
    value_rows = (dot(hidden, value_weight_ref[...]) + as_row(value_bias_ref)).astype(BF16)
    return [a.reshape(count, half, model_width) for a in (hidden, normed, key_rows, value_rows)]


def put_half(values, at, refs):
    hidden, normed, key_rows, value_rows = values
    hidden_ref, normed_ref, key_ref, value_ref = refs
    count, groups, _, width = key_ref.shape
    half = hidden.shape[1]
    ones = jnp.ones((count, half, width), BF16)
    hidden_ref[:, at] = hidden
    normed_ref[:, at] = normed
    for t in range(groups):
        lanes = slice(t * width, (t + 1) * width)
        key_ref[:, t, at] = key_rows[:, :, lanes]
        value_ref[:, t, at, :width] = value_rows[:, :, lanes]
        value_ref[:, t, at, width:] = ones


def half_rows(row, other, rows):
    which = row >> 1
    which = 1 - which if other else which
    return pl.ds(pl.multiple_of(which * 2 * rows, 2 * rows), 2 * rows)


def near_half_kernel(
    head_size,
    stages,
    ahead,
    place_ref,
    own_ref,
    one_ref,
    gain_ref,
    shift_ref,
    query_weight_ref,
    query_bias_ref,
    key_weight_ref,
    value_weight_ref,
    value_bias_ref,
    *refs,
):
    refs = refs[ahead:]
    later_ref, atoms_scratch = refs[-2:]
    later_ref[...] = own_ref[own_ref.shape[0] - later_ref.shape[0] :]
    row = place_ref[1]
    rows, model_width = own_ref.shape[1:]
    factor = head_size**-0.5
    parameters = (gain_ref, shift_ref, key_weight_ref, value_weight_ref, value_bias_ref)
    for stage in range(stages):
        hidden_ref, normed_ref, key_ref, value_ref, query_ref = refs[5 * stage : 5 * stage + 5]
        outs = (hidden_ref, normed_ref, key_ref, value_ref)
        count, groups, _, width = key_ref.shape
        values = project((own_ref, one_ref), stage * count, parameters, row, outs, atoms_scratch)
        put_half(values, half_rows(row, False, rows), outs)
        mine = pl.ds(pl.multiple_of(row * rows, rows), rows)
        own = jnp.concatenate([hidden_ref[m, mine] for m in range(count)], 0)
        query_rows = (dot(own, query_weight_ref[...]) + as_row(query_bias_ref)) * factor
        query_rows = query_rows.astype(BF16).reshape(count, rows, model_width)
        for t in range(groups):
            query_ref[:, t] = query_rows[:, :, t * width : (t + 1) * width]


def near_half(head_size, stages, place, atoms, one, parameters, after):
    molecules, rows, model_width = atoms.shape
    keys = 4 * rows
    count = molecules // stages
    groups = model_width // LANES
    operands = (place, atoms, one, *parameters, *after)
    return pl.pallas_call(
        functools.partial(near_half_kernel, head_size, stages, len(after)),
        grid_spec=pltpu.PrefetchScalarGridSpec(
            num_scalar_prefetch=1,
            grid=(1,),
            in_specs=[whole(atoms), near_spec()]
            + [near_spec() for a in parameters]
            + [pl.BlockSpec(memory_space=pl.ANY)] * len(after),
            out_specs=[near_spec()] * (5 * stages + 1),
            scratch_shapes=[pltpu.VMEM((count * 2 * rows, model_width), BF16)],
        ),
        out_shape=[
            near((count, keys, model_width), BF16),
            near((count, keys, model_width), BF16),
            near((count, groups, keys, LANES), BF16),
            near((count, groups, keys, 2 * LANES), BF16),
            near((count, groups, rows, LANES), BF16),
        ]
        * stages
        + [near((molecules - count, rows, model_width), BF16)],
        compiler_params=params(10),
        name="near_half",
    )(*operands)


def forward_kernel(
    head_size,
    chunk,
    first,
    extra,
    place_ref,
    length_ref,
    two_ref,
    three_ref,
    pair_ref,
    query_ref,
    gain_ref,
    shift_ref,
    key_weight_ref,
    value_weight_ref,
    value_bias_ref,
    *refs,
):
    (
        pair_out_ref,
        weights_ref,
        mixed_ref,
        inverse_ref,
        hidden_ref,
        normed_ref,
        key_ref,
        value_ref,
    ) = refs[5 + extra : 13 + extra]
    atoms_scratch, semaphores = refs[-2:]
    copies = copies_beside(refs[5 : 5 + extra], refs[13 + extra : 13 + 2 * extra], semaphores)
    molecule = pl.program_id(0)
    group = pl.program_id(1)
    count, groups, keys, width = key_ref.shape
    heads = width // head_size
    rows = query_ref.shape[2]

    @pl.when((molecule == 0) & (group == 0))
    def _():
        for copy in copies:
            copy.start()
        row = place_ref[1]
        outs = (hidden_ref, normed_ref, key_ref, value_ref)
        parameters = (gain_ref, shift_ref, key_weight_ref, value_weight_ref, value_bias_ref)
        values = project((two_ref, three_ref), 0, parameters, row, outs, atoms_scratch)
        put_half(values, half_rows(row, True, rows), outs)

    query = query_ref[molecule, group]
    key = key_ref[molecule, group]
    value = value_ref[molecule, group]
    valid = lax.broadcasted_iota(jnp.int32, (1, keys), 1) < length_ref[molecule + first]
    lane = lax.broadcasted_iota(jnp.int32, (1, width), 1) // head_size
    lane_pair = lax.broadcasted_iota(jnp.int32, (1, 2 * width), 1) % width // head_size
    total = jnp.zeros((rows, 2 * width), F32)
    zero = jnp.zeros((), BF16)
    for c in range(0, heads, chunk):
        here = slice(c, c + chunk)
        there = pl.ds(group * heads + c, chunk)
        spread = jnp.concatenate([jnp.where(lane == c + t, query, zero) for t in range(chunk)], 0)
        pair = pair_ref[molecule + first, there].reshape(chunk * rows, keys)
        scores = against(spread, key) + pair.astype(F32)
        pair_out_ref[0, here] = scores.astype(BF16).reshape(chunk, rows, keys)
        masked = jnp.where(valid, scores, MASKED)
        weights = jnp.exp(masked - jnp.max(masked, -1, keepdims=True)).astype(BF16)
        weights_ref[molecule, there] = weights.reshape(chunk, rows, keys)
        product = dot(weights, value)
        for t in range(chunk):
            total = jnp.where(lane_pair == c + t, product[t * rows : (t + 1) * rows], total)
    inverse = 1.0 / total[:, width:]
    inverse_ref[molecule, group] = inverse
    mixed_ref[molecule, group] = total[:, :width] * inverse

    @pl.when((molecule == count - 1) & (group == groups - 1))
    def _():
        for copy in copies:
            copy.wait()


def attention_forward(
    head_size, first, place, lengths, pieces, pair_bias, parameters, projected, held, extra
):
    _, head_count, rows, keys = pair_bias.shape
    hidden, normed, key, value, query = projected
    count, groups = key.shape[:2]
    model_width = groups * LANES
    heads = LANES // head_size
    pair_spec = pl.BlockSpec((1, heads, rows, keys), lambda m, g, *_: (m + first, g, 0, 0))
    elements = count * head_count * rows * keys
    operands = [place, lengths, *pieces, pair_bias, query, *parameters]
    in_specs = [near_spec()] * (len(pieces) + 2)
    in_specs += [near_spec() for a in parameters]
    start = len(operands)
    operands += [hidden, normed, key, value, held]
    in_specs += [near_spec()] * 4 + [pl.BlockSpec(memory_space=pl.ANY)]
    aliases = {start + i: 4 + i for i in range(4)}
    if held.ndim > 1:
        aliases[start + 4] = 0
    operands += extra
    in_specs += [pl.BlockSpec(memory_space=pltpu.HBM)] * len(extra)
    outs = pl.pallas_call(
        functools.partial(forward_kernel, head_size, 4, first, len(extra)),
        grid_spec=pltpu.PrefetchScalarGridSpec(
            num_scalar_prefetch=2,
            grid=(count, groups),
            in_specs=in_specs,
            out_specs=[pair_spec] + [near_spec()] * (7 + len(extra)),
            scratch_shapes=[
                pltpu.VMEM((count * 2 * rows, model_width), BF16),
                pltpu.SemaphoreType.DMA((max(len(extra), 1),)),
            ],
        ),
        out_shape=[
            shape_of(pair_bias.shape, BF16),
            near((count, head_count, rows, keys), BF16),
            near((count, groups, rows, LANES), F32),
            near((count, groups, rows, LANES), F32),
            near(hidden.shape, BF16),
            near(normed.shape, BF16),
            near(key.shape, BF16),
            near(value.shape, BF16),
        ]
        + [near(a.shape, a.dtype) for a in extra],
        input_output_aliases=aliases,
        compiler_params=params(10),
        cost_estimate=pl.CostEstimate(
            flops=elements * 2 * 384, transcendentals=elements, bytes_accessed=elements * 6
        ),
        name="attention_forward",
    )(*operands)
    pair_out, weights, mixed, inverse, hidden, normed, key, value = outs[:8]
    return pair_out, (weights, mixed, inverse, hidden, normed, query, key, value), outs[8:]


def dense_kernel(
    mixed_count,
    place_ref,
    *refs,
):
    mixed_refs = refs[:mixed_count]
    (
        atoms_ref,
        cotangent_ref,
        out_weight_ref,
        out_bias_ref,
        gain_ref,
        shift_ref,
        inner_weight_ref,
        inner_bias_ref,
        outer_weight_ref,
        outer_bias_ref,
        far_ref,
        atoms_out_ref,
        send_ref,
        keep_ref,
        grad_middle_ref,
        grad_mixed_ref,
        vectors_ref,
        copied_ref,
        hidden_scratch,
        turned_scratch,
        normed_scratch,
        inverse_scratch,
        result_scratch,
        upstream_scratch,
        outer_scratch,
        inner_scratch,
        semaphores,
    ) = refs[mixed_count:]
    (copy,) = copies_beside([far_ref], [copied_ref], semaphores)
    step = pl.program_id(0)
    steps = pl.num_programs(0)
    core = place_ref[2]
    tokens, model_width = hidden_scratch.shape
    cotangent = cotangent_ref[...].reshape(tokens, model_width)

    def mixed_rows():
        parts = []
        for ref in mixed_refs:
            count, groups, rows, width = ref.shape
            join = [ref[:, t].reshape(count * rows, width) for t in range(groups)]
            parts.append(jnp.concatenate(join, 1))
        return jnp.concatenate(parts, 0)

    @pl.when(step == 0)
    def _():
        copy.start()
        mixed_low = mixed_rows().astype(BF16)
        middle = (
            atoms_ref[...].reshape(tokens, model_width).astype(F32)
            + dot(mixed_low, out_weight_ref[...])
            + as_row(out_bias_ref)
        )
        hidden, normed, inverse = norm_forward(
            middle, as_row(gain_ref), as_row(shift_ref)
        )
        hidden_scratch[...] = hidden.astype(BF16)
        turned_scratch[...] = jnp.transpose(hidden).astype(BF16)
        normed_scratch[...] = normed
        inverse_scratch[...] = inverse
        result_scratch[...] = middle + as_row(outer_bias_ref)
        upstream_scratch[...] = jnp.zeros_like(upstream_scratch)
        vectors_ref[0:1] = column_sum(cotangent)

    hidden = hidden_scratch[...]
    width = outer_weight_ref.shape[1]
    at = pl.ds(pl.multiple_of(step * width, width), width)
    inner_weight = inner_weight_ref[:, at]
    outer_weight = outer_weight_ref[at]
    pre = dot(hidden, inner_weight) + inner_bias_ref[at].astype(F32).reshape(1, -1)
    slope = math.sqrt(2.0 / math.pi)
    square = pre * pre
    tanh = jnp.tanh(slope * (pre + 0.044715 * (pre * square)))
    half = 0.5 * (1.0 + tanh)
    active = (pre * half).astype(BF16)
    result_scratch[...] += dot(active, outer_weight)
    derivative = half + (0.5 * slope) * pre * (1.0 - tanh * tanh) * (1.0 + 0.134145 * square)
    grad_pre = against(cotangent, outer_weight) * derivative
    vectors_ref[pl.ds(4 + step, 1)] = column_sum(grad_pre.astype(BF16))
    grad_pre = grad_pre.astype(BF16)
    outer_scratch[...] = across(active, cotangent).reshape(outer_scratch.shape)
    ratio = send_ref.shape[1] // 2
    outer_pairs = outer_scratch.shape[0]
    outer_shape = (outer_pairs, ratio) + send_ref.shape[2:]
    outer_at = (pl.ds(step * outer_pairs, outer_pairs), slice(0, ratio))
    send_ref[outer_at] = outer_scratch[:, 1 - core].reshape(outer_shape).astype(BF16)
    keep_ref[outer_at] = outer_scratch[:, core].reshape(outer_shape).astype(BF16)
    inner_scratch[...] = dot(turned_scratch[...], grad_pre).reshape(inner_scratch.shape)
    send_ref[:, ratio + step] = inner_scratch[:, 1 - core].astype(BF16)
    keep_ref[:, ratio + step] = inner_scratch[:, core].astype(BF16)
    upstream_scratch[...] += against(grad_pre, inner_weight)

    @pl.when(step == steps - 1)
    def _():
        atoms_out_ref[...] = result_scratch[...].astype(BF16).reshape(atoms_out_ref.shape)
        upstream = upstream_scratch[...]
        normed = normed_scratch[...]
        vectors_ref[1:2] = column_sum(upstream * normed)
        vectors_ref[2:3] = column_sum(upstream)
        grad_middle = cotangent.astype(F32) + norm_backward(
            upstream, normed, inverse_scratch[...], as_row(gain_ref)
        )
        grad_middle_ref[...] = grad_middle.reshape(grad_middle_ref.shape)
        branch = grad_middle.astype(BF16)
        vectors_ref[3:4] = column_sum(branch)
        grad_mixed = against(branch, out_weight_ref[...]).astype(BF16)
        molecules, groups, rows, lanes = grad_mixed_ref.shape
        grad_mixed = grad_mixed.reshape(molecules, rows, model_width)
        for t in range(groups):
            grad_mixed_ref[:, t] = grad_mixed[:, :, t * lanes : (t + 1) * lanes]
        turned = jnp.transpose(mixed_rows()).astype(BF16)
        inner_scratch[...] = dot(turned, branch).reshape(inner_scratch.shape)
        send_ref[:, 2 * ratio] = inner_scratch[:, 1 - core].astype(BF16)
        keep_ref[:, 2 * ratio] = inner_scratch[:, core].astype(BF16)
        copy.wait()


def dense(place, mixed, atoms, cotangent, parameters, batch_count, extra):
    (
        out_weight,
        out_bias,
        gain,
        shift,
        inner_weight,
        inner_bias,
        outer_weight,
        outer_bias,
    ) = parameters
    model_width, inner_width = inner_weight.shape
    tokens = atoms.shape[0] * atoms.shape[1]
    width = model_width
    steps = inner_width // width
    pairs = batch_count // 2
    outer_rows = inner_width // batch_count
    outer_pairs = width // (2 * outer_rows)
    own_rows = model_width // batch_count
    operands = (
        place,
        *mixed,
        atoms,
        cotangent,
        out_weight,
        out_bias,
        gain,
        shift,
        inner_weight,
        inner_bias,
        outer_weight,
        outer_bias,
        extra,
    )
    part = near((pairs, 2 * steps + 1, own_rows, model_width), BF16)
    out_shapes = [
        shape_of(atoms.shape, BF16),
        part,
        part,
        near(atoms.shape, F32),
        near((atoms.shape[0], model_width // LANES, atoms.shape[1], LANES), BF16),
        shape_of((4 + steps, model_width), F32),
        near(extra.shape, extra.dtype),
    ]
    fixed = lambda s: pl.BlockSpec(s.shape, lambda *_: (0,) * len(s.shape))
    out_specs = [fixed(s) for s in out_shapes]
    out_specs[1:5] = [near_spec()] * 4
    out_specs[6] = near_spec()
    in_specs = [whole(a) for a in operands[1:]]
    for i, a in enumerate(operands[1:]):
        if i != len(mixed):
            in_specs[i] = near_spec()
    in_specs[-1] = pl.BlockSpec(memory_space=pltpu.HBM)
    return pl.pallas_call(
        functools.partial(dense_kernel, len(mixed)),
        grid_spec=pltpu.PrefetchScalarGridSpec(
            num_scalar_prefetch=1,
            grid=(steps,),
            in_specs=in_specs,
            out_specs=out_specs,
            scratch_shapes=[
                pltpu.VMEM((tokens, model_width), BF16),
                pltpu.VMEM((model_width, tokens), BF16),
                pltpu.VMEM((tokens, model_width), F32),
                pltpu.VMEM((tokens, 1), F32),
                pltpu.VMEM((tokens, model_width), F32),
                pltpu.VMEM((tokens, model_width), F32),
                pltpu.VMEM((outer_pairs, 2, outer_rows, model_width), F32),
                pltpu.VMEM((pairs, 2, own_rows, width), F32),
                pltpu.SemaphoreType.DMA((1,)),
            ],
        ),
        out_shape=out_shapes,
        compiler_params=params(14),
        cost_estimate=pl.CostEstimate(
            flops=12 * tokens * model_width * inner_width,
            transcendentals=tokens * inner_width,
            bytes_accessed=12 * model_width * inner_width,
        ),
        name="dense",
    )(*operands)


def backward_kernel(
    head_size,
    chunk,
    first,
    base,
    start,
    fresh,
    joined,
    place_ref,
    weights_ref,
    cotangent_ref,
    grad_mixed_ref,
    mixed_ref,
    inverse_ref,
    query_ref,
    key_ref,
    value_ref,
    normed_ref,
    query_weight_ref,
    key_weight_ref,
    value_weight_ref,
    *refs,
):
    before_ref = refs[start - 1] if joined else None
    refs = refs[start:]
    pair_grad_ref, near_ref, cross_ref, own_ref, vectors_ref = refs[:5]
    query_grad_ref, key_grad_ref, value_grad_ref = refs[5:8]
    grad_query_scratch, grad_key_scratch, grad_value_scratch, grad_scratch = refs[-4:]
    molecule = pl.program_id(0) + base
    group = pl.program_id(1)
    _, groups, rows, width = query_ref.shape
    keys = key_ref.shape[2]
    heads = width // head_size
    factor = head_size**-0.5
    query = query_ref[molecule, group]
    key = key_ref[molecule, group]
    value = value_ref[molecule, group]
    upstream = grad_mixed_ref[molecule + first, group].astype(F32) * inverse_ref[molecule, group]
    upstream = upstream.astype(BF16)
    offset = (-(upstream.astype(F32) * mixed_ref[molecule, group])).astype(BF16)
    both = jnp.concatenate([upstream, offset], 1)
    lane = lax.broadcasted_iota(jnp.int32, (1, width), 1) // head_size
    lane_pair = lax.broadcasted_iota(jnp.int32, (1, 2 * width), 1) % width // head_size
    query_turned = jnp.transpose(query.astype(F32)).astype(BF16)
    upstream_turned = jnp.transpose(upstream.astype(F32)).astype(BF16)
    query_turned = jnp.concatenate([query_turned] * chunk, 1)
    upstream_turned = jnp.concatenate([upstream_turned] * chunk, 1)
    turned_shape = (chunk * head_size, chunk * rows)
    same = (
        lax.broadcasted_iota(jnp.int32, turned_shape, 0) // head_size
        == lax.broadcasted_iota(jnp.int32, turned_shape, 1) // rows
    )
    zero = jnp.zeros((), BF16)
    total = jnp.zeros((rows, width), F32)
    key_parts = []
    value_parts = []
    for c in range(0, heads, chunk):
        here = slice(c, c + chunk)
        feature = slice(c * head_size, (c + chunk) * head_size)
        spread = jnp.concatenate([jnp.where(lane_pair == c + t, both, zero) for t in range(chunk)], 0)
        centred = against(spread, value)
        there = pl.ds(group * heads + c, chunk)
        weights = weights_ref[molecule, there].reshape(chunk * rows, keys)
        cotangent = cotangent_ref[molecule + first, there].reshape(chunk * rows, keys)
        grad = (weights.astype(F32) * centred + cotangent.astype(F32)).astype(BF16)
        pair_grad_ref[molecule + first, there] = grad.reshape(chunk, rows, keys)
        product = dot(grad, key)
        for t in range(chunk):
            total = jnp.where(lane == c + t, product[t * rows : (t + 1) * rows], total)
        key_parts.append(dot(jnp.where(same, query_turned[feature], zero), grad))
        value_parts.append(dot(jnp.where(same, upstream_turned[feature], zero), weights))
    grad_query_scratch[group] = (total * factor).astype(BF16)
    grad_key_scratch[group] = jnp.transpose(jnp.concatenate(key_parts, 0)).astype(BF16)
    grad_value_scratch[group] = jnp.transpose(jnp.concatenate(value_parts, 0)).astype(BF16)

    if fresh:

        @pl.when((pl.program_id(0) == 0) & (group == 0))
        def _():
            vectors_ref[...] = jnp.zeros_like(vectors_ref)

    @pl.when(group == groups - 1)
    def _():
        row = place_ref[1]
        mine = pl.ds(pl.multiple_of(row * rows, rows), rows)
        join = lambda ref: jnp.concatenate([ref[t] for t in range(groups)], 1)
        grad_query = join(grad_query_scratch)
        grad_key = join(grad_key_scratch)
        grad_value = join(grad_value_scratch)
        query_grad_ref[0] = grad_query
        key_grad_ref[0] = grad_key
        value_grad_ref[0] = grad_value
        grad_scratch[...] = against(grad_key, key_weight_ref[...]) + against(
            grad_value, value_weight_ref[...]
        )
        grad_scratch[mine] += against(grad_query, query_weight_ref[...])
        grad = grad_scratch[...]
        vectors_ref[0:1] += column_sum(grad * normed_ref[molecule].astype(F32))
        vectors_ref[1:2] += column_sum(grad)
        vectors_ref[2:3] += column_sum(grad_query)
        vectors_ref[3:4] += column_sum(grad_value)
        at = lambda other: pl.ds(pl.multiple_of((row ^ other) * rows, rows), rows)
        slot = near_ref.shape[1] - 1
        near_ref[0, slot] = grad_scratch[at(1)].astype(BF16)
        near_ref[1, slot] = grad_scratch[at(3)].astype(BF16)
        if joined:
            near_ref[:, 0] = before_ref[:, 0]
        cross_ref[0] = grad_scratch[at(2)].astype(BF16)
        own_ref[0] = grad_scratch[mine]


def attention_backward(
    head_size, first, base, place, stage, cotangent, grad_mixed, parameters, held, sums, after, before
):
    weights, mixed, inverse, _, normed, query, key, value = stage
    _, head_count, rows, keys = weights.shape
    count = 1
    groups = query.shape[1]
    model_width = groups * LANES
    elements = count * head_count * rows * keys
    operands = [
        place,
        weights,
        cotangent,
        grad_mixed,
        mixed,
        inverse,
        query,
        key,
        value,
        normed,
        *parameters,
    ]
    in_specs = [near_spec()] * (len(operands) - 1)
    aliases = {}
    start = len(operands)
    if sums is not None:
        aliases = {start: 0, start + 1: 4}
        operands += [held, sums]
        in_specs += [near_spec(), near_spec()]
    operands += list(after)
    in_specs += [pl.BlockSpec(memory_space=pl.ANY)] * len(after)
    joined = before is not None
    if joined:
        operands.append(before)
        in_specs.append(near_spec())
    out_shape = [
        near(cotangent.shape, BF16),
        near((2, 1 + joined, rows, model_width), BF16),
        near((count, rows, model_width), BF16),
        near((count, rows, model_width), F32),
        near((8, model_width), F32),
        near((count, rows, model_width), BF16),
        near((count, keys, model_width), BF16),
        near((count, keys, model_width), BF16),
    ]
    out_specs = [
        near_spec(),
        near_spec(),
        near_spec(),
        near_spec(),
        near_spec(),
        near_spec(),
        near_spec(),
        near_spec(),
    ]
    return pl.pallas_call(
        functools.partial(
            backward_kernel, head_size, 4, first, base, len(operands) - start, sums is None, joined
        ),
        grid_spec=pltpu.PrefetchScalarGridSpec(
            num_scalar_prefetch=1,
            grid=(count, groups),
            in_specs=in_specs,
            out_specs=out_specs,
            scratch_shapes=[
                pltpu.VMEM((groups, rows, LANES), BF16),
                pltpu.VMEM((groups, keys, LANES), BF16),
                pltpu.VMEM((groups, keys, LANES), BF16),
                pltpu.VMEM((keys, model_width), F32),
            ],
        ),
        out_shape=out_shape,
        input_output_aliases=aliases,
        compiler_params=params(8),
        cost_estimate=pl.CostEstimate(
            flops=elements * 2 * 768, transcendentals=0, bytes_accessed=elements * 6
        ),
        name="attention_backward",
    )(*operands)


def weight_kernel(calls, stages, place_ref, *refs):
    hidden_refs = refs[:stages]
    grads = refs[stages : stages + 3 * calls]
    out_refs = refs[stages + 3 * calls : -1]
    total_ref = refs[-1]
    rows = grads[0].shape[1]
    row = place_ref[1]
    core = place_ref[2]
    mine = pl.ds(pl.multiple_of(row * rows, rows), rows)
    hidden = [(ref, m) for ref in hidden_refs for m in range(ref.shape[0])]
    width = hidden_refs[0].shape[2]
    own = jnp.concatenate([ref[m, mine] for ref, m in hidden], 0)
    every = jnp.concatenate([ref[m] for ref, m in hidden], 0)
    own = jnp.transpose(own.astype(F32)).astype(BF16)
    every = jnp.transpose(every.astype(F32)).astype(BF16)
    for j, left in enumerate((own, every, every)):
        right = jnp.concatenate([grads[3 * c + j][...].reshape(-1, width) for c in range(calls)], 0)
        total_ref[...] = dot(left, right).reshape(total_ref.shape)
        send_ref, keep_ref = out_refs
        send_ref[:, j] = total_ref[:, 1 - core].astype(BF16)
        keep_ref[:, j] = total_ref[:, core].astype(BF16)


def store_kernel(source_ref, *refs):
    target_ref, semaphore = refs[-2:]
    copy = pltpu.make_async_copy(source_ref, target_ref, semaphore)
    copy.start()
    copy.wait()


def store(array, after):
    return pl.pallas_call(
        store_kernel,
        in_specs=[near_spec()] + [pl.BlockSpec(memory_space=pl.ANY)] * len(after),
        out_specs=pl.BlockSpec(memory_space=pltpu.HBM),
        out_shape=pltpu.HBM(array.shape, array.dtype),
        scratch_shapes=[pltpu.SemaphoreType.DMA],
        compiler_params=params(),
        name="store",
    )(array, *after)


def swap(value, axis, mask):
    size = lax.axis_size(axis)
    return lax.ppermute(value, axis, [(i, i ^ mask) for i in range(size)])


VECTOR_ROWS = 8


def first_sum_kernel(counts, place_ref, *refs):
    terms = sum(counts)
    mine_ref, other_ref = refs[terms : terms + 2]
    along_x_ref, along_y_ref, keep_x_ref, keep_y_ref, vectors_ref = refs[terms + 2 :]
    x, y = place_ref[3], place_ref[4]
    half = along_x_ref.shape[1]
    size = keep_x_ref.shape[1]
    low, high = slice(0, half), slice(half, None)
    row = 0
    start = 0
    for count in counts:
        group = refs[start : start + count]
        start += count
        for s in range(group[0].shape[1]):
            rows = group[0].shape[2]

            def total(at, lanes):
                values = [r[at, s, :, lanes].astype(F32) for r in group]
                return functools.reduce(lambda a, b: a + b, values)

            for k in range(2):
                to = slice(k * size + row, k * size + row + rows)
                here = slice(row, row + rows)
                along_x_ref[to] = total(2 * k + (1 - x), low).astype(BF16)
                keep_x_ref[k, here] = total(2 * k + x, low)
                along_y_ref[to] = total(2 * (1 - y) + k, high).astype(BF16)
                keep_y_ref[k, here] = total(2 * y + k, high)
            row += rows
    vectors = (mine_ref[...] + other_ref[...]).astype(BF16)
    vectors_ref[...] = vectors
    put_vectors(vectors, along_x_ref, along_y_ref)


def put_vectors(vectors, low_ref, high_ref):
    half = vectors.shape[1] // 2
    low_ref[low_ref.shape[0] - VECTOR_ROWS :] = vectors[:, :half]
    high_ref[high_ref.shape[0] - VECTOR_ROWS :] = vectors[:, half:]


def get_vectors(low_ref, high_ref):
    low = low_ref[low_ref.shape[0] - VECTOR_ROWS :]
    return jnp.concatenate([low, high_ref[high_ref.shape[0] - VECTOR_ROWS :]], 1).astype(F32)


def second_sum_kernel(
    place_ref,
    keep_x_ref,
    came_x_ref,
    keep_y_ref,
    came_y_ref,
    vectors_ref,
    send_y_ref,
    send_x_ref,
    left_x_ref,
    left_y_ref,
    vectors_out_ref,
):
    size = keep_x_ref.shape[1]
    for keep, came, send, left, me in (
        (keep_x_ref, came_x_ref, send_y_ref, left_x_ref, place_ref[4]),
        (keep_y_ref, came_y_ref, send_x_ref, left_y_ref, place_ref[3]),
    ):
        at = lambda i: pl.ds(pl.multiple_of(i * size, size), size)
        send[:size] = (keep[1 - me] + came[at(1 - me)].astype(F32)).astype(BF16)
        left[...] = keep[me] + came[at(me)].astype(F32)
    vectors = vectors_ref[...].astype(F32) + get_vectors(came_x_ref, came_y_ref)
    vectors = vectors.astype(BF16)
    vectors_out_ref[...] = vectors
    put_vectors(vectors, send_y_ref, send_x_ref)


def third_sum_kernel(left_x_ref, came_x_ref, left_y_ref, came_y_ref, vectors_ref, total_ref):
    size, half = left_x_ref.shape
    total_ref[:size, :half] = (left_x_ref[...] + came_x_ref[:size].astype(F32)).astype(BF16)
    total_ref[:size, half:] = (left_y_ref[...] + came_y_ref[:size].astype(F32)).astype(BF16)
    vectors = vectors_ref[...].astype(F32) + get_vectors(came_x_ref, came_y_ref)
    total_ref[size : size + VECTOR_ROWS] = vectors.astype(BF16)
    filled = size + VECTOR_ROWS
    if filled < total_ref.shape[0]:
        total_ref[filled:] = jnp.zeros((total_ref.shape[0] - filled, 2 * half), BF16)


def third_cut_kernel(place_ref, *refs):
    third_sum_kernel(*refs[:-1])
    total_ref, sent_ref = refs[-2:]
    half = sent_ref.shape[0]
    away = pl.multiple_of((1 - (place_ref[1] & 1)) * half, half)
    sent_ref[...] = total_ref[pl.ds(away, half)]


def near_sum_kernel(place_ref, total_ref, came_ref, out_ref):
    half = came_ref.shape[0]
    mine = total_ref[pl.ds(pl.multiple_of((place_ref[1] & 1) * half, half), half)]
    out_ref[...] = (mine.astype(F32) + came_ref[...].astype(F32)).astype(BF16)


def far_sum_kernel(left_ref, right_ref, out_ref):
    at = slice(0, out_ref.shape[0])
    out_ref[...] = (left_ref[at].astype(F32) + right_ref[at].astype(F32)).astype(BF16)


def add_kernel(left_ref, right_ref, out_ref):
    out_ref[...] = (left_ref[...].astype(F32) + right_ref[...].astype(F32)).astype(out_ref.dtype)


def join_rows(place, mine_ref, other_ref, out_ref):
    part = mine_ref.shape[0]
    out_ref[pl.ds(pl.multiple_of(place * part, part), part)] = mine_ref[...]
    out_ref[pl.ds(pl.multiple_of((1 - place) * part, part), part)] = other_ref[...]


def finish_kernel(ratio, place_ref, low_ref, came_ref, mine_ref, other_ref, *refs):
    query_ref, key_ref, value_ref, outer_ref, inner_ref, out_ref = refs[:6]
    tail_refs, dense_refs, wide_ref, total_scratch, row_scratch = refs[6:10], refs[10:14], *refs[14:]
    rows, width = out_ref.shape
    total = lambda at: low_ref[at].astype(F32) + came_ref[at].astype(F32)
    for s, ref in enumerate((query_ref, key_ref, value_ref)):
        ref[...] = total(slice(s * rows, (s + 1) * rows))
    put_slices(total(slice(3 * rows, 3 * rows + VECTOR_ROWS)), place_ref[0], tail_refs)
    join_rows(place_ref[1] & 1, mine_ref, other_ref, total_scratch)
    outer_ref[...] = total_scratch[: ratio * rows].astype(F32)
    for s in range(ratio):
        at = (ratio + s) * rows
        inner_ref[:, s * width : (s + 1) * width] = total_scratch[at : at + rows].astype(F32)
    at = 2 * ratio * rows
    out_ref[...] = total_scratch[at : at + rows].astype(F32)
    vectors = total_scratch[at + rows : at + rows + VECTOR_ROWS].astype(F32)
    put_slices(vectors, place_ref[0], dense_refs)
    row_scratch[...] = vectors
    size = wide_ref.shape[0]
    start = place_ref[0] * size
    row = row_scratch[pl.ds(len(dense_refs) + start // width, 1)]
    wide_ref[...] = pltpu.roll(row, lax.rem(width - lax.rem(start, width), width), 1)[0, :size]


def put_slices(vectors, index, refs):
    width, size = vectors.shape[1], refs[0].shape[0]
    turned = pltpu.roll(vectors, lax.rem(width - index * size, width), 1)
    for i, ref in enumerate(refs):
        ref[...] = turned[i, :size]


def small_call(kernel, place, operands, out_shapes, name, after=(), inside=True, scratch=(), mib=4, size=None):
    ahead = 0 if place is None else 1
    count = len(operands)

    def body(*refs):
        kernel(*refs[: ahead + count], *refs[ahead + count + len(after) :])

    if size is None:
        size = sum(math.prod(a.shape) * a.dtype.itemsize for a in list(operands) + list(out_shapes))
    return pl.pallas_call(
        body,
        grid_spec=pltpu.PrefetchScalarGridSpec(
            num_scalar_prefetch=ahead,
            grid=(1,),
            in_specs=[near_spec() for a in operands] + [pl.BlockSpec(memory_space=pl.ANY)] * len(after),
            out_specs=[near_spec() for s in out_shapes],
            scratch_shapes=list(scratch),
        ),
        out_shape=[near(s.shape, s.dtype) if inside else s for s in out_shapes],
        compiler_params=params(mib),
        cost_estimate=pl.CostEstimate(flops=0, transcendentals=0, bytes_accessed=size),
        name=name,
    )(*(() if place is None else (place,)), *operands, *after)


def sum_core(place, groups, vectors, name, after=()):
    groups = [list(g) + [swap(a, "batch", 1) for a in sent] for g, sent in groups]
    vectors_other = swap(vectors, "batch", 1)
    _, _, rows, width = groups[0][0].shape
    size = sum(g[0].shape[1] for g in groups) * rows
    half = width // 2
    counts = tuple(len(g) for g in groups)
    message = shape_of((2 * size + VECTOR_ROWS, half), BF16)
    kept = shape_of((2, size, half), F32)
    along_x, along_y, keep_x, keep_y, vectors = small_call(
        functools.partial(first_sum_kernel, counts),
        place,
        [a for g in groups for a in g] + [vectors, vectors_other],
        [message, message, kept, kept, shape_of(vectors.shape, BF16)],
        name + "_sum_core",
        after,
    )
    came_x, came_y = swap(along_x, "batch", 2), swap(along_y, "batch", 4)
    return (keep_x, came_x, keep_y, came_y, vectors), along_x


def sum_first(place, pieces, name, after=()):
    keep_x, _, _, _, vectors = pieces
    _, size, half = keep_x.shape
    message = shape_of((size + VECTOR_ROWS, half), BF16)
    kept = shape_of((size, half), F32)
    send_y, send_x, left_x, left_y, vectors = small_call(
        second_sum_kernel,
        place,
        pieces,
        [message, message, kept, kept, shape_of(vectors.shape, BF16)],
        name + "_sum_first",
        after,
    )
    came_x, came_y = swap(send_y, "batch", 4), swap(send_x, "batch", 2)
    return (left_x, came_x, left_y, came_y, vectors), send_y


def sum_second(pieces, name, after=()):
    size, half = pieces[0].shape
    rows = -(-(size + VECTOR_ROWS) // 32) * 32
    shape = shape_of((rows, 2 * half), BF16)
    return small_call(third_sum_kernel, None, pieces, [shape], name + "_sum_second", after)[0]


def sum_second_cut(place, pieces, name, after=()):
    size, half = pieces[0].shape
    rows = -(-(size + VECTOR_ROWS) // 32) * 32
    total, sent = small_call(
        third_cut_kernel,
        place,
        pieces,
        [shape_of((rows, 2 * half), BF16), shape_of((rows // 2, 2 * half), BF16)],
        name + "_sum_second",
        after,
    )
    return total, swap(sent, "rows", 1)


def batch_slices_any(groups, vectors):
    me = lax.axis_index("batch")
    bits = lax.axis_size("batch").bit_length() - 1
    pieces = []
    for kept, sent in groups:
        values = [a.astype(F32) for a in kept] + [swap(a, "batch", 1).astype(F32) for a in sent]
        pieces.append(functools.reduce(lambda a, b: a + b, values))
    total = jnp.concatenate(pieces, 1)
    total = total.reshape((2,) * (bits - 1) + total.shape[1:])
    for bit in range(bits - 1, 0, -1):
        mine = (me >> bit) & 1
        sent = lax.dynamic_index_in_dim(total, 1 - mine, 0, keepdims=False).astype(BF16)
        total = lax.dynamic_index_in_dim(total, mine, 0, keepdims=False)
        total = total + swap(sent, "batch", 1 << bit).astype(F32)
    total = lax.psum(total.astype(BF16), "rows").astype(F32)
    return total, lax.psum(vectors, ("batch", "rows"))


def cross_kernel(count, *refs):
    out_ref = refs[-1]
    came = [(ref, i) for ref in refs[count:-1] for i in range(ref.shape[1])]
    for m, (term, (ref, i)) in enumerate(zip(refs[:count], came)):
        out_ref[m] = (term[0].astype(F32) + ref[1, i].astype(F32)).astype(BF16)


def cross_sum(terms, came, name, after=()):
    shape = (len(terms),) + terms[0].shape[1:]
    return small_call(
        functools.partial(cross_kernel, len(terms)),
        None,
        list(terms) + list(came),
        [shape_of(shape, BF16)],
        name,
        after,
    )[0]


def final_kernel(count, *refs):
    owns, nears, crosses = refs[:count], refs[count : 2 * count], refs[2 * count : 3 * count]
    atoms_ref, gain_ref, shift_ref, grad_middle_ref, out_ref = refs[3 * count :]
    gain = as_row(gain_ref)
    shift = as_row(shift_ref)
    for m in range(count):
        grad = owns[m][0] + nears[m][...].astype(F32) + crosses[m][...].astype(F32)
        _, normed, inverse = norm_forward(atoms_ref[m].astype(F32), gain, shift)
        result = grad_middle_ref[m] + norm_backward(grad, normed, inverse, gain)
        out_ref[m] = result.astype(BF16)


def first_norm_backward(owns, nears, crosses, others, after=()):
    count = len(owns)
    arrays = [a for a, _ in nears + crosses]
    spots = [at for _, at in nears + crosses]

    def kernel(*refs):
        picked = [r.at[at] for r, at in zip(refs[count : 3 * count], spots)]
        final_kernel(count, *refs[:count], *picked, *refs[3 * count :])

    return small_call(
        kernel,
        None,
        list(owns) + arrays + list(others),
        [shape_of(others[0].shape, BF16)],
        "first_norm_backward",
        after,
        inside=False,
    )[0]


def shards(
    atoms,
    pair_bias,
    lengths,
    first_gain,
    first_shift,
    query_weight,
    query_bias,
    key_weight,
    value_weight,
    value_bias,
    out_weight,
    out_bias,
    second_gain,
    second_shift,
    inner_weight,
    inner_bias,
    outer_weight,
    outer_bias,
    atoms_cotangent,
    pair_cotangent,
):
    molecules, rows, model_width = atoms.shape
    head_count = pair_bias.shape[1]
    head_size = model_width // head_count
    batch_count = lax.axis_size("batch")
    batch_index = lax.axis_index("batch")
    row = lax.axis_index("rows")
    (
        atoms_far,
        pair_bias,
        first_gain,
        first_shift,
        query_weight,
        query_bias,
        key_weight,
        value_weight,
        value_bias,
        out_weight,
        out_bias,
        second_gain,
        second_shift,
        inner_weight,
        inner_bias,
        outer_weight,
        outer_bias,
        atoms_cotangent,
        pair_cotangent,
    ) = [
        pltpu.with_memory_space_constraint(a, pltpu.HBM)
        for a in (
            atoms,
            pair_bias,
            first_gain,
            first_shift,
            query_weight,
            query_bias,
            key_weight,
            value_weight,
            value_bias,
            out_weight,
            out_bias,
            second_gain,
            second_shift,
            inner_weight,
            inner_bias,
            outer_weight,
            outer_bias,
            atoms_cotangent,
            pair_cotangent,
        )
    ]
    place = jnp.stack(
        [batch_index, row, batch_index & 1, (batch_index >> 1) & 1, (batch_index >> 2) & 1]
    ).astype(jnp.int32)
    line = lambda v: v
    count = molecules // STAGES
    stages = []
    pair_out = jnp.zeros((1,), BF16)
    one = swap(atoms, "rows", 1)
    (
        pair_near,
        query_near,
        key_near,
        value_near,
        first_gain,
        first_shift,
        query_bias,
        value_bias,
        out_bias,
        second_gain,
        second_shift,
        inner_bias,
        outer_bias,
        out_weight,
        inner_weight,
        outer_weight,
        atoms_cotangent,
    ) = load(
        [
            pair_bias,
            query_weight,
            key_weight,
            value_weight,
            first_gain,
            first_shift,
            query_bias,
            value_bias,
            out_bias,
            second_gain,
            second_shift,
            inner_bias,
            outer_bias,
            out_weight,
            inner_weight,
            outer_weight,
            atoms_cotangent,
        ],
        "load_first",
        None,
        (place,),
    )
    projected = near_half(
        head_size,
        STAGES,
        place,
        atoms_far,
        one,
        (
            first_gain,
            first_shift,
            query_near,
            query_bias,
            key_near,
            value_near,
            value_bias,
        ),
        (),
    )
    mine = [atoms[:count], projected[-1]]
    gathered = [[swap(a, "rows", mask) for mask in (2, 3)] for a in mine]
    for stage in range(STAGES):
        pair_out, kept, _ = attention_forward(
            head_size,
            stage * count,
            place,
            lengths,
            gathered[stage],
            pair_near,
            (first_gain, first_shift, key_near, value_near, value_bias),
            projected[5 * stage : 5 * stage + 5],
            pair_out,
            [],
        )
        stages.append(kept)
    (
        atoms_out,
        send,
        keep,
        grad_middle,
        grad_mixed,
        dense_vectors,
        pair_cotangent,
    ) = dense(
        place,
        [s[1] for s in stages],
        atoms,
        atoms_cotangent,
        (
            out_weight,
            line(out_bias),
            line(second_gain),
            line(second_shift),
            inner_weight,
            line(inner_bias),
            outer_weight,
            line(outer_bias),
        ),
        batch_count,
        pair_cotangent,
    )
    pairs = batch_count // 2
    own_rows = model_width // batch_count
    dense_groups = [([keep], [send])]
    usual = batch_count == 8

    def backward(molecule, held, sums, after, before=None):
        stage = molecule // count
        return attention_backward(
            head_size,
            stage * count,
            molecule % count,
            place,
            stages[stage],
            pair_cotangent,
            grad_mixed,
            (query_near, key_near, value_near),
            held,
            sums,
            after,
            before,
        )

    pair_grad, near0, cross0, own0, sums, *grads0 = backward(0, None, None, [])
    after = []
    if usual:
        dense_pieces, held = sum_core(place, dense_groups, dense_vectors, "dense", (own0,))
        after = [held]
    else:
        dense_total, dense_vectors = batch_slices_any(dense_groups, dense_vectors)
    pair_grad, near1, cross1, own1, sums, *grads1 = backward(1, pair_grad, sums, after, near0)
    near1 = swap(near1, "rows", 1)
    pair_grad, near2, cross2, own2, sums, *grads2 = backward(2, pair_grad, sums, [own1])
    near2 = swap(near2, "rows", 1)
    cross0 = cross_sum([cross0, cross1], [near1], "cross_first", (own2,))
    far0 = swap(cross0, "rows", 2)
    pair_grad, near3, cross3, own3, tail_vectors, *grads3 = backward(3, pair_grad, sums, [cross0])
    near3 = swap(near3, "rows", 1)
    owns = [own0, own1, own2, own3]
    after = [far0]
    if usual:
        dense_pieces, held = sum_first(place, dense_pieces, "dense", (own3,))
        after.append(held)
    part = shape_of((pairs, 3, own_rows, model_width), BF16)
    send, keep = small_call(
        functools.partial(weight_kernel, 4, STAGES),
        place,
        [s[3] for s in stages] + grads0 + grads1 + grads2 + grads3,
        [part] * 2,
        "attention_weights",
        after,
        scratch=[pltpu.VMEM((pairs, 2, own_rows, model_width), F32)],
        mib=14,
    )
    groups = [([keep], [send])]
    matrix = shape_of((own_rows, model_width), F32)
    ratio = inner_weight.shape[1] // model_width
    vector = shape_of((own_rows,), F32)
    finish = (atoms, line(first_gain), line(first_shift), grad_middle)
    if usual:
        pieces, held = sum_core(place, groups, tail_vectors, "tail")
        cross2 = cross_sum([cross2, cross3], [near2, near3], "cross_second", (held,))
        far2 = swap(cross2, "rows", 2)
        dense_total, came = sum_second_cut(place, dense_pieces, "dense", (cross2,))
        pieces, held = sum_first(place, pieces, "tail", (dense_total,))
        start = dense_total.shape[0] // 2
        mine = small_call(
            near_sum_kernel, place, [dense_total, came], [came], "dense_near_sum", (held, far2)
        )[0]
        far = swap(mine, "rows", 2)
        total = sum_second(pieces, "tail", (mine,))
        tail_came = swap(total, "rows", 1)
        total = small_call(add_kernel, None, [total, tail_came], [total], "tail_near_sum")[0]
        tail_came = swap(total, "rows", 2)
        part = shape_of((start, model_width), BF16)
        mine = small_call(far_sum_kernel, None, [mine, far], [part], "dense_far_sum", (total,))[0]
        other = swap(mine, "rows", 1)
        pair_grad = store(pair_grad, (mine,))
        atoms_grad = first_norm_backward(
            owns,
            [(near1, (0, 0)), (near1, (0, 1)), (near2, (0, 0)), (near3, (0, 0))],
            [(far0, 0), (far0, 1), (far2, 0), (far2, 1)],
            finish,
            (mine,),
        )
        outs = small_call(
            functools.partial(finish_kernel, ratio),
            place,
            [total, tail_came, mine, other],
            [matrix] * 3
            + [
                shape_of((ratio * own_rows, model_width), F32),
                shape_of((own_rows, ratio * model_width), F32),
                matrix,
            ]
            + [vector] * 8
            + [shape_of((ratio * own_rows,), F32)],
            "finish",
            inside=False,
            scratch=[
                pltpu.VMEM((2 * part.shape[0], model_width), BF16),
                pltpu.VMEM((VECTOR_ROWS, model_width), F32),
            ],
        )
        query_grad, key_grad, value_grad, outer_grad, inner_grad, out_grad = outs[:6]
        tail_parts, dense_parts = outs[6:10], outs[10:]
    else:
        pair_grad = store(pair_grad, ())
        far2 = swap(cross_sum([cross2, cross3], [near2, near3], "cross_second"), "rows", 2)
        atoms_grad = first_norm_backward(
            owns,
            [(near1, (0, 0)), (near1, (0, 1)), (near2, (0, 0)), (near3, (0, 0))],
            [(far0, 0), (far0, 1), (far2, 0), (far2, 1)],
            finish,
        )
        total, tail_vectors = batch_slices_any(groups, tail_vectors)
        query_grad, key_grad, value_grad = total[0], total[1], total[2]
        outer_grad = dense_total[:ratio].reshape(-1, model_width)
        inner_grad = dense_total[ratio : 2 * ratio].transpose(1, 0, 2).reshape(own_rows, -1)
        out_grad = dense_total[2 * ratio]
        part = lambda v: lax.dynamic_slice_in_dim(
            v, batch_index * (v.shape[0] // batch_count), v.shape[0] // batch_count
        )
        tail_parts = [part(v) for v in tail_vectors[:4]]
        dense_parts = [part(v) for v in dense_vectors[:4]] + [part(dense_vectors[4:].reshape(-1))]
    return (
        atoms_out,
        pair_out,
        atoms_grad,
        pair_grad,
        tail_parts[0],
        tail_parts[1],
        query_grad,
        tail_parts[2],
        key_grad,
        value_grad,
        tail_parts[3],
        out_grad,
        dense_parts[3],
        dense_parts[1],
        dense_parts[2],
        inner_grad,
        dense_parts[4],
        outer_grad,
        dense_parts[0],
    )


def solution(mesh):
    tokens = P("batch", "rows", None)
    pairs = P("batch", None, "rows", None)
    vector = P("batch")
    matrix = P("batch", None)
    return jax.shard_map(
        shards,
        mesh=mesh,
        in_specs=(tokens, pairs, P("batch")) + (P(),) * 15 + (tokens, pairs),
        out_specs=(
            tokens,
            pairs,
            tokens,
            pairs,
            vector,
            vector,
            matrix,
            vector,
            matrix,
            matrix,
            vector,
            matrix,
            vector,
            vector,
            vector,
            matrix,
            vector,
            matrix,
            vector,
        ),
        check_vma=False,
    )
```

```python
import functools
import math

import jax
import jax.numpy as jnp
from jax import lax
from jax.experimental import pallas as pl
from jax.experimental.pallas import tpu as pltpu
from jax.sharding import PartitionSpec as P

EPSILON = 1e-05
MASKED = -1000000000.0
F32 = jnp.float32
BF16 = jnp.bfloat16
LANES = 128
STAGES = 2
VMEM_LIMIT = 18 << 20


def shape_of(shape, dtype):
    return jax.ShapeDtypeStruct(tuple(shape), dtype)


def norm_forward(values_in, gain, shift):
    centre = values_in - jnp.mean(values_in, -1, keepdims=True)
    inverse = lax.rsqrt(jnp.mean(centre * centre, -1, keepdims=True) + EPSILON)
    normed = centre * inverse
    return (normed * gain + shift, normed, inverse)


def norm_backward(upstream, normed, inverse, gain):
    scaled = upstream * gain
    return inverse * (
        scaled
        - jnp.mean(scaled, -1, keepdims=True)
        - normed * jnp.mean(scaled * normed, -1, keepdims=True)
    )


def dot(left, right):
    return jnp.dot(left, right, preferred_element_type=F32)


def across(left, right):
    return lax.dot_general(left, right, (((0,), (0,)), ((), ())), preferred_element_type=F32)


def against(left, right):
    return lax.dot_general(left, right, (((1,), (1,)), ((), ())), preferred_element_type=F32)


def column_sum(values_in):
    return jnp.sum(values_in.astype(F32), 0, keepdims=True)


def near(shape, dtype):
    return pltpu.VMEM(tuple(shape), dtype)


def near_spec():
    return pl.BlockSpec(memory_space=pltpu.VMEM)


def as_row(ref):
    return ref[...].astype(F32).reshape(1, -1)


def whole(array):
    return pl.BlockSpec(array.shape, lambda *_: (0,) * array.ndim)


def params(mib=10):
    return pltpu.CompilerParams(vmem_limit_bytes=mib << 20)


def load_kernel(count, starts, *refs):
    sources, targets, semaphores = refs[:count], refs[-count - 1 : -1], refs[-1]
    copies = [
        pltpu.make_async_copy(source.at[pl.ds(start, target.shape[0])], target, semaphores.at[i])
        for i, (source, target, start) in enumerate(zip(sources, targets, starts))
    ]
    for copy in copies:
        copy.start()
    for copy in copies:
        copy.wait()


def copies_beside(sources, targets, semaphores):
    return [
        pltpu.make_async_copy(source, target, semaphores.at[i])
        for i, (source, target) in enumerate(zip(sources, targets))
    ]


def load(arrays, name, starts=None, after=()):
    count = len(arrays)
    starts = starts or (0,) * count
    return pl.pallas_call(
        functools.partial(load_kernel, count, starts),
        in_specs=[pl.BlockSpec(memory_space=pltpu.HBM)] * count
        + [pl.BlockSpec(memory_space=pl.ANY)] * len(after),
        out_specs=[near_spec()] * count,
        out_shape=[
            near((a.shape[0] - start,) + a.shape[1:], a.dtype) for a, start in zip(arrays, starts)
        ],
        scratch_shapes=[pltpu.SemaphoreType.DMA((count,))],
        compiler_params=params(),
        name=name,
    )(*arrays, *after)


def project(pieces, first, parameters, row, refs, atoms_scratch):
    gain_ref, shift_ref, key_weight_ref, value_weight_ref, value_bias_ref = parameters
    hidden_ref, normed_ref, key_ref, value_ref = refs
    count = hidden_ref.shape[0]
    _, groups, keys, width = key_ref.shape
    rows = keys // 4
    half = 2 * rows
    model_width = hidden_ref.shape[2]
    for m in range(count):
        for i, piece in enumerate(pieces):
            start = pl.multiple_of(m * half + ((row ^ i) & 1) * rows, rows)
            atoms_scratch[pl.ds(start, rows)] = piece[m + first]
    hidden, normed, _ = norm_forward(
        atoms_scratch[...].astype(F32), as_row(gain_ref), as_row(shift_ref)
    )
    hidden = hidden.astype(BF16)
    normed = normed.astype(BF16)
    key_rows = dot(hidden, key_weight_ref[...]).astype(BF16)
    value_rows = (dot(hidden, value_weight_ref[...]) + as_row(value_bias_ref)).astype(BF16)
    return [a.reshape(count, half, model_width) for a in (hidden, normed, key_rows, value_rows)]


def put_half(values, at, refs):
    hidden, normed, key_rows, value_rows = values
    hidden_ref, normed_ref, key_ref, value_ref = refs
    count, groups, _, width = key_ref.shape
    half = hidden.shape[1]
    ones = jnp.ones((count, half, width), BF16)
    hidden_ref[:, at] = hidden
    normed_ref[:, at] = normed
    for t in range(groups):
        lanes = slice(t * width, (t + 1) * width)
        key_ref[:, t, at] = key_rows[:, :, lanes]
        value_ref[:, t, at, :width] = value_rows[:, :, lanes]
        value_ref[:, t, at, width:] = ones


def half_rows(row, other, rows):
    which = row >> 1
    which = 1 - which if other else which
    return pl.ds(pl.multiple_of(which * 2 * rows, 2 * rows), 2 * rows)


def near_half_kernel(
    head_size,
    stages,
    ahead,
    place_ref,
    own_ref,
    one_ref,
    gain_ref,
    shift_ref,
    query_weight_ref,
    query_bias_ref,
    key_weight_ref,
    value_weight_ref,
    value_bias_ref,
    *refs,
):
    refs = refs[ahead:]
    later_ref, atoms_scratch = refs[-2:]
    later_ref[...] = own_ref[own_ref.shape[0] - later_ref.shape[0] :]
    row = place_ref[1]
    rows, model_width = own_ref.shape[1:]
    factor = head_size**-0.5
    parameters = (gain_ref, shift_ref, key_weight_ref, value_weight_ref, value_bias_ref)
    for stage in range(stages):
        hidden_ref, normed_ref, key_ref, value_ref, query_ref = refs[5 * stage : 5 * stage + 5]
        outs = (hidden_ref, normed_ref, key_ref, value_ref)
        count, groups, _, width = key_ref.shape
        values = project((own_ref, one_ref), stage * count, parameters, row, outs, atoms_scratch)
        put_half(values, half_rows(row, False, rows), outs)
        mine = pl.ds(pl.multiple_of(row * rows, rows), rows)
        own = jnp.concatenate([hidden_ref[m, mine] for m in range(count)], 0)
        query_rows = (dot(own, query_weight_ref[...]) + as_row(query_bias_ref)) * factor
        query_rows = query_rows.astype(BF16).reshape(count, rows, model_width)
        for t in range(groups):
            query_ref[:, t] = query_rows[:, :, t * width : (t + 1) * width]


def near_half(head_size, stages, place, atoms, one, parameters, after):
    molecules, rows, model_width = atoms.shape
    keys = 4 * rows
    count = molecules // stages
    groups = model_width // LANES
    operands = (place, atoms, one, *parameters, *after)
    return pl.pallas_call(
        functools.partial(near_half_kernel, head_size, stages, len(after)),
        grid_spec=pltpu.PrefetchScalarGridSpec(
            num_scalar_prefetch=1,
            grid=(1,),
            in_specs=[whole(atoms), near_spec()]
            + [near_spec() for a in parameters]
            + [pl.BlockSpec(memory_space=pl.ANY)] * len(after),
            out_specs=[near_spec()] * (5 * stages + 1),
            scratch_shapes=[pltpu.VMEM((count * 2 * rows, model_width), BF16)],
        ),
        out_shape=[
            near((count, keys, model_width), BF16),
            near((count, keys, model_width), BF16),
            near((count, groups, keys, LANES), BF16),
            near((count, groups, keys, 2 * LANES), BF16),
            near((count, groups, rows, LANES), BF16),
        ]
        * stages
        + [near((molecules - count, rows, model_width), BF16)],
        compiler_params=params(10),
        name="near_half",
    )(*operands)


def forward_kernel(
    head_size,
    chunk,
    first,
    extra,
    place_ref,
    length_ref,
    two_ref,
    three_ref,
    pair_ref,
    query_ref,
    gain_ref,
    shift_ref,
    key_weight_ref,
    value_weight_ref,
    value_bias_ref,
    *refs,
):
    (
        pair_out_ref,
        weights_ref,
        mixed_ref,
        inverse_ref,
        hidden_ref,
        normed_ref,
        key_ref,
        value_ref,
    ) = refs[5 + extra : 13 + extra]
    atoms_scratch, semaphores = refs[-2:]
    copies = copies_beside(refs[5 : 5 + extra], refs[13 + extra : 13 + 2 * extra], semaphores)
    molecule = pl.program_id(0)
    group = pl.program_id(1)
    count, groups, keys, width = key_ref.shape
    heads = width // head_size
    rows = query_ref.shape[2]

    @pl.when((molecule == 0) & (group == 0))
    def _():
        for copy in copies:
            copy.start()
        row = place_ref[1]
        outs = (hidden_ref, normed_ref, key_ref, value_ref)
        parameters = (gain_ref, shift_ref, key_weight_ref, value_weight_ref, value_bias_ref)
        values = project((two_ref, three_ref), 0, parameters, row, outs, atoms_scratch)
        put_half(values, half_rows(row, True, rows), outs)

    query = query_ref[molecule, group]
    key = key_ref[molecule, group]
    value = value_ref[molecule, group]
    valid = lax.broadcasted_iota(jnp.int32, (1, keys), 1) < length_ref[molecule + first]
    lane = lax.broadcasted_iota(jnp.int32, (1, width), 1) // head_size
    lane_pair = lax.broadcasted_iota(jnp.int32, (1, 2 * width), 1) % width // head_size
    total = jnp.zeros((rows, 2 * width), F32)
    zero = jnp.zeros((), BF16)
    for c in range(0, heads, chunk):
        here = slice(c, c + chunk)
        there = pl.ds(group * heads + c, chunk)
        spread = jnp.concatenate([jnp.where(lane == c + t, query, zero) for t in range(chunk)], 0)
        pair = pair_ref[molecule + first, there].reshape(chunk * rows, keys)
        scores = against(spread, key) + pair.astype(F32)
        pair_out_ref[0, here] = scores.astype(BF16).reshape(chunk, rows, keys)
        masked = jnp.where(valid, scores, MASKED)
        weights = jnp.exp(masked - jnp.max(masked, -1, keepdims=True)).astype(BF16)
        weights_ref[molecule, there] = weights.reshape(chunk, rows, keys)
        product = dot(weights, value)
        for t in range(chunk):
            total = jnp.where(lane_pair == c + t, product[t * rows : (t + 1) * rows], total)
    inverse = 1.0 / total[:, width:]
    inverse_ref[molecule, group] = inverse
    mixed_ref[molecule, group] = total[:, :width] * inverse

    @pl.when((molecule == count - 1) & (group == groups - 1))
    def _():
        for copy in copies:
            copy.wait()


def attention_forward(
    head_size, first, place, lengths, pieces, pair_bias, parameters, projected, held, extra
):
    _, head_count, rows, keys = pair_bias.shape
    hidden, normed, key, value, query = projected
    count, groups = key.shape[:2]
    model_width = groups * LANES
    heads = LANES // head_size
    pair_spec = pl.BlockSpec((1, heads, rows, keys), lambda m, g, *_: (m + first, g, 0, 0))
    elements = count * head_count * rows * keys
    operands = [place, lengths, *pieces, pair_bias, query, *parameters]
    in_specs = [near_spec()] * (len(pieces) + 2)
    in_specs += [near_spec() for a in parameters]
    start = len(operands)
    operands += [hidden, normed, key, value, held]
    in_specs += [near_spec()] * 4 + [pl.BlockSpec(memory_space=pl.ANY)]
    aliases = {start + i: 4 + i for i in range(4)}
    if held.ndim > 1:
        aliases[start + 4] = 0
    operands += extra
    in_specs += [pl.BlockSpec(memory_space=pltpu.HBM)] * len(extra)
    outs = pl.pallas_call(
        functools.partial(forward_kernel, head_size, 4, first, len(extra)),
        grid_spec=pltpu.PrefetchScalarGridSpec(
            num_scalar_prefetch=2,
            grid=(count, groups),
            in_specs=in_specs,
            out_specs=[pair_spec] + [near_spec()] * (7 + len(extra)),
            scratch_shapes=[
                pltpu.VMEM((count * 2 * rows, model_width), BF16),
                pltpu.SemaphoreType.DMA((max(len(extra), 1),)),
            ],
        ),
        out_shape=[
            shape_of(pair_bias.shape, BF16),
            near((count, head_count, rows, keys), BF16),
            near((count, groups, rows, LANES), F32),
            near((count, groups, rows, LANES), F32),
            near(hidden.shape, BF16),
            near(normed.shape, BF16),
            near(key.shape, BF16),
            near(value.shape, BF16),
        ]
        + [near(a.shape, a.dtype) for a in extra],
        input_output_aliases=aliases,
        compiler_params=params(10),
        cost_estimate=pl.CostEstimate(
            flops=elements * 2 * 384, transcendentals=elements, bytes_accessed=elements * 6
        ),
        name="attention_forward",
    )(*operands)
    pair_out, weights, mixed, inverse, hidden, normed, key, value = outs[:8]
    return pair_out, (weights, mixed, inverse, hidden, normed, query, key, value), outs[8:]


def dense_kernel(
    mixed_count,
    place_ref,
    *refs,
):
    mixed_refs = refs[:mixed_count]
    (
        atoms_ref,
        cotangent_ref,
        out_weight_ref,
        out_bias_ref,
        gain_ref,
        shift_ref,
        inner_weight_ref,
        inner_bias_ref,
        outer_weight_ref,
        outer_bias_ref,
        far_ref,
        atoms_out_ref,
        send_ref,
        keep_ref,
        grad_middle_ref,
        grad_mixed_ref,
        vectors_ref,
        copied_ref,
        hidden_scratch,
        turned_scratch,
        normed_scratch,
        inverse_scratch,
        result_scratch,
        upstream_scratch,
        outer_scratch,
        inner_scratch,
        semaphores,
    ) = refs[mixed_count:]
    (copy,) = copies_beside([far_ref], [copied_ref], semaphores)
    step = pl.program_id(0)
    steps = pl.num_programs(0)
    core = place_ref[2]
    tokens, model_width = hidden_scratch.shape
    cotangent = cotangent_ref[...].reshape(tokens, model_width)

    def mixed_rows():
        parts = []
        for ref in mixed_refs:
            count, groups, rows, width = ref.shape
            join = [ref[:, t].reshape(count * rows, width) for t in range(groups)]
            parts.append(jnp.concatenate(join, 1))
        return jnp.concatenate(parts, 0)

    @pl.when(step == 0)
    def _():
        copy.start()
        mixed_low = mixed_rows().astype(BF16)
        middle = (
            atoms_ref[...].reshape(tokens, model_width).astype(F32)
            + dot(mixed_low, out_weight_ref[...])
            + as_row(out_bias_ref)
        )
        hidden, normed, inverse = norm_forward(
            middle, as_row(gain_ref), as_row(shift_ref)
        )
        hidden_scratch[...] = hidden.astype(BF16)
        turned_scratch[...] = jnp.transpose(hidden).astype(BF16)
        normed_scratch[...] = normed
        inverse_scratch[...] = inverse
        result_scratch[...] = middle + as_row(outer_bias_ref)
        upstream_scratch[...] = jnp.zeros_like(upstream_scratch)
        vectors_ref[0:1] = column_sum(cotangent)

    hidden = hidden_scratch[...]
    width = outer_weight_ref.shape[1]
    at = pl.ds(pl.multiple_of(step * width, width), width)
    inner_weight = inner_weight_ref[:, at]
    outer_weight = outer_weight_ref[at]
    pre = dot(hidden, inner_weight) + inner_bias_ref[at].astype(F32).reshape(1, -1)
    slope = math.sqrt(2.0 / math.pi)
    square = pre * pre
    tanh = jnp.tanh(slope * (pre + 0.044715 * (pre * square)))
    half = 0.5 * (1.0 + tanh)
    active = (pre * half).astype(BF16)
    result_scratch[...] += dot(active, outer_weight)
    derivative = half + (0.5 * slope) * pre * (1.0 - tanh * tanh) * (1.0 + 0.134145 * square)
    grad_pre = against(cotangent, outer_weight) * derivative
    vectors_ref[pl.ds(4 + step, 1)] = column_sum(grad_pre.astype(BF16))
    grad_pre = grad_pre.astype(BF16)
    outer_scratch[...] = across(active, cotangent).reshape(outer_scratch.shape)
    ratio = send_ref.shape[1] // 2
    outer_pairs = outer_scratch.shape[0]
    outer_shape = (outer_pairs, ratio) + send_ref.shape[2:]
    outer_at = (pl.ds(step * outer_pairs, outer_pairs), slice(0, ratio))
    send_ref[outer_at] = outer_scratch[:, 1 - core].reshape(outer_shape).astype(BF16)
    keep_ref[outer_at] = outer_scratch[:, core].reshape(outer_shape).astype(BF16)
    inner_scratch[...] = dot(turned_scratch[...], grad_pre).reshape(inner_scratch.shape)
    send_ref[:, ratio + step] = inner_scratch[:, 1 - core].astype(BF16)
    keep_ref[:, ratio + step] = inner_scratch[:, core].astype(BF16)
    upstream_scratch[...] += against(grad_pre, inner_weight)

    @pl.when(step == steps - 1)
    def _():
        atoms_out_ref[...] = result_scratch[...].astype(BF16).reshape(atoms_out_ref.shape)
        upstream = upstream_scratch[...]
        normed = normed_scratch[...]
        vectors_ref[1:2] = column_sum(upstream * normed)
        vectors_ref[2:3] = column_sum(upstream)
        grad_middle = cotangent.astype(F32) + norm_backward(
            upstream, normed, inverse_scratch[...], as_row(gain_ref)
        )
        grad_middle_ref[...] = grad_middle.reshape(grad_middle_ref.shape)
        branch = grad_middle.astype(BF16)
        vectors_ref[3:4] = column_sum(branch)
        grad_mixed = against(branch, out_weight_ref[...]).astype(BF16)
        molecules, groups, rows, lanes = grad_mixed_ref.shape
        grad_mixed = grad_mixed.reshape(molecules, rows, model_width)
        for t in range(groups):
            grad_mixed_ref[:, t] = grad_mixed[:, :, t * lanes : (t + 1) * lanes]
        turned = jnp.transpose(mixed_rows()).astype(BF16)
        inner_scratch[...] = dot(turned, branch).reshape(inner_scratch.shape)
        send_ref[:, 2 * ratio] = inner_scratch[:, 1 - core].astype(BF16)
        keep_ref[:, 2 * ratio] = inner_scratch[:, core].astype(BF16)
        copy.wait()


def dense(place, mixed, atoms, cotangent, parameters, batch_count, extra):
    (
        out_weight,
        out_bias,
        gain,
        shift,
        inner_weight,
        inner_bias,
        outer_weight,
        outer_bias,
    ) = parameters
    model_width, inner_width = inner_weight.shape
    tokens = atoms.shape[0] * atoms.shape[1]
    width = model_width
    steps = inner_width // width
    pairs = batch_count // 2
    outer_rows = inner_width // batch_count
    outer_pairs = width // (2 * outer_rows)
    own_rows = model_width // batch_count
    operands = (
        place,
        *mixed,
        atoms,
        cotangent,
        out_weight,
        out_bias,
        gain,
        shift,
        inner_weight,
        inner_bias,
        outer_weight,
        outer_bias,
        extra,
    )
    part = near((pairs, 2 * steps + 1, own_rows, model_width), BF16)
    out_shapes = [
        shape_of(atoms.shape, BF16),
        part,
        part,
        near(atoms.shape, F32),
        near((atoms.shape[0], model_width // LANES, atoms.shape[1], LANES), BF16),
        shape_of((4 + steps, model_width), F32),
        near(extra.shape, extra.dtype),
    ]
    fixed = lambda s: pl.BlockSpec(s.shape, lambda *_: (0,) * len(s.shape))
    out_specs = [fixed(s) for s in out_shapes]
    out_specs[1:5] = [near_spec()] * 4
    out_specs[6] = near_spec()
    in_specs = [whole(a) for a in operands[1:]]
    for i, a in enumerate(operands[1:]):
        if i != len(mixed):
            in_specs[i] = near_spec()
    in_specs[-1] = pl.BlockSpec(memory_space=pltpu.HBM)
    return pl.pallas_call(
        functools.partial(dense_kernel, len(mixed)),
        grid_spec=pltpu.PrefetchScalarGridSpec(
            num_scalar_prefetch=1,
            grid=(steps,),
            in_specs=in_specs,
            out_specs=out_specs,
            scratch_shapes=[
                pltpu.VMEM((tokens, model_width), BF16),
                pltpu.VMEM((model_width, tokens), BF16),
                pltpu.VMEM((tokens, model_width), F32),
                pltpu.VMEM((tokens, 1), F32),
                pltpu.VMEM((tokens, model_width), F32),
                pltpu.VMEM((tokens, model_width), F32),
                pltpu.VMEM((outer_pairs, 2, outer_rows, model_width), F32),
                pltpu.VMEM((pairs, 2, own_rows, width), F32),
                pltpu.SemaphoreType.DMA((1,)),
            ],
        ),
        out_shape=out_shapes,
        compiler_params=params(14),
        cost_estimate=pl.CostEstimate(
            flops=12 * tokens * model_width * inner_width,
            transcendentals=tokens * inner_width,
            bytes_accessed=12 * model_width * inner_width,
        ),
        name="dense",
    )(*operands)


def backward_kernel(
    head_size,
    chunk,
    first,
    base,
    start,
    fresh,
    joined,
    place_ref,
    weights_ref,
    cotangent_ref,
    grad_mixed_ref,
    mixed_ref,
    inverse_ref,
    query_ref,
    key_ref,
    value_ref,
    normed_ref,
    query_weight_ref,
    key_weight_ref,
    value_weight_ref,
    *refs,
):
    before_ref = refs[start - 1] if joined else None
    refs = refs[start:]
    pair_grad_ref, near_ref, cross_ref, own_ref, vectors_ref = refs[:5]
    query_grad_ref, key_grad_ref, value_grad_ref = refs[5:8]
    grad_query_scratch, grad_key_scratch, grad_value_scratch, grad_scratch = refs[-4:]
    molecule = pl.program_id(0) + base
    group = pl.program_id(1)
    _, groups, rows, width = query_ref.shape
    keys = key_ref.shape[2]
    heads = width // head_size
    factor = head_size**-0.5
    query = query_ref[molecule, group]
    key = key_ref[molecule, group]
    value = value_ref[molecule, group]
    upstream = grad_mixed_ref[molecule + first, group].astype(F32) * inverse_ref[molecule, group]
    upstream = upstream.astype(BF16)
    offset = (-(upstream.astype(F32) * mixed_ref[molecule, group])).astype(BF16)
    both = jnp.concatenate([upstream, offset], 1)
    lane = lax.broadcasted_iota(jnp.int32, (1, width), 1) // head_size
    lane_pair = lax.broadcasted_iota(jnp.int32, (1, 2 * width), 1) % width // head_size
    query_turned = jnp.transpose(query.astype(F32)).astype(BF16)
    upstream_turned = jnp.transpose(upstream.astype(F32)).astype(BF16)
    query_turned = jnp.concatenate([query_turned] * chunk, 1)
    upstream_turned = jnp.concatenate([upstream_turned] * chunk, 1)
    turned_shape = (chunk * head_size, chunk * rows)
    same = (
        lax.broadcasted_iota(jnp.int32, turned_shape, 0) // head_size
        == lax.broadcasted_iota(jnp.int32, turned_shape, 1) // rows
    )
    zero = jnp.zeros((), BF16)
    total = jnp.zeros((rows, width), F32)
    key_parts = []
    value_parts = []
    for c in range(0, heads, chunk):
        here = slice(c, c + chunk)
        feature = slice(c * head_size, (c + chunk) * head_size)
        spread = jnp.concatenate([jnp.where(lane_pair == c + t, both, zero) for t in range(chunk)], 0)
        centred = against(spread, value)
        there = pl.ds(group * heads + c, chunk)
        weights = weights_ref[molecule, there].reshape(chunk * rows, keys)
        cotangent = cotangent_ref[molecule + first, there].reshape(chunk * rows, keys)
        grad = (weights.astype(F32) * centred + cotangent.astype(F32)).astype(BF16)
        pair_grad_ref[molecule + first, there] = grad.reshape(chunk, rows, keys)
        product = dot(grad, key)
        for t in range(chunk):
            total = jnp.where(lane == c + t, product[t * rows : (t + 1) * rows], total)
        key_parts.append(dot(jnp.where(same, query_turned[feature], zero), grad))
        value_parts.append(dot(jnp.where(same, upstream_turned[feature], zero), weights))
    grad_query_scratch[group] = (total * factor).astype(BF16)
    grad_key_scratch[group] = jnp.transpose(jnp.concatenate(key_parts, 0)).astype(BF16)
    grad_value_scratch[group] = jnp.transpose(jnp.concatenate(value_parts, 0)).astype(BF16)

    if fresh:

        @pl.when((pl.program_id(0) == 0) & (group == 0))
        def _():
            vectors_ref[...] = jnp.zeros_like(vectors_ref)

    @pl.when(group == groups - 1)
    def _():
        row = place_ref[1]
        mine = pl.ds(pl.multiple_of(row * rows, rows), rows)
        join = lambda ref: jnp.concatenate([ref[t] for t in range(groups)], 1)
        grad_query = join(grad_query_scratch)
        grad_key = join(grad_key_scratch)
        grad_value = join(grad_value_scratch)
        query_grad_ref[0] = grad_query
        key_grad_ref[0] = grad_key
        value_grad_ref[0] = grad_value
        grad_scratch[...] = against(grad_key, key_weight_ref[...]) + against(
            grad_value, value_weight_ref[...]
        )
        grad_scratch[mine] += against(grad_query, query_weight_ref[...])
        grad = grad_scratch[...]
        vectors_ref[0:1] += column_sum(grad * normed_ref[molecule].astype(F32))
        vectors_ref[1:2] += column_sum(grad)
        vectors_ref[2:3] += column_sum(grad_query)
        vectors_ref[3:4] += column_sum(grad_value)
        at = lambda other: pl.ds(pl.multiple_of((row ^ other) * rows, rows), rows)
        slot = near_ref.shape[1] - 1
        near_ref[0, slot] = grad_scratch[at(1)].astype(BF16)
        near_ref[1, slot] = grad_scratch[at(3)].astype(BF16)
        if joined:
            near_ref[:, 0] = before_ref[:, 0]
        cross_ref[0] = grad_scratch[at(2)].astype(BF16)
        own_ref[0] = grad_scratch[mine]


def attention_backward(
    head_size, first, base, place, stage, cotangent, grad_mixed, parameters, held, sums, after, before
):
    weights, mixed, inverse, _, normed, query, key, value = stage
    _, head_count, rows, keys = weights.shape
    count = 1
    groups = query.shape[1]
    model_width = groups * LANES
    elements = count * head_count * rows * keys
    operands = [
        place,
        weights,
        cotangent,
        grad_mixed,
        mixed,
        inverse,
        query,
        key,
        value,
        normed,
        *parameters,
    ]
    in_specs = [near_spec()] * (len(operands) - 1)
    aliases = {}
    start = len(operands)
    if sums is not None:
        aliases = {start: 0, start + 1: 4}
        operands += [held, sums]
        in_specs += [near_spec(), near_spec()]
    operands += list(after)
    in_specs += [pl.BlockSpec(memory_space=pl.ANY)] * len(after)
    joined = before is not None
    if joined:
        operands.append(before)
        in_specs.append(near_spec())
    out_shape = [
        near(cotangent.shape, BF16),
        near((2, 1 + joined, rows, model_width), BF16),
        near((count, rows, model_width), BF16),
        near((count, rows, model_width), F32),
        near((8, model_width), F32),
        near((count, rows, model_width), BF16),
        near((count, keys, model_width), BF16),
        near((count, keys, model_width), BF16),
    ]
    out_specs = [
        near_spec(),
        near_spec(),
        near_spec(),
        near_spec(),
        near_spec(),
        near_spec(),
        near_spec(),
        near_spec(),
    ]
    return pl.pallas_call(
        functools.partial(
            backward_kernel, head_size, 4, first, base, len(operands) - start, sums is None, joined
        ),
        grid_spec=pltpu.PrefetchScalarGridSpec(
            num_scalar_prefetch=1,
            grid=(count, groups),
            in_specs=in_specs,
            out_specs=out_specs,
            scratch_shapes=[
                pltpu.VMEM((groups, rows, LANES), BF16),
                pltpu.VMEM((groups, keys, LANES), BF16),
                pltpu.VMEM((groups, keys, LANES), BF16),
                pltpu.VMEM((keys, model_width), F32),
            ],
        ),
        out_shape=out_shape,
        input_output_aliases=aliases,
        compiler_params=params(8),
        cost_estimate=pl.CostEstimate(
            flops=elements * 2 * 768, transcendentals=0, bytes_accessed=elements * 6
        ),
        name="attention_backward",
    )(*operands)


def weight_kernel(calls, stages, place_ref, *refs):
    hidden_refs = refs[:stages]
    grads = refs[stages : stages + 3 * calls]
    out_refs = refs[stages + 3 * calls : -1]
    total_ref = refs[-1]
    rows = grads[0].shape[1]
    row = place_ref[1]
    core = place_ref[2]
    mine = pl.ds(pl.multiple_of(row * rows, rows), rows)
    hidden = [(ref, m) for ref in hidden_refs for m in range(ref.shape[0])]
    width = hidden_refs[0].shape[2]
    own = jnp.concatenate([ref[m, mine] for ref, m in hidden], 0)
    every = jnp.concatenate([ref[m] for ref, m in hidden], 0)
    own = jnp.transpose(own.astype(F32)).astype(BF16)
    every = jnp.transpose(every.astype(F32)).astype(BF16)
    for j, left in enumerate((own, every, every)):
        right = jnp.concatenate([grads[3 * c + j][...].reshape(-1, width) for c in range(calls)], 0)
        total_ref[...] = dot(left, right).reshape(total_ref.shape)
        send_ref, keep_ref = out_refs
        send_ref[:, j] = total_ref[:, 1 - core].astype(BF16)
        keep_ref[:, j] = total_ref[:, core].astype(BF16)


def store_kernel(source_ref, *refs):
    target_ref, semaphore = refs[-2:]
    copy = pltpu.make_async_copy(source_ref, target_ref, semaphore)
    copy.start()
    copy.wait()


def store(array, after):
    return pl.pallas_call(
        store_kernel,
        in_specs=[near_spec()] + [pl.BlockSpec(memory_space=pl.ANY)] * len(after),
        out_specs=pl.BlockSpec(memory_space=pltpu.HBM),
        out_shape=pltpu.HBM(array.shape, array.dtype),
        scratch_shapes=[pltpu.SemaphoreType.DMA],
        compiler_params=params(),
        name="store",
    )(array, *after)


def swap(value, axis, mask):
    size = lax.axis_size(axis)
    return lax.ppermute(value, axis, [(i, i ^ mask) for i in range(size)])


VECTOR_ROWS = 8


def first_sum_kernel(counts, place_ref, *refs):
    terms = sum(counts)
    mine_ref, other_ref = refs[terms : terms + 2]
    along_x_ref, along_y_ref, keep_x_ref, keep_y_ref, vectors_ref = refs[terms + 2 :]
    x, y = place_ref[3], place_ref[4]
    half = along_x_ref.shape[1]
    size = keep_x_ref.shape[1]
    low, high = slice(0, half), slice(half, None)
    row = 0
    start = 0
    for count in counts:
        group = refs[start : start + count]
        start += count
        for s in range(group[0].shape[1]):
            rows = group[0].shape[2]

            def total(at, lanes):
                values = [r[at, s, :, lanes].astype(F32) for r in group]
                return functools.reduce(lambda a, b: a + b, values)

            for k in range(2):
                to = slice(k * size + row, k * size + row + rows)
                here = slice(row, row + rows)
                along_x_ref[to] = total(2 * k + (1 - x), low).astype(BF16)
                keep_x_ref[k, here] = total(2 * k + x, low)
                along_y_ref[to] = total(2 * (1 - y) + k, high).astype(BF16)
                keep_y_ref[k, here] = total(2 * y + k, high)
            row += rows
    vectors = (mine_ref[...] + other_ref[...]).astype(BF16)
    vectors_ref[...] = vectors
    put_vectors(vectors, along_x_ref, along_y_ref)


def put_vectors(vectors, low_ref, high_ref):
    half = vectors.shape[1] // 2
    low_ref[low_ref.shape[0] - VECTOR_ROWS :] = vectors[:, :half]
    high_ref[high_ref.shape[0] - VECTOR_ROWS :] = vectors[:, half:]


def get_vectors(low_ref, high_ref):
    low = low_ref[low_ref.shape[0] - VECTOR_ROWS :]
    return jnp.concatenate([low, high_ref[high_ref.shape[0] - VECTOR_ROWS :]], 1).astype(F32)


def second_sum_kernel(
    place_ref,
    keep_x_ref,
    came_x_ref,
    keep_y_ref,
    came_y_ref,
    vectors_ref,
    send_y_ref,
    send_x_ref,
    left_x_ref,
    left_y_ref,
    vectors_out_ref,
):
    size = keep_x_ref.shape[1]
    for keep, came, send, left, me in (
        (keep_x_ref, came_x_ref, send_y_ref, left_x_ref, place_ref[4]),
        (keep_y_ref, came_y_ref, send_x_ref, left_y_ref, place_ref[3]),
    ):
        at = lambda i: pl.ds(pl.multiple_of(i * size, size), size)
        send[:size] = (keep[1 - me] + came[at(1 - me)].astype(F32)).astype(BF16)
        left[...] = keep[me] + came[at(me)].astype(F32)
    vectors = vectors_ref[...].astype(F32) + get_vectors(came_x_ref, came_y_ref)
    vectors = vectors.astype(BF16)
    vectors_out_ref[...] = vectors
    put_vectors(vectors, send_y_ref, send_x_ref)


def third_sum_kernel(left_x_ref, came_x_ref, left_y_ref, came_y_ref, vectors_ref, total_ref):
    size, half = left_x_ref.shape
    total_ref[:size, :half] = (left_x_ref[...] + came_x_ref[:size].astype(F32)).astype(BF16)
    total_ref[:size, half:] = (left_y_ref[...] + came_y_ref[:size].astype(F32)).astype(BF16)
    vectors = vectors_ref[...].astype(F32) + get_vectors(came_x_ref, came_y_ref)
    total_ref[size : size + VECTOR_ROWS] = vectors.astype(BF16)
    filled = size + VECTOR_ROWS
    if filled < total_ref.shape[0]:
        total_ref[filled:] = jnp.zeros((total_ref.shape[0] - filled, 2 * half), BF16)


def third_cut_kernel(place_ref, *refs):
    third_sum_kernel(*refs[:-1])
    total_ref, sent_ref = refs[-2:]
    half = sent_ref.shape[0]
    away = pl.multiple_of((1 - (place_ref[1] & 1)) * half, half)
    sent_ref[...] = total_ref[pl.ds(away, half)]


def near_sum_kernel(place_ref, total_ref, came_ref, out_ref):
    half = came_ref.shape[0]
    mine = total_ref[pl.ds(pl.multiple_of((place_ref[1] & 1) * half, half), half)]
    out_ref[...] = (mine.astype(F32) + came_ref[...].astype(F32)).astype(BF16)


def far_sum_kernel(left_ref, right_ref, out_ref):
    at = slice(0, out_ref.shape[0])
    out_ref[...] = (left_ref[at].astype(F32) + right_ref[at].astype(F32)).astype(BF16)


def add_kernel(left_ref, right_ref, out_ref):
    out_ref[...] = (left_ref[...].astype(F32) + right_ref[...].astype(F32)).astype(out_ref.dtype)


def join_rows(place, mine_ref, other_ref, out_ref):
    part = mine_ref.shape[0]
    out_ref[pl.ds(pl.multiple_of(place * part, part), part)] = mine_ref[...]
    out_ref[pl.ds(pl.multiple_of((1 - place) * part, part), part)] = other_ref[...]


def finish_kernel(ratio, place_ref, low_ref, came_ref, mine_ref, other_ref, *refs):
    query_ref, key_ref, value_ref, outer_ref, inner_ref, out_ref = refs[:6]
    tail_refs, dense_refs, wide_ref, total_scratch, row_scratch = refs[6:10], refs[10:14], *refs[14:]
    rows, width = out_ref.shape
    total = lambda at: low_ref[at].astype(F32) + came_ref[at].astype(F32)
    for s, ref in enumerate((query_ref, key_ref, value_ref)):
        ref[...] = total(slice(s * rows, (s + 1) * rows))
    put_slices(total(slice(3 * rows, 3 * rows + VECTOR_ROWS)), place_ref[0], tail_refs)
    join_rows(place_ref[1] & 1, mine_ref, other_ref, total_scratch)
    outer_ref[...] = total_scratch[: ratio * rows].astype(F32)
    for s in range(ratio):
        at = (ratio + s) * rows
        inner_ref[:, s * width : (s + 1) * width] = total_scratch[at : at + rows].astype(F32)
    at = 2 * ratio * rows
    out_ref[...] = total_scratch[at : at + rows].astype(F32)
    vectors = total_scratch[at + rows : at + rows + VECTOR_ROWS].astype(F32)
    put_slices(vectors, place_ref[0], dense_refs)
    row_scratch[...] = vectors
    size = wide_ref.shape[0]
    start = place_ref[0] * size
    row = row_scratch[pl.ds(len(dense_refs) + start // width, 1)]
    wide_ref[...] = pltpu.roll(row, lax.rem(width - lax.rem(start, width), width), 1)[0, :size]


def put_slices(vectors, index, refs):
    width, size = vectors.shape[1], refs[0].shape[0]
    turned = pltpu.roll(vectors, lax.rem(width - index * size, width), 1)
    for i, ref in enumerate(refs):
        ref[...] = turned[i, :size]


def small_call(kernel, place, operands, out_shapes, name, after=(), inside=True, scratch=(), mib=4, size=None):
    ahead = 0 if place is None else 1
    count = len(operands)

    def body(*refs):
        kernel(*refs[: ahead + count], *refs[ahead + count + len(after) :])

    if size is None:
        size = sum(math.prod(a.shape) * a.dtype.itemsize for a in list(operands) + list(out_shapes))
    return pl.pallas_call(
        body,
        grid_spec=pltpu.PrefetchScalarGridSpec(
            num_scalar_prefetch=ahead,
            grid=(1,),
            in_specs=[near_spec() for a in operands] + [pl.BlockSpec(memory_space=pl.ANY)] * len(after),
            out_specs=[near_spec() for s in out_shapes],
            scratch_shapes=list(scratch),
        ),
        out_shape=[near(s.shape, s.dtype) if inside else s for s in out_shapes],
        compiler_params=params(mib),
        cost_estimate=pl.CostEstimate(flops=0, transcendentals=0, bytes_accessed=size),
        name=name,
    )(*(() if place is None else (place,)), *operands, *after)


def sum_core(place, groups, vectors, name, after=()):
    groups = [list(g) + [swap(a, "batch", 1) for a in sent] for g, sent in groups]
    vectors_other = swap(vectors, "batch", 1)
    _, _, rows, width = groups[0][0].shape
    size = sum(g[0].shape[1] for g in groups) * rows
    half = width // 2
    counts = tuple(len(g) for g in groups)
    message = shape_of((2 * size + VECTOR_ROWS, half), BF16)
    kept = shape_of((2, size, half), F32)
    along_x, along_y, keep_x, keep_y, vectors = small_call(
        functools.partial(first_sum_kernel, counts),
        place,
        [a for g in groups for a in g] + [vectors, vectors_other],
        [message, message, kept, kept, shape_of(vectors.shape, BF16)],
        name + "_sum_core",
        after,
    )
    came_x, came_y = swap(along_x, "batch", 2), swap(along_y, "batch", 4)
    return (keep_x, came_x, keep_y, came_y, vectors), along_x


def sum_first(place, pieces, name, after=()):
    keep_x, _, _, _, vectors = pieces
    _, size, half = keep_x.shape
    message = shape_of((size + VECTOR_ROWS, half), BF16)
    kept = shape_of((size, half), F32)
    send_y, send_x, left_x, left_y, vectors = small_call(
        second_sum_kernel,
        place,
        pieces,
        [message, message, kept, kept, shape_of(vectors.shape, BF16)],
        name + "_sum_first",
        after,
    )
    came_x, came_y = swap(send_y, "batch", 4), swap(send_x, "batch", 2)
    return (left_x, came_x, left_y, came_y, vectors), send_y


def sum_second(pieces, name, after=()):
    size, half = pieces[0].shape
    rows = -(-(size + VECTOR_ROWS) // 32) * 32
    shape = shape_of((rows, 2 * half), BF16)
    return small_call(third_sum_kernel, None, pieces, [shape], name + "_sum_second", after)[0]


def sum_second_cut(place, pieces, name, after=()):
    size, half = pieces[0].shape
    rows = -(-(size + VECTOR_ROWS) // 32) * 32
    total, sent = small_call(
        third_cut_kernel,
        place,
        pieces,
        [shape_of((rows, 2 * half), BF16), shape_of((rows // 2, 2 * half), BF16)],
        name + "_sum_second",
        after,
    )
    return total, swap(sent, "rows", 1)


def batch_slices_any(groups, vectors):
    me = lax.axis_index("batch")
    bits = lax.axis_size("batch").bit_length() - 1
    pieces = []
    for kept, sent in groups:
        values = [a.astype(F32) for a in kept] + [swap(a, "batch", 1).astype(F32) for a in sent]
        pieces.append(functools.reduce(lambda a, b: a + b, values))
    total = jnp.concatenate(pieces, 1)
    total = total.reshape((2,) * (bits - 1) + total.shape[1:])
    for bit in range(bits - 1, 0, -1):
        mine = (me >> bit) & 1
        sent = lax.dynamic_index_in_dim(total, 1 - mine, 0, keepdims=False).astype(BF16)
        total = lax.dynamic_index_in_dim(total, mine, 0, keepdims=False)
        total = total + swap(sent, "batch", 1 << bit).astype(F32)
    total = lax.psum(total.astype(BF16), "rows").astype(F32)
    return total, lax.psum(vectors, ("batch", "rows"))


def cross_kernel(count, *refs):
    out_ref = refs[-1]
    came = [(ref, i) for ref in refs[count:-1] for i in range(ref.shape[1])]
    for m, (term, (ref, i)) in enumerate(zip(refs[:count], came)):
        out_ref[m] = (term[0].astype(F32) + ref[1, i].astype(F32)).astype(BF16)


def cross_sum(terms, came, name, after=()):
    shape = (len(terms),) + terms[0].shape[1:]
    return small_call(
        functools.partial(cross_kernel, len(terms)),
        None,
        list(terms) + list(came),
        [shape_of(shape, BF16)],
        name,
        after,
    )[0]


def final_kernel(count, *refs):
    owns, nears, crosses = refs[:count], refs[count : 2 * count], refs[2 * count : 3 * count]
    atoms_ref, gain_ref, shift_ref, grad_middle_ref, out_ref = refs[3 * count :]
    gain = as_row(gain_ref)
    shift = as_row(shift_ref)
    for m in range(count):
        grad = owns[m][0] + nears[m][...].astype(F32) + crosses[m][...].astype(F32)
        _, normed, inverse = norm_forward(atoms_ref[m].astype(F32), gain, shift)
        result = grad_middle_ref[m] + norm_backward(grad, normed, inverse, gain)
        out_ref[m] = result.astype(BF16)


def first_norm_backward(owns, nears, crosses, others, after=()):
    count = len(owns)
    arrays = [a for a, _ in nears + crosses]
    spots = [at for _, at in nears + crosses]

    def kernel(*refs):
        picked = [r.at[at] for r, at in zip(refs[count : 3 * count], spots)]
        final_kernel(count, *refs[:count], *picked, *refs[3 * count :])

    return small_call(
        kernel,
        None,
        list(owns) + arrays + list(others),
        [shape_of(others[0].shape, BF16)],
        "first_norm_backward",
        after,
        inside=False,
    )[0]


def shards(
    atoms,
    pair_bias,
    lengths,
    first_gain,
    first_shift,
    query_weight,
    query_bias,
    key_weight,
    value_weight,
    value_bias,
    out_weight,
    out_bias,
    second_gain,
    second_shift,
    inner_weight,
    inner_bias,
    outer_weight,
    outer_bias,
    atoms_cotangent,
    pair_cotangent,
):
    molecules, rows, model_width = atoms.shape
    head_count = pair_bias.shape[1]
    head_size = model_width // head_count
    batch_count = lax.axis_size("batch")
    batch_index = lax.axis_index("batch")
    row = lax.axis_index("rows")
    (
        atoms_far,
        pair_bias,
        first_gain,
        first_shift,
        query_weight,
        query_bias,
        key_weight,
        value_weight,
        value_bias,
        out_weight,
        out_bias,
        second_gain,
        second_shift,
        inner_weight,
        inner_bias,
        outer_weight,
        outer_bias,
        atoms_cotangent,
        pair_cotangent,
    ) = [
        pltpu.with_memory_space_constraint(a, pltpu.HBM)
        for a in (
            atoms,
            pair_bias,
            first_gain,
            first_shift,
            query_weight,
            query_bias,
            key_weight,
            value_weight,
            value_bias,
            out_weight,
            out_bias,
            second_gain,
            second_shift,
            inner_weight,
            inner_bias,
            outer_weight,
            outer_bias,
            atoms_cotangent,
            pair_cotangent,
        )
    ]
    place = jnp.stack(
        [batch_index, row, batch_index & 1, (batch_index >> 1) & 1, (batch_index >> 2) & 1]
    ).astype(jnp.int32)
    line = lambda v: v
    count = molecules // STAGES
    stages = []
    pair_out = jnp.zeros((1,), BF16)
    one = swap(atoms, "rows", 1)
    (
        pair_near,
        query_near,
        key_near,
        value_near,
        first_gain,
        first_shift,
        query_bias,
        value_bias,
        out_bias,
        second_gain,
        second_shift,
        inner_bias,
        outer_bias,
        out_weight,
        inner_weight,
        outer_weight,
        atoms_cotangent,
    ) = load(
        [
            pair_bias,
            query_weight,
            key_weight,
            value_weight,
            first_gain,
            first_shift,
            query_bias,
            value_bias,
            out_bias,
            second_gain,
            second_shift,
            inner_bias,
            outer_bias,
            out_weight,
            inner_weight,
            outer_weight,
            atoms_cotangent,
        ],
        "load_first",
        None,
        (place,),
    )
    projected = near_half(
        head_size,
        STAGES,
        place,
        atoms_far,
        one,
        (
            first_gain,
            first_shift,
            query_near,
            query_bias,
            key_near,
            value_near,
            value_bias,
        ),
        (),
    )
    mine = [atoms[:count], projected[-1]]
    gathered = [[swap(a, "rows", mask) for mask in (2, 3)] for a in mine]
    for stage in range(STAGES):
        pair_out, kept, _ = attention_forward(
            head_size,
            stage * count,
            place,
            lengths,
            gathered[stage],
            pair_near,
            (first_gain, first_shift, key_near, value_near, value_bias),
            projected[5 * stage : 5 * stage + 5],
            pair_out,
            [],
        )
        stages.append(kept)
    (
        atoms_out,
        send,
        keep,
        grad_middle,
        grad_mixed,
        dense_vectors,
        pair_cotangent,
    ) = dense(
        place,
        [s[1] for s in stages],
        atoms,
        atoms_cotangent,
        (
            out_weight,
            line(out_bias),
            line(second_gain),
            line(second_shift),
            inner_weight,
            line(inner_bias),
            outer_weight,
            line(outer_bias),
        ),
        batch_count,
        pair_cotangent,
    )
    pairs = batch_count // 2
    own_rows = model_width // batch_count
    dense_groups = [([keep], [send])]
    usual = batch_count == 8

    def backward(molecule, held, sums, after, before=None):
        stage = molecule // count
        return attention_backward(
            head_size,
            stage * count,
            molecule % count,
            place,
            stages[stage],
            pair_cotangent,
            grad_mixed,
            (query_near, key_near, value_near),
            held,
            sums,
            after,
            before,
        )

    pair_grad, near0, cross0, own0, sums, *grads0 = backward(0, None, None, [])
    after = []
    if usual:
        dense_pieces, held = sum_core(place, dense_groups, dense_vectors, "dense", (own0,))
        after = [held]
    else:
        dense_total, dense_vectors = batch_slices_any(dense_groups, dense_vectors)
    pair_grad, near1, cross1, own1, sums, *grads1 = backward(1, pair_grad, sums, after, near0)
    near1 = swap(near1, "rows", 1)
    pair_grad, near2, cross2, own2, sums, *grads2 = backward(2, pair_grad, sums, [own1])
    near2 = swap(near2, "rows", 1)
    cross0 = cross_sum([cross0, cross1], [near1], "cross_first", (own2,))
    far0 = swap(cross0, "rows", 2)
    pair_grad, near3, cross3, own3, tail_vectors, *grads3 = backward(3, pair_grad, sums, [cross0])
    near3 = swap(near3, "rows", 1)
    owns = [own0, own1, own2, own3]
    after = [far0]
    if usual:
        dense_pieces, held = sum_first(place, dense_pieces, "dense", (own3,))
        after.append(held)
    part = shape_of((pairs, 3, own_rows, model_width), BF16)
    send, keep = small_call(
        functools.partial(weight_kernel, 4, STAGES),
        place,
        [s[3] for s in stages] + grads0 + grads1 + grads2 + grads3,
        [part] * 2,
        "attention_weights",
        after,
        scratch=[pltpu.VMEM((pairs, 2, own_rows, model_width), F32)],
        mib=14,
    )
    groups = [([keep], [send])]
    matrix = shape_of((own_rows, model_width), F32)
    ratio = inner_weight.shape[1] // model_width
    vector = shape_of((own_rows,), F32)
    finish = (atoms, line(first_gain), line(first_shift), grad_middle)
    if usual:
        pieces, held = sum_core(place, groups, tail_vectors, "tail")
        cross2 = cross_sum([cross2, cross3], [near2, near3], "cross_second", (held,))
        far2 = swap(cross2, "rows", 2)
        dense_total, came = sum_second_cut(place, dense_pieces, "dense", (cross2,))
        pieces, held = sum_first(place, pieces, "tail", (dense_total,))
        start = dense_total.shape[0] // 2
        mine = small_call(
            near_sum_kernel, place, [dense_total, came], [came], "dense_near_sum", (held, far2)
        )[0]
        far = swap(mine, "rows", 2)
        total = sum_second(pieces, "tail")
        tail_came = swap(total, "rows", 1)
        total = small_call(add_kernel, None, [total, tail_came], [total], "tail_near_sum")[0]
        tail_came = swap(total, "rows", 2)
        part = shape_of((start, model_width), BF16)
        mine = small_call(far_sum_kernel, None, [mine, far], [part], "dense_far_sum", (total,))[0]
        other = swap(mine, "rows", 1)
        pair_grad = store(pair_grad, (mine,))
        atoms_grad = first_norm_backward(
            owns,
            [(near1, (0, 0)), (near1, (0, 1)), (near2, (0, 0)), (near3, (0, 0))],
            [(far0, 0), (far0, 1), (far2, 0), (far2, 1)],
            finish,
            (mine,),
        )
        outs = small_call(
            functools.partial(finish_kernel, ratio),
            place,
            [total, tail_came, mine, other],
            [matrix] * 3
            + [
                shape_of((ratio * own_rows, model_width), F32),
                shape_of((own_rows, ratio * model_width), F32),
                matrix,
            ]
            + [vector] * 8
            + [shape_of((ratio * own_rows,), F32)],
            "finish",
            inside=False,
            scratch=[
                pltpu.VMEM((2 * part.shape[0], model_width), BF16),
                pltpu.VMEM((VECTOR_ROWS, model_width), F32),
            ],
        )
        query_grad, key_grad, value_grad, outer_grad, inner_grad, out_grad = outs[:6]
        tail_parts, dense_parts = outs[6:10], outs[10:]
    else:
        pair_grad = store(pair_grad, ())
        far2 = swap(cross_sum([cross2, cross3], [near2, near3], "cross_second"), "rows", 2)
        atoms_grad = first_norm_backward(
            owns,
            [(near1, (0, 0)), (near1, (0, 1)), (near2, (0, 0)), (near3, (0, 0))],
            [(far0, 0), (far0, 1), (far2, 0), (far2, 1)],
            finish,
        )
        total, tail_vectors = batch_slices_any(groups, tail_vectors)
        query_grad, key_grad, value_grad = total[0], total[1], total[2]
        outer_grad = dense_total[:ratio].reshape(-1, model_width)
        inner_grad = dense_total[ratio : 2 * ratio].transpose(1, 0, 2).reshape(own_rows, -1)
        out_grad = dense_total[2 * ratio]
        part = lambda v: lax.dynamic_slice_in_dim(
            v, batch_index * (v.shape[0] // batch_count), v.shape[0] // batch_count
        )
        tail_parts = [part(v) for v in tail_vectors[:4]]
        dense_parts = [part(v) for v in dense_vectors[:4]] + [part(dense_vectors[4:].reshape(-1))]
    return (
        atoms_out,
        pair_out,
        atoms_grad,
        pair_grad,
        tail_parts[0],
        tail_parts[1],
        query_grad,
        tail_parts[2],
        key_grad,
        value_grad,
        tail_parts[3],
        out_grad,
        dense_parts[3],
        dense_parts[1],
        dense_parts[2],
        inner_grad,
        dense_parts[4],
        outer_grad,
        dense_parts[0],
    )


def solution(mesh):
    tokens = P("batch", "rows", None)
    pairs = P("batch", None, "rows", None)
    vector = P("batch")
    matrix = P("batch", None)
    return jax.shard_map(
        shards,
        mesh=mesh,
        in_specs=(tokens, pairs, P("batch")) + (P(),) * 15 + (tokens, pairs),
        out_specs=(
            tokens,
            pairs,
            tokens,
            pairs,
            vector,
            vector,
            matrix,
            vector,
            matrix,
            matrix,
            vector,
            matrix,
            vector,
            vector,
            vector,
            matrix,
            vector,
            matrix,
            vector,
        ),
        check_vma=False,
    )
```
